32 devices in a mesh: fsdp: 8 (over y, x, core), seq: 4 (over z).
Axes of the slice: x: 2, y: 2, z: 4, core: 2. Of those that a mesh axis runs over, the one named last changes fastest.
Arguments:
- tokens: bfloat16 [8192, 1024], P(('fsdp', 'seq')), may hold values from -6 to 6
- clip_lengths: int32 [8, 3], P('fsdp'), may hold values from 1 to 896, 1024 in all within a row
- target_pos: int32 [8, 4, 128], P('fsdp', 'seq'), may hold values from 0 to 255, as said below
- out_grad: bfloat16 [8192, 384], P(('fsdp', 'seq')), may hold values from -6 to 6
- norm1_gain: bfloat16 [1024], P('fsdp'), may hold values from 0.25 to 1.75
- norm1_bias: bfloat16 [1024], P('fsdp'), may hold values from -1.75 to 1.75
- w_qkv: bfloat16 [1024, 3072], P('fsdp'), may hold values from -0.1875 to 0.1875
- w_out: bfloat16 [1024, 1024], P('fsdp'), may hold values from -3.5 to 3.5
- norm2_gain: bfloat16 [1024], P('fsdp'), may hold values from 0.25 to 1.75
- norm2_bias: bfloat16 [1024], P('fsdp'), may hold values from -1.75 to 1.75
- w_fc1: bfloat16 [1024, 4096], P('fsdp'), may hold values from -0.1875 to 0.1875
- w_fc2: bfloat16 [4096, 1024], P('fsdp'), may hold values from -0.09375 to 0.09375
- w_embed: bfloat16 [1024, 384], P('fsdp'), may hold values from -0.1875 to 0.1875
- mask_token: bfloat16 [384], P('fsdp'), may hold values from -6 to 6
- pred_norm1_gain: bfloat16 [384], P('fsdp'), may hold values from 0.25 to 1.75
- pred_norm1_bias: bfloat16 [384], P('fsdp'), may hold values from -1.75 to 1.75
- pred_qkv: bfloat16 [384, 1152], P('fsdp'), may hold values from -0.3125 to 0.3125
- pred_out: bfloat16 [384, 384], P('fsdp'), may hold values from -6 to 6
- pred_norm2_gain: bfloat16 [384], P('fsdp'), may hold values from 0.25 to 1.75
- pred_norm2_bias: bfloat16 [384], P('fsdp'), may hold values from -1.75 to 1.75
- pred_fc1: bfloat16 [384, 1536], P('fsdp'), may hold values from -0.3125 to 0.3125
- pred_fc2: bfloat16 [1536, 384], P('fsdp'), may hold values from -0.15625 to 0.15625
Outputs:
- context_out: bfloat16 [8192, 1024], P(('fsdp', 'seq'))
- predicted: bfloat16 [8192, 384], P(('fsdp', 'seq'))
- token_grad: bfloat16 [8192, 1024], P(('fsdp', 'seq'))
- grad_norm1_gain: float32 [1024], P('fsdp')
- grad_norm1_bias: float32 [1024], P('fsdp')
- grad_w_qkv: float32 [1024, 3072], P('fsdp')
- grad_w_out: float32 [1024, 1024], P('fsdp')
- grad_norm2_gain: float32 [1024], P('fsdp')
- grad_norm2_bias: float32 [1024], P('fsdp')
- grad_w_fc1: float32 [1024, 4096], P('fsdp')
- grad_w_fc2: float32 [4096, 1024], P('fsdp')
- grad_w_embed: float32 [1024, 384], P('fsdp')
- grad_mask_token: float32 [384], P('fsdp')
- grad_pred_norm1_gain: float32 [384], P('fsdp')
- grad_pred_norm1_bias: float32 [384], P('fsdp')
- grad_pred_qkv: float32 [384, 1152], P('fsdp')
- grad_pred_out: float32 [384, 384], P('fsdp')
- grad_pred_norm2_gain: float32 [384], P('fsdp')
- grad_pred_norm2_bias: float32 [384], P('fsdp')
- grad_pred_fc1: float32 [384, 1536], P('fsdp')
- grad_pred_fc2: float32 [1536, 384], P('fsdp')
The draws below stay inside these ranges and needn't reach their ends.
Inputs may be any that keep to these rules, and one draw needn't show every extreme that they name: `clip_lengths`: each row sums to 1024; the longest clip of every row has exactly 896 tokens. `target_pos`: the 128 entries of one device's block are distinct rows of its 256.
All inputs are finite; a program needn't handle non-finite values.
Results may differ from the reference program's by a relative error of at most 0.02.
Values may be sent and summed in bfloat16 or wider, within the bound.
A program may use at most 256 MiB of HBM per device.

```python
import math
import jax
import jax.numpy as jnp
import numpy as np
from jax import lax

D = 1024
HEADS = 16
FF = 4096
PD = 384
P_HEADS = 12
PFF = 1536
TOK_DEV = 256
CLIPS = 3
GROUPS = 8
SPLITS = 4
GROUP = 1024
MOST = 896
TGT = 128
TOKENS = 8192


def pick_rows(one_key):
    return jax.random.permutation(one_key, TOK_DEV)[:TGT]


def draw_target_pos(key, part):
    key_list = jax.random.split(key, GROUPS * SPLITS)
    picks = jax.vmap(pick_rows)(key_list)
    return picks.reshape(GROUPS, SPLITS, TGT).astype(jnp.int32)


def shard_levels(key, shape, pieces, least, largest):
    loudness, own = 1.0, jax.random.fold_in(key, 6)
    for position, shards_of in pieces:
        steps = jnp.exp(jax.random.uniform(jax.random.fold_in(own, position), (shards_of,), jnp.float32, least / len(pieces), largest / len(pieces)))
        loudness = loudness * jnp.repeat(steps, shape[position] // shards_of).reshape([-1 if axis == position else 1 for axis in range(len(shape))])
    return loudness


def profile(count, total, bound, skew):
    portions = [(1 << 20) // math.isqrt(rank ** skew) + 1 for rank in range(2, count + 1)]
    rest, given = total - bound - (count - 1), [1] * (count - 1)
    while rest > 0:
        free = [i for i in range(count - 1) if given[i] < bound]
        mass, left = sum([portions[i] for i in free]), rest
        for i in free:
            extra = min(bound - given[i], max(1, left * portions[i] // mass), rest)
            given[i] = given[i] + extra
            rest = rest - extra
    return np.array([bound] + given)


def ragged_sizes(key, amount, total, most, lean):
    if amount == 2:
        one = jax.random.randint(key, (), max(1, total - most), min(most, total - 1) + 1)
        return jnp.stack([one, total - one])
    tallies = jnp.asarray(profile(amount, total, most, lean), jnp.int32)
    pairs = (amount - 1) // 2
    donor, sink = tallies[1:1 + 2 * pairs:2], tallies[2:2 + 2 * pairs:2]
    margin = jnp.minimum(donor - 1, most - sink)
    shifted = jax.random.randint(jax.random.fold_in(key, 1), (pairs,), 0, 1 << 20) % (margin + 1)
    tallies = tallies.at[1:1 + 2 * pairs:2].set(donor - shifted).at[2:2 + 2 * pairs:2].set(sink + shifted)
    return tallies[jax.random.permutation(jax.random.fold_in(key, 2), amount)]


def normal_values(own_key, extent, scale, most, pieces=(), kind=jnp.bfloat16):
    entries = jax.random.normal(own_key, extent, jnp.float32) * scale
    if len(pieces) > 0:
        entries = shard_levels(own_key, extent, pieces, -0.22, 0.18) * entries
    return jnp.clip(entries, min=-most, max=most).astype(kind)


def setup_inputs(seed: int = 0) -> dict:
    arg_keys = jax.random.split(jax.random.key(seed), 23)
    tokens = normal_values(arg_keys[0], (TOKENS, D), 1.0, 6.0, ((0, 32),))
    clip_lengths = jax.vmap(lambda own: ragged_sizes(own, CLIPS, GROUP, MOST, 1))(jax.random.split(arg_keys[1], GROUPS)).reshape((GROUPS, CLIPS)).astype(jnp.int32)
    target_pos = draw_target_pos(jax.random.fold_in(arg_keys[22], 71), 0)
    out_grad = normal_values(arg_keys[3], (TOKENS, PD), 1.0, 6.0, ((0, 32),))
    norm1_gain = jnp.clip(1.0 + 0.15 * jax.random.normal(arg_keys[4], (D,), jnp.float32), 0.25, 1.75).astype(jnp.bfloat16)
    norm1_bias = normal_values(arg_keys[5], (D,), 0.3, 1.75, ((0, 8),))
    w_qkv = normal_values(arg_keys[6], (D, 3 * D), D ** -0.5, 0.1875, ((0, 8),))
    w_out = normal_values(arg_keys[7], (D, D), (max(1, 3 * D // GROUP)) ** -0.5, 3.5, ((0, 8),))
    norm2_gain = jnp.clip(1.0 + 0.15 * jax.random.normal(arg_keys[8], (D,), jnp.float32), 0.25, 1.75).astype(jnp.bfloat16)
    norm2_bias = normal_values(arg_keys[9], (D,), 0.3, 1.75, ((0, 8),))
    w_fc1 = normal_values(arg_keys[10], (D, FF), D ** -0.5, 0.1875, ((0, 8),))
    w_fc2 = normal_values(arg_keys[11], (FF, D), FF ** -0.5, 0.09375, ((0, 8),))
    w_embed = normal_values(arg_keys[12], (D, PD), D ** -0.5, 0.1875, ((0, 8),))
    mask_token = normal_values(arg_keys[13], (PD,), 1.0, 6.0, ((0, 8),))
    pred_norm1_gain = jnp.clip(1.0 + 0.15 * jax.random.normal(arg_keys[14], (PD,), jnp.float32), 0.25, 1.75).astype(jnp.bfloat16)
    pred_norm1_bias = normal_values(arg_keys[15], (PD,), 0.3, 1.75, ((0, 8),))
    pred_qkv = normal_values(arg_keys[16], (PD, 3 * PD), PD ** -0.5, 0.3125, ((0, 8),))
    pred_out = normal_values(arg_keys[17], (PD, PD), (max(1, 3 * PD // GROUP)) ** -0.5, 6.0, ((0, 8),))
    pred_norm2_gain = jnp.clip(1.0 + 0.15 * jax.random.normal(arg_keys[18], (PD,), jnp.float32), 0.25, 1.75).astype(jnp.bfloat16)
    pred_norm2_bias = normal_values(arg_keys[19], (PD,), 0.3, 1.75, ((0, 8),))
    pred_fc1 = normal_values(arg_keys[20], (PD, PFF), PD ** -0.5, 0.3125, ((0, 8),))
    pred_fc2 = normal_values(arg_keys[21], (PFF, PD), PFF ** -0.5, 0.15625, ((0, 8),))
    return dict(tokens=tokens, clip_lengths=clip_lengths, target_pos=target_pos, out_grad=out_grad, norm1_gain=norm1_gain, norm1_bias=norm1_bias, w_qkv=w_qkv, w_out=w_out, norm2_gain=norm2_gain, norm2_bias=norm2_bias, w_fc1=w_fc1, w_fc2=w_fc2, w_embed=w_embed, mask_token=mask_token, pred_norm1_gain=pred_norm1_gain, pred_norm1_bias=pred_norm1_bias, pred_qkv=pred_qkv, pred_out=pred_out, pred_norm2_gain=pred_norm2_gain, pred_norm2_bias=pred_norm2_bias, pred_fc1=pred_fc1, pred_fc2=pred_fc2)


@jax.custom_vjp
def low(v):
    return lax.optimization_barrier(v.astype(jnp.bfloat16)).astype(jnp.float32)

@jax.custom_vjp
def low_back(v):
    return v

def low_keep(v):
    return (low(v), None)

def low_pass(kept, grad):
    return (grad,)

def back_keep(v):
    return (v, None)

def back_low(kept, grad):
    return (low(grad),)
low.defvjp(low_keep, low_pass)
low_back.defvjp(back_keep, back_low)
EPSILON = 1e-06
NEG_FILL = -1e+30
HIGH = lax.Precision.HIGHEST

def product_high(left, right):
    return jnp.dot(left, right, precision=HIGH, preferred_element_type=jnp.float32)

def layer_norm(values, norm_gain, norm_shift):
    center = values - lax.optimization_barrier(jnp.mean(values, axis=-1, keepdims=True))
    spread = lax.optimization_barrier(jnp.mean(center * center, axis=-1, keepdims=True))
    return center * lax.rsqrt(spread + EPSILON) * norm_gain + norm_shift

def position_table(positions, table_width):
    half_width = table_width // 2
    angle_rates = jnp.exp(jnp.arange(half_width, dtype=jnp.float32) * (-2.0 * math.log(10000.0) / table_width))
    angles = positions.astype(jnp.float32)[:, None] * angle_rates[None, :]
    return jnp.concatenate([jnp.sin(angles), jnp.cos(angles)], axis=1)

def block_forward(residual, norm_params, w_qkv, w_out, w_up, w_down, head_count, clip_of):
    row_count, model_width = residual.shape
    head_size = model_width // head_count
    normed = low(layer_norm(residual, norm_params[:, 0], norm_params[:, 1]))
    qkv = low(low_back(product_high(normed, w_qkv)))
    queries = qkv[:, :model_width].reshape(row_count, head_count, head_size)
    key_part = qkv[:, model_width:2 * model_width].reshape(row_count, head_count, head_size)
    value_part = qkv[:, 2 * model_width:].reshape(row_count, head_count, head_size)
    scores = low_back(jnp.einsum('qhe,khe->hqk', queries, key_part, precision=HIGH) * head_size ** (-0.5))
    same_clip = clip_of[:, None] == clip_of[None, :]
    soft_weights = low(jax.nn.softmax(jnp.where(same_clip[None], scores, NEG_FILL), axis=-1))
    attended = jnp.einsum('hqk,khe->qhe', soft_weights, value_part, precision=HIGH).reshape(row_count, model_width)
    mixed = low(low_back(attended))
    middle = residual + low_back(product_high(mixed, w_out))
    normed_mid = low(layer_norm(middle, norm_params[:, 2], norm_params[:, 3]))
    hidden = low(jax.nn.gelu(low_back(product_high(normed_mid, w_up)), approximate=False))
    return middle + low_back(product_high(hidden, w_down))

def group_forward(param_list, token_values, lengths, targets):
    norm1_gain, norm1_bias, w_qkv, w_out, norm2_gain, norm2_bias, w_fc1, w_fc2, w_embed, mask_token, pred_norm1_gain, pred_norm1_bias, pred_qkv, pred_out, pred_norm2_gain, pred_norm2_bias, pred_fc1, pred_fc2 = param_list
    group_rows = jnp.arange(GROUP, dtype=jnp.int32)
    clip_ends = jnp.cumsum(lengths).astype(jnp.int32)
    past_end = (group_rows[:, None] >= clip_ends[None, :]).astype(jnp.int32)
    clip_of = lax.optimization_barrier(jnp.sum(past_end, axis=1))
    rel_rows = group_rows - lax.optimization_barrier(jnp.sum(lengths[None, :] * past_end, axis=1))
    ctx_norms = jnp.stack([norm1_gain, norm1_bias, norm2_gain, norm2_bias], axis=1)
    context = low(block_forward(token_values, ctx_norms, w_qkv, w_out, w_fc1, w_fc2, HEADS, clip_of))
    embedded = low_back(product_high(context, w_embed))
    target_rows = (jnp.arange(SPLITS, dtype=jnp.int32)[:, None] * TOK_DEV + targets).reshape(-1)
    matches = group_rows[:, None] == target_rows[None, :]
    placement = matches.astype(jnp.float32)
    target_hit = lax.optimization_barrier(jnp.sum(placement, axis=1))
    target_rel = lax.optimization_barrier(jnp.sum(jnp.where(matches, rel_rows[:, None], 0), axis=0))
    mask_rows = mask_token[None, :] + position_table(target_rel, PD)
    pred_in = embedded * (1.0 - target_hit[:, None]) + product_high(placement, mask_rows)
    pred_norms = jnp.stack([pred_norm1_gain, pred_norm1_bias, pred_norm2_gain, pred_norm2_bias], axis=1)
    predicted = block_forward(pred_in, pred_norms, pred_qkv, pred_out, pred_fc1, pred_fc2, P_HEADS, clip_of)
    return (context, predicted)

def reference(tokens, clip_lengths, target_pos, out_grad, norm1_gain, norm1_bias, w_qkv, w_out, norm2_gain, norm2_bias, w_fc1, w_fc2, w_embed, mask_token, pred_norm1_gain, pred_norm1_bias, pred_qkv, pred_out, pred_norm2_gain, pred_norm2_bias, pred_fc1, pred_fc2):
    param_list = tuple((one_param.astype(jnp.float32) for one_param in (norm1_gain, norm1_bias, w_qkv, w_out, norm2_gain, norm2_bias, w_fc1, w_fc2, w_embed, mask_token, pred_norm1_gain, pred_norm1_bias, pred_qkv, pred_out, pred_norm2_gain, pred_norm2_bias, pred_fc1, pred_fc2)))

    def forward(float_params, token_values):
        grouped = token_values.reshape(GROUPS, GROUP, D)

        def one_group(scan_carry, inputs):
            return (scan_carry, jax.checkpoint(group_forward)(float_params, inputs[0], inputs[1], inputs[2]))
        final_carry, outputs = lax.scan(one_group, jnp.zeros((), jnp.float32), (grouped, clip_lengths, target_pos))
        return (outputs[0].reshape(TOKENS, D), outputs[1].reshape(TOKENS, PD))
    primal, pull_back = jax.vjp(forward, param_list, tokens.astype(jnp.float32))
    grad_list, token_grad = pull_back((jnp.zeros_like(primal[0]), out_grad.astype(jnp.float32)))
    return (primal[0].astype(jnp.bfloat16), primal[1].astype(jnp.bfloat16), token_grad.astype(jnp.bfloat16), grad_list[0], grad_list[1], grad_list[2], grad_list[3], grad_list[4], grad_list[5], grad_list[6], grad_list[7], grad_list[8], grad_list[9], grad_list[10], grad_list[11], grad_list[12], grad_list[13], grad_list[14], grad_list[15], grad_list[16], grad_list[17])
```

```python
import math

import jax
import jax.numpy as jnp
from jax import lax
from jax.experimental import pallas as pl
from jax.experimental.pallas import tpu as pltpu
from jax.sharding import PartitionSpec as P

HEADS = 16
PD = 384
P_HEADS = 12


EPSILON = 1e-06
NEG_FILL = -1e30
block_rows = 512


def layer_norm(values, norm_gain, norm_shift):
    center = values - jnp.mean(values, axis=-1, keepdims=True)
    spread = jnp.mean(center * center, axis=-1, keepdims=True)
    return center * lax.rsqrt(spread + EPSILON) * norm_gain + norm_shift


def gelu_exact(values):
    return jax.nn.gelu(values, approximate=False)


def position_table(positions, table_width):
    half_width = table_width // 2
    angle_rates = jnp.exp(
        jnp.arange(half_width, dtype=jnp.float32) * (-2.0 * math.log(10000.0) / table_width)
    )
    angles = positions.astype(jnp.float32)[:, None] * angle_rates[None, :]
    return jnp.concatenate([jnp.sin(angles), jnp.cos(angles)], axis=1)


def clip_index(positions, clip_ends):
    return jnp.sum((positions[:, None] >= clip_ends[None, :]).astype(jnp.int32), axis=1)


def key_step(total_keys):
    return max(min(total_keys, block_rows), total_keys // 8)


def block_scores(queries, key_part, query_clip, key_clip_part, score_scale):
    raw_scores = (
        jnp.einsum("the,khe->htk", queries, key_part, preferred_element_type=jnp.float32)
        * score_scale
    )
    same_clip = query_clip[:, None] == key_clip_part[None, :]
    return jnp.where(same_clip[None], raw_scores, NEG_FILL)


def attend_forward(queries, key_heads, value_heads, query_clip, key_clip):
    row_count, head_count, head_size = queries.shape
    score_scale = head_size ** (-0.5)
    total_keys = key_heads.shape[0]
    step_rows = key_step(total_keys)
    run_max = jnp.full((head_count, row_count), NEG_FILL, jnp.float32)
    run_total = jnp.zeros((head_count, row_count), jnp.float32)
    for key_start in range(0, total_keys, step_rows):
        scores = block_scores(
            queries,
            key_heads[key_start : key_start + step_rows],
            query_clip,
            key_clip[key_start : key_start + step_rows],
            score_scale,
        )
        new_max = jnp.maximum(run_max, jnp.max(scores, axis=2))
        run_total = run_total * jnp.exp(run_max - new_max) + jnp.sum(
            jnp.exp(scores - new_max[:, :, None]), axis=2
        )
        run_max = new_max
    log_total = run_max + jnp.log(run_total)
    output = jnp.zeros((row_count, head_count, head_size), jnp.float32)
    for key_start in range(0, total_keys, step_rows):
        scores = block_scores(
            queries,
            key_heads[key_start : key_start + step_rows],
            query_clip,
            key_clip[key_start : key_start + step_rows],
            score_scale,
        )
        soft_weights = jnp.exp(scores - log_total[:, :, None]).astype(jnp.bfloat16)
        output = output + jnp.einsum(
            "htk,khe->the",
            soft_weights,
            value_heads[key_start : key_start + step_rows],
            preferred_element_type=jnp.float32,
        )
    return (output, log_total)


def attend_backward(
    queries, key_heads, value_heads, query_clip, key_clip, log_total, grad_mixed, output
):
    row_count, head_count, head_size = queries.shape
    score_scale = head_size ** (-0.5)
    total_keys = key_heads.shape[0]
    step_rows = key_step(total_keys)
    row_delta = jnp.sum(grad_mixed.astype(jnp.float32) * output, axis=2).T
    grad_query = jnp.zeros((row_count, head_count, head_size), jnp.float32)
    key_pieces = []
    value_pieces = []
    for key_start in range(0, total_keys, step_rows):
        key_part = key_heads[key_start : key_start + step_rows]
        value_part = value_heads[key_start : key_start + step_rows]
        scores = block_scores(
            queries, key_part, query_clip, key_clip[key_start : key_start + step_rows], score_scale
        )
        soft_weights = jnp.exp(scores - log_total[:, :, None])
        grad_soft = jnp.einsum(
            "the,khe->htk", grad_mixed, value_part, preferred_element_type=jnp.float32
        )
        grad_scores = (soft_weights * (grad_soft - row_delta[:, :, None])).astype(jnp.bfloat16)
        grad_query = grad_query + jnp.einsum(
            "htk,khe->the", grad_scores, key_part, preferred_element_type=jnp.float32
        )
        key_pieces.append(
            jnp.einsum("htk,the->khe", grad_scores, queries, preferred_element_type=jnp.float32)
        )
        value_pieces.append(
            jnp.einsum(
                "htk,the->khe",
                soft_weights.astype(jnp.bfloat16),
                grad_mixed,
                preferred_element_type=jnp.float32,
            )
        )
    key_terms = jnp.concatenate(key_pieces, axis=0) * score_scale
    value_terms = jnp.concatenate(value_pieces, axis=0)
    return (grad_query * score_scale, key_terms, value_terms)


def block_forward(
    residual, norm_params, w_qkv, w_out, w_up, w_down, head_count, query_clip, key_clip
):
    row_count, model_width = residual.shape
    head_size = model_width // head_count
    norm_float = norm_params.astype(jnp.float32)
    normed = layer_norm(residual, norm_float[:, 0], norm_float[:, 1]).astype(jnp.bfloat16)
    qkv = jnp.dot(normed, w_qkv, preferred_element_type=jnp.float32).astype(jnp.bfloat16)
    queries = qkv[:, :model_width].reshape(row_count, head_count, head_size)
    key_local = qkv[:, model_width : 2 * model_width]
    value_local = qkv[:, 2 * model_width :]
    key_full, value_full = (
        lax.all_gather(key_local, "seq", axis=0, tiled=True),
        lax.all_gather(value_local, "seq", axis=0, tiled=True),
    )
    key_heads = key_full.reshape(-1, head_count, head_size)
    value_heads = value_full.reshape(-1, head_count, head_size)
    output, log_total = attend_forward(queries, key_heads, value_heads, query_clip, key_clip)
    mixed = output.reshape(row_count, model_width).astype(jnp.bfloat16)
    middle = residual + jnp.dot(mixed, w_out, preferred_element_type=jnp.float32)
    normed_mid = layer_norm(middle, norm_float[:, 2], norm_float[:, 3]).astype(jnp.bfloat16)
    pre_act = jnp.dot(normed_mid, w_up, preferred_element_type=jnp.float32)
    hidden = gelu_exact(pre_act).astype(jnp.bfloat16)
    result = middle + jnp.dot(hidden, w_down, preferred_element_type=jnp.float32)
    kept = (
        residual,
        normed,
        queries,
        key_local,
        value_local,
        key_heads,
        value_heads,
        output,
        log_total,
        mixed,
        middle,
        normed_mid,
        pre_act,
        hidden,
    )
    return (result, kept)


def block_backward(
    grad_result, kept, norm_params, w_qkv, w_out, w_up, w_down, head_count, query_clip, key_clip
):
    (
        residual,
        normed,
        queries,
        key_local,
        value_local,
        key_heads,
        value_heads,
        output,
        log_total,
        mixed,
        middle,
        normed_mid,
        pre_act,
        hidden,
    ) = kept
    row_count, model_width = residual.shape
    head_size = model_width // head_count
    norm_float = norm_params.astype(jnp.float32)
    grad_low = grad_result.astype(jnp.bfloat16)
    grad_down = jnp.einsum("tf,tw->fw", hidden, grad_low, preferred_element_type=jnp.float32)
    grad_hidden = jnp.einsum("tw,fw->tf", grad_low, w_down, preferred_element_type=jnp.float32)
    gelu_value, gelu_pull = jax.vjp(gelu_exact, pre_act)
    grad_pre = gelu_pull(grad_hidden)[0].astype(jnp.bfloat16)
    grad_up = jnp.einsum("tw,tf->wf", normed_mid, grad_pre, preferred_element_type=jnp.float32)
    grad_normed_mid = jnp.einsum("tf,wf->tw", grad_pre, w_up, preferred_element_type=jnp.float32)
    second_value, second_pull = jax.vjp(layer_norm, middle, norm_float[:, 2], norm_float[:, 3])
    grad_mid_norm, grad_gain_two, grad_shift_two = second_pull(grad_normed_mid)
    grad_middle = grad_result + grad_mid_norm
    grad_branch = grad_middle.astype(jnp.bfloat16)
    grad_out_w = jnp.einsum("tv,tw->vw", mixed, grad_branch, preferred_element_type=jnp.float32)
    grad_mixed = jnp.einsum(
        "tw,vw->tv", grad_branch, w_out, preferred_element_type=jnp.float32
    ).astype(jnp.bfloat16)
    key_full, value_full = (
        lax.all_gather(key_local, "seq", axis=0, tiled=True),
        lax.all_gather(value_local, "seq", axis=0, tiled=True),
    )
    key_heads = key_full.reshape(-1, head_count, head_size)
    value_heads = value_full.reshape(-1, head_count, head_size)
    grad_query, key_terms, value_terms = attend_backward(
        queries,
        key_heads,
        value_heads,
        query_clip,
        key_clip,
        log_total,
        grad_mixed.reshape(row_count, head_count, head_size),
        output,
    )
    grad_key, grad_value = (
        lax.psum_scatter(
            key_terms.reshape(-1, model_width).astype(jnp.bfloat16),
            "seq",
            scatter_dimension=0,
            tiled=True,
        ).astype(jnp.float32),
        lax.psum_scatter(
            value_terms.reshape(-1, model_width).astype(jnp.bfloat16),
            "seq",
            scatter_dimension=0,
            tiled=True,
        ).astype(jnp.float32),
    )
    grad_qkv = jnp.concatenate(
        [grad_query.reshape(row_count, model_width), grad_key, grad_value], axis=1
    ).astype(jnp.bfloat16)
    grad_qkv_w = jnp.einsum("tw,tc->wc", normed, grad_qkv, preferred_element_type=jnp.float32)
    grad_normed = jnp.einsum("tc,wc->tw", grad_qkv, w_qkv, preferred_element_type=jnp.float32)
    first_value, first_pull = jax.vjp(layer_norm, residual, norm_float[:, 0], norm_float[:, 1])
    grad_first_norm, grad_gain_one, grad_shift_one = first_pull(grad_normed)
    grad_norms = jnp.stack([grad_gain_one, grad_shift_one, grad_gain_two, grad_shift_two], axis=1)
    return (grad_middle + grad_first_norm, (grad_norms, grad_qkv_w, grad_out_w, grad_up, grad_down))


def local(
    tokens,
    clip_lengths,
    target_pos,
    out_grad,
    norm1_gain,
    norm1_bias,
    w_qkv,
    w_out,
    norm2_gain,
    norm2_bias,
    w_fc1,
    w_fc2,
    w_embed,
    mask_token,
    pred_norm1_gain,
    pred_norm1_bias,
    pred_qkv,
    pred_out,
    pred_norm2_gain,
    pred_norm2_bias,
    pred_fc1,
    pred_fc2,
):
    row_count = tokens.shape[0]
    group_count = row_count * lax.axis_size("seq")
    lengths = clip_lengths[0]
    clip_ends = jnp.cumsum(lengths)
    local_rows = lax.axis_index("seq") * row_count + jnp.arange(row_count, dtype=jnp.int32)
    query_clip = clip_index(local_rows, clip_ends)
    key_clip = clip_index(jnp.arange(group_count, dtype=jnp.int32), clip_ends)
    past_end = (local_rows[:, None] >= clip_ends[None, :]).astype(jnp.int32)
    rel_rows = local_rows - jnp.sum(lengths[None, :] * past_end, axis=1)
    ctx_small = jnp.stack([norm1_gain, norm1_bias, norm2_gain, norm2_bias], axis=1)
    pred_small = jnp.stack(
        [pred_norm1_gain, pred_norm1_bias, pred_norm2_gain, pred_norm2_bias, mask_token], axis=1
    )
    ctx_params = (
        lax.all_gather(ctx_small, "fsdp", axis=0, tiled=True),
        lax.all_gather(w_qkv, "fsdp", axis=0, tiled=True),
        lax.all_gather(w_out, "fsdp", axis=0, tiled=True),
        lax.all_gather(w_fc1, "fsdp", axis=0, tiled=True),
        lax.all_gather(w_fc2, "fsdp", axis=0, tiled=True),
    )
    pred_params = (
        lax.all_gather(pred_small, "fsdp", axis=0, tiled=True),
        lax.all_gather(w_embed, "fsdp", axis=0, tiled=True),
        lax.all_gather(pred_qkv, "fsdp", axis=0, tiled=True),
        lax.all_gather(pred_out, "fsdp", axis=0, tiled=True),
        lax.all_gather(pred_fc1, "fsdp", axis=0, tiled=True),
        lax.all_gather(pred_fc2, "fsdp", axis=0, tiled=True),
    )
    ctx_result, ctx_kept = block_forward(
        tokens.astype(jnp.float32),
        ctx_params[0],
        ctx_params[1],
        ctx_params[2],
        ctx_params[3],
        ctx_params[4],
        HEADS,
        query_clip,
        key_clip,
    )
    context_out = ctx_result.astype(jnp.bfloat16)
    embedded = jnp.dot(context_out, pred_params[1], preferred_element_type=jnp.float32)
    targets = target_pos[0, 0]
    matches = jnp.arange(row_count, dtype=jnp.int32)[:, None] == targets[None, :]
    placement = matches.astype(jnp.float32)
    target_hit = jnp.sum(placement, axis=1)
    target_rel = jnp.sum(jnp.where(matches, rel_rows[:, None], 0), axis=0)
    mask_rows = pred_params[0][:, 4].astype(jnp.float32)[None, :] + position_table(target_rel, PD)
    placed = jnp.dot(
        placement, mask_rows, precision=lax.Precision.HIGHEST, preferred_element_type=jnp.float32
    )
    pred_in = embedded * (1.0 - target_hit[:, None]) + placed
    pred_result, pred_kept = block_forward(
        pred_in,
        pred_params[0],
        pred_params[2],
        pred_params[3],
        pred_params[4],
        pred_params[5],
        P_HEADS,
        query_clip,
        key_clip,
    )
    predicted = pred_result.astype(jnp.bfloat16)
    pred_back = (
        lax.all_gather(pred_small, "fsdp", axis=0, tiled=True),
        lax.all_gather(w_embed, "fsdp", axis=0, tiled=True),
        lax.all_gather(pred_qkv, "fsdp", axis=0, tiled=True),
        lax.all_gather(pred_out, "fsdp", axis=0, tiled=True),
        lax.all_gather(pred_fc1, "fsdp", axis=0, tiled=True),
        lax.all_gather(pred_fc2, "fsdp", axis=0, tiled=True),
    )
    ctx_back = (
        lax.all_gather(ctx_small, "fsdp", axis=0, tiled=True),
        lax.all_gather(w_qkv, "fsdp", axis=0, tiled=True),
        lax.all_gather(w_out, "fsdp", axis=0, tiled=True),
        lax.all_gather(w_fc1, "fsdp", axis=0, tiled=True),
        lax.all_gather(w_fc2, "fsdp", axis=0, tiled=True),
    )
    grad_pred_in, pred_grads = block_backward(
        out_grad.astype(jnp.float32),
        pred_kept,
        pred_back[0],
        pred_back[2],
        pred_back[3],
        pred_back[4],
        pred_back[5],
        P_HEADS,
        query_clip,
        key_clip,
    )
    grad_mask = jnp.sum(target_hit[:, None] * grad_pred_in, axis=0)
    grad_embedded = (grad_pred_in * (1.0 - target_hit[:, None])).astype(jnp.bfloat16)
    grad_embed_w = jnp.einsum(
        "td,tp->dp", context_out, grad_embedded, preferred_element_type=jnp.float32
    )
    grad_context = jnp.einsum(
        "tp,dp->td", grad_embedded, pred_back[1], preferred_element_type=jnp.float32
    )
    grad_tokens, ctx_grads = block_backward(
        grad_context,
        ctx_kept,
        ctx_back[0],
        ctx_back[1],
        ctx_back[2],
        ctx_back[3],
        ctx_back[4],
        HEADS,
        query_clip,
        key_clip,
    )
    pred_small_grad = jnp.concatenate([pred_grads[0], grad_mask[:, None]], axis=1)
    row_sums = (
        lax.psum_scatter(ctx_grads[0], "fsdp", scatter_dimension=0, tiled=True),
        lax.psum_scatter(ctx_grads[1], "fsdp", scatter_dimension=0, tiled=True),
        lax.psum_scatter(ctx_grads[2], "fsdp", scatter_dimension=0, tiled=True),
        lax.psum_scatter(ctx_grads[3], "fsdp", scatter_dimension=0, tiled=True),
        lax.psum_scatter(ctx_grads[4], "fsdp", scatter_dimension=0, tiled=True),
        lax.psum_scatter(grad_embed_w, "fsdp", scatter_dimension=0, tiled=True),
        lax.psum_scatter(pred_small_grad, "fsdp", scatter_dimension=0, tiled=True),
        lax.psum_scatter(pred_grads[1], "fsdp", scatter_dimension=0, tiled=True),
        lax.psum_scatter(pred_grads[2], "fsdp", scatter_dimension=0, tiled=True),
        lax.psum_scatter(pred_grads[3], "fsdp", scatter_dimension=0, tiled=True),
        lax.psum_scatter(pred_grads[4], "fsdp", scatter_dimension=0, tiled=True),
    )
    summed = (
        lax.psum(row_sums[0].astype(jnp.bfloat16), "seq").astype(jnp.float32),
        lax.psum(row_sums[1].astype(jnp.bfloat16), "seq").astype(jnp.float32),
        lax.psum(row_sums[2].astype(jnp.bfloat16), "seq").astype(jnp.float32),
        lax.psum(row_sums[3].astype(jnp.bfloat16), "seq").astype(jnp.float32),
        lax.psum(row_sums[4].astype(jnp.bfloat16), "seq").astype(jnp.float32),
        lax.psum(row_sums[5].astype(jnp.bfloat16), "seq").astype(jnp.float32),
        lax.psum(row_sums[6].astype(jnp.bfloat16), "seq").astype(jnp.float32),
        lax.psum(row_sums[7].astype(jnp.bfloat16), "seq").astype(jnp.float32),
        lax.psum(row_sums[8].astype(jnp.bfloat16), "seq").astype(jnp.float32),
        lax.psum(row_sums[9].astype(jnp.bfloat16), "seq").astype(jnp.float32),
        lax.psum(row_sums[10].astype(jnp.bfloat16), "seq").astype(jnp.float32),
    )
    return (
        context_out,
        predicted,
        grad_tokens.astype(jnp.bfloat16),
        summed[0][:, 0],
        summed[0][:, 1],
        summed[1],
        summed[2],
        summed[0][:, 2],
        summed[0][:, 3],
        summed[3],
        summed[4],
        summed[5],
        summed[6][:, 4],
        summed[6][:, 0],
        summed[6][:, 1],
        summed[7],
        summed[8],
        summed[6][:, 2],
        summed[6][:, 3],
        summed[9],
        summed[10],
    )


BF16 = jnp.bfloat16
F32 = jnp.float32
MESH = pl.DeviceIdType.MESH
LOG2E = 1.4426950408889634
LN2 = 0.6931471805599453
LANES = 128
SMALL_ROWS = 16
ANYWHERE = pl.BlockSpec(memory_space=pl.ANY)
IN_VMEM = pl.BlockSpec(memory_space=pltpu.VMEM)


def fits_fast(mesh):
    return mesh.shape["fsdp"] == 8 and mesh.shape["seq"] == 4


def fsdp_peer(bit):
    return (lax.axis_index("fsdp") ^ bit, lax.axis_index("seq"))


def seq_peer(index):
    return (lax.axis_index("fsdp"), index)


def enter(peers):
    barrier = pltpu.get_barrier_semaphore()
    for peer in peers:
        pl.semaphore_signal(barrier, inc=1, device_id=peer, device_id_type=MESH)
    pl.semaphore_wait(barrier, len(peers))


def send(src, dst, send_sem, recv_sem, peer):
    return pltpu.make_async_remote_copy(
        src_ref=src,
        dst_ref=dst,
        send_sem=send_sem,
        recv_sem=recv_sem,
        device_id=peer,
        device_id_type=MESH,
    )


def remote_params(collective_id, vmem=None):
    return pltpu.CompilerParams(
        collective_id=collective_id, has_side_effects=True, vmem_limit_bytes=vmem
    )


def cut_units(shapes):
    units = []
    flip = False
    for index, (rows, columns) in enumerate(shapes):
        if rows * columns >= 100000 and rows % 32 == 0:
            half = rows // 2
            units.append((index, 0, half, 2, 4))
            units.append((index, half, half, 4, 2))
        else:
            units.append((index, 0, rows, 4, 2) if flip else (index, 0, rows, 2, 4))
            flip = not flip
    return units


def gather_weights(shards):
    shapes = [shard.shape for shard in shards]
    units = cut_units(shapes)
    count = len(units)
    array_count = len(shards)

    def kernel(*refs):
        sources = refs[:array_count]
        gathered = refs[array_count : 2 * array_count]
        send_sems, recv_sems, local_sems = refs[2 * array_count :]
        me = lax.axis_index("fsdp")
        enter([fsdp_peer(1), fsdp_peer(2), fsdp_peer(4)])

        def part(unit, owner):
            index, first, rows, _, _ = units[unit]
            return gathered[index].at[owner, pl.ds(first, rows)]

        def own(unit):
            index, first, rows, _, _ = units[unit]
            return sources[index].at[pl.ds(first, rows)]

        def copy(unit, slot, owner, bit, first_hand=False):
            src = own(unit) if first_hand else part(unit, owner)
            return send(
                src,
                part(unit, owner),
                send_sems.at[unit, slot],
                recv_sems.at[unit, slot],
                fsdp_peer(bit),
            )

        def launch(unit):
            _, _, _, near, far = units[unit]
            copies = [
                copy(unit, 0, me, near, True),
                copy(unit, 1, me, far, True),
                copy(unit, 3, me, 1, True),
            ]
            for one in copies:
                one.start()
            local_copy = pltpu.make_async_copy(own(unit), part(unit, me), local_sems.at[unit])
            local_copy.start()
            return copies + [local_copy]

        def arrive(unit):
            _, _, _, near, far = units[unit]
            copy(unit, 0, me, near, True).wait_recv()
            forward = [copy(unit, 2, me ^ near, far), copy(unit, 4, me ^ near, 1)]
            for one in forward:
                one.start()
            copy(unit, 1, me, far, True).wait_recv()
            last = copy(unit, 5, me ^ far, 1)
            last.start()
            return forward + [last]

        def relay(unit):
            _, _, _, near, far = units[unit]
            copy(unit, 2, me ^ near, far).wait_recv()
            last = copy(unit, 6, me ^ near ^ far, 1)
            last.start()
            return [last]

        sent = []
        local_copies = []
        ahead = 3
        for unit in range(min(ahead, count)):
            started = launch(unit)
            sent += started[:3]
            local_copies.append(started[3])
        for unit in range(count + 1):
            if unit < count:
                sent += arrive(unit)
                if unit + ahead < count:
                    started = launch(unit + ahead)
                    sent += started[:3]
                    local_copies.append(started[3])
            if unit >= 1:
                sent += relay(unit - 1)
        for unit in range(count):
            _, _, _, near, far = units[unit]
            copy(unit, 3, me, 1, True).wait_recv()
            copy(unit, 4, me ^ near, 1).wait_recv()
            copy(unit, 5, me ^ far, 1).wait_recv()
            copy(unit, 6, me ^ near ^ far, 1).wait_recv()
        for one in sent:
            one.wait_send()
        for one in local_copies:
            one.wait()

    return pl.pallas_call(
        kernel,
        out_shape=[jax.ShapeDtypeStruct((8,) + shard.shape, shard.dtype) for shard in shards],
        in_specs=[ANYWHERE] * array_count,
        out_specs=[ANYWHERE] * array_count,
        scratch_shapes=[
            pltpu.SemaphoreType.DMA((count, 7)),
            pltpu.SemaphoreType.DMA((count, 7)),
            pltpu.SemaphoreType.DMA((count,)),
        ],
        compiler_params=remote_params(1),
        name="gather_weights",
    )(*shards)


def sum_gradients(partials):
    shapes = [partial.shape[1:] for partial in partials]
    units = cut_units(shapes)
    count = len(units)
    array_count = len(partials)
    own_depth = 3
    widest = {}
    for index, _, rows, _, _ in units:
        key = (rows, shapes[index][1])
        widest[key] = widest.get(key, 0) + 1
    keys = list(widest)

    def shape_of(unit):
        index, _, rows, _, _ = units[unit]
        return (rows, shapes[index][1])

    def place_of(unit):
        key = shape_of(unit)
        return sum(1 for other in range(unit) if shape_of(other) == key)

    def kernel(*refs):
        sources = refs[:array_count]
        results = refs[array_count : 2 * array_count]
        rest = list(refs[2 * array_count :])
        own_bufs, core_bufs, near_bufs, far_bufs, outer_bufs, inner_bufs = [
            {key: rest[group * len(keys) + i] for i, key in enumerate(keys)} for group in range(6)
        ]
        send_sems, recv_sems, own_sems, out_sems = rest[6 * len(keys) :]
        me = lax.axis_index("fsdp")
        place = lax.axis_index("seq")
        core = me & 1
        inner = jnp.logical_or(place == 1, place == 2)
        outward = jnp.where(place == 1, 0, 3)
        inward = jnp.where(place == 0, 1, 2)
        across = 3 - place

        barrier = pltpu.get_barrier_semaphore()
        for bit in (1, 2, 4):
            pl.semaphore_signal(barrier, inc=1, device_id=fsdp_peer(bit), device_id_type=MESH)

        @pl.when(inner)
        def _():
            pl.semaphore_signal(barrier, inc=1, device_id=seq_peer(outward), device_id_type=MESH)
            pl.semaphore_signal(barrier, inc=1, device_id=seq_peer(across), device_id_type=MESH)
            pl.semaphore_wait(barrier, 5)

        @pl.when(jnp.logical_not(inner))
        def _():
            pl.semaphore_signal(barrier, inc=1, device_id=seq_peer(inward), device_id_type=MESH)
            pl.semaphore_wait(barrier, 4)

        def buf(group, unit):
            return group[shape_of(unit)].at[place_of(unit)]

        def rows_of(unit):
            _, first, rows, _, _ = units[unit]
            return pl.ds(first, rows)

        def source(unit, owner):
            return sources[units[unit][0]].at[owner, rows_of(unit)]

        def result(unit):
            return results[units[unit][0]].at[rows_of(unit)]

        def chip_bits(unit, slot):
            _, _, _, near, far = units[unit]
            return (slot // 2) * near + (slot % 2) * far

        def core_copy(unit, slot):
            owner = me ^ chip_bits(unit, slot) ^ 1
            return send(
                source(unit, owner),
                buf(core_bufs, unit).at[slot],
                send_sems.at[unit, slot],
                recv_sems.at[unit, slot],
                fsdp_peer(1),
            )

        def own_copy(unit, slot):
            owner = me ^ chip_bits(unit, slot)
            dst = own_bufs[shape_of(unit)].at[place_of(unit) % own_depth, slot]
            return pltpu.make_async_copy(source(unit, owner), dst, own_sems.at[unit, slot])

        def near_copy(unit, slot):
            _, _, _, near, _ = units[unit]
            return send(
                buf(core_bufs, unit).at[2 + slot],
                buf(near_bufs, unit).at[slot],
                send_sems.at[unit, 4 + slot],
                recv_sems.at[unit, 4 + slot],
                fsdp_peer(near),
            )

        def far_copy(unit):
            _, _, _, _, far = units[unit]
            return send(
                buf(near_bufs, unit).at[1],
                buf(far_bufs, unit),
                send_sems.at[unit, 6],
                recv_sems.at[unit, 6],
                fsdp_peer(far),
            )

        def inward_copy(unit):
            return send(
                buf(far_bufs, unit),
                buf(outer_bufs, unit),
                send_sems.at[unit, 7],
                recv_sems.at[unit, 7],
                seq_peer(inward),
            )

        def across_copy(unit):
            return send(
                buf(outer_bufs, unit),
                buf(inner_bufs, unit),
                send_sems.at[unit, 8],
                recv_sems.at[unit, 8],
                seq_peer(across),
            )

        def outward_copy(unit):
            return send(
                buf(far_bufs, unit),
                result(unit),
                send_sems.at[unit, 9],
                recv_sems.at[unit, 9],
                seq_peer(outward),
            )

        def out_copy(unit):
            return pltpu.make_async_copy(buf(far_bufs, unit), result(unit), out_sems.at[unit])

        def add_into(dst, *terms):
            rows, columns = dst.shape
            step = 16 if rows % 16 == 0 else rows

            @pl.loop(0, rows // step)
            def _(i):
                part = pl.ds(pl.multiple_of(i * step, step), step)
                total = terms[0][part].astype(F32)
                for term in terms[1:]:
                    total = total + term[part].astype(F32)
                dst[part] = total.astype(BF16)

        def start_core(unit):
            for slot in (2, 3, 0, 1):
                core_copy(unit, slot).start()

        def start_own(unit):
            for slot in range(4):
                own_copy(unit, slot).start()

        def stage_near(unit):
            for slot in range(4):
                core_copy(unit, slot).wait_recv()
                own_copy(unit, slot).wait()
            for slot in (2, 3, 0, 1):
                target = buf(core_bufs, unit).at[slot]
                add_into(target, target, own_bufs[shape_of(unit)].at[place_of(unit) % own_depth, slot])
                if slot >= 2:
                    near_copy(unit, slot - 2).start()

        def stage_far(unit):
            for slot in (1, 0):
                near_copy(unit, slot).wait_recv()
                target = buf(near_bufs, unit).at[slot]
                add_into(target, target, buf(core_bufs, unit).at[slot])
                if slot == 1:
                    far_copy(unit).start()

        def stage_inward(unit):
            far_copy(unit).wait_recv()
            target = buf(far_bufs, unit)
            add_into(target, target, buf(near_bufs, unit).at[0])

            @pl.when(jnp.logical_not(inner))
            def _():
                inward_copy(unit).start()

        def stage_across(unit):
            @pl.when(inner)
            def _():
                inward_copy(unit).wait_recv()
                target = buf(outer_bufs, unit)
                add_into(target, target, buf(far_bufs, unit))
                across_copy(unit).start()

        def stage_outward(unit):
            @pl.when(inner)
            def _():
                across_copy(unit).wait_recv()
                add_into(buf(far_bufs, unit), buf(outer_bufs, unit), buf(inner_bufs, unit))
                outward_copy(unit).start()
                out_copy(unit).start()

        same_key = {}
        for unit in range(count):
            same_key.setdefault(shape_of(unit), []).append(unit)
        later = {}
        first_own = []
        for members in same_key.values():
            for i, unit in enumerate(members):
                if i < own_depth:
                    first_own.append(unit)
                else:
                    later.setdefault(members[i - own_depth], []).append(unit)
        for unit in first_own:
            start_own(unit)
        ahead = 4
        for unit in range(min(ahead, count)):
            start_core(unit)
        stages = [stage_near, stage_far, stage_inward, stage_across, stage_outward]
        for tick in range(count + len(stages) - 1):
            for lag, stage in enumerate(stages):
                unit = tick - lag
                if 0 <= unit < count:
                    stage(unit)
                    if lag == 0:
                        for other in later.get(unit, []):
                            start_own(other)
                        if unit + ahead < count:
                            start_core(unit + ahead)
        for unit in range(count):
            for slot in range(4):
                core_copy(unit, slot).wait_send()
            for slot in range(2):
                near_copy(unit, slot).wait_send()
            far_copy(unit).wait_send()

            @pl.when(inner)
            def _():
                across_copy(unit).wait_send()
                outward_copy(unit).wait_send()
                out_copy(unit).wait()

            @pl.when(jnp.logical_not(inner))
            def _():
                inward_copy(unit).wait_send()
                outward_copy(unit).wait_recv()

    scratch = []
    for slots, capped in (((4,), True), ((4,), False), ((2,), False), ((), False), ((), False), ((), False)):
        for key in keys:
            depth = min(own_depth, widest[key]) if capped else widest[key]
            scratch.append(pltpu.VMEM((depth,) + slots + key, BF16))
    scratch += [
        pltpu.SemaphoreType.DMA((count, 10)),
        pltpu.SemaphoreType.DMA((count, 10)),
        pltpu.SemaphoreType.DMA((count, 4)),
        pltpu.SemaphoreType.DMA((count,)),
    ]
    return pl.pallas_call(
        kernel,
        out_shape=[jax.ShapeDtypeStruct(shape, BF16) for shape in shapes],
        in_specs=[ANYWHERE] * array_count,
        out_specs=[ANYWHERE] * array_count,
        scratch_shapes=scratch,
        compiler_params=remote_params(2, 60 << 20),
        name="sum_gradients",
    )(*partials)


def mate_z():
    return seq_peer(lax.axis_index("seq") ^ 1)


def quarter():
    return (lax.axis_index("fsdp") & 1) * 2 + (lax.axis_index("seq") & 1)


def gather_keys(qkv, collective_id):
    rows, triple = qkv.shape
    width = triple // 3
    pieces = 4
    step = rows // pieces

    def kernel(qkv_ref, out_ref, send_sems, recv_sems, local_sem):
        mine = quarter()
        enter([fsdp_peer(1), mate_z()])
        columns = pl.ds(width, 2 * width)

        def own(piece):
            return qkv_ref.at[pl.ds(piece * step, step), columns]

        def part(owner, piece):
            return out_ref.at[owner, pl.ds(piece * step, step)]

        def copy(kind, piece):
            src = part(mine ^ 1, piece) if kind == 2 else own(piece)
            owner = mine ^ 1 if kind == 2 else mine
            return send(
                src,
                part(owner, piece),
                send_sems.at[kind, piece],
                recv_sems.at[kind, piece],
                mate_z() if kind == 0 else fsdp_peer(1),
            )

        for piece in range(pieces):
            copy(0, piece).start()
        for piece in range(pieces):
            copy(1, piece).start()
        local_copy = pltpu.make_async_copy(
            qkv_ref.at[:, columns], out_ref.at[mine], local_sem
        )
        local_copy.start()
        for piece in range(pieces):
            copy(0, piece).wait_recv()
            copy(2, piece).start()
        for piece in range(pieces):
            copy(1, piece).wait_recv()
            copy(2, piece).wait_recv()
            for kind in range(3):
                copy(kind, piece).wait_send()
        local_copy.wait()

    return pl.pallas_call(
        kernel,
        out_shape=jax.ShapeDtypeStruct((4, rows, 2 * width), qkv.dtype),
        in_specs=[ANYWHERE],
        out_specs=ANYWHERE,
        scratch_shapes=[
            pltpu.SemaphoreType.DMA((3, pieces)),
            pltpu.SemaphoreType.DMA((3, pieces)),
            pltpu.SemaphoreType.DMA,
        ],
        compiler_params=remote_params(collective_id),
        name="gather_keys",
    )(qkv)


def sum_keys(terms, collective_id):
    _, rows, width = terms[0].shape
    pieces = 4
    step = rows // pieces
    kinds = len(terms)

    def kernel(*refs):
        sources = refs[:kinds]
        results = refs[kinds : 2 * kinds]
        core_buf, far_buf, send_sems, recv_sems = refs[2 * kinds :]
        mine = quarter()
        enter([fsdp_peer(1), mate_z()])

        def core_copy(kind, piece, other):
            owner = mine ^ 2 ^ other
            return send(
                sources[kind].at[owner, pl.ds(piece * step, step)],
                core_buf.at[kind, other, pl.ds(piece * step, step)],
                send_sems.at[kind, piece, other],
                recv_sems.at[kind, piece, other],
                fsdp_peer(1),
            )

        def far_copy(kind, piece):
            part = pl.ds(piece * step, step)
            return send(
                core_buf.at[kind, 1, part],
                far_buf.at[kind, part],
                send_sems.at[kind, piece, 2],
                recv_sems.at[kind, piece, 2],
                mate_z(),
            )

        order = [(kind, piece) for piece in range(pieces) for kind in range(kinds)]
        for other in (1, 0):
            for kind, piece in order:
                core_copy(kind, piece, other).start()
        for kind, piece in order:
            core_copy(kind, piece, 1).wait_recv()

            @pl.loop(0, step // 16)
            def _(i):
                part = pl.ds(pl.multiple_of(piece * step + i * 16, 16), 16)
                total = core_buf[kind, 1, part].astype(F32) + sources[kind][mine ^ 1, part].astype(F32)
                core_buf[kind, 1, part] = total.astype(BF16)

            far_copy(kind, piece).start()
        for kind, piece in order:
            core_copy(kind, piece, 0).wait_recv()
            far_copy(kind, piece).wait_recv()

            @pl.loop(0, step // 16)
            def _(i):
                part = pl.ds(pl.multiple_of(piece * step + i * 16, 16), 16)
                total = core_buf[kind, 0, part].astype(F32) + sources[kind][mine, part].astype(F32)
                results[kind][part] = (total + far_buf[kind, part].astype(F32)).astype(BF16)

        for kind, piece in order:
            core_copy(kind, piece, 0).wait_send()
            core_copy(kind, piece, 1).wait_send()
            far_copy(kind, piece).wait_send()

    return pl.pallas_call(
        kernel,
        out_shape=[jax.ShapeDtypeStruct((rows, width), BF16)] * kinds,
        in_specs=[IN_VMEM] * kinds,
        out_specs=[IN_VMEM] * kinds,
        scratch_shapes=[
            pltpu.VMEM((kinds, 2, rows, width), BF16),
            pltpu.VMEM((kinds, rows, width), BF16),
            pltpu.SemaphoreType.DMA((kinds, pieces, 3)),
            pltpu.SemaphoreType.DMA((kinds, pieces, 3)),
        ],
        compiler_params=remote_params(collective_id, 40 << 20),
        name="sum_keys",
    )(*terms)


def across_lanes(left, right):
    return lax.dot_general(left, right, (((1,), (1,)), ((), ())), preferred_element_type=F32)


def fill_bias(bias, query_ref, key_ref):
    @pl.when(pl.program_id(0) == 0)
    def _():
        bias[...] = jnp.where(key_ref[...] == query_ref[...], 0.0, NEG_FILL)


def attend_local(qkv, keys_values, query_clip, key_clip, head_count):
    rows, triple = qkv.shape
    width = triple // 3
    keys = keys_values.shape[0]
    slabs = width // LANES
    head_size = width // head_count
    per_slab = LANES // head_size
    factor = head_size ** (-0.5) * LOG2E

    def kernel(q_ref, k_ref, v_ref, query_ref, key_ref, out_ref, log_ref, bias):
        fill_bias(bias, query_ref, key_ref)
        lane = lax.broadcasted_iota(jnp.int32, (rows, LANES), 1) // head_size
        sub = lax.broadcasted_iota(jnp.int32, (LANES, rows), 0) // head_size
        queries = q_ref[...]
        values_t = v_ref[...].T
        output = jnp.zeros((LANES, rows), F32)
        log_ref[...] = jnp.zeros_like(log_ref)
        for head in range(per_slab):
            own = jnp.where(lane == head, queries, jnp.zeros_like(queries))
            scores = across_lanes(k_ref[...], own) * factor + bias[...]
            top = jnp.max(scores, axis=0, keepdims=True)
            weights = jnp.exp2(scores - top)
            total = jnp.sum(weights, axis=0, keepdims=True)
            mixed = jnp.dot(values_t, weights.astype(BF16), preferred_element_type=F32) / total
            output = jnp.where(sub == head, mixed, output)
            log_ref[0, head : head + 1, :] = top + jnp.log2(total)
        out_ref[...] = output.T.astype(BF16)

    return pl.pallas_call(
        kernel,
        grid=(slabs,),
        out_shape=[
            jax.ShapeDtypeStruct((rows, width), BF16),
            jax.ShapeDtypeStruct((slabs, 8, rows), F32),
        ],
        in_specs=[
            pl.BlockSpec((rows, LANES), lambda j: (0, j)),
            pl.BlockSpec((keys, LANES), lambda j: (0, j)),
            pl.BlockSpec((keys, LANES), lambda j: (0, slabs + j)),
            pl.BlockSpec((1, rows), lambda j: (0, 0)),
            pl.BlockSpec((keys, 1), lambda j: (0, 0)),
        ],
        out_specs=[
            pl.BlockSpec((rows, LANES), lambda j: (0, j)),
            pl.BlockSpec((1, 8, rows), lambda j: (j, 0, 0)),
        ],
        scratch_shapes=[pltpu.VMEM((keys, rows), F32)],
        compiler_params=pltpu.CompilerParams(vmem_limit_bytes=40 << 20),
        name="attend_local",
    )(qkv, keys_values, keys_values, query_clip[None, :], key_clip[:, None])


def attend_local_back(qkv, keys_values, mixed, logs, grad_mixed, query_clip, key_clip, head_count):
    rows, triple = qkv.shape
    width = triple // 3
    keys = keys_values.shape[0]
    slabs = width // LANES
    head_size = width // head_count
    per_slab = LANES // head_size
    scale = head_size ** (-0.5)
    factor = scale * LOG2E

    def kernel(
        q_ref, k_ref, v_ref, mixed_ref, grad_ref, log_ref, query_ref, key_ref, dq_ref, dk_ref, dv_ref, bias
    ):
        fill_bias(bias, query_ref, key_ref)
        lane = lax.broadcasted_iota(jnp.int32, (rows, LANES), 1) // head_size
        key_lane = lax.broadcasted_iota(jnp.int32, (keys, LANES), 1) // head_size
        sub = lax.broadcasted_iota(jnp.int32, (LANES, rows), 0) // head_size
        queries = q_ref[...]
        grads = grad_ref[...]
        pick = (
            lax.broadcasted_iota(jnp.int32, (8, LANES), 1) // head_size
            == lax.broadcasted_iota(jnp.int32, (8, LANES), 0)
        ).astype(F32)
        deltas = lax.dot_general(
            pick,
            grads.astype(F32) * mixed_ref[...].astype(F32),
            (((1,), (1,)), ((), ())),
            precision=lax.Precision.HIGHEST,
            preferred_element_type=F32,
        )
        keys_t = k_ref[...].T
        dq = jnp.zeros((LANES, rows), F32)
        dk = jnp.zeros((keys, LANES), F32)
        dv = jnp.zeros((keys, LANES), F32)
        for head in range(per_slab):
            own = jnp.where(lane == head, queries, jnp.zeros_like(queries))
            own_grad = jnp.where(lane == head, grads, jnp.zeros_like(grads))
            scores = across_lanes(k_ref[...], own) * factor + bias[...]
            weights = jnp.exp2(scores - log_ref[0, head : head + 1, :])
            grad_soft = across_lanes(v_ref[...], own_grad)
            grad_scores = (weights * (grad_soft - deltas[head : head + 1, :])).astype(BF16)
            dv = jnp.where(
                key_lane == head, jnp.dot(weights.astype(BF16), grads, preferred_element_type=F32), dv
            )
            dk = jnp.where(key_lane == head, jnp.dot(grad_scores, queries, preferred_element_type=F32), dk)
            dq = jnp.where(sub == head, jnp.dot(keys_t, grad_scores, preferred_element_type=F32), dq)
        dq_ref[...] = (dq.T * scale).astype(BF16)
        dk_ref[...] = (dk * scale).astype(BF16)
        dv_ref[...] = dv.astype(BF16)

    return pl.pallas_call(
        kernel,
        grid=(slabs,),
        out_shape=[
            jax.ShapeDtypeStruct((rows, width), BF16),
            jax.ShapeDtypeStruct((keys, width), BF16),
            jax.ShapeDtypeStruct((keys, width), BF16),
        ],
        in_specs=[
            pl.BlockSpec((rows, LANES), lambda j: (0, j)),
            pl.BlockSpec((keys, LANES), lambda j: (0, j)),
            pl.BlockSpec((keys, LANES), lambda j: (0, slabs + j)),
            pl.BlockSpec((rows, LANES), lambda j: (0, j)),
            pl.BlockSpec((rows, LANES), lambda j: (0, j)),
            pl.BlockSpec((1, 8, rows), lambda j: (j, 0, 0)),
            pl.BlockSpec((1, rows), lambda j: (0, 0)),
            pl.BlockSpec((keys, 1), lambda j: (0, 0)),
        ],
        out_specs=[
            pl.BlockSpec((rows, LANES), lambda j: (0, j)),
            pl.BlockSpec((keys, LANES), lambda j: (0, j)),
            pl.BlockSpec((keys, LANES), lambda j: (0, j)),
        ],
        scratch_shapes=[pltpu.VMEM((keys, rows), F32)],
        compiler_params=pltpu.CompilerParams(vmem_limit_bytes=50 << 20),
        name="attend_local_back",
    )(
        qkv,
        keys_values,
        keys_values,
        mixed,
        grad_mixed,
        logs,
        query_clip[None, :],
        key_clip[:, None],
    )


def fast_forward(residual, norms, w_qkv, w_out, w_up, w_down, head_count, clips, collective_id):
    rows, width = residual.shape
    normed = layer_norm(residual, norms[0], norms[1]).astype(BF16)
    qkv = jnp.dot(normed, w_qkv, preferred_element_type=F32).astype(BF16)
    keys_values = gather_keys(qkv, collective_id).reshape(4 * rows, 2 * width)
    mixed, logs = attend_local(qkv, keys_values, clips[0], clips[1], head_count)
    middle = residual + jnp.dot(mixed, w_out, preferred_element_type=F32)
    normed_mid = layer_norm(middle, norms[2], norms[3]).astype(BF16)
    pre = jnp.dot(normed_mid, w_up, preferred_element_type=F32)
    hidden = gelu_exact(pre).astype(BF16)
    result = middle + jnp.dot(hidden, w_down, preferred_element_type=F32)
    return result, (residual, normed, qkv, keys_values, mixed, logs, middle, normed_mid, pre, hidden)


def fast_backward(grad_result, kept, norms, w_qkv, w_out, w_up, w_down, head_count, clips, collective_id):
    residual, normed, qkv, keys_values, mixed, logs, middle, normed_mid, pre, hidden = kept
    rows, width = residual.shape
    grad_low = grad_result.astype(BF16)
    grad_down = jnp.einsum("tf,tw->fw", hidden, grad_low, preferred_element_type=F32)
    grad_hidden = jnp.einsum("tw,fw->tf", grad_low, w_down, preferred_element_type=F32)
    _, gelu_pull = jax.vjp(gelu_exact, pre)
    grad_pre = gelu_pull(grad_hidden)[0].astype(BF16)
    grad_up = jnp.einsum("tw,tf->wf", normed_mid, grad_pre, preferred_element_type=F32)
    grad_normed_mid = jnp.einsum("tf,wf->tw", grad_pre, w_up, preferred_element_type=F32)
    _, second_pull = jax.vjp(layer_norm, middle, norms[2], norms[3])
    grad_mid_norm, grad_gain_two, grad_shift_two = second_pull(grad_normed_mid)
    grad_middle = grad_result + grad_mid_norm
    grad_branch = grad_middle.astype(BF16)
    grad_out_w = jnp.einsum("tv,tw->vw", mixed, grad_branch, preferred_element_type=F32)
    grad_mixed = jnp.einsum("tw,vw->tv", grad_branch, w_out, preferred_element_type=F32).astype(BF16)
    dq, dk, dv = attend_local_back(
        qkv, keys_values, mixed, logs, grad_mixed, clips[0], clips[1], head_count
    )
    dk, dv = sum_keys([dk.reshape(4, rows, width), dv.reshape(4, rows, width)], collective_id)
    grad_qkv = jnp.concatenate([dq, dk, dv], axis=1)
    grad_qkv_w = jnp.einsum("tw,tc->wc", normed, grad_qkv, preferred_element_type=F32)
    grad_normed = jnp.einsum("tc,wc->tw", grad_qkv, w_qkv, preferred_element_type=F32)
    _, first_pull = jax.vjp(layer_norm, residual, norms[0], norms[1])
    grad_first_norm, grad_gain_one, grad_shift_one = first_pull(grad_normed)
    small = [grad_gain_one, grad_shift_one, grad_gain_two, grad_shift_two]
    return grad_middle + grad_first_norm, small, (grad_qkv_w, grad_out_w, grad_up, grad_down)


def trade_pairs():
    pairs = []
    for f in range(8):
        for s in range(4):
            core, high, low = f & 1, s >> 1, s & 1
            if core != high:
                pairs.append((f * 4 + s, ((f & 6) | high) * 4 + (core * 2 + low)))
    return pairs


def trade(values):
    moved = lax.ppermute(values, ("fsdp", "seq"), trade_pairs())
    stays = (lax.axis_index("fsdp") & 1) == (lax.axis_index("seq") >> 1)
    return jnp.where(stays, values, moved)


def pack_small(wide, narrow, wide_count, narrow_count):
    block = jnp.concatenate(
        [wide, jnp.pad(narrow, ((0, 0), (0, LANES - narrow.shape[1])))], axis=0
    )
    return jnp.pad(block, ((0, SMALL_ROWS - block.shape[0]), (0, 0)))


def fast_local(
    tokens,
    clip_lengths,
    target_pos,
    out_grad,
    norm1_gain,
    norm1_bias,
    w_qkv,
    w_out,
    norm2_gain,
    norm2_bias,
    w_fc1,
    w_fc2,
    w_embed,
    mask_token,
    pred_norm1_gain,
    pred_norm1_bias,
    pred_qkv,
    pred_out,
    pred_norm2_gain,
    pred_norm2_bias,
    pred_fc1,
    pred_fc2,
):
    rows, width = tokens.shape
    narrow_width = out_grad.shape[1]
    wide_part = norm1_gain.shape[0]
    narrow_part = mask_token.shape[0]
    small = pack_small(
        jnp.stack([norm1_gain, norm1_bias, norm2_gain, norm2_bias]),
        jnp.stack([pred_norm1_gain, pred_norm1_bias, pred_norm2_gain, pred_norm2_bias, mask_token]),
        4,
        5,
    )
    gathered = gather_weights(
        [small, w_qkv, w_out, w_fc1, w_fc2, w_embed, pred_qkv, pred_out, pred_fc1, pred_fc2]
    )
    smalls = gathered[0].astype(F32)
    norms = [smalls[:, i, :wide_part].reshape(-1) for i in range(4)]
    pred_norms = [smalls[:, 4 + i, :narrow_part].reshape(-1) for i in range(5)]
    whole = [one.reshape(-1, one.shape[-1]) for one in gathered[1:]]

    core = lax.axis_index("fsdp") & 1
    high = lax.axis_index("seq") >> 1
    tokens = trade(tokens)
    out_grad = trade(out_grad)
    target_pos = trade(target_pos)
    other_lengths = lax.ppermute(clip_lengths, "fsdp", [(f, f ^ 1) for f in range(8)])
    lengths = jnp.where(core == high, clip_lengths, other_lengths)[0]

    clip_ends = jnp.cumsum(lengths)
    local_rows = quarter() * rows + jnp.arange(rows, dtype=jnp.int32)
    query_clip = clip_index(local_rows, clip_ends)
    key_clip = clip_index(jnp.arange(4 * rows, dtype=jnp.int32), clip_ends)
    past_end = (local_rows[:, None] >= clip_ends[None, :]).astype(jnp.int32)
    rel_rows = local_rows - jnp.sum(lengths[None, :] * past_end, axis=1)
    clips = (query_clip, key_clip)

    ctx_result, ctx_kept = fast_forward(
        tokens.astype(F32), norms, whole[0], whole[1], whole[2], whole[3], HEADS, clips, 3
    )
    context_out = ctx_result.astype(BF16)
    embedded = jnp.dot(context_out, whole[4], preferred_element_type=F32)
    targets = target_pos[0, 0]
    matches = jnp.arange(rows, dtype=jnp.int32)[:, None] == targets[None, :]
    placement = matches.astype(F32)
    target_hit = jnp.sum(placement, axis=1)
    target_rel = jnp.sum(jnp.where(matches, rel_rows[:, None], 0), axis=0)
    mask_rows = pred_norms[4][None, :] + position_table(target_rel, narrow_width)
    placed = jnp.dot(placement, mask_rows, precision=lax.Precision.HIGHEST, preferred_element_type=F32)
    pred_in = embedded * (1.0 - target_hit[:, None]) + placed
    pred_result, pred_kept = fast_forward(
        pred_in, pred_norms, whole[5], whole[6], whole[7], whole[8], P_HEADS, clips, 4
    )
    predicted = pred_result.astype(BF16)
    grad_pred_in, pred_small, pred_grads = fast_backward(
        out_grad.astype(F32), pred_kept, pred_norms, whole[5], whole[6], whole[7], whole[8], P_HEADS, clips, 5
    )
    grad_mask = jnp.sum(target_hit[:, None] * grad_pred_in, axis=0)
    grad_embedded = (grad_pred_in * (1.0 - target_hit[:, None])).astype(BF16)
    grad_embed_w = jnp.einsum("td,tp->dp", context_out, grad_embedded, preferred_element_type=F32)
    grad_context = jnp.einsum("tp,dp->td", grad_embedded, whole[4], preferred_element_type=F32)
    grad_tokens, ctx_small, ctx_grads = fast_backward(
        grad_context, ctx_kept, norms, whole[0], whole[1], whole[2], whole[3], HEADS, clips, 6
    )

    wide_grads = jnp.stack(ctx_small).reshape(4, 8, wide_part).transpose(1, 0, 2)
    narrow_grads = jnp.stack(pred_small + [grad_mask]).reshape(5, 8, narrow_part).transpose(1, 0, 2)
    small_grads = jnp.concatenate(
        [wide_grads, jnp.pad(narrow_grads, ((0, 0), (0, 0), (0, LANES - narrow_part)))], axis=1
    )
    small_grads = jnp.pad(small_grads, ((0, 0), (0, SMALL_ROWS - 9), (0, 0)))

    def split(grad):
        return grad.reshape(8, grad.shape[0] // 8, grad.shape[1]).astype(BF16)

    sums = sum_gradients(
        [split(one) for one in (pred_grads[3], pred_grads[2], pred_grads[1], pred_grads[0], grad_embed_w)]
        + [split(one) for one in (ctx_grads[3], ctx_grads[2], ctx_grads[1], ctx_grads[0])]
        + [small_grads.astype(BF16)]
    )
    sums = [one.astype(F32) for one in sums]
    final_small = sums[9]
    wide_out = [final_small[i, :wide_part] for i in range(4)]
    narrow_out = [final_small[4 + i, :narrow_part] for i in range(5)]
    return (
        trade(context_out),
        trade(predicted),
        trade(grad_tokens.astype(BF16)),
        wide_out[0],
        wide_out[1],
        sums[8],
        sums[7],
        wide_out[2],
        wide_out[3],
        sums[6],
        sums[5],
        sums[4],
        narrow_out[4],
        narrow_out[0],
        narrow_out[1],
        sums[3],
        sums[2],
        narrow_out[2],
        narrow_out[3],
        sums[1],
        sums[0],
    )


def solution(mesh):
    body = fast_local if fits_fast(mesh) else local
    return jax.shard_map(
        body,
        mesh=mesh,
        in_specs=(
            P(("fsdp", "seq"), None),
            P("fsdp", None),
            P("fsdp", "seq", None),
            P(("fsdp", "seq"), None),
            P("fsdp"),
            P("fsdp"),
            P("fsdp", None),
            P("fsdp", None),
            P("fsdp"),
            P("fsdp"),
            P("fsdp", None),
            P("fsdp", None),
            P("fsdp", None),
            P("fsdp"),
            P("fsdp"),
            P("fsdp"),
            P("fsdp", None),
            P("fsdp", None),
            P("fsdp"),
            P("fsdp"),
            P("fsdp", None),
            P("fsdp", None),
        ),
        out_specs=(
            P(("fsdp", "seq"), None),
            P(("fsdp", "seq"), None),
            P(("fsdp", "seq"), None),
            P("fsdp"),
            P("fsdp"),
            P("fsdp", None),
            P("fsdp", None),
            P("fsdp"),
            P("fsdp"),
            P("fsdp", None),
            P("fsdp", None),
            P("fsdp", None),
            P("fsdp"),
            P("fsdp"),
            P("fsdp"),
            P("fsdp", None),
            P("fsdp", None),
            P("fsdp"),
            P("fsdp"),
            P("fsdp", None),
            P("fsdp", None),
        ),
        check_vma=False,
    )
```

```python
import math

import jax
import jax.numpy as jnp
from jax import lax
from jax.experimental import pallas as pl
from jax.experimental.pallas import tpu as pltpu
from jax.sharding import PartitionSpec as P

HEADS = 16
PD = 384
P_HEADS = 12


EPSILON = 1e-06
NEG_FILL = -1e30
block_rows = 512


def layer_norm(values, norm_gain, norm_shift):
    center = values - jnp.mean(values, axis=-1, keepdims=True)
    spread = jnp.mean(center * center, axis=-1, keepdims=True)
    return center * lax.rsqrt(spread + EPSILON) * norm_gain + norm_shift


def gelu_exact(values):
    return jax.nn.gelu(values, approximate=False)


def position_table(positions, table_width):
    half_width = table_width // 2
    angle_rates = jnp.exp(
        jnp.arange(half_width, dtype=jnp.float32) * (-2.0 * math.log(10000.0) / table_width)
    )
    angles = positions.astype(jnp.float32)[:, None] * angle_rates[None, :]
    return jnp.concatenate([jnp.sin(angles), jnp.cos(angles)], axis=1)


def clip_index(positions, clip_ends):
    return jnp.sum((positions[:, None] >= clip_ends[None, :]).astype(jnp.int32), axis=1)


def key_step(total_keys):
    return max(min(total_keys, block_rows), total_keys // 8)


def block_scores(queries, key_part, query_clip, key_clip_part, score_scale):
    raw_scores = (
        jnp.einsum("the,khe->htk", queries, key_part, preferred_element_type=jnp.float32)
        * score_scale
    )
    same_clip = query_clip[:, None] == key_clip_part[None, :]
    return jnp.where(same_clip[None], raw_scores, NEG_FILL)


def attend_forward(queries, key_heads, value_heads, query_clip, key_clip):
    row_count, head_count, head_size = queries.shape
    score_scale = head_size ** (-0.5)
    total_keys = key_heads.shape[0]
    step_rows = key_step(total_keys)
    run_max = jnp.full((head_count, row_count), NEG_FILL, jnp.float32)
    run_total = jnp.zeros((head_count, row_count), jnp.float32)
    for key_start in range(0, total_keys, step_rows):
        scores = block_scores(
            queries,
            key_heads[key_start : key_start + step_rows],
            query_clip,
            key_clip[key_start : key_start + step_rows],
            score_scale,
        )
        new_max = jnp.maximum(run_max, jnp.max(scores, axis=2))
        run_total = run_total * jnp.exp(run_max - new_max) + jnp.sum(
            jnp.exp(scores - new_max[:, :, None]), axis=2
        )
        run_max = new_max
    log_total = run_max + jnp.log(run_total)
    output = jnp.zeros((row_count, head_count, head_size), jnp.float32)
    for key_start in range(0, total_keys, step_rows):
        scores = block_scores(
            queries,
            key_heads[key_start : key_start + step_rows],
            query_clip,
            key_clip[key_start : key_start + step_rows],
            score_scale,
        )
        soft_weights = jnp.exp(scores - log_total[:, :, None]).astype(jnp.bfloat16)
        output = output + jnp.einsum(
            "htk,khe->the",
            soft_weights,
            value_heads[key_start : key_start + step_rows],
            preferred_element_type=jnp.float32,
        )
    return (output, log_total)


def attend_backward(
    queries, key_heads, value_heads, query_clip, key_clip, log_total, grad_mixed, output
):
    row_count, head_count, head_size = queries.shape
    score_scale = head_size ** (-0.5)
    total_keys = key_heads.shape[0]
    step_rows = key_step(total_keys)
    row_delta = jnp.sum(grad_mixed.astype(jnp.float32) * output, axis=2).T
    grad_query = jnp.zeros((row_count, head_count, head_size), jnp.float32)
    key_pieces = []
    value_pieces = []
    for key_start in range(0, total_keys, step_rows):
        key_part = key_heads[key_start : key_start + step_rows]
        value_part = value_heads[key_start : key_start + step_rows]
        scores = block_scores(
            queries, key_part, query_clip, key_clip[key_start : key_start + step_rows], score_scale
        )
        soft_weights = jnp.exp(scores - log_total[:, :, None])
        grad_soft = jnp.einsum(
            "the,khe->htk", grad_mixed, value_part, preferred_element_type=jnp.float32
        )
        grad_scores = (soft_weights * (grad_soft - row_delta[:, :, None])).astype(jnp.bfloat16)
        grad_query = grad_query + jnp.einsum(
            "htk,khe->the", grad_scores, key_part, preferred_element_type=jnp.float32
        )
        key_pieces.append(
            jnp.einsum("htk,the->khe", grad_scores, queries, preferred_element_type=jnp.float32)
        )
        value_pieces.append(
            jnp.einsum(
                "htk,the->khe",
                soft_weights.astype(jnp.bfloat16),
                grad_mixed,
                preferred_element_type=jnp.float32,
            )
        )
    key_terms = jnp.concatenate(key_pieces, axis=0) * score_scale
    value_terms = jnp.concatenate(value_pieces, axis=0)
    return (grad_query * score_scale, key_terms, value_terms)


def block_forward(
    residual, norm_params, w_qkv, w_out, w_up, w_down, head_count, query_clip, key_clip
):
    row_count, model_width = residual.shape
    head_size = model_width // head_count
    norm_float = norm_params.astype(jnp.float32)
    normed = layer_norm(residual, norm_float[:, 0], norm_float[:, 1]).astype(jnp.bfloat16)
    qkv = jnp.dot(normed, w_qkv, preferred_element_type=jnp.float32).astype(jnp.bfloat16)
    queries = qkv[:, :model_width].reshape(row_count, head_count, head_size)
    key_local = qkv[:, model_width : 2 * model_width]
    value_local = qkv[:, 2 * model_width :]
    key_full, value_full = (
        lax.all_gather(key_local, "seq", axis=0, tiled=True),
        lax.all_gather(value_local, "seq", axis=0, tiled=True),
    )
    key_heads = key_full.reshape(-1, head_count, head_size)
    value_heads = value_full.reshape(-1, head_count, head_size)
    output, log_total = attend_forward(queries, key_heads, value_heads, query_clip, key_clip)
    mixed = output.reshape(row_count, model_width).astype(jnp.bfloat16)
    middle = residual + jnp.dot(mixed, w_out, preferred_element_type=jnp.float32)
    normed_mid = layer_norm(middle, norm_float[:, 2], norm_float[:, 3]).astype(jnp.bfloat16)
    pre_act = jnp.dot(normed_mid, w_up, preferred_element_type=jnp.float32)
    hidden = gelu_exact(pre_act).astype(jnp.bfloat16)
    result = middle + jnp.dot(hidden, w_down, preferred_element_type=jnp.float32)
    kept = (
        residual,
        normed,
        queries,
        key_local,
        value_local,
        key_heads,
        value_heads,
        output,
        log_total,
        mixed,
        middle,
        normed_mid,
        pre_act,
        hidden,
    )
    return (result, kept)


def block_backward(
    grad_result, kept, norm_params, w_qkv, w_out, w_up, w_down, head_count, query_clip, key_clip
):
    (
        residual,
        normed,
        queries,
        key_local,
        value_local,
        key_heads,
        value_heads,
        output,
        log_total,
        mixed,
        middle,
        normed_mid,
        pre_act,
        hidden,
    ) = kept
    row_count, model_width = residual.shape
    head_size = model_width // head_count
    norm_float = norm_params.astype(jnp.float32)
    grad_low = grad_result.astype(jnp.bfloat16)
    grad_down = jnp.einsum("tf,tw->fw", hidden, grad_low, preferred_element_type=jnp.float32)
    grad_hidden = jnp.einsum("tw,fw->tf", grad_low, w_down, preferred_element_type=jnp.float32)
    gelu_value, gelu_pull = jax.vjp(gelu_exact, pre_act)
    grad_pre = gelu_pull(grad_hidden)[0].astype(jnp.bfloat16)
    grad_up = jnp.einsum("tw,tf->wf", normed_mid, grad_pre, preferred_element_type=jnp.float32)
    grad_normed_mid = jnp.einsum("tf,wf->tw", grad_pre, w_up, preferred_element_type=jnp.float32)
    second_value, second_pull = jax.vjp(layer_norm, middle, norm_float[:, 2], norm_float[:, 3])
    grad_mid_norm, grad_gain_two, grad_shift_two = second_pull(grad_normed_mid)
    grad_middle = grad_result + grad_mid_norm
    grad_branch = grad_middle.astype(jnp.bfloat16)
    grad_out_w = jnp.einsum("tv,tw->vw", mixed, grad_branch, preferred_element_type=jnp.float32)
    grad_mixed = jnp.einsum(
        "tw,vw->tv", grad_branch, w_out, preferred_element_type=jnp.float32
    ).astype(jnp.bfloat16)
    key_full, value_full = (
        lax.all_gather(key_local, "seq", axis=0, tiled=True),
        lax.all_gather(value_local, "seq", axis=0, tiled=True),
    )
    key_heads = key_full.reshape(-1, head_count, head_size)
    value_heads = value_full.reshape(-1, head_count, head_size)
    grad_query, key_terms, value_terms = attend_backward(
        queries,
        key_heads,
        value_heads,
        query_clip,
        key_clip,
        log_total,
        grad_mixed.reshape(row_count, head_count, head_size),
        output,
    )
    grad_key, grad_value = (
        lax.psum_scatter(
            key_terms.reshape(-1, model_width).astype(jnp.bfloat16),
            "seq",
            scatter_dimension=0,
            tiled=True,
        ).astype(jnp.float32),
        lax.psum_scatter(
            value_terms.reshape(-1, model_width).astype(jnp.bfloat16),
            "seq",
            scatter_dimension=0,
            tiled=True,
        ).astype(jnp.float32),
    )
    grad_qkv = jnp.concatenate(
        [grad_query.reshape(row_count, model_width), grad_key, grad_value], axis=1
    ).astype(jnp.bfloat16)
    grad_qkv_w = jnp.einsum("tw,tc->wc", normed, grad_qkv, preferred_element_type=jnp.float32)
    grad_normed = jnp.einsum("tc,wc->tw", grad_qkv, w_qkv, preferred_element_type=jnp.float32)
    first_value, first_pull = jax.vjp(layer_norm, residual, norm_float[:, 0], norm_float[:, 1])
    grad_first_norm, grad_gain_one, grad_shift_one = first_pull(grad_normed)
    grad_norms = jnp.stack([grad_gain_one, grad_shift_one, grad_gain_two, grad_shift_two], axis=1)
    return (grad_middle + grad_first_norm, (grad_norms, grad_qkv_w, grad_out_w, grad_up, grad_down))


def local(
    tokens,
    clip_lengths,
    target_pos,
    out_grad,
    norm1_gain,
    norm1_bias,
    w_qkv,
    w_out,
    norm2_gain,
    norm2_bias,
    w_fc1,
    w_fc2,
    w_embed,
    mask_token,
    pred_norm1_gain,
    pred_norm1_bias,
    pred_qkv,
    pred_out,
    pred_norm2_gain,
    pred_norm2_bias,
    pred_fc1,
    pred_fc2,
):
    row_count = tokens.shape[0]
    group_count = row_count * lax.axis_size("seq")
    lengths = clip_lengths[0]
    clip_ends = jnp.cumsum(lengths)
    local_rows = lax.axis_index("seq") * row_count + jnp.arange(row_count, dtype=jnp.int32)
    query_clip = clip_index(local_rows, clip_ends)
    key_clip = clip_index(jnp.arange(group_count, dtype=jnp.int32), clip_ends)
    past_end = (local_rows[:, None] >= clip_ends[None, :]).astype(jnp.int32)
    rel_rows = local_rows - jnp.sum(lengths[None, :] * past_end, axis=1)
    ctx_small = jnp.stack([norm1_gain, norm1_bias, norm2_gain, norm2_bias], axis=1)
    pred_small = jnp.stack(
        [pred_norm1_gain, pred_norm1_bias, pred_norm2_gain, pred_norm2_bias, mask_token], axis=1
    )
    ctx_params = (
        lax.all_gather(ctx_small, "fsdp", axis=0, tiled=True),
        lax.all_gather(w_qkv, "fsdp", axis=0, tiled=True),
        lax.all_gather(w_out, "fsdp", axis=0, tiled=True),
        lax.all_gather(w_fc1, "fsdp", axis=0, tiled=True),
        lax.all_gather(w_fc2, "fsdp", axis=0, tiled=True),
    )
    pred_params = (
        lax.all_gather(pred_small, "fsdp", axis=0, tiled=True),
        lax.all_gather(w_embed, "fsdp", axis=0, tiled=True),
        lax.all_gather(pred_qkv, "fsdp", axis=0, tiled=True),
        lax.all_gather(pred_out, "fsdp", axis=0, tiled=True),
        lax.all_gather(pred_fc1, "fsdp", axis=0, tiled=True),
        lax.all_gather(pred_fc2, "fsdp", axis=0, tiled=True),
    )
    ctx_result, ctx_kept = block_forward(
        tokens.astype(jnp.float32),
        ctx_params[0],
        ctx_params[1],
        ctx_params[2],
        ctx_params[3],
        ctx_params[4],
        HEADS,
        query_clip,
        key_clip,
    )
    context_out = ctx_result.astype(jnp.bfloat16)
    embedded = jnp.dot(context_out, pred_params[1], preferred_element_type=jnp.float32)
    targets = target_pos[0, 0]
    matches = jnp.arange(row_count, dtype=jnp.int32)[:, None] == targets[None, :]
    placement = matches.astype(jnp.float32)
    target_hit = jnp.sum(placement, axis=1)
    target_rel = jnp.sum(jnp.where(matches, rel_rows[:, None], 0), axis=0)
    mask_rows = pred_params[0][:, 4].astype(jnp.float32)[None, :] + position_table(target_rel, PD)
    placed = jnp.dot(
        placement, mask_rows, precision=lax.Precision.HIGHEST, preferred_element_type=jnp.float32
    )
    pred_in = embedded * (1.0 - target_hit[:, None]) + placed
    pred_result, pred_kept = block_forward(
        pred_in,
        pred_params[0],
        pred_params[2],
        pred_params[3],
        pred_params[4],
        pred_params[5],
        P_HEADS,
        query_clip,
        key_clip,
    )
    predicted = pred_result.astype(jnp.bfloat16)
    pred_back = (
        lax.all_gather(pred_small, "fsdp", axis=0, tiled=True),
        lax.all_gather(w_embed, "fsdp", axis=0, tiled=True),
        lax.all_gather(pred_qkv, "fsdp", axis=0, tiled=True),
        lax.all_gather(pred_out, "fsdp", axis=0, tiled=True),
        lax.all_gather(pred_fc1, "fsdp", axis=0, tiled=True),
        lax.all_gather(pred_fc2, "fsdp", axis=0, tiled=True),
    )
    ctx_back = (
        lax.all_gather(ctx_small, "fsdp", axis=0, tiled=True),
        lax.all_gather(w_qkv, "fsdp", axis=0, tiled=True),
        lax.all_gather(w_out, "fsdp", axis=0, tiled=True),
        lax.all_gather(w_fc1, "fsdp", axis=0, tiled=True),
        lax.all_gather(w_fc2, "fsdp", axis=0, tiled=True),
    )
    grad_pred_in, pred_grads = block_backward(
        out_grad.astype(jnp.float32),
        pred_kept,
        pred_back[0],
        pred_back[2],
        pred_back[3],
        pred_back[4],
        pred_back[5],
        P_HEADS,
        query_clip,
        key_clip,
    )
    grad_mask = jnp.sum(target_hit[:, None] * grad_pred_in, axis=0)
    grad_embedded = (grad_pred_in * (1.0 - target_hit[:, None])).astype(jnp.bfloat16)
    grad_embed_w = jnp.einsum(
        "td,tp->dp", context_out, grad_embedded, preferred_element_type=jnp.float32
    )
    grad_context = jnp.einsum(
        "tp,dp->td", grad_embedded, pred_back[1], preferred_element_type=jnp.float32
    )
    grad_tokens, ctx_grads = block_backward(
        grad_context,
        ctx_kept,
        ctx_back[0],
        ctx_back[1],
        ctx_back[2],
        ctx_back[3],
        ctx_back[4],
        HEADS,
        query_clip,
        key_clip,
    )
    pred_small_grad = jnp.concatenate([pred_grads[0], grad_mask[:, None]], axis=1)
    row_sums = (
        lax.psum_scatter(ctx_grads[0], "fsdp", scatter_dimension=0, tiled=True),
        lax.psum_scatter(ctx_grads[1], "fsdp", scatter_dimension=0, tiled=True),
        lax.psum_scatter(ctx_grads[2], "fsdp", scatter_dimension=0, tiled=True),
        lax.psum_scatter(ctx_grads[3], "fsdp", scatter_dimension=0, tiled=True),
        lax.psum_scatter(ctx_grads[4], "fsdp", scatter_dimension=0, tiled=True),
        lax.psum_scatter(grad_embed_w, "fsdp", scatter_dimension=0, tiled=True),
        lax.psum_scatter(pred_small_grad, "fsdp", scatter_dimension=0, tiled=True),
        lax.psum_scatter(pred_grads[1], "fsdp", scatter_dimension=0, tiled=True),
        lax.psum_scatter(pred_grads[2], "fsdp", scatter_dimension=0, tiled=True),
        lax.psum_scatter(pred_grads[3], "fsdp", scatter_dimension=0, tiled=True),
        lax.psum_scatter(pred_grads[4], "fsdp", scatter_dimension=0, tiled=True),
    )
    summed = (
        lax.psum(row_sums[0].astype(jnp.bfloat16), "seq").astype(jnp.float32),
        lax.psum(row_sums[1].astype(jnp.bfloat16), "seq").astype(jnp.float32),
        lax.psum(row_sums[2].astype(jnp.bfloat16), "seq").astype(jnp.float32),
        lax.psum(row_sums[3].astype(jnp.bfloat16), "seq").astype(jnp.float32),
        lax.psum(row_sums[4].astype(jnp.bfloat16), "seq").astype(jnp.float32),
        lax.psum(row_sums[5].astype(jnp.bfloat16), "seq").astype(jnp.float32),
        lax.psum(row_sums[6].astype(jnp.bfloat16), "seq").astype(jnp.float32),
        lax.psum(row_sums[7].astype(jnp.bfloat16), "seq").astype(jnp.float32),
        lax.psum(row_sums[8].astype(jnp.bfloat16), "seq").astype(jnp.float32),
        lax.psum(row_sums[9].astype(jnp.bfloat16), "seq").astype(jnp.float32),
        lax.psum(row_sums[10].astype(jnp.bfloat16), "seq").astype(jnp.float32),
    )
    return (
        context_out,
        predicted,
        grad_tokens.astype(jnp.bfloat16),
        summed[0][:, 0],
        summed[0][:, 1],
        summed[1],
        summed[2],
        summed[0][:, 2],
        summed[0][:, 3],
        summed[3],
        summed[4],
        summed[5],
        summed[6][:, 4],
        summed[6][:, 0],
        summed[6][:, 1],
        summed[7],
        summed[8],
        summed[6][:, 2],
        summed[6][:, 3],
        summed[9],
        summed[10],
    )


BF16 = jnp.bfloat16
F32 = jnp.float32
MESH = pl.DeviceIdType.MESH
LOG2E = 1.4426950408889634
LN2 = 0.6931471805599453
LANES = 128
SMALL_ROWS = 16
ANYWHERE = pl.BlockSpec(memory_space=pl.ANY)
IN_VMEM = pl.BlockSpec(memory_space=pltpu.VMEM)


def fits_fast(mesh):
    return mesh.shape["fsdp"] == 8 and mesh.shape["seq"] == 4


def fsdp_peer(bit):
    return (lax.axis_index("fsdp") ^ bit, lax.axis_index("seq"))


def seq_peer(index):
    return (lax.axis_index("fsdp"), index)


def enter(peers):
    barrier = pltpu.get_barrier_semaphore()
    for peer in peers:
        pl.semaphore_signal(barrier, inc=1, device_id=peer, device_id_type=MESH)
    pl.semaphore_wait(barrier, len(peers))


def send(src, dst, send_sem, recv_sem, peer):
    return pltpu.make_async_remote_copy(
        src_ref=src,
        dst_ref=dst,
        send_sem=send_sem,
        recv_sem=recv_sem,
        device_id=peer,
        device_id_type=MESH,
    )


def remote_params(collective_id, vmem=None):
    return pltpu.CompilerParams(
        collective_id=collective_id, has_side_effects=True, vmem_limit_bytes=vmem
    )


def cut_units(shapes):
    units = []
    flip = False
    for index, (rows, columns) in enumerate(shapes):
        if rows * columns >= 100000 and rows % 32 == 0:
            half = rows // 2
            units.append((index, 0, half, 2, 4))
            units.append((index, half, half, 4, 2))
        else:
            units.append((index, 0, rows, 4, 2) if flip else (index, 0, rows, 2, 4))
            flip = not flip
    return units


def gather_weights(shards):
    shapes = [shard.shape for shard in shards]
    units = cut_units(shapes)
    count = len(units)
    array_count = len(shards)

    def kernel(*refs):
        sources = refs[:array_count]
        gathered = refs[array_count : 2 * array_count]
        send_sems, recv_sems, local_sems = refs[2 * array_count :]
        me = lax.axis_index("fsdp")
        enter([fsdp_peer(1), fsdp_peer(2), fsdp_peer(4)])

        def part(unit, owner):
            index, first, rows, _, _ = units[unit]
            return gathered[index].at[owner, pl.ds(first, rows)]

        def own(unit):
            index, first, rows, _, _ = units[unit]
            return sources[index].at[pl.ds(first, rows)]

        def copy(unit, slot, owner, bit, first_hand=False):
            src = own(unit) if first_hand else part(unit, owner)
            return send(
                src,
                part(unit, owner),
                send_sems.at[unit, slot],
                recv_sems.at[unit, slot],
                fsdp_peer(bit),
            )

        def launch(unit):
            _, _, _, near, far = units[unit]
            copies = [
                copy(unit, 0, me, near, True),
                copy(unit, 1, me, far, True),
                copy(unit, 3, me, 1, True),
            ]
            for one in copies:
                one.start()
            local_copy = pltpu.make_async_copy(own(unit), part(unit, me), local_sems.at[unit])
            local_copy.start()
            return copies + [local_copy]

        def arrive(unit):
            _, _, _, near, far = units[unit]
            copy(unit, 0, me, near, True).wait_recv()
            forward = [copy(unit, 2, me ^ near, far), copy(unit, 4, me ^ near, 1)]
            for one in forward:
                one.start()
            copy(unit, 1, me, far, True).wait_recv()
            last = copy(unit, 5, me ^ far, 1)
            last.start()
            return forward + [last]

        def relay(unit):
            _, _, _, near, far = units[unit]
            copy(unit, 2, me ^ near, far).wait_recv()
            last = copy(unit, 6, me ^ near ^ far, 1)
            last.start()
            return [last]

        sent = []
        local_copies = []
        ahead = 3
        for unit in range(min(ahead, count)):
            started = launch(unit)
            sent += started[:3]
            local_copies.append(started[3])
        for unit in range(count + 1):
            if unit < count:
                sent += arrive(unit)
                if unit + ahead < count:
                    started = launch(unit + ahead)
                    sent += started[:3]
                    local_copies.append(started[3])
            if unit >= 1:
                sent += relay(unit - 1)
        for unit in range(count):
            _, _, _, near, far = units[unit]
            copy(unit, 3, me, 1, True).wait_recv()
            copy(unit, 4, me ^ near, 1).wait_recv()
            copy(unit, 5, me ^ far, 1).wait_recv()
            copy(unit, 6, me ^ near ^ far, 1).wait_recv()
        for one in sent:
            one.wait_send()
        for one in local_copies:
            one.wait()

    return pl.pallas_call(
        kernel,
        out_shape=[jax.ShapeDtypeStruct((8,) + shard.shape, shard.dtype) for shard in shards],
        in_specs=[ANYWHERE] * array_count,
        out_specs=[ANYWHERE] * array_count,
        scratch_shapes=[
            pltpu.SemaphoreType.DMA((count, 7)),
            pltpu.SemaphoreType.DMA((count, 7)),
            pltpu.SemaphoreType.DMA((count,)),
        ],
        compiler_params=remote_params(1),
        name="gather_weights",
    )(*shards)


class Unit:
    def __init__(self, index, first, columns, order, place):
        self.index = index
        self.first = first
        self.columns = columns
        self.near, self.far = order
        self.place = place


def cut_columns(shapes, most):
    units = []
    for index, (rows, columns) in enumerate(shapes):
        pieces = 1
        while rows * (columns // pieces) > most and (columns // pieces) % (2 * LANES) == 0:
            pieces *= 2
        for place in range(pieces):
            order = (2, 4) if len(units) % 2 == 0 else (4, 2)
            units.append(Unit(index, place * (columns // pieces), columns // pieces, order, place))
    return units


def back_and_sum(
    partials,
    qkv,
    keys_values,
    mixed,
    grad_mixed,
    logs,
    query_clip,
    key_clip,
    normed_both_t,
    w_qkv,
    tokens,
    grad_middle,
    gain,
    head_count,
    collective_id,
):
    rows, triple = qkv.shape
    width = triple // 3
    keys = keys_values.shape[0]
    slabs = width // LANES
    head_size = width // head_count
    per_slab = LANES // head_size
    scale = head_size ** (-0.5)
    factor = scale * LOG2E
    part_rows = w_qkv.shape[1]

    given = len(partials)
    shapes = [partial.shape[1:] for partial in partials] + [(part_rows, triple), (SMALL_ROWS, LANES)]
    qkv_index, small_index = given, given + 1
    array_count = given + 2
    units = cut_columns(shapes, 70000)
    count = len(units)
    pieces = [sum(1 for unit in units if unit.index == index) for index in range(array_count)]

    def kernel(*refs):
        sources = refs[:given]
        (
            qkv_ref,
            kv_ref,
            mixed_ref,
            grad_ref,
            log_ref,
            query_ref,
            key_ref,
            normed_t_ref,
            w_ref,
            tokens_ref,
            middle_ref,
            gain_ref,
        ) = refs[given : given + 12]
        results = refs[given + 12 : given + 12 + array_count]
        token_out = refs[given + 12 + array_count]
        rest = list(refs[given + 13 + array_count :])
        acc, near_in, far_in, outer_in, inner_in = [
            rest[group * array_count : (group + 1) * array_count] for group in range(5)
        ]
        (
            late_out,
            small_out,
            bias,
            dkv,
            core_in,
            z_in,
            dqkv,
            w_buf,
            grad_normed,
            token_buf,
            norm_sums,
            norm_sums_in,
            send_sems,
            recv_sems,
            own_sems,
            out_sems,
            key_send,
            key_recv,
            row_send,
            row_recv,
            w_sems,
        ) = rest[5 * array_count :]

        me = lax.axis_index("fsdp")
        place = lax.axis_index("seq")
        core = me & 1
        chip = me >> 1
        high = place >> 1
        low = place & 1
        inner = jnp.logical_or(place == 1, place == 2)
        outer = jnp.logical_not(inner)
        trades = core != high
        trade_peer = ((me & 6) | high, core * 2 + low)
        mate = seq_peer(place ^ 1)
        across = seq_peer(3 - place)

        barrier = pltpu.get_barrier_semaphore()
        for peer in (fsdp_peer(1), fsdp_peer(2), fsdp_peer(4), mate):
            pl.semaphore_signal(barrier, inc=1, device_id=peer, device_id_type=MESH)

        @pl.when(inner)
        def _():
            pl.semaphore_signal(barrier, inc=1, device_id=across, device_id_type=MESH)

        @pl.when(trades)
        def _():
            pl.semaphore_signal(barrier, inc=1, device_id=trade_peer, device_id_type=MESH)

        pl.semaphore_wait(barrier, 4 + inner.astype(jnp.int32) + trades.astype(jnp.int32))


        def span(unit):
            return pl.ds(unit.first, unit.columns)

        def chip_of(unit, slot):
            return chip ^ (((slot // 2) * unit.near + (slot % 2) * unit.far) // 2)

        def near_copy(u, slot):
            unit = units[u]
            if unit.index == qkv_index:
                src = late_out.at[unit.place, slot]
            elif unit.index == small_index:
                src = small_out.at[slot]
            else:
                src = sources[unit.index].at[chip_of(unit, 2 + slot), :, span(unit)]
            return send(
                src,
                near_in[unit.index].at[unit.place, slot],
                send_sems.at[u, slot],
                recv_sems.at[u, slot],
                fsdp_peer(unit.near),
            )

        def own_copy(u, slot):
            unit = units[u]
            return pltpu.make_async_copy(
                sources[unit.index].at[chip_of(unit, slot), :, span(unit)],
                acc[unit.index].at[unit.place, slot],
                own_sems.at[u, slot],
            )

        def far_copy(u):
            unit = units[u]
            return send(
                acc[unit.index].at[unit.place, 1],
                far_in[unit.index].at[unit.place],
                send_sems.at[u, 2],
                recv_sems.at[u, 2],
                fsdp_peer(unit.far),
            )

        def inward_copy(u):
            unit = units[u]
            return send(
                acc[unit.index].at[unit.place, 0],
                outer_in[unit.index].at[unit.place],
                send_sems.at[u, 3],
                recv_sems.at[u, 3],
                mate,
            )

        def across_copy(u):
            unit = units[u]
            return send(
                outer_in[unit.index].at[unit.place],
                inner_in[unit.index].at[unit.place],
                send_sems.at[u, 4],
                recv_sems.at[u, 4],
                across,
            )

        def outward_copy(u):
            unit = units[u]
            return send(
                acc[unit.index].at[unit.place, 0],
                results[unit.index].at[:, span(unit)],
                send_sems.at[u, 5],
                recv_sems.at[u, 5],
                mate,
            )

        def out_copy(u):
            unit = units[u]
            return pltpu.make_async_copy(
                acc[unit.index].at[unit.place, 0], results[unit.index].at[:, span(unit)], out_sems.at[u]
            )

        def add_into(dst, left, right):
            total_rows, columns = dst.shape
            step = 16
            while total_rows % (2 * step) == 0 and 2 * step * columns <= 32768:
                step *= 2

            @pl.loop(0, total_rows // step)
            def _(i):
                part = pl.ds(pl.multiple_of(i * step, step), step)
                dst[part] = (left[part].astype(F32) + right[part].astype(F32)).astype(BF16)

        def early(u):
            return units[u].index < given

        def near_start(u):
            if units[u].index == qkv_index:
                form_qkv(u)
            elif units[u].index == small_index:
                form_small(u)
            near_copy(u, 1).start()
            near_copy(u, 0).start()

        def stage_far(u):
            unit = units[u]
            for slot in (1, 0):
                near_copy(u, slot).wait_recv()
                if early(u):
                    own_copy(u, slot).wait()
                target = acc[unit.index].at[unit.place, slot]
                add_into(target, target, near_in[unit.index].at[unit.place, slot])
                if slot == 1:
                    far_copy(u).start()

        def stage_inward(u):
            unit = units[u]
            far_copy(u).wait_recv()
            target = acc[unit.index].at[unit.place, 0]
            add_into(target, target, far_in[unit.index].at[unit.place])

            @pl.when(outer)
            def _():
                inward_copy(u).start()

        def stage_across(u):
            unit = units[u]

            @pl.when(inner)
            def _():
                inward_copy(u).wait_recv()
                target = outer_in[unit.index].at[unit.place]
                add_into(target, target, acc[unit.index].at[unit.place, 0])
                across_copy(u).start()

        def stage_outward(u):
            unit = units[u]

            @pl.when(inner)
            def _():
                across_copy(u).wait_recv()
                add_into(
                    acc[unit.index].at[unit.place, 0],
                    outer_in[unit.index].at[unit.place],
                    inner_in[unit.index].at[unit.place],
                )
                outward_copy(u).start()
                out_copy(u).start()

        ahead = 4
        lags = ((stage_far, 0), (stage_inward, 2), (stage_across, 4), (stage_outward, 6))
        total_ticks = count + 6

        def tick(t):
            if t + ahead < count:
                near_start(t + ahead)
            for stage, lag in lags:
                if 0 <= t - lag < count:
                    stage(t - lag)


        half = 2 * rows

        def group(g):
            return pl.ds(2 * g, 2)

        def key_core_copy(g):
            return send(
                dkv.at[:, group(g), pl.ds((core ^ 1) * half, half)],
                core_in.at[:, group(g)],
                key_send.at[0, g],
                key_recv.at[0, g],
                fsdp_peer(1),
            )

        def key_far_copy(g):
            return send(
                core_in.at[:, group(g), pl.ds((low ^ 1) * rows, rows)],
                z_in.at[:, group(g)],
                key_send.at[1, g],
                key_recv.at[1, g],
                mate,
            )

        def key_middle(g):
            key_core_copy(g).wait_recv()
            for kind in range(2):
                for k in range(2):

                    @pl.loop(0, half // LANES)
                    def _(i):
                        part = pl.ds(pl.multiple_of(i * LANES, LANES), LANES)
                        own = pl.ds(pl.multiple_of(core * half + i * LANES, LANES), LANES)
                        core_in[kind, 2 * g + k, part] = (
                            core_in[kind, 2 * g + k, part].astype(F32) + dkv[kind, 2 * g + k, own].astype(F32)
                        ).astype(BF16)

            key_far_copy(g).start()

        def key_end(g):
            key_far_copy(g).wait_recv()
            for kind in range(2):
                for k in range(2):
                    slab = 2 * g + k

                    @pl.loop(0, rows // LANES)
                    def _(i):
                        part = pl.ds(pl.multiple_of(i * LANES, LANES), LANES)
                        own = pl.ds(pl.multiple_of(low * rows + i * LANES, LANES), LANES)
                        total = core_in[kind, slab, own].astype(F32) + z_in[kind, slab, part].astype(F32)
                        dqkv[part, pl.ds((1 + kind) * width + slab * LANES, LANES)] = total.astype(BF16)


        lane = lax.broadcasted_iota(jnp.int32, (rows, LANES), 1) // head_size
        key_lane = lax.broadcasted_iota(jnp.int32, (keys, LANES), 1) // head_size
        sub = lax.broadcasted_iota(jnp.int32, (LANES, rows), 0) // head_size

        def slab_back(j):
            at = pl.ds(pl.multiple_of(j * LANES, LANES), LANES)
            value_at = pl.ds(pl.multiple_of(width + j * LANES, LANES), LANES)
            queries = qkv_ref[:, at]
            grads = grad_ref[:, at]
            pick = (
                lax.broadcasted_iota(jnp.int32, (8, LANES), 1) // head_size
                == lax.broadcasted_iota(jnp.int32, (8, LANES), 0)
            ).astype(F32)
            deltas = lax.dot_general(
                pick,
                grads.astype(F32) * mixed_ref[:, at].astype(F32),
                (((1,), (1,)), ((), ())),
                precision=lax.Precision.HIGHEST,
                preferred_element_type=F32,
            )
            key_slab = kv_ref[:, at]
            keys_t = key_slab.T
            dq = jnp.zeros((LANES, rows), F32)
            dk = jnp.zeros((keys, LANES), F32)
            dv = jnp.zeros((keys, LANES), F32)
            slab_logs = log_ref[j]
            for head in range(per_slab):
                own = jnp.where(lane == head, queries, jnp.zeros_like(queries))
                own_grad = jnp.where(lane == head, grads, jnp.zeros_like(grads))
                scores = across_lanes(key_slab, own) * factor + bias[...]
                weights = jnp.exp2(scores - slab_logs[head : head + 1, :])
                grad_soft = across_lanes(kv_ref[:, value_at], own_grad)
                grad_scores = (weights * (grad_soft - deltas[head : head + 1, :])).astype(BF16)
                dv = jnp.where(
                    key_lane == head, jnp.dot(weights.astype(BF16), grads, preferred_element_type=F32), dv
                )
                dk = jnp.where(
                    key_lane == head, jnp.dot(grad_scores, queries, preferred_element_type=F32), dk
                )
                dq = jnp.where(sub == head, jnp.dot(keys_t, grad_scores, preferred_element_type=F32), dq)
            dqkv[pl.ds(0, rows), at] = (dq.T * scale).astype(BF16)
            dkv[0, j] = (dk * scale).astype(BF16)
            dkv[1, j] = dv.astype(BF16)


        def row_copy(part):
            columns = pl.ds(0, width) if part == 0 else pl.ds(width, 2 * width)
            return send(
                dqkv.at[pl.ds(0, rows), columns],
                dqkv.at[pl.ds(rows, rows), columns],
                row_send.at[part],
                row_recv.at[part],
                fsdp_peer(1),
            )

        def form_qkv(u):
            unit = units[u]
            right = dqkv[:, span(unit)]
            for slot in range(4):
                left = normed_t_ref[pl.ds(pl.multiple_of(chip_of(unit, slot) * part_rows, part_rows), part_rows)]
                block = jnp.dot(left, right, preferred_element_type=F32).astype(BF16)
                if slot < 2:
                    acc[unit.index][unit.place, slot] = block
                else:
                    late_out[unit.place, slot - 2] = block


        blocks = 8

        def w_copy(block):
            return pltpu.make_async_copy(w_ref.at[block], w_buf.at[block % 2], w_sems.at[block % 2])

        def norm_copy():
            return send(norm_sums, norm_sums_in, row_send.at[2], row_recv.at[2], fsdp_peer(1))

        def input_gradient():
            for block in range(blocks):
                w_copy(block).wait()
                grad_normed[:, pl.ds(block * part_rows, part_rows)] = across_lanes(
                    dqkv[pl.ds(0, rows), :], w_buf[block % 2]
                )
                if block + 2 < blocks:
                    w_copy(block + 2).start()
            gain_row = gain_ref[...]
            norm_sums[...] = jnp.zeros_like(norm_sums)
            step = 64
            gain_sum = jnp.zeros((1, width), F32)
            shift_sum = jnp.zeros((1, width), F32)
            for i in range(rows // step):
                part = pl.ds(i * step, step)
                value = tokens_ref[part].astype(F32)
                value = value - jnp.mean(value, axis=1, keepdims=True)
                inverse = lax.rsqrt(jnp.mean(value * value, axis=1, keepdims=True) + EPSILON)
                unit_value = value * inverse
                upper = grad_normed[part]
                gain_sum = gain_sum + jnp.sum(upper * unit_value, axis=0, keepdims=True)
                shift_sum = shift_sum + jnp.sum(upper, axis=0, keepdims=True)
                scaled = upper * gain_row
                inside = (
                    scaled
                    - jnp.mean(scaled, axis=1, keepdims=True)
                    - unit_value * jnp.mean(scaled * unit_value, axis=1, keepdims=True)
                )
                token_buf[part] = (middle_ref[part] + inverse * inside).astype(BF16)
            norm_sums[0:1, :] = gain_sum
            norm_sums[1:2, :] = shift_sum
            norm_copy().start()

            @pl.when(trades)
            def _():
                token_send().start()

            @pl.when(jnp.logical_not(trades))
            def _():
                token_keep().start()

        def token_send():
            return send(token_buf, token_out, row_send.at[3], row_recv.at[3], trade_peer)

        def token_keep():
            return pltpu.make_async_copy(token_buf, token_out, w_sems.at[2])

        def form_small(u):
            unit = units[u]
            norm_copy().wait_recv()
            both = norm_sums[...] + norm_sums_in[...]
            norm_sums_in[...] = both
            for slot in range(4):
                owner = chip_of(unit, slot) * 2 + core
                block = norm_sums_in[:, pl.ds(pl.multiple_of(owner * LANES, LANES), LANES)].astype(BF16)
                if slot < 2:
                    acc[unit.index][unit.place, slot] = block
                else:
                    small_out[slot - 2] = block


        first_late = min(u for u in range(count) if not early(u))
        for u in range(first_late):
            for slot in range(2):
                own_copy(u, slot).start()
        for u in range(ahead):
            near_start(u)
        w_copy(0).start()
        w_copy(1).start()
        bias[...] = jnp.where(key_ref[...] == query_ref[...], 0.0, NEG_FILL)
        ticks_inside = first_late - ahead

        @pl.loop(0, slabs)
        def _(j):
            slab_back(j)

            @pl.when(j % 2 == 1)
            def _():
                key_core_copy(j // 2).start()

            @pl.when(jnp.logical_and(j % 2 == 0, j >= 2))
            def _():
                key_middle(j // 2 - 1)

            done = 0
            for k in range(slabs):
                until = (k + 1) * ticks_inside // slabs

                @pl.when(j == k)
                def _(done=done, until=until):
                    for t in range(done, until):
                        tick(t)

                done = until

        row_copy(0).start()
        key_middle(slabs // 2 - 1)
        for g in range(slabs // 2):
            key_end(g)
        row_copy(1).start()
        row_copy(0).wait_recv()
        row_copy(1).wait_recv()
        done_input = False
        for t in range(ticks_inside, total_ticks):
            if not done_input and t + ahead >= count - 1:
                input_gradient()
                done_input = True
            tick(t)

        for u in range(count):
            near_copy(u, 0).wait_send()
            near_copy(u, 1).wait_send()
            far_copy(u).wait_send()

        for u in range(count):

            @pl.when(inner)
            def _():
                across_copy(u).wait_send()
                outward_copy(u).wait_send()
                out_copy(u).wait()

            @pl.when(outer)
            def _():
                inward_copy(u).wait_send()
                outward_copy(u).wait_recv()

        for g in range(slabs // 2):
            key_core_copy(g).wait_send()
            key_far_copy(g).wait_send()
        row_copy(0).wait_send()
        row_copy(1).wait_send()
        norm_copy().wait_send()

        @pl.when(trades)
        def _():
            token_send().wait()

        @pl.when(jnp.logical_not(trades))
        def _():
            token_keep().wait()

    def piece_shape(index):
        return (shapes[index][0], shapes[index][1] // pieces[index])

    scratch = []
    for slots in ((2,), (2,), (), (), ()):
        for index in range(array_count):
            scratch.append(pltpu.VMEM((pieces[index],) + slots + piece_shape(index), BF16))
    scratch += [
        pltpu.VMEM((pieces[qkv_index], 2) + piece_shape(qkv_index), BF16),
        pltpu.VMEM((2, SMALL_ROWS, LANES), BF16),
        pltpu.VMEM((keys, rows), F32),
        pltpu.VMEM((2, slabs, keys, LANES), BF16),
        pltpu.VMEM((2, slabs, 2 * rows, LANES), BF16),
        pltpu.VMEM((2, slabs, rows, LANES), BF16),
        pltpu.VMEM((2 * rows, triple), BF16),
        pltpu.VMEM((2, part_rows, triple), BF16),
        pltpu.VMEM((rows, width), F32),
        pltpu.VMEM((rows, width), BF16),
        pltpu.VMEM((SMALL_ROWS, width), F32),
        pltpu.VMEM((SMALL_ROWS, width), F32),
        pltpu.SemaphoreType.DMA((count, 6)),
        pltpu.SemaphoreType.DMA((count, 6)),
        pltpu.SemaphoreType.DMA((count, 2)),
        pltpu.SemaphoreType.DMA((count,)),
        pltpu.SemaphoreType.DMA((2, slabs // 2)),
        pltpu.SemaphoreType.DMA((2, slabs // 2)),
        pltpu.SemaphoreType.DMA((4,)),
        pltpu.SemaphoreType.DMA((4,)),
        pltpu.SemaphoreType.DMA((3,)),
    ]
    return pl.pallas_call(
        kernel,
        out_shape=[jax.ShapeDtypeStruct(shape, BF16) for shape in shapes]
        + [jax.ShapeDtypeStruct((rows, width), BF16)],
        in_specs=[ANYWHERE] * given + [IN_VMEM] * 8 + [ANYWHERE] + [IN_VMEM] * 3,
        out_specs=[ANYWHERE] * (array_count + 1),
        scratch_shapes=scratch,
        compiler_params=remote_params(collective_id, 61 << 20),
        name="back_and_sum",
    )(
        *partials,
        qkv,
        keys_values,
        mixed,
        grad_mixed,
        logs,
        query_clip[None, :],
        key_clip[:, None],
        normed_both_t,
        w_qkv,
        tokens,
        grad_middle,
        gain[None, :],
    )


def mate_z():
    return seq_peer(lax.axis_index("seq") ^ 1)


def quarter():
    return (lax.axis_index("fsdp") & 1) * 2 + (lax.axis_index("seq") & 1)


def gather_keys(qkv, collective_id):
    rows, triple = qkv.shape
    width = triple // 3
    pieces = 4
    step = rows // pieces

    def kernel(qkv_ref, out_ref, send_sems, recv_sems, local_sem):
        mine = quarter()
        enter([fsdp_peer(1), mate_z()])
        columns = pl.ds(width, 2 * width)

        def own(piece):
            return qkv_ref.at[pl.ds(piece * step, step), columns]

        def part(owner, piece):
            return out_ref.at[owner, pl.ds(piece * step, step)]

        def copy(kind, piece):
            src = part(mine ^ 1, piece) if kind == 2 else own(piece)
            owner = mine ^ 1 if kind == 2 else mine
            return send(
                src,
                part(owner, piece),
                send_sems.at[kind, piece],
                recv_sems.at[kind, piece],
                mate_z() if kind == 0 else fsdp_peer(1),
            )

        for piece in range(pieces):
            copy(0, piece).start()
        for piece in range(pieces):
            copy(1, piece).start()
        local_copy = pltpu.make_async_copy(
            qkv_ref.at[:, columns], out_ref.at[mine], local_sem
        )
        local_copy.start()
        for piece in range(pieces):
            copy(0, piece).wait_recv()
            copy(2, piece).start()
        for piece in range(pieces):
            copy(1, piece).wait_recv()
            copy(2, piece).wait_recv()
            for kind in range(3):
                copy(kind, piece).wait_send()
        local_copy.wait()

    return pl.pallas_call(
        kernel,
        out_shape=jax.ShapeDtypeStruct((4, rows, 2 * width), qkv.dtype),
        in_specs=[ANYWHERE],
        out_specs=ANYWHERE,
        scratch_shapes=[
            pltpu.SemaphoreType.DMA((3, pieces)),
            pltpu.SemaphoreType.DMA((3, pieces)),
            pltpu.SemaphoreType.DMA,
        ],
        compiler_params=remote_params(collective_id),
        name="gather_keys",
    )(qkv)


def sum_keys(terms, collective_id):
    _, rows, width = terms[0].shape
    pieces = 4
    step = rows // pieces
    kinds = len(terms)

    def kernel(*refs):
        sources = refs[:kinds]
        results = refs[kinds : 2 * kinds]
        core_buf, far_buf, send_sems, recv_sems = refs[2 * kinds :]
        mine = quarter()
        enter([fsdp_peer(1), mate_z()])

        def core_copy(kind, piece, other):
            owner = mine ^ 2 ^ other
            return send(
                sources[kind].at[owner, pl.ds(piece * step, step)],
                core_buf.at[kind, other, pl.ds(piece * step, step)],
                send_sems.at[kind, piece, other],
                recv_sems.at[kind, piece, other],
                fsdp_peer(1),
            )

        def far_copy(kind, piece):
            part = pl.ds(piece * step, step)
            return send(
                core_buf.at[kind, 1, part],
                far_buf.at[kind, part],
                send_sems.at[kind, piece, 2],
                recv_sems.at[kind, piece, 2],
                mate_z(),
            )

        order = [(kind, piece) for piece in range(pieces) for kind in range(kinds)]
        for other in (1, 0):
            for kind, piece in order:
                core_copy(kind, piece, other).start()
        for kind, piece in order:
            core_copy(kind, piece, 1).wait_recv()

            @pl.loop(0, step // 16)
            def _(i):
                part = pl.ds(pl.multiple_of(piece * step + i * 16, 16), 16)
                total = core_buf[kind, 1, part].astype(F32) + sources[kind][mine ^ 1, part].astype(F32)
                core_buf[kind, 1, part] = total.astype(BF16)

            far_copy(kind, piece).start()
        for kind, piece in order:
            core_copy(kind, piece, 0).wait_recv()
            far_copy(kind, piece).wait_recv()

            @pl.loop(0, step // 16)
            def _(i):
                part = pl.ds(pl.multiple_of(piece * step + i * 16, 16), 16)
                total = core_buf[kind, 0, part].astype(F32) + sources[kind][mine, part].astype(F32)
                results[kind][part] = (total + far_buf[kind, part].astype(F32)).astype(BF16)

        for kind, piece in order:
            core_copy(kind, piece, 0).wait_send()
            core_copy(kind, piece, 1).wait_send()
            far_copy(kind, piece).wait_send()

    return pl.pallas_call(
        kernel,
        out_shape=[jax.ShapeDtypeStruct((rows, width), BF16)] * kinds,
        in_specs=[IN_VMEM] * kinds,
        out_specs=[IN_VMEM] * kinds,
        scratch_shapes=[
            pltpu.VMEM((kinds, 2, rows, width), BF16),
            pltpu.VMEM((kinds, rows, width), BF16),
            pltpu.SemaphoreType.DMA((kinds, pieces, 3)),
            pltpu.SemaphoreType.DMA((kinds, pieces, 3)),
        ],
        compiler_params=remote_params(collective_id, 40 << 20),
        name="sum_keys",
    )(*terms)


def across_lanes(left, right):
    return lax.dot_general(left, right, (((1,), (1,)), ((), ())), preferred_element_type=F32)


def fill_bias(bias, query_ref, key_ref):
    @pl.when(pl.program_id(0) == 0)
    def _():
        bias[...] = jnp.where(key_ref[...] == query_ref[...], 0.0, NEG_FILL)


def attend_local(qkv, keys_values, query_clip, key_clip, head_count):
    rows, triple = qkv.shape
    width = triple // 3
    keys = keys_values.shape[0]
    slabs = width // LANES
    head_size = width // head_count
    per_slab = LANES // head_size
    factor = head_size ** (-0.5) * LOG2E

    def kernel(q_ref, k_ref, v_ref, query_ref, key_ref, out_ref, log_ref, bias):
        fill_bias(bias, query_ref, key_ref)
        lane = lax.broadcasted_iota(jnp.int32, (rows, LANES), 1) // head_size
        sub = lax.broadcasted_iota(jnp.int32, (LANES, rows), 0) // head_size
        queries = q_ref[...]
        values_t = v_ref[...].T
        output = jnp.zeros((LANES, rows), F32)
        log_ref[...] = jnp.zeros_like(log_ref)
        for head in range(per_slab):
            own = jnp.where(lane == head, queries, jnp.zeros_like(queries))
            scores = across_lanes(k_ref[...], own) * factor + bias[...]
            top = jnp.max(scores, axis=0, keepdims=True)
            weights = jnp.exp2(scores - top)
            total = jnp.sum(weights, axis=0, keepdims=True)
            mixed = jnp.dot(values_t, weights.astype(BF16), preferred_element_type=F32) / total
            output = jnp.where(sub == head, mixed, output)
            log_ref[0, head : head + 1, :] = top + jnp.log2(total)
        out_ref[...] = output.T.astype(BF16)

    return pl.pallas_call(
        kernel,
        grid=(slabs,),
        out_shape=[
            jax.ShapeDtypeStruct((rows, width), BF16),
            jax.ShapeDtypeStruct((slabs, 8, rows), F32),
        ],
        in_specs=[
            pl.BlockSpec((rows, LANES), lambda j: (0, j)),
            pl.BlockSpec((keys, LANES), lambda j: (0, j)),
            pl.BlockSpec((keys, LANES), lambda j: (0, slabs + j)),
            pl.BlockSpec((1, rows), lambda j: (0, 0)),
            pl.BlockSpec((keys, 1), lambda j: (0, 0)),
        ],
        out_specs=[
            pl.BlockSpec((rows, LANES), lambda j: (0, j)),
            pl.BlockSpec((1, 8, rows), lambda j: (j, 0, 0)),
        ],
        scratch_shapes=[pltpu.VMEM((keys, rows), F32)],
        compiler_params=pltpu.CompilerParams(vmem_limit_bytes=40 << 20),
        name="attend_local",
    )(qkv, keys_values, keys_values, query_clip[None, :], key_clip[:, None])


def attend_local_back(qkv, keys_values, mixed, logs, grad_mixed, query_clip, key_clip, head_count):
    rows, triple = qkv.shape
    width = triple // 3
    keys = keys_values.shape[0]
    slabs = width // LANES
    head_size = width // head_count
    per_slab = LANES // head_size
    scale = head_size ** (-0.5)
    factor = scale * LOG2E

    def kernel(
        q_ref, k_ref, v_ref, mixed_ref, grad_ref, log_ref, query_ref, key_ref, dq_ref, dk_ref, dv_ref, bias
    ):
        fill_bias(bias, query_ref, key_ref)
        lane = lax.broadcasted_iota(jnp.int32, (rows, LANES), 1) // head_size
        key_lane = lax.broadcasted_iota(jnp.int32, (keys, LANES), 1) // head_size
        sub = lax.broadcasted_iota(jnp.int32, (LANES, rows), 0) // head_size
        queries = q_ref[...]
        grads = grad_ref[...]
        pick = (
            lax.broadcasted_iota(jnp.int32, (8, LANES), 1) // head_size
            == lax.broadcasted_iota(jnp.int32, (8, LANES), 0)
        ).astype(F32)
        deltas = lax.dot_general(
            pick,
            grads.astype(F32) * mixed_ref[...].astype(F32),
            (((1,), (1,)), ((), ())),
            precision=lax.Precision.HIGHEST,
            preferred_element_type=F32,
        )
        keys_t = k_ref[...].T
        dq = jnp.zeros((LANES, rows), F32)
        dk = jnp.zeros((keys, LANES), F32)
        dv = jnp.zeros((keys, LANES), F32)
        for head in range(per_slab):
            own = jnp.where(lane == head, queries, jnp.zeros_like(queries))
            own_grad = jnp.where(lane == head, grads, jnp.zeros_like(grads))
            scores = across_lanes(k_ref[...], own) * factor + bias[...]
            weights = jnp.exp2(scores - log_ref[0, head : head + 1, :])
            grad_soft = across_lanes(v_ref[...], own_grad)
            grad_scores = (weights * (grad_soft - deltas[head : head + 1, :])).astype(BF16)
            dv = jnp.where(
                key_lane == head, jnp.dot(weights.astype(BF16), grads, preferred_element_type=F32), dv
            )
            dk = jnp.where(key_lane == head, jnp.dot(grad_scores, queries, preferred_element_type=F32), dk)
            dq = jnp.where(sub == head, jnp.dot(keys_t, grad_scores, preferred_element_type=F32), dq)
        dq_ref[...] = (dq.T * scale).astype(BF16)
        dk_ref[...] = (dk * scale).astype(BF16)
        dv_ref[...] = dv.astype(BF16)

    return pl.pallas_call(
        kernel,
        grid=(slabs,),
        out_shape=[
            jax.ShapeDtypeStruct((rows, width), BF16),
            jax.ShapeDtypeStruct((keys, width), BF16),
            jax.ShapeDtypeStruct((keys, width), BF16),
        ],
        in_specs=[
            pl.BlockSpec((rows, LANES), lambda j: (0, j)),
            pl.BlockSpec((keys, LANES), lambda j: (0, j)),
            pl.BlockSpec((keys, LANES), lambda j: (0, slabs + j)),
            pl.BlockSpec((rows, LANES), lambda j: (0, j)),
            pl.BlockSpec((rows, LANES), lambda j: (0, j)),
            pl.BlockSpec((1, 8, rows), lambda j: (j, 0, 0)),
            pl.BlockSpec((1, rows), lambda j: (0, 0)),
            pl.BlockSpec((keys, 1), lambda j: (0, 0)),
        ],
        out_specs=[
            pl.BlockSpec((rows, LANES), lambda j: (0, j)),
            pl.BlockSpec((keys, LANES), lambda j: (0, j)),
            pl.BlockSpec((keys, LANES), lambda j: (0, j)),
        ],
        scratch_shapes=[pltpu.VMEM((keys, rows), F32)],
        compiler_params=pltpu.CompilerParams(vmem_limit_bytes=50 << 20),
        name="attend_local_back",
    )(
        qkv,
        keys_values,
        keys_values,
        mixed,
        grad_mixed,
        logs,
        query_clip[None, :],
        key_clip[:, None],
    )


def fast_forward(residual, norms, w_qkv, w_out, w_up, w_down, head_count, clips, collective_id):
    rows, width = residual.shape
    normed = layer_norm(residual, norms[0], norms[1]).astype(BF16)
    qkv = jnp.dot(normed, w_qkv, preferred_element_type=F32).astype(BF16)
    keys_values = gather_keys(qkv, collective_id).reshape(4 * rows, 2 * width)
    mixed, logs = attend_local(qkv, keys_values, clips[0], clips[1], head_count)
    middle = residual + jnp.dot(mixed, w_out, preferred_element_type=F32)
    normed_mid = layer_norm(middle, norms[2], norms[3]).astype(BF16)
    pre = jnp.dot(normed_mid, w_up, preferred_element_type=F32)
    hidden = gelu_exact(pre).astype(BF16)
    result = middle + jnp.dot(hidden, w_down, preferred_element_type=F32)
    return result, (residual, normed, qkv, keys_values, mixed, logs, middle, normed_mid, pre, hidden)


def swap_cores(values):
    return lax.ppermute(values, "fsdp", [(f, f ^ 1) for f in range(8)])


def own_columns(values, mine):
    rows, columns = values.shape
    parts = values.reshape(rows, 4, 2, columns // 8)
    core = lax.axis_index("fsdp") & 1
    return jnp.where(core == (0 if mine else 1), parts[:, :, 0], parts[:, :, 1]).reshape(rows, columns // 2)


def both_cores(values):
    return jnp.concatenate([own_columns(values, True), swap_cores(own_columns(values, False))], axis=0)


def chip_gradient(left, right):
    all_right = jnp.concatenate([right, swap_cores(right)], axis=0)
    grad = jnp.einsum("tv,tw->vw", both_cores(left), all_right, preferred_element_type=F32)
    return grad.astype(BF16).reshape(4, grad.shape[0] // 4, grad.shape[1])


def back_to_mixed(grad_result, kept, norms, w_out, w_up, w_down):
    residual, normed, qkv, keys_values, mixed, logs, middle, normed_mid, pre, hidden = kept
    grad_low = grad_result.astype(BF16)
    grad_down = chip_gradient(hidden, grad_low)
    grad_hidden = jnp.einsum("tw,fw->tf", grad_low, w_down, preferred_element_type=F32)
    _, gelu_pull = jax.vjp(gelu_exact, pre)
    grad_pre = gelu_pull(grad_hidden)[0].astype(BF16)
    grad_up = chip_gradient(normed_mid, grad_pre)
    grad_normed_mid = jnp.einsum("tf,wf->tw", grad_pre, w_up, preferred_element_type=F32)
    _, second_pull = jax.vjp(layer_norm, middle, norms[2], norms[3])
    grad_mid_norm, grad_gain_two, grad_shift_two = second_pull(grad_normed_mid)
    grad_middle = grad_result + grad_mid_norm
    grad_branch = grad_middle.astype(BF16)
    grad_out_w = chip_gradient(mixed, grad_branch)
    grad_mixed = jnp.einsum("tw,vw->tv", grad_branch, w_out, preferred_element_type=F32).astype(BF16)
    return grad_middle, grad_mixed, [grad_gain_two, grad_shift_two], (grad_out_w, grad_up, grad_down)


def fast_backward(grad_result, kept, norms, w_qkv, w_out, w_up, w_down, head_count, clips, collective_id):
    residual, normed, qkv, keys_values, mixed, logs, middle, normed_mid, pre, hidden = kept
    rows, width = residual.shape
    grad_middle, grad_mixed, small_two, weight_grads = back_to_mixed(grad_result, kept, norms, w_out, w_up, w_down)
    dq, dk, dv = attend_local_back(
        qkv, keys_values, mixed, logs, grad_mixed, clips[0], clips[1], head_count
    )
    dk, dv = sum_keys([dk.reshape(4, rows, width), dv.reshape(4, rows, width)], collective_id)
    grad_qkv = jnp.concatenate([dq, dk, dv], axis=1)
    grad_qkv_w = chip_gradient(normed, grad_qkv)
    grad_normed = jnp.einsum("tc,wc->tw", grad_qkv, w_qkv, preferred_element_type=F32)
    _, first_pull = jax.vjp(layer_norm, residual, norms[0], norms[1])
    grad_first_norm, grad_gain_one, grad_shift_one = first_pull(grad_normed)
    return grad_middle + grad_first_norm, [grad_gain_one, grad_shift_one] + small_two, (grad_qkv_w,) + weight_grads


def trade_pairs():
    pairs = []
    for f in range(8):
        for s in range(4):
            core, high, low = f & 1, s >> 1, s & 1
            if core != high:
                pairs.append((f * 4 + s, ((f & 6) | high) * 4 + (core * 2 + low)))
    return pairs


def trade(values):
    moved = lax.ppermute(values, ("fsdp", "seq"), trade_pairs())
    stays = (lax.axis_index("fsdp") & 1) == (lax.axis_index("seq") >> 1)
    return jnp.where(stays, values, moved)


def pack_small(wide, narrow, wide_count, narrow_count):
    block = jnp.concatenate(
        [wide, jnp.pad(narrow, ((0, 0), (0, LANES - narrow.shape[1])))], axis=0
    )
    return jnp.pad(block, ((0, SMALL_ROWS - block.shape[0]), (0, 0)))


def fast_local(
    tokens,
    clip_lengths,
    target_pos,
    out_grad,
    norm1_gain,
    norm1_bias,
    w_qkv,
    w_out,
    norm2_gain,
    norm2_bias,
    w_fc1,
    w_fc2,
    w_embed,
    mask_token,
    pred_norm1_gain,
    pred_norm1_bias,
    pred_qkv,
    pred_out,
    pred_norm2_gain,
    pred_norm2_bias,
    pred_fc1,
    pred_fc2,
):
    rows, width = tokens.shape
    narrow_width = out_grad.shape[1]
    wide_part = norm1_gain.shape[0]
    narrow_part = mask_token.shape[0]
    small = pack_small(
        jnp.stack([norm1_gain, norm1_bias, norm2_gain, norm2_bias]),
        jnp.stack([pred_norm1_gain, pred_norm1_bias, pred_norm2_gain, pred_norm2_bias, mask_token]),
        4,
        5,
    )
    gathered = gather_weights(
        [small, w_qkv, w_out, w_fc1, w_fc2, w_embed, pred_qkv, pred_out, pred_fc1, pred_fc2]
    )
    smalls = gathered[0].astype(F32)
    norms = [smalls[:, i, :wide_part].reshape(-1) for i in range(4)]
    pred_norms = [smalls[:, 4 + i, :narrow_part].reshape(-1) for i in range(5)]
    whole = [one.reshape(-1, one.shape[-1]) for one in gathered[1:]]

    core = lax.axis_index("fsdp") & 1
    high = lax.axis_index("seq") >> 1
    tokens = trade(tokens)
    out_grad = trade(out_grad)
    target_pos = trade(target_pos)
    other_lengths = lax.ppermute(clip_lengths, "fsdp", [(f, f ^ 1) for f in range(8)])
    lengths = jnp.where(core == high, clip_lengths, other_lengths)[0]

    clip_ends = jnp.cumsum(lengths)
    local_rows = quarter() * rows + jnp.arange(rows, dtype=jnp.int32)
    query_clip = clip_index(local_rows, clip_ends)
    key_clip = clip_index(jnp.arange(4 * rows, dtype=jnp.int32), clip_ends)
    past_end = (local_rows[:, None] >= clip_ends[None, :]).astype(jnp.int32)
    rel_rows = local_rows - jnp.sum(lengths[None, :] * past_end, axis=1)
    clips = (query_clip, key_clip)

    ctx_result, ctx_kept = fast_forward(
        tokens.astype(F32), norms, whole[0], whole[1], whole[2], whole[3], HEADS, clips, 3
    )
    context_out = ctx_result.astype(BF16)
    embedded = jnp.dot(context_out, whole[4], preferred_element_type=F32)
    targets = target_pos[0, 0]
    matches = jnp.arange(rows, dtype=jnp.int32)[:, None] == targets[None, :]
    placement = matches.astype(F32)
    target_hit = jnp.sum(placement, axis=1)
    target_rel = jnp.sum(jnp.where(matches, rel_rows[:, None], 0), axis=0)
    mask_rows = pred_norms[4][None, :] + position_table(target_rel, narrow_width)
    placed = jnp.dot(placement, mask_rows, precision=lax.Precision.HIGHEST, preferred_element_type=F32)
    pred_in = embedded * (1.0 - target_hit[:, None]) + placed
    pred_result, pred_kept = fast_forward(
        pred_in, pred_norms, whole[5], whole[6], whole[7], whole[8], P_HEADS, clips, 4
    )
    predicted = pred_result.astype(BF16)
    grad_pred_in, pred_small, pred_grads = fast_backward(
        out_grad.astype(F32), pred_kept, pred_norms, whole[5], whole[6], whole[7], whole[8], P_HEADS, clips, 5
    )
    grad_mask = jnp.sum(target_hit[:, None] * grad_pred_in, axis=0)
    grad_embedded = (grad_pred_in * (1.0 - target_hit[:, None])).astype(BF16)
    grad_embed_w = chip_gradient(context_out, grad_embedded)
    grad_context = jnp.einsum("tp,dp->td", grad_embedded, whole[4], preferred_element_type=F32)
    grad_middle, grad_mixed, ctx_two, ctx_grads = back_to_mixed(
        grad_context, ctx_kept, norms, whole[1], whole[2], whole[3]
    )
    wide_grads = jnp.stack(ctx_two).reshape(2, 4, 2, wide_part)
    narrow_grads = jnp.pad(
        jnp.stack(pred_small + [grad_mask]).reshape(5, 4, 2, narrow_part),
        ((0, 0), (0, 0), (0, 0), (0, LANES - narrow_part)),
    )
    small_grads = jnp.concatenate([wide_grads, narrow_grads], axis=0).transpose(2, 1, 0, 3)
    mine = jnp.where(core == 0, small_grads[0], small_grads[1])
    other = jnp.where(core == 0, small_grads[1], small_grads[0])
    small_grads = jnp.pad(mine + swap_cores(other), ((0, 0), (0, SMALL_ROWS - 7), (0, 0)))

    _, normed, qkv, keys_values, mixed, logs, _, _, _, _ = ctx_kept
    results = back_and_sum(
        [pred_grads[3], pred_grads[2], pred_grads[1], pred_grads[0], grad_embed_w, small_grads.astype(BF16)]
        + [ctx_grads[2], ctx_grads[1], ctx_grads[0]],
        qkv,
        keys_values,
        mixed,
        grad_mixed,
        logs,
        query_clip,
        key_clip,
        both_cores(normed).T,
        gathered[1],
        tokens,
        grad_middle,
        norms[0],
        HEADS,
        6,
    )
    token_grad = results[-1]
    sums = [one.astype(F32) for one in results[:-1]]
    small_a, small_b = sums[5], sums[10]
    narrow_out = [small_a[2 + i, :narrow_part] for i in range(5)]
    return (
        trade(context_out),
        trade(predicted),
        token_grad,
        small_b[0],
        small_b[1],
        sums[9],
        sums[8],
        small_a[0],
        small_a[1],
        sums[7],
        sums[6],
        sums[4],
        narrow_out[4],
        narrow_out[0],
        narrow_out[1],
        sums[3],
        sums[2],
        narrow_out[2],
        narrow_out[3],
        sums[1],
        sums[0],
    )


def solution(mesh):
    body = fast_local if fits_fast(mesh) else local
    return jax.shard_map(
        body,
        mesh=mesh,
        in_specs=(
            P(("fsdp", "seq"), None),
            P("fsdp", None),
            P("fsdp", "seq", None),
            P(("fsdp", "seq"), None),
            P("fsdp"),
            P("fsdp"),
            P("fsdp", None),
            P("fsdp", None),
            P("fsdp"),
            P("fsdp"),
            P("fsdp", None),
            P("fsdp", None),
            P("fsdp", None),
            P("fsdp"),
            P("fsdp"),
            P("fsdp"),
            P("fsdp", None),
            P("fsdp", None),
            P("fsdp"),
            P("fsdp"),
            P("fsdp", None),
            P("fsdp", None),
        ),
        out_specs=(
            P(("fsdp", "seq"), None),
            P(("fsdp", "seq"), None),
            P(("fsdp", "seq"), None),
            P("fsdp"),
            P("fsdp"),
            P("fsdp", None),
            P("fsdp", None),
            P("fsdp"),
            P("fsdp"),
            P("fsdp", None),
            P("fsdp", None),
            P("fsdp", None),
            P("fsdp"),
            P("fsdp"),
            P("fsdp"),
            P("fsdp", None),
            P("fsdp", None),
            P("fsdp"),
            P("fsdp"),
            P("fsdp", None),
            P("fsdp", None),
        ),
        check_vma=False,
    )
```

```python
import math

import jax
import jax.numpy as jnp
from jax import lax
from jax.experimental import pallas as pl
from jax.experimental.pallas import tpu as pltpu
from jax.sharding import PartitionSpec as P

HEADS = 16
PD = 384
P_HEADS = 12


EPSILON = 1e-06
NEG_FILL = -1e30
block_rows = 512


def layer_norm(values, norm_gain, norm_shift):
    center = values - jnp.mean(values, axis=-1, keepdims=True)
    spread = jnp.mean(center * center, axis=-1, keepdims=True)
    return center * lax.rsqrt(spread + EPSILON) * norm_gain + norm_shift


def gelu_exact(values):
    return jax.nn.gelu(values, approximate=False)


def position_table(positions, table_width):
    half_width = table_width // 2
    angle_rates = jnp.exp(
        jnp.arange(half_width, dtype=jnp.float32) * (-2.0 * math.log(10000.0) / table_width)
    )
    angles = positions.astype(jnp.float32)[:, None] * angle_rates[None, :]
    return jnp.concatenate([jnp.sin(angles), jnp.cos(angles)], axis=1)


def clip_index(positions, clip_ends):
    return jnp.sum((positions[:, None] >= clip_ends[None, :]).astype(jnp.int32), axis=1)


def key_step(total_keys):
    return max(min(total_keys, block_rows), total_keys // 8)


def block_scores(queries, key_part, query_clip, key_clip_part, score_scale):
    raw_scores = (
        jnp.einsum("the,khe->htk", queries, key_part, preferred_element_type=jnp.float32)
        * score_scale
    )
    same_clip = query_clip[:, None] == key_clip_part[None, :]
    return jnp.where(same_clip[None], raw_scores, NEG_FILL)


def attend_forward(queries, key_heads, value_heads, query_clip, key_clip):
    row_count, head_count, head_size = queries.shape
    score_scale = head_size ** (-0.5)
    total_keys = key_heads.shape[0]
    step_rows = key_step(total_keys)
    run_max = jnp.full((head_count, row_count), NEG_FILL, jnp.float32)
    run_total = jnp.zeros((head_count, row_count), jnp.float32)
    for key_start in range(0, total_keys, step_rows):
        scores = block_scores(
            queries,
            key_heads[key_start : key_start + step_rows],
            query_clip,
            key_clip[key_start : key_start + step_rows],
            score_scale,
        )
        new_max = jnp.maximum(run_max, jnp.max(scores, axis=2))
        run_total = run_total * jnp.exp(run_max - new_max) + jnp.sum(
            jnp.exp(scores - new_max[:, :, None]), axis=2
        )
        run_max = new_max
    log_total = run_max + jnp.log(run_total)
    output = jnp.zeros((row_count, head_count, head_size), jnp.float32)
    for key_start in range(0, total_keys, step_rows):
        scores = block_scores(
            queries,
            key_heads[key_start : key_start + step_rows],
            query_clip,
            key_clip[key_start : key_start + step_rows],
            score_scale,
        )
        soft_weights = jnp.exp(scores - log_total[:, :, None]).astype(jnp.bfloat16)
        output = output + jnp.einsum(
            "htk,khe->the",
            soft_weights,
            value_heads[key_start : key_start + step_rows],
            preferred_element_type=jnp.float32,
        )
    return (output, log_total)


def attend_backward(
    queries, key_heads, value_heads, query_clip, key_clip, log_total, grad_mixed, output
):
    row_count, head_count, head_size = queries.shape
    score_scale = head_size ** (-0.5)
    total_keys = key_heads.shape[0]
    step_rows = key_step(total_keys)
    row_delta = jnp.sum(grad_mixed.astype(jnp.float32) * output, axis=2).T
    grad_query = jnp.zeros((row_count, head_count, head_size), jnp.float32)
    key_pieces = []
    value_pieces = []
    for key_start in range(0, total_keys, step_rows):
        key_part = key_heads[key_start : key_start + step_rows]
        value_part = value_heads[key_start : key_start + step_rows]
        scores = block_scores(
            queries, key_part, query_clip, key_clip[key_start : key_start + step_rows], score_scale
        )
        soft_weights = jnp.exp(scores - log_total[:, :, None])
        grad_soft = jnp.einsum(
            "the,khe->htk", grad_mixed, value_part, preferred_element_type=jnp.float32
        )
        grad_scores = (soft_weights * (grad_soft - row_delta[:, :, None])).astype(jnp.bfloat16)
        grad_query = grad_query + jnp.einsum(
            "htk,khe->the", grad_scores, key_part, preferred_element_type=jnp.float32
        )
        key_pieces.append(
            jnp.einsum("htk,the->khe", grad_scores, queries, preferred_element_type=jnp.float32)
        )
        value_pieces.append(
            jnp.einsum(
                "htk,the->khe",
                soft_weights.astype(jnp.bfloat16),
                grad_mixed,
                preferred_element_type=jnp.float32,
            )
        )
    key_terms = jnp.concatenate(key_pieces, axis=0) * score_scale
    value_terms = jnp.concatenate(value_pieces, axis=0)
    return (grad_query * score_scale, key_terms, value_terms)


def block_forward(
    residual, norm_params, w_qkv, w_out, w_up, w_down, head_count, query_clip, key_clip
):
    row_count, model_width = residual.shape
    head_size = model_width // head_count
    norm_float = norm_params.astype(jnp.float32)
    normed = layer_norm(residual, norm_float[:, 0], norm_float[:, 1]).astype(jnp.bfloat16)
    qkv = jnp.dot(normed, w_qkv, preferred_element_type=jnp.float32).astype(jnp.bfloat16)
    queries = qkv[:, :model_width].reshape(row_count, head_count, head_size)
    key_local = qkv[:, model_width : 2 * model_width]
    value_local = qkv[:, 2 * model_width :]
    key_full, value_full = (
        lax.all_gather(key_local, "seq", axis=0, tiled=True),
        lax.all_gather(value_local, "seq", axis=0, tiled=True),
    )
    key_heads = key_full.reshape(-1, head_count, head_size)
    value_heads = value_full.reshape(-1, head_count, head_size)
    output, log_total = attend_forward(queries, key_heads, value_heads, query_clip, key_clip)
    mixed = output.reshape(row_count, model_width).astype(jnp.bfloat16)
    middle = residual + jnp.dot(mixed, w_out, preferred_element_type=jnp.float32)
    normed_mid = layer_norm(middle, norm_float[:, 2], norm_float[:, 3]).astype(jnp.bfloat16)
    pre_act = jnp.dot(normed_mid, w_up, preferred_element_type=jnp.float32)
    hidden = gelu_exact(pre_act).astype(jnp.bfloat16)
    result = middle + jnp.dot(hidden, w_down, preferred_element_type=jnp.float32)
    kept = (
        residual,
        normed,
        queries,
        key_local,
        value_local,
        key_heads,
        value_heads,
        output,
        log_total,
        mixed,
        middle,
        normed_mid,
        pre_act,
        hidden,
    )
    return (result, kept)


def block_backward(
    grad_result, kept, norm_params, w_qkv, w_out, w_up, w_down, head_count, query_clip, key_clip
):
    (
        residual,
        normed,
        queries,
        key_local,
        value_local,
        key_heads,
        value_heads,
        output,
        log_total,
        mixed,
        middle,
        normed_mid,
        pre_act,
        hidden,
    ) = kept
    row_count, model_width = residual.shape
    head_size = model_width // head_count
    norm_float = norm_params.astype(jnp.float32)
    grad_low = grad_result.astype(jnp.bfloat16)
    grad_down = jnp.einsum("tf,tw->fw", hidden, grad_low, preferred_element_type=jnp.float32)
    grad_hidden = jnp.einsum("tw,fw->tf", grad_low, w_down, preferred_element_type=jnp.float32)
    gelu_value, gelu_pull = jax.vjp(gelu_exact, pre_act)
    grad_pre = gelu_pull(grad_hidden)[0].astype(jnp.bfloat16)
    grad_up = jnp.einsum("tw,tf->wf", normed_mid, grad_pre, preferred_element_type=jnp.float32)
    grad_normed_mid = jnp.einsum("tf,wf->tw", grad_pre, w_up, preferred_element_type=jnp.float32)
    second_value, second_pull = jax.vjp(layer_norm, middle, norm_float[:, 2], norm_float[:, 3])
    grad_mid_norm, grad_gain_two, grad_shift_two = second_pull(grad_normed_mid)
    grad_middle = grad_result + grad_mid_norm
    grad_branch = grad_middle.astype(jnp.bfloat16)
    grad_out_w = jnp.einsum("tv,tw->vw", mixed, grad_branch, preferred_element_type=jnp.float32)
    grad_mixed = jnp.einsum(
        "tw,vw->tv", grad_branch, w_out, preferred_element_type=jnp.float32
    ).astype(jnp.bfloat16)
    key_full, value_full = (
        lax.all_gather(key_local, "seq", axis=0, tiled=True),
        lax.all_gather(value_local, "seq", axis=0, tiled=True),
    )
    key_heads = key_full.reshape(-1, head_count, head_size)
    value_heads = value_full.reshape(-1, head_count, head_size)
    grad_query, key_terms, value_terms = attend_backward(
        queries,
        key_heads,
        value_heads,
        query_clip,
        key_clip,
        log_total,
        grad_mixed.reshape(row_count, head_count, head_size),
        output,
    )
    grad_key, grad_value = (
        lax.psum_scatter(
            key_terms.reshape(-1, model_width).astype(jnp.bfloat16),
            "seq",
            scatter_dimension=0,
            tiled=True,
        ).astype(jnp.float32),
        lax.psum_scatter(
            value_terms.reshape(-1, model_width).astype(jnp.bfloat16),
            "seq",
            scatter_dimension=0,
            tiled=True,
        ).astype(jnp.float32),
    )
    grad_qkv = jnp.concatenate(
        [grad_query.reshape(row_count, model_width), grad_key, grad_value], axis=1
    ).astype(jnp.bfloat16)
    grad_qkv_w = jnp.einsum("tw,tc->wc", normed, grad_qkv, preferred_element_type=jnp.float32)
    grad_normed = jnp.einsum("tc,wc->tw", grad_qkv, w_qkv, preferred_element_type=jnp.float32)
    first_value, first_pull = jax.vjp(layer_norm, residual, norm_float[:, 0], norm_float[:, 1])
    grad_first_norm, grad_gain_one, grad_shift_one = first_pull(grad_normed)
    grad_norms = jnp.stack([grad_gain_one, grad_shift_one, grad_gain_two, grad_shift_two], axis=1)
    return (grad_middle + grad_first_norm, (grad_norms, grad_qkv_w, grad_out_w, grad_up, grad_down))


def local(
    tokens,
    clip_lengths,
    target_pos,
    out_grad,
    norm1_gain,
    norm1_bias,
    w_qkv,
    w_out,
    norm2_gain,
    norm2_bias,
    w_fc1,
    w_fc2,
    w_embed,
    mask_token,
    pred_norm1_gain,
    pred_norm1_bias,
    pred_qkv,
    pred_out,
    pred_norm2_gain,
    pred_norm2_bias,
    pred_fc1,
    pred_fc2,
):
    row_count = tokens.shape[0]
    group_count = row_count * lax.axis_size("seq")
    lengths = clip_lengths[0]
    clip_ends = jnp.cumsum(lengths)
    local_rows = lax.axis_index("seq") * row_count + jnp.arange(row_count, dtype=jnp.int32)
    query_clip = clip_index(local_rows, clip_ends)
    key_clip = clip_index(jnp.arange(group_count, dtype=jnp.int32), clip_ends)
    past_end = (local_rows[:, None] >= clip_ends[None, :]).astype(jnp.int32)
    rel_rows = local_rows - jnp.sum(lengths[None, :] * past_end, axis=1)
    ctx_small = jnp.stack([norm1_gain, norm1_bias, norm2_gain, norm2_bias], axis=1)
    pred_small = jnp.stack(
        [pred_norm1_gain, pred_norm1_bias, pred_norm2_gain, pred_norm2_bias, mask_token], axis=1
    )
    ctx_params = (
        lax.all_gather(ctx_small, "fsdp", axis=0, tiled=True),
        lax.all_gather(w_qkv, "fsdp", axis=0, tiled=True),
        lax.all_gather(w_out, "fsdp", axis=0, tiled=True),
        lax.all_gather(w_fc1, "fsdp", axis=0, tiled=True),
        lax.all_gather(w_fc2, "fsdp", axis=0, tiled=True),
    )
    pred_params = (
        lax.all_gather(pred_small, "fsdp", axis=0, tiled=True),
        lax.all_gather(w_embed, "fsdp", axis=0, tiled=True),
        lax.all_gather(pred_qkv, "fsdp", axis=0, tiled=True),
        lax.all_gather(pred_out, "fsdp", axis=0, tiled=True),
        lax.all_gather(pred_fc1, "fsdp", axis=0, tiled=True),
        lax.all_gather(pred_fc2, "fsdp", axis=0, tiled=True),
    )
    ctx_result, ctx_kept = block_forward(
        tokens.astype(jnp.float32),
        ctx_params[0],
        ctx_params[1],
        ctx_params[2],
        ctx_params[3],
        ctx_params[4],
        HEADS,
        query_clip,
        key_clip,
    )
    context_out = ctx_result.astype(jnp.bfloat16)
    embedded = jnp.dot(context_out, pred_params[1], preferred_element_type=jnp.float32)
    targets = target_pos[0, 0]
    matches = jnp.arange(row_count, dtype=jnp.int32)[:, None] == targets[None, :]
    placement = matches.astype(jnp.float32)
    target_hit = jnp.sum(placement, axis=1)
    target_rel = jnp.sum(jnp.where(matches, rel_rows[:, None], 0), axis=0)
    mask_rows = pred_params[0][:, 4].astype(jnp.float32)[None, :] + position_table(target_rel, PD)
    placed = jnp.dot(
        placement, mask_rows, precision=lax.Precision.HIGHEST, preferred_element_type=jnp.float32
    )
    pred_in = embedded * (1.0 - target_hit[:, None]) + placed
    pred_result, pred_kept = block_forward(
        pred_in,
        pred_params[0],
        pred_params[2],
        pred_params[3],
        pred_params[4],
        pred_params[5],
        P_HEADS,
        query_clip,
        key_clip,
    )
    predicted = pred_result.astype(jnp.bfloat16)
    pred_back = (
        lax.all_gather(pred_small, "fsdp", axis=0, tiled=True),
        lax.all_gather(w_embed, "fsdp", axis=0, tiled=True),
        lax.all_gather(pred_qkv, "fsdp", axis=0, tiled=True),
        lax.all_gather(pred_out, "fsdp", axis=0, tiled=True),
        lax.all_gather(pred_fc1, "fsdp", axis=0, tiled=True),
        lax.all_gather(pred_fc2, "fsdp", axis=0, tiled=True),
    )
    ctx_back = (
        lax.all_gather(ctx_small, "fsdp", axis=0, tiled=True),
        lax.all_gather(w_qkv, "fsdp", axis=0, tiled=True),
        lax.all_gather(w_out, "fsdp", axis=0, tiled=True),
        lax.all_gather(w_fc1, "fsdp", axis=0, tiled=True),
        lax.all_gather(w_fc2, "fsdp", axis=0, tiled=True),
    )
    grad_pred_in, pred_grads = block_backward(
        out_grad.astype(jnp.float32),
        pred_kept,
        pred_back[0],
        pred_back[2],
        pred_back[3],
        pred_back[4],
        pred_back[5],
        P_HEADS,
        query_clip,
        key_clip,
    )
    grad_mask = jnp.sum(target_hit[:, None] * grad_pred_in, axis=0)
    grad_embedded = (grad_pred_in * (1.0 - target_hit[:, None])).astype(jnp.bfloat16)
    grad_embed_w = jnp.einsum(
        "td,tp->dp", context_out, grad_embedded, preferred_element_type=jnp.float32
    )
    grad_context = jnp.einsum(
        "tp,dp->td", grad_embedded, pred_back[1], preferred_element_type=jnp.float32
    )
    grad_tokens, ctx_grads = block_backward(
        grad_context,
        ctx_kept,
        ctx_back[0],
        ctx_back[1],
        ctx_back[2],
        ctx_back[3],
        ctx_back[4],
        HEADS,
        query_clip,
        key_clip,
    )
    pred_small_grad = jnp.concatenate([pred_grads[0], grad_mask[:, None]], axis=1)
    row_sums = (
        lax.psum_scatter(ctx_grads[0], "fsdp", scatter_dimension=0, tiled=True),
        lax.psum_scatter(ctx_grads[1], "fsdp", scatter_dimension=0, tiled=True),
        lax.psum_scatter(ctx_grads[2], "fsdp", scatter_dimension=0, tiled=True),
        lax.psum_scatter(ctx_grads[3], "fsdp", scatter_dimension=0, tiled=True),
        lax.psum_scatter(ctx_grads[4], "fsdp", scatter_dimension=0, tiled=True),
        lax.psum_scatter(grad_embed_w, "fsdp", scatter_dimension=0, tiled=True),
        lax.psum_scatter(pred_small_grad, "fsdp", scatter_dimension=0, tiled=True),
        lax.psum_scatter(pred_grads[1], "fsdp", scatter_dimension=0, tiled=True),
        lax.psum_scatter(pred_grads[2], "fsdp", scatter_dimension=0, tiled=True),
        lax.psum_scatter(pred_grads[3], "fsdp", scatter_dimension=0, tiled=True),
        lax.psum_scatter(pred_grads[4], "fsdp", scatter_dimension=0, tiled=True),
    )
    summed = (
        lax.psum(row_sums[0].astype(jnp.bfloat16), "seq").astype(jnp.float32),
        lax.psum(row_sums[1].astype(jnp.bfloat16), "seq").astype(jnp.float32),
        lax.psum(row_sums[2].astype(jnp.bfloat16), "seq").astype(jnp.float32),
        lax.psum(row_sums[3].astype(jnp.bfloat16), "seq").astype(jnp.float32),
        lax.psum(row_sums[4].astype(jnp.bfloat16), "seq").astype(jnp.float32),
        lax.psum(row_sums[5].astype(jnp.bfloat16), "seq").astype(jnp.float32),
        lax.psum(row_sums[6].astype(jnp.bfloat16), "seq").astype(jnp.float32),
        lax.psum(row_sums[7].astype(jnp.bfloat16), "seq").astype(jnp.float32),
        lax.psum(row_sums[8].astype(jnp.bfloat16), "seq").astype(jnp.float32),
        lax.psum(row_sums[9].astype(jnp.bfloat16), "seq").astype(jnp.float32),
        lax.psum(row_sums[10].astype(jnp.bfloat16), "seq").astype(jnp.float32),
    )
    return (
        context_out,
        predicted,
        grad_tokens.astype(jnp.bfloat16),
        summed[0][:, 0],
        summed[0][:, 1],
        summed[1],
        summed[2],
        summed[0][:, 2],
        summed[0][:, 3],
        summed[3],
        summed[4],
        summed[5],
        summed[6][:, 4],
        summed[6][:, 0],
        summed[6][:, 1],
        summed[7],
        summed[8],
        summed[6][:, 2],
        summed[6][:, 3],
        summed[9],
        summed[10],
    )


BF16 = jnp.bfloat16
F32 = jnp.float32
MESH = pl.DeviceIdType.MESH
LOG2E = 1.4426950408889634
LN2 = 0.6931471805599453
LANES = 128
SMALL_ROWS = 16
ANYWHERE = pl.BlockSpec(memory_space=pl.ANY)
IN_VMEM = pl.BlockSpec(memory_space=pltpu.VMEM)


def fits_fast(mesh):
    return mesh.shape["fsdp"] == 8 and mesh.shape["seq"] == 4


def fsdp_peer(bit):
    return (lax.axis_index("fsdp") ^ bit, lax.axis_index("seq"))


def seq_peer(index):
    return (lax.axis_index("fsdp"), index)


def enter(peers):
    barrier = pltpu.get_barrier_semaphore()
    for peer in peers:
        pl.semaphore_signal(barrier, inc=1, device_id=peer, device_id_type=MESH)
    pl.semaphore_wait(barrier, len(peers))


def send(src, dst, send_sem, recv_sem, peer):
    return pltpu.make_async_remote_copy(
        src_ref=src,
        dst_ref=dst,
        send_sem=send_sem,
        recv_sem=recv_sem,
        device_id=peer,
        device_id_type=MESH,
    )


def remote_params(collective_id, vmem=None):
    return pltpu.CompilerParams(
        collective_id=collective_id, has_side_effects=True, vmem_limit_bytes=vmem
    )


def mate_z():
    return seq_peer(lax.axis_index("seq") ^ 1)


def quarter():
    return (lax.axis_index("fsdp") & 1) * 2 + (lax.axis_index("seq") & 1)


def across_lanes(left, right):
    return lax.dot_general(left, right, (((1,), (1,)), ((), ())), preferred_element_type=F32)


def forward_pass(tokens, out_grad, side, ends, shards, heads, narrow_heads):
    rows, width = tokens.shape
    narrow = out_grad.shape[1]
    hidden_width = shards[4].shape[1]
    narrow_hidden = shards[9].shape[1]
    shapes = [shard.shape for shard in shards]
    array_count = len(shards)
    units = []
    for index, (shard_rows, columns) in enumerate(shapes):
        if shard_rows * columns >= 100000:
            half = shard_rows // 2
            units.append((index, 0, half, 2, 4))
            units.append((index, half, half, 4, 2))
        else:
            near, far = (2, 4) if len(units) % 2 == 0 else (4, 2)
            units.append((index, 0, shard_rows, near, far))
    count = len(units)
    ahead = 3
    last_unit = {}
    for u, unit in enumerate(units):
        last_unit[unit[0]] = u

    block_widths = ((width, heads, hidden_width, 2), (narrow, narrow_heads, narrow_hidden, 1))
    saved_shapes = []
    for w, _, ff, _ in block_widths:
        saved_shapes += [
            ((rows, w), BF16),
            ((rows, w), BF16),
            ((2, w // LANES, 4, rows, LANES), BF16),
            ((rows, w), BF16),
            ((w // LANES, 8, rows), F32),
            ((rows, w), F32),
            ((rows, w), BF16),
            ((rows, ff), BF16),
            ((rows, ff), BF16),
        ]
    per_block = len(saved_shapes) // 2
    saved_shapes += [((rows, width), BF16), ((rows, narrow), F32), (side.shape, F32), ((rows, width), BF16)]
    saved_count = len(saved_shapes)

    def kernel(*refs):
        tokens_ref, out_grad_ref, side_ref, ends_ref = refs[:4]
        sources = refs[4 : 4 + array_count]
        base = 4 + array_count
        weight_outs = refs[base : base + array_count]
        base += array_count
        saved_outs = refs[base : base + saved_count]
        base += saved_count
        out_grad_out, ends_out, context_out, predicted_out = refs[base : base + 4]
        base += 4
        weights = refs[base : base + array_count]
        base += array_count
        saved = refs[base : base + saved_count]
        base += saved_count
        (
            bias,
            gains,
            narrow_gains,
            ends_buf,
            predicted,
            send_sems,
            recv_sems,
            local_sems,
            weight_sems,
            saved_sems,
            trade_send,
            trade_recv,
            trade_keep,
            key_send,
            key_recv,
        ) = refs[base:]
        context, entry, side_buf, token_buf = saved[2 * per_block :]

        me = lax.axis_index("fsdp")
        place = lax.axis_index("seq")
        core = me & 1
        high = place >> 1
        low = place & 1
        mine = quarter()
        trades = core != high
        trade_peer = ((me & 6) | high, core * 2 + low)

        barrier = pltpu.get_barrier_semaphore()
        for peer in (fsdp_peer(1), fsdp_peer(2), fsdp_peer(4), mate_z()):
            pl.semaphore_signal(barrier, inc=1, device_id=peer, device_id_type=MESH)

        @pl.when(trades)
        def _():
            pl.semaphore_signal(barrier, inc=1, device_id=trade_peer, device_id_type=MESH)

        pl.semaphore_wait(barrier, 4 + trades.astype(jnp.int32))


        def trade_copy(i, src, dst):
            return send(src, dst, trade_send.at[i], trade_recv.at[i], trade_peer)

        def keep_copy(i, src, dst):
            return pltpu.make_async_copy(src, dst, trade_keep.at[i])

        traded = [
            (tokens_ref, token_buf),
            (side_ref, side_buf),
            (ends_ref, ends_buf),
            (out_grad_ref, out_grad_out),
            (context, context_out),
            (predicted, predicted_out),
        ]

        def trade_start(i):
            @pl.when(trades)
            def _():
                trade_copy(i, *traded[i]).start()

            @pl.when(jnp.logical_not(trades))
            def _():
                keep_copy(i, *traded[i]).start()

        def trade_arrived(i):
            @pl.when(trades)
            def _():
                trade_copy(i, *traded[i]).wait_recv()

            @pl.when(jnp.logical_not(trades))
            def _():
                keep_copy(i, *traded[i]).wait()

        def trade_sent(i):
            @pl.when(trades)
            def _():
                trade_copy(i, *traded[i]).wait_send()


        def place_of(u, owner):
            index, first, unit_rows, _, _ = units[u]
            start = owner * shapes[index][0] + first
            return weights[index].at[pl.ds(pl.multiple_of(start, 16), unit_rows)]

        def own_shard(u):
            index, first, unit_rows, _, _ = units[u]
            return sources[index].at[pl.ds(first, unit_rows)]

        def weight_copy(u, slot):
            _, _, _, near, far = units[u]
            owner = me ^ (0, 0, near, 0, near, far, near ^ far)[slot]
            bit = (near, far, far, 1, 1, 1, 1)[slot]
            src = own_shard(u) if slot in (0, 1, 3) else place_of(u, owner)
            return send(src, place_of(u, owner), send_sems.at[u, slot], recv_sems.at[u, slot], fsdp_peer(bit))

        def own_weight(u):
            return pltpu.make_async_copy(own_shard(u), place_of(u, me), local_sems.at[u])

        def weight_out(index):
            return pltpu.make_async_copy(weights[index], weight_outs[index], weight_sems.at[index])

        def launch(u):
            for slot in (0, 1, 3):
                weight_copy(u, slot).start()
            own_weight(u).start()

        def arrive(u):
            weight_copy(u, 0).wait_recv()
            weight_copy(u, 2).start()
            weight_copy(u, 4).start()
            weight_copy(u, 1).wait_recv()
            weight_copy(u, 5).start()
            if u + ahead < count:
                launch(u + ahead)

        def relay(u):
            weight_copy(u, 2).wait_recv()
            weight_copy(u, 6).start()

        def complete(u):
            for slot in (3, 4, 5, 6):
                weight_copy(u, slot).wait_recv()
            own_weight(u).wait()
            index = units[u][0]
            if last_unit[index] == u:
                weight_out(index).start()

        ticks = []
        ready = {}
        for u in range(count + 2):
            if u < count:
                ticks.append((arrive, u))
            if 1 <= u <= count:
                ticks.append((relay, u - 1))
            if u >= 2:
                ticks.append((complete, u - 2))
                ready[units[u - 2][0]] = len(ticks)
        position = [0]

        def advance(steps):
            for _ in range(steps):
                if position[0] < len(ticks):
                    step, u = ticks[position[0]]
                    step(u)
                    position[0] += 1

        def need(index):
            while position[0] < ready[index]:
                advance(1)


        def save(i):
            return pltpu.make_async_copy(saved[i], saved_outs[i], saved_sems.at[i])

        def norm_into(dst, get, table, gain_at):
            @pl.loop(0, rows // 64)
            def _(i):
                part = pl.ds(pl.multiple_of(i * 64, 64), 64)
                value = get(part)
                value = value - jnp.mean(value, axis=1, keepdims=True)
                inverse = lax.rsqrt(jnp.mean(value * value, axis=1, keepdims=True) + EPSILON)
                dst[part] = (
                    value * inverse * table[gain_at : gain_at + 1, :] + table[gain_at + 1 : gain_at + 2, :]
                ).astype(BF16)

        def run_block(which, get, table, first_weight, finish, inside):
            w, head_count, ff, in_group = block_widths[which]
            (normed, queries, kv, mixed, logs, middle, normed_mid, hidden, slope) = saved[
                which * per_block : (which + 1) * per_block
            ]
            w_qkv, w_out, w_up, w_down = [weights[first_weight[i]] for i in range(4)]
            slabs = w // LANES
            groups = slabs // in_group
            head_size = w // head_count
            per_slab = LANES // head_size
            factor = head_size ** (-0.5) * LOG2E
            columns = in_group * LANES

            def kv_copy(kind, g):
                owner = mine ^ 1 if kind == 2 else mine
                part = kv.at[:, pl.ds(g * in_group, in_group), owner]
                return send(
                    part,
                    part,
                    key_send.at[which, kind, g],
                    key_recv.at[which, kind, g],
                    mate_z() if kind == 0 else fsdp_peer(1),
                )

            norm_into(normed, get, table, 0)
            save(which * per_block).start()
            need(first_weight[0])
            for g in range(groups):
                for kind in range(2):
                    tile = jnp.dot(
                        normed[...],
                        w_qkv[:, pl.ds((1 + kind) * w + g * columns, columns)],
                        preferred_element_type=F32,
                    ).astype(BF16)
                    for k in range(in_group):
                        kv[kind, g * in_group + k, mine] = tile[:, k * LANES : (k + 1) * LANES]
                kv_copy(0, g).start()
                kv_copy(1, g).start()
            for g in range(groups):
                at = pl.ds(g * columns, columns)
                queries[:, at] = jnp.dot(normed[...], w_qkv[:, at], preferred_element_type=F32).astype(BF16)
            save(which * per_block + 1).start()
            advance(inside[0])
            kv_copy(0, 0).wait_recv()
            kv_copy(2, 0).start()

            lane = lax.broadcasted_iota(jnp.int32, (rows, LANES), 1) // head_size
            sub = lax.broadcasted_iota(jnp.int32, (LANES, rows), 0) // head_size

            @pl.loop(0, slabs)
            def _(j):
                g = j // in_group

                @pl.when(j % in_group == 0)
                def _():
                    kv_copy(1, g).wait_recv()
                    kv_copy(2, g).wait_recv()

                at = pl.ds(pl.multiple_of(j * LANES, LANES), LANES)
                own_queries = queries[:, at]
                key_slab = kv[0, j].reshape(4 * rows, LANES)
                values_t = kv[1, j].reshape(4 * rows, LANES).T
                output = jnp.zeros((LANES, rows), F32)
                logs[j] = jnp.zeros((8, rows), F32)
                for head in range(per_slab):
                    own = jnp.where(lane == head, own_queries, jnp.zeros_like(own_queries))
                    scores = across_lanes(key_slab, own) * factor + bias[...]
                    top = jnp.max(scores, axis=0, keepdims=True)
                    soft = jnp.exp2(scores - top)
                    total = jnp.sum(soft, axis=0, keepdims=True)
                    attended = jnp.dot(values_t, soft.astype(BF16), preferred_element_type=F32) / total
                    output = jnp.where(sub == head, attended, output)
                    logs[j, head : head + 1, :] = top + jnp.log2(total)
                mixed[:, at] = output.T.astype(BF16)

                @pl.when(jnp.logical_and(j % in_group == 0, g + 1 < groups))
                def _():
                    kv_copy(0, g + 1).wait_recv()
                    kv_copy(2, g + 1).start()

                for k in range(slabs):

                    @pl.when(j == k)
                    def _():
                        advance(inside[1])

            for i in (2, 3, 4):
                save(which * per_block + i).start()
            need(first_weight[1])
            step = 2 * LANES if w % (2 * LANES) == 0 else LANES
            for c in range(w // step):
                at = pl.ds(c * step, step)
                middle[:, at] = get(pl.ds(0, rows), at) + jnp.dot(
                    mixed[...], w_out[:, at], preferred_element_type=F32
                )
            save(which * per_block + 5).start()
            norm_into(normed_mid, lambda part: middle[part], table, 2)
            save(which * per_block + 6).start()
            need(first_weight[2])

            @pl.loop(0, ff // (2 * LANES))
            def _(c):
                at = pl.ds(pl.multiple_of(c * 2 * LANES, 2 * LANES), 2 * LANES)
                pre = jnp.dot(normed_mid[...], w_up[:, at], preferred_element_type=F32)
                below = 0.5 * (1.0 + lax.erf(pre * (0.5**0.5)))
                bell = jnp.exp2(pre * pre * (-0.5 * LOG2E)) * (1.0 / math.sqrt(2.0 * math.pi))
                hidden[:, at] = (pre * below).astype(BF16)
                slope[:, at] = (below + pre * bell).astype(BF16)

            save(which * per_block + 7).start()
            save(which * per_block + 8).start()
            need(first_weight[3])
            for c in range(w // step):
                at = pl.ds(c * step, step)
                finish(
                    at, middle[:, at] + jnp.dot(hidden[...], w_down[:, at], preferred_element_type=F32)
                )
            for g in range(groups):
                for kind in range(3):
                    kv_copy(kind, g).wait_send()


        for i in (0, 2, 1):
            trade_start(i)
        for u in range(ahead):
            launch(u)
        trade_start(3)
        need(1)
        for owner in range(8):
            gains[:, owner * LANES : (owner + 1) * LANES] = weights[0][
                owner * SMALL_ROWS : (owner + 1) * SMALL_ROWS, :
            ].astype(F32)
        total = weights[1][0:SMALL_ROWS, :].astype(F32)
        for owner in range(1, 8):
            total = total + weights[1][owner * SMALL_ROWS : (owner + 1) * SMALL_ROWS, :].astype(F32)
        narrow_gains[...] = total
        trade_arrived(2)
        key_row = lax.broadcasted_iota(jnp.int32, (4 * rows, rows), 0)
        query_row = mine * rows + lax.broadcasted_iota(jnp.int32, (4 * rows, rows), 1)
        key_clip = jnp.zeros((4 * rows, rows), jnp.int32)
        query_clip = jnp.zeros((4 * rows, rows), jnp.int32)
        for c in range(3):
            end = ends_buf[c : c + 1, 0:1]
            key_clip = key_clip + (key_row >= end).astype(jnp.int32)
            query_clip = query_clip + (query_row >= end).astype(jnp.int32)
        bias[...] = jnp.where(key_clip == query_clip, 0.0, NEG_FILL)
        trade_arrived(0)
        save(2 * per_block + 3).start()

        def token_rows(part, at=slice(None)):
            return token_buf[part, at].astype(F32)

        def finish_context(at, value):
            context[:, at] = value.astype(BF16)

        run_block(0, token_rows, gains, (2, 3, 4, 5), finish_context, (1, 1))
        trade_start(4)
        save(2 * per_block).start()
        need(6)
        trade_arrived(1)
        save(2 * per_block + 2).start()
        embedded = jnp.dot(context[...], weights[6][...], preferred_element_type=F32)
        hit = side_buf[:, narrow : narrow + 1]
        entry[...] = jnp.where(hit > 0.0, narrow_gains[4:5, :] + side_buf[:, 0:narrow], embedded)
        save(2 * per_block + 1).start()

        def entry_rows(part, at=slice(None)):
            return entry[part, at]

        def finish_predicted(at, value):
            predicted[:, at] = value.astype(BF16)

        run_block(1, entry_rows, narrow_gains, (7, 8, 9, 10), finish_predicted, (0, 0))
        trade_start(5)
        advance(len(ticks))
        for u in range(count):
            for slot in range(7):
                weight_copy(u, slot).wait_send()
        for index in range(array_count):
            weight_out(index).wait()
        for i in range(saved_count):
            save(i).wait()
        keep_copy(6, ends_buf, ends_out).start()
        for i in (3, 4, 5):
            trade_arrived(i)
        for i in range(6):
            trade_sent(i)
        keep_copy(6, ends_buf, ends_out).wait()

    gathered = [(8 * shape[0], shape[1]) for shape in shapes]
    out_shape = (
        [jax.ShapeDtypeStruct(shape, BF16) for shape in gathered]
        + [jax.ShapeDtypeStruct(shape, kind) for shape, kind in saved_shapes]
        + [
            jax.ShapeDtypeStruct(out_grad.shape, BF16),
            jax.ShapeDtypeStruct(ends.shape, jnp.int32),
            jax.ShapeDtypeStruct((rows, width), BF16),
            jax.ShapeDtypeStruct((rows, narrow), BF16),
        ]
    )
    scratch = (
        [pltpu.VMEM(shape, BF16) for shape in gathered]
        + [pltpu.VMEM(shape, kind) for shape, kind in saved_shapes]
        + [
            pltpu.VMEM((4 * rows, rows), F32),
            pltpu.VMEM((SMALL_ROWS, width), F32),
            pltpu.VMEM((SMALL_ROWS, narrow), F32),
            pltpu.VMEM(ends.shape, jnp.int32),
            pltpu.VMEM((rows, narrow), BF16),
            pltpu.SemaphoreType.DMA((count, 7)),
            pltpu.SemaphoreType.DMA((count, 7)),
            pltpu.SemaphoreType.DMA((count,)),
            pltpu.SemaphoreType.DMA((array_count,)),
            pltpu.SemaphoreType.DMA((saved_count,)),
            pltpu.SemaphoreType.DMA((6,)),
            pltpu.SemaphoreType.DMA((6,)),
            pltpu.SemaphoreType.DMA((7,)),
            pltpu.SemaphoreType.DMA((2, 3, 4)),
            pltpu.SemaphoreType.DMA((2, 3, 4)),
        ]
    )
    results = pl.pallas_call(
        kernel,
        out_shape=out_shape,
        in_specs=[ANYWHERE] * (4 + array_count),
        out_specs=[ANYWHERE] * len(out_shape),
        scratch_shapes=scratch,
        compiler_params=remote_params(1, 62 << 20),
        name="forward_pass",
    )(tokens, out_grad, side, ends, *shards)
    saved = results[array_count : array_count + saved_count]
    return (
        results[:array_count],
        saved[:per_block],
        saved[per_block : 2 * per_block],
        saved[2 * per_block :],
        results[array_count + saved_count :],
    )


class Unit:
    def __init__(self, index, first, columns, order, place):
        self.index = index
        self.first = first
        self.columns = columns
        self.near, self.far = order
        self.place = place


def cut_columns(shapes, most):
    units = []
    for index, (rows, columns) in enumerate(shapes):
        pieces = 1
        while rows * (columns // pieces) > most and (columns // pieces) % (2 * LANES) == 0:
            pieces *= 2
        for place in range(pieces):
            order = (2, 4) if len(units) % 2 == 0 else (4, 2)
            units.append(Unit(index, place * (columns // pieces), columns // pieces, order, place))
    return units


def back_and_sum(
    partials,
    queries,
    keys_values,
    mixed,
    grad_mixed,
    logs,
    query_clip,
    key_clip,
    normed_both_t,
    w_qkv,
    tokens,
    grad_middle,
    gain,
    head_count,
    collective_id,
):
    rows, width = queries.shape
    triple = 3 * width
    keys = 4 * rows
    slabs = width // LANES
    head_size = width // head_count
    per_slab = LANES // head_size
    scale = head_size ** (-0.5)
    factor = scale * LOG2E
    part_rows = w_qkv.shape[1]

    given = len(partials)
    shapes = [partial.shape[1:] for partial in partials] + [(part_rows, triple), (SMALL_ROWS, LANES)]
    qkv_index, small_index = given, given + 1
    array_count = given + 2
    units = cut_columns(shapes, 70000)
    count = len(units)
    pieces = [sum(1 for unit in units if unit.index == index) for index in range(array_count)]

    def kernel(*refs):
        sources = refs[:given]
        (
            q_ref,
            kv_ref,
            mixed_ref,
            grad_ref,
            log_ref,
            query_ref,
            key_ref,
            normed_t_ref,
            w_ref,
            tokens_ref,
            middle_ref,
            gain_ref,
        ) = refs[given : given + 12]
        results = refs[given + 12 : given + 12 + array_count]
        token_out = refs[given + 12 + array_count]
        rest = list(refs[given + 13 + array_count :])
        acc, near_in, far_in, outer_in, inner_in = [
            rest[group * array_count : (group + 1) * array_count] for group in range(5)
        ]
        (
            late_out,
            small_out,
            bias,
            dkv,
            core_in,
            z_in,
            dqkv,
            w_buf,
            grad_normed,
            token_buf,
            norm_sums,
            norm_sums_in,
            send_sems,
            recv_sems,
            own_sems,
            out_sems,
            key_send,
            key_recv,
            row_send,
            row_recv,
            w_sems,
        ) = rest[5 * array_count :]

        me = lax.axis_index("fsdp")
        place = lax.axis_index("seq")
        core = me & 1
        chip = me >> 1
        high = place >> 1
        low = place & 1
        inner = jnp.logical_or(place == 1, place == 2)
        outer = jnp.logical_not(inner)
        trades = core != high
        trade_peer = ((me & 6) | high, core * 2 + low)
        mate = seq_peer(place ^ 1)
        across = seq_peer(3 - place)

        barrier = pltpu.get_barrier_semaphore()
        for peer in (fsdp_peer(1), fsdp_peer(2), fsdp_peer(4), mate):
            pl.semaphore_signal(barrier, inc=1, device_id=peer, device_id_type=MESH)

        @pl.when(inner)
        def _():
            pl.semaphore_signal(barrier, inc=1, device_id=across, device_id_type=MESH)

        @pl.when(trades)
        def _():
            pl.semaphore_signal(barrier, inc=1, device_id=trade_peer, device_id_type=MESH)

        pl.semaphore_wait(barrier, 4 + inner.astype(jnp.int32) + trades.astype(jnp.int32))


        def span(unit):
            return pl.ds(unit.first, unit.columns)

        def chip_of(unit, slot):
            return chip ^ (((slot // 2) * unit.near + (slot % 2) * unit.far) // 2)

        def near_copy(u, slot):
            unit = units[u]
            if unit.index == qkv_index:
                src = late_out.at[unit.place, slot]
            elif unit.index == small_index:
                src = small_out.at[slot]
            else:
                src = sources[unit.index].at[chip_of(unit, 2 + slot), :, span(unit)]
            return send(
                src,
                near_in[unit.index].at[unit.place, slot],
                send_sems.at[u, slot],
                recv_sems.at[u, slot],
                fsdp_peer(unit.near),
            )

        def own_copy(u, slot):
            unit = units[u]
            return pltpu.make_async_copy(
                sources[unit.index].at[chip_of(unit, slot), :, span(unit)],
                acc[unit.index].at[unit.place, slot],
                own_sems.at[u, slot],
            )

        def far_copy(u):
            unit = units[u]
            return send(
                acc[unit.index].at[unit.place, 1],
                far_in[unit.index].at[unit.place],
                send_sems.at[u, 2],
                recv_sems.at[u, 2],
                fsdp_peer(unit.far),
            )

        def inward_copy(u):
            unit = units[u]
            return send(
                acc[unit.index].at[unit.place, 0],
                outer_in[unit.index].at[unit.place],
                send_sems.at[u, 3],
                recv_sems.at[u, 3],
                mate,
            )

        def across_copy(u):
            unit = units[u]
            return send(
                outer_in[unit.index].at[unit.place],
                inner_in[unit.index].at[unit.place],
                send_sems.at[u, 4],
                recv_sems.at[u, 4],
                across,
            )

        def outward_copy(u):
            unit = units[u]
            return send(
                acc[unit.index].at[unit.place, 0],
                results[unit.index].at[:, span(unit)],
                send_sems.at[u, 5],
                recv_sems.at[u, 5],
                mate,
            )

        def out_copy(u):
            unit = units[u]
            return pltpu.make_async_copy(
                acc[unit.index].at[unit.place, 0], results[unit.index].at[:, span(unit)], out_sems.at[u]
            )

        def add_into(dst, left, right):
            total_rows, columns = dst.shape
            step = 16
            while total_rows % (2 * step) == 0 and 2 * step * columns <= 32768:
                step *= 2

            @pl.loop(0, total_rows // step)
            def _(i):
                part = pl.ds(pl.multiple_of(i * step, step), step)
                dst[part] = (left[part].astype(F32) + right[part].astype(F32)).astype(BF16)

        def early(u):
            return units[u].index < given

        def near_start(u):
            if units[u].index == qkv_index:
                form_qkv(u)
            elif units[u].index == small_index:
                form_small(u)
            near_copy(u, 1).start()
            near_copy(u, 0).start()

        def stage_far(u):
            unit = units[u]
            for slot in (1, 0):
                near_copy(u, slot).wait_recv()
                if early(u):
                    own_copy(u, slot).wait()
                target = acc[unit.index].at[unit.place, slot]
                add_into(target, target, near_in[unit.index].at[unit.place, slot])
                if slot == 1:
                    far_copy(u).start()

        def stage_inward(u):
            unit = units[u]
            far_copy(u).wait_recv()
            target = acc[unit.index].at[unit.place, 0]
            add_into(target, target, far_in[unit.index].at[unit.place])

            @pl.when(outer)
            def _():
                inward_copy(u).start()

        def stage_across(u):
            unit = units[u]

            @pl.when(inner)
            def _():
                inward_copy(u).wait_recv()
                target = outer_in[unit.index].at[unit.place]
                add_into(target, target, acc[unit.index].at[unit.place, 0])
                across_copy(u).start()

        def stage_outward(u):
            unit = units[u]

            @pl.when(inner)
            def _():
                across_copy(u).wait_recv()
                add_into(
                    acc[unit.index].at[unit.place, 0],
                    outer_in[unit.index].at[unit.place],
                    inner_in[unit.index].at[unit.place],
                )
                outward_copy(u).start()
                out_copy(u).start()

        ahead = 4
        lags = ((stage_far, 0), (stage_inward, 2), (stage_across, 4), (stage_outward, 6))
        total_ticks = count + 6

        def tick(t):
            if t + ahead < count:
                near_start(t + ahead)
            for stage, lag in lags:
                if 0 <= t - lag < count:
                    stage(t - lag)


        half = 2 * rows

        def group(g):
            return pl.ds(2 * g, 2)

        def key_core_copy(g):
            return send(
                dkv.at[:, group(g), pl.ds((core ^ 1) * half, half)],
                core_in.at[:, group(g)],
                key_send.at[0, g],
                key_recv.at[0, g],
                fsdp_peer(1),
            )

        def key_far_copy(g):
            return send(
                core_in.at[:, group(g), pl.ds((low ^ 1) * rows, rows)],
                z_in.at[:, group(g)],
                key_send.at[1, g],
                key_recv.at[1, g],
                mate,
            )

        def key_middle(g):
            key_core_copy(g).wait_recv()
            for kind in range(2):
                for k in range(2):

                    @pl.loop(0, half // LANES)
                    def _(i):
                        part = pl.ds(pl.multiple_of(i * LANES, LANES), LANES)
                        own = pl.ds(pl.multiple_of(core * half + i * LANES, LANES), LANES)
                        core_in[kind, 2 * g + k, part] = (
                            core_in[kind, 2 * g + k, part].astype(F32) + dkv[kind, 2 * g + k, own].astype(F32)
                        ).astype(BF16)

            key_far_copy(g).start()

        def key_end(g):
            key_far_copy(g).wait_recv()
            for kind in range(2):
                for k in range(2):
                    slab = 2 * g + k

                    @pl.loop(0, rows // LANES)
                    def _(i):
                        part = pl.ds(pl.multiple_of(i * LANES, LANES), LANES)
                        own = pl.ds(pl.multiple_of(low * rows + i * LANES, LANES), LANES)
                        total = core_in[kind, slab, own].astype(F32) + z_in[kind, slab, part].astype(F32)
                        dqkv[part, pl.ds((1 + kind) * width + slab * LANES, LANES)] = total.astype(BF16)


        lane = lax.broadcasted_iota(jnp.int32, (rows, LANES), 1) // head_size
        key_lane = lax.broadcasted_iota(jnp.int32, (keys, LANES), 1) // head_size
        sub = lax.broadcasted_iota(jnp.int32, (LANES, rows), 0) // head_size

        def slab_back(j):
            at = pl.ds(pl.multiple_of(j * LANES, LANES), LANES)
            queries = q_ref[:, at]
            grads = grad_ref[:, at]
            pick = (
                lax.broadcasted_iota(jnp.int32, (8, LANES), 1) // head_size
                == lax.broadcasted_iota(jnp.int32, (8, LANES), 0)
            ).astype(F32)
            deltas = lax.dot_general(
                pick,
                grads.astype(F32) * mixed_ref[:, at].astype(F32),
                (((1,), (1,)), ((), ())),
                precision=lax.Precision.HIGHEST,
                preferred_element_type=F32,
            )
            key_slab = kv_ref[0, j]
            keys_t = key_slab.T
            dq = jnp.zeros((LANES, rows), F32)
            dk = jnp.zeros((keys, LANES), F32)
            dv = jnp.zeros((keys, LANES), F32)
            slab_logs = log_ref[j]
            for head in range(per_slab):
                own = jnp.where(lane == head, queries, jnp.zeros_like(queries))
                own_grad = jnp.where(lane == head, grads, jnp.zeros_like(grads))
                scores = across_lanes(key_slab, own) * factor + bias[...]
                weights = jnp.exp2(scores - slab_logs[head : head + 1, :])
                grad_soft = across_lanes(kv_ref[1, j], own_grad)
                grad_scores = (weights * (grad_soft - deltas[head : head + 1, :])).astype(BF16)
                dv = jnp.where(
                    key_lane == head, jnp.dot(weights.astype(BF16), grads, preferred_element_type=F32), dv
                )
                dk = jnp.where(
                    key_lane == head, jnp.dot(grad_scores, queries, preferred_element_type=F32), dk
                )
                dq = jnp.where(sub == head, jnp.dot(keys_t, grad_scores, preferred_element_type=F32), dq)
            dqkv[pl.ds(0, rows), at] = (dq.T * scale).astype(BF16)
            dkv[0, j] = (dk * scale).astype(BF16)
            dkv[1, j] = dv.astype(BF16)


        def row_copy(part):
            columns = pl.ds(0, width) if part == 0 else pl.ds(width, 2 * width)
            return send(
                dqkv.at[pl.ds(0, rows), columns],
                dqkv.at[pl.ds(rows, rows), columns],
                row_send.at[part],
                row_recv.at[part],
                fsdp_peer(1),
            )

        def form_qkv(u):
            unit = units[u]
            right = dqkv[:, span(unit)]
            for slot in range(4):
                left = normed_t_ref[pl.ds(pl.multiple_of(chip_of(unit, slot) * part_rows, part_rows), part_rows)]
                block = jnp.dot(left, right, preferred_element_type=F32).astype(BF16)
                if slot < 2:
                    acc[unit.index][unit.place, slot] = block
                else:
                    late_out[unit.place, slot - 2] = block


        blocks = 8

        def w_copy(block):
            return pltpu.make_async_copy(w_ref.at[block], w_buf.at[block % 2], w_sems.at[block % 2])

        def norm_copy():
            return send(norm_sums, norm_sums_in, row_send.at[2], row_recv.at[2], fsdp_peer(1))

        def input_gradient():
            for block in range(blocks):
                w_copy(block).wait()
                grad_normed[:, pl.ds(block * part_rows, part_rows)] = across_lanes(
                    dqkv[pl.ds(0, rows), :], w_buf[block % 2]
                )
                if block + 2 < blocks:
                    w_copy(block + 2).start()
            gain_row = gain_ref[...]
            norm_sums[...] = jnp.zeros_like(norm_sums)
            step = 64
            gain_sum = jnp.zeros((1, width), F32)
            shift_sum = jnp.zeros((1, width), F32)
            for i in range(rows // step):
                part = pl.ds(i * step, step)
                value = tokens_ref[part].astype(F32)
                value = value - jnp.mean(value, axis=1, keepdims=True)
                inverse = lax.rsqrt(jnp.mean(value * value, axis=1, keepdims=True) + EPSILON)
                unit_value = value * inverse
                upper = grad_normed[part]
                gain_sum = gain_sum + jnp.sum(upper * unit_value, axis=0, keepdims=True)
                shift_sum = shift_sum + jnp.sum(upper, axis=0, keepdims=True)
                scaled = upper * gain_row
                inside = (
                    scaled
                    - jnp.mean(scaled, axis=1, keepdims=True)
                    - unit_value * jnp.mean(scaled * unit_value, axis=1, keepdims=True)
                )
                token_buf[part] = (middle_ref[part] + inverse * inside).astype(BF16)
            norm_sums[0:1, :] = gain_sum
            norm_sums[1:2, :] = shift_sum
            norm_copy().start()

            @pl.when(trades)
            def _():
                token_send().start()

            @pl.when(jnp.logical_not(trades))
            def _():
                token_keep().start()

        def token_send():
            return send(token_buf, token_out, row_send.at[3], row_recv.at[3], trade_peer)

        def token_keep():
            return pltpu.make_async_copy(token_buf, token_out, w_sems.at[2])

        def form_small(u):
            unit = units[u]
            norm_copy().wait_recv()
            both = norm_sums[...] + norm_sums_in[...]
            norm_sums_in[...] = both
            for slot in range(4):
                owner = chip_of(unit, slot) * 2 + core
                block = norm_sums_in[:, pl.ds(pl.multiple_of(owner * LANES, LANES), LANES)].astype(BF16)
                if slot < 2:
                    acc[unit.index][unit.place, slot] = block
                else:
                    small_out[slot - 2] = block


        first_late = min(u for u in range(count) if not early(u))
        for u in range(first_late):
            for slot in range(2):
                own_copy(u, slot).start()
        for u in range(ahead):
            near_start(u)
        w_copy(0).start()
        w_copy(1).start()
        bias[...] = jnp.where(key_ref[...] == query_ref[...], 0.0, NEG_FILL)
        ticks_inside = first_late - ahead

        @pl.loop(0, slabs)
        def _(j):
            slab_back(j)

            @pl.when(j % 2 == 1)
            def _():
                key_core_copy(j // 2).start()

            @pl.when(jnp.logical_and(j % 2 == 0, j >= 2))
            def _():
                key_middle(j // 2 - 1)

            done = 0
            for k in range(slabs):
                until = (k + 1) * ticks_inside // slabs

                @pl.when(j == k)
                def _(done=done, until=until):
                    for t in range(done, until):
                        tick(t)

                done = until

        row_copy(0).start()
        key_middle(slabs // 2 - 1)
        for g in range(slabs // 2):
            key_end(g)
        row_copy(1).start()
        row_copy(0).wait_recv()
        row_copy(1).wait_recv()
        done_input = False
        for t in range(ticks_inside, total_ticks):
            if not done_input and t + ahead >= count - 1:
                input_gradient()
                done_input = True
            tick(t)

        for u in range(count):
            near_copy(u, 0).wait_send()
            near_copy(u, 1).wait_send()
            far_copy(u).wait_send()

        for u in range(count):

            @pl.when(inner)
            def _():
                across_copy(u).wait_send()
                outward_copy(u).wait_send()
                out_copy(u).wait()

            @pl.when(outer)
            def _():
                inward_copy(u).wait_send()
                outward_copy(u).wait_recv()

        for g in range(slabs // 2):
            key_core_copy(g).wait_send()
            key_far_copy(g).wait_send()
        row_copy(0).wait_send()
        row_copy(1).wait_send()
        norm_copy().wait_send()

        @pl.when(trades)
        def _():
            token_send().wait()

        @pl.when(jnp.logical_not(trades))
        def _():
            token_keep().wait()

    def piece_shape(index):
        return (shapes[index][0], shapes[index][1] // pieces[index])

    scratch = []
    for slots in ((2,), (2,), (), (), ()):
        for index in range(array_count):
            scratch.append(pltpu.VMEM((pieces[index],) + slots + piece_shape(index), BF16))
    scratch += [
        pltpu.VMEM((pieces[qkv_index], 2) + piece_shape(qkv_index), BF16),
        pltpu.VMEM((2, SMALL_ROWS, LANES), BF16),
        pltpu.VMEM((keys, rows), F32),
        pltpu.VMEM((2, slabs, keys, LANES), BF16),
        pltpu.VMEM((2, slabs, 2 * rows, LANES), BF16),
        pltpu.VMEM((2, slabs, rows, LANES), BF16),
        pltpu.VMEM((2 * rows, triple), BF16),
        pltpu.VMEM((2, part_rows, triple), BF16),
        pltpu.VMEM((rows, width), F32),
        pltpu.VMEM((rows, width), BF16),
        pltpu.VMEM((SMALL_ROWS, width), F32),
        pltpu.VMEM((SMALL_ROWS, width), F32),
        pltpu.SemaphoreType.DMA((count, 6)),
        pltpu.SemaphoreType.DMA((count, 6)),
        pltpu.SemaphoreType.DMA((count, 2)),
        pltpu.SemaphoreType.DMA((count,)),
        pltpu.SemaphoreType.DMA((2, slabs // 2)),
        pltpu.SemaphoreType.DMA((2, slabs // 2)),
        pltpu.SemaphoreType.DMA((4,)),
        pltpu.SemaphoreType.DMA((4,)),
        pltpu.SemaphoreType.DMA((3,)),
    ]
    return pl.pallas_call(
        kernel,
        out_shape=[jax.ShapeDtypeStruct(shape, BF16) for shape in shapes]
        + [jax.ShapeDtypeStruct((rows, width), BF16)],
        in_specs=[ANYWHERE] * given + [IN_VMEM] * 8 + [ANYWHERE] + [IN_VMEM] * 3,
        out_specs=[ANYWHERE] * (array_count + 1),
        scratch_shapes=scratch,
        compiler_params=remote_params(collective_id, 61 << 20),
        name="back_and_sum",
    )(
        *partials,
        queries,
        keys_values,
        mixed,
        grad_mixed,
        logs,
        query_clip[None, :],
        key_clip[:, None],
        normed_both_t,
        w_qkv,
        tokens,
        grad_middle,
        gain[None, :],
    )


def sum_keys(terms, collective_id):
    _, rows, width = terms[0].shape
    pieces = 4
    step = rows // pieces
    kinds = len(terms)

    def kernel(*refs):
        sources = refs[:kinds]
        results = refs[kinds : 2 * kinds]
        core_buf, far_buf, send_sems, recv_sems = refs[2 * kinds :]
        mine = quarter()
        enter([fsdp_peer(1), mate_z()])

        def core_copy(kind, piece, other):
            owner = mine ^ 2 ^ other
            return send(
                sources[kind].at[owner, pl.ds(piece * step, step)],
                core_buf.at[kind, other, pl.ds(piece * step, step)],
                send_sems.at[kind, piece, other],
                recv_sems.at[kind, piece, other],
                fsdp_peer(1),
            )

        def far_copy(kind, piece):
            part = pl.ds(piece * step, step)
            return send(
                core_buf.at[kind, 1, part],
                far_buf.at[kind, part],
                send_sems.at[kind, piece, 2],
                recv_sems.at[kind, piece, 2],
                mate_z(),
            )

        order = [(kind, piece) for piece in range(pieces) for kind in range(kinds)]
        for other in (1, 0):
            for kind, piece in order:
                core_copy(kind, piece, other).start()
        for kind, piece in order:
            core_copy(kind, piece, 1).wait_recv()

            @pl.loop(0, step // 16)
            def _(i):
                part = pl.ds(pl.multiple_of(piece * step + i * 16, 16), 16)
                total = core_buf[kind, 1, part].astype(F32) + sources[kind][mine ^ 1, part].astype(F32)
                core_buf[kind, 1, part] = total.astype(BF16)

            far_copy(kind, piece).start()
        for kind, piece in order:
            core_copy(kind, piece, 0).wait_recv()
            far_copy(kind, piece).wait_recv()

            @pl.loop(0, step // 16)
            def _(i):
                part = pl.ds(pl.multiple_of(piece * step + i * 16, 16), 16)
                total = core_buf[kind, 0, part].astype(F32) + sources[kind][mine, part].astype(F32)
                results[kind][part] = (total + far_buf[kind, part].astype(F32)).astype(BF16)

        for kind, piece in order:
            core_copy(kind, piece, 0).wait_send()
            core_copy(kind, piece, 1).wait_send()
            far_copy(kind, piece).wait_send()

    return pl.pallas_call(
        kernel,
        out_shape=[jax.ShapeDtypeStruct((rows, width), BF16)] * kinds,
        in_specs=[IN_VMEM] * kinds,
        out_specs=[IN_VMEM] * kinds,
        scratch_shapes=[
            pltpu.VMEM((kinds, 2, rows, width), BF16),
            pltpu.VMEM((kinds, rows, width), BF16),
            pltpu.SemaphoreType.DMA((kinds, pieces, 3)),
            pltpu.SemaphoreType.DMA((kinds, pieces, 3)),
        ],
        compiler_params=remote_params(collective_id, 40 << 20),
        name="sum_keys",
    )(*terms)


def fill_bias(bias, query_ref, key_ref):
    @pl.when(pl.program_id(0) == 0)
    def _():
        bias[...] = jnp.where(key_ref[...] == query_ref[...], 0.0, NEG_FILL)


def attend_local_back(queries, keys_values, mixed, logs, grad_mixed, query_clip, key_clip, head_count):
    rows, width = queries.shape
    keys = 4 * rows
    slabs = width // LANES
    head_size = width // head_count
    per_slab = LANES // head_size
    scale = head_size ** (-0.5)
    factor = scale * LOG2E

    def kernel(
        q_ref, k_ref, v_ref, mixed_ref, grad_ref, log_ref, query_ref, key_ref, dq_ref, dk_ref, dv_ref, bias
    ):
        fill_bias(bias, query_ref, key_ref)
        lane = lax.broadcasted_iota(jnp.int32, (rows, LANES), 1) // head_size
        key_lane = lax.broadcasted_iota(jnp.int32, (keys, LANES), 1) // head_size
        sub = lax.broadcasted_iota(jnp.int32, (LANES, rows), 0) // head_size
        queries = q_ref[...]
        grads = grad_ref[...]
        pick = (
            lax.broadcasted_iota(jnp.int32, (8, LANES), 1) // head_size
            == lax.broadcasted_iota(jnp.int32, (8, LANES), 0)
        ).astype(F32)
        deltas = lax.dot_general(
            pick,
            grads.astype(F32) * mixed_ref[...].astype(F32),
            (((1,), (1,)), ((), ())),
            precision=lax.Precision.HIGHEST,
            preferred_element_type=F32,
        )
        keys_t = k_ref[...].T
        dq = jnp.zeros((LANES, rows), F32)
        dk = jnp.zeros((keys, LANES), F32)
        dv = jnp.zeros((keys, LANES), F32)
        for head in range(per_slab):
            own = jnp.where(lane == head, queries, jnp.zeros_like(queries))
            own_grad = jnp.where(lane == head, grads, jnp.zeros_like(grads))
            scores = across_lanes(k_ref[...], own) * factor + bias[...]
            weights = jnp.exp2(scores - log_ref[0, head : head + 1, :])
            grad_soft = across_lanes(v_ref[...], own_grad)
            grad_scores = (weights * (grad_soft - deltas[head : head + 1, :])).astype(BF16)
            dv = jnp.where(
                key_lane == head, jnp.dot(weights.astype(BF16), grads, preferred_element_type=F32), dv
            )
            dk = jnp.where(key_lane == head, jnp.dot(grad_scores, queries, preferred_element_type=F32), dk)
            dq = jnp.where(sub == head, jnp.dot(keys_t, grad_scores, preferred_element_type=F32), dq)
        dq_ref[...] = (dq.T * scale).astype(BF16)
        dk_ref[...] = (dk * scale).astype(BF16)
        dv_ref[...] = dv.astype(BF16)

    return pl.pallas_call(
        kernel,
        grid=(slabs,),
        out_shape=[
            jax.ShapeDtypeStruct((rows, width), BF16),
            jax.ShapeDtypeStruct((keys, width), BF16),
            jax.ShapeDtypeStruct((keys, width), BF16),
        ],
        in_specs=[
            pl.BlockSpec((rows, LANES), lambda j: (0, j)),
            pl.BlockSpec((None, None, keys, LANES), lambda j: (0, j, 0, 0)),
            pl.BlockSpec((None, None, keys, LANES), lambda j: (1, j, 0, 0)),
            pl.BlockSpec((rows, LANES), lambda j: (0, j)),
            pl.BlockSpec((rows, LANES), lambda j: (0, j)),
            pl.BlockSpec((1, 8, rows), lambda j: (j, 0, 0)),
            pl.BlockSpec((1, rows), lambda j: (0, 0)),
            pl.BlockSpec((keys, 1), lambda j: (0, 0)),
        ],
        out_specs=[
            pl.BlockSpec((rows, LANES), lambda j: (0, j)),
            pl.BlockSpec((keys, LANES), lambda j: (0, j)),
            pl.BlockSpec((keys, LANES), lambda j: (0, j)),
        ],
        scratch_shapes=[pltpu.VMEM((keys, rows), F32)],
        compiler_params=pltpu.CompilerParams(vmem_limit_bytes=50 << 20),
        name="attend_local_back",
    )(
        queries,
        keys_values,
        keys_values,
        mixed,
        grad_mixed,
        logs,
        query_clip[None, :],
        key_clip[:, None],
    )


def swap_cores(values):
    return lax.ppermute(values, "fsdp", [(f, f ^ 1) for f in range(8)])


def own_columns(values, mine):
    rows, columns = values.shape
    parts = values.reshape(rows, 4, 2, columns // 8)
    core = lax.axis_index("fsdp") & 1
    return jnp.where(core == (0 if mine else 1), parts[:, :, 0], parts[:, :, 1]).reshape(rows, columns // 2)


def both_cores(values):
    return jnp.concatenate([own_columns(values, True), swap_cores(own_columns(values, False))], axis=0)


def chip_gradient(left, right):
    all_right = jnp.concatenate([right, swap_cores(right)], axis=0)
    grad = jnp.einsum("tv,tw->vw", both_cores(left), all_right, preferred_element_type=F32)
    return grad.astype(BF16).reshape(4, grad.shape[0] // 4, grad.shape[1])


def back_to_mixed(grad_result, kept, norms, w_out, w_up, w_down):
    normed, queries, keys_values, mixed, logs, middle, normed_mid, hidden, slope = kept
    grad_low = grad_result.astype(BF16)
    grad_down = chip_gradient(hidden, grad_low)
    grad_hidden = jnp.einsum("tw,fw->tf", grad_low, w_down, preferred_element_type=F32)
    grad_pre = (grad_hidden * slope.astype(F32)).astype(BF16)
    grad_up = chip_gradient(normed_mid, grad_pre)
    grad_normed_mid = jnp.einsum("tf,wf->tw", grad_pre, w_up, preferred_element_type=F32)
    _, second_pull = jax.vjp(layer_norm, middle, norms[2], norms[3])
    grad_mid_norm, grad_gain_two, grad_shift_two = second_pull(grad_normed_mid)
    grad_middle = grad_result + grad_mid_norm
    grad_branch = grad_middle.astype(BF16)
    grad_out_w = chip_gradient(mixed, grad_branch)
    grad_mixed = jnp.einsum("tw,vw->tv", grad_branch, w_out, preferred_element_type=F32).astype(BF16)
    return grad_middle, grad_mixed, [grad_gain_two, grad_shift_two], (grad_out_w, grad_up, grad_down)


def fast_backward(
    grad_result, residual, kept, norms, w_qkv, w_out, w_up, w_down, head_count, clips, collective_id
):
    normed, queries, keys_values, mixed, logs, middle, normed_mid, hidden, slope = kept
    rows, width = normed.shape
    grad_middle, grad_mixed, small_two, weight_grads = back_to_mixed(
        grad_result, kept, norms, w_out, w_up, w_down
    )
    dq, dk, dv = attend_local_back(
        queries,
        keys_values.reshape(2, width // LANES, 4 * rows, LANES),
        mixed,
        logs,
        grad_mixed,
        clips[0],
        clips[1],
        head_count,
    )
    dk, dv = sum_keys([dk.reshape(4, rows, width), dv.reshape(4, rows, width)], collective_id)
    grad_qkv = jnp.concatenate([dq, dk, dv], axis=1)
    grad_qkv_w = chip_gradient(normed, grad_qkv)
    grad_normed = jnp.einsum("tc,wc->tw", grad_qkv, w_qkv, preferred_element_type=F32)
    _, first_pull = jax.vjp(layer_norm, residual, norms[0], norms[1])
    grad_first_norm, grad_gain_one, grad_shift_one = first_pull(grad_normed)
    return (
        grad_middle + grad_first_norm,
        [grad_gain_one, grad_shift_one] + small_two,
        (grad_qkv_w,) + weight_grads,
    )


def fast_local(
    tokens,
    clip_lengths,
    target_pos,
    out_grad,
    norm1_gain,
    norm1_bias,
    w_qkv,
    w_out,
    norm2_gain,
    norm2_bias,
    w_fc1,
    w_fc2,
    w_embed,
    mask_token,
    pred_norm1_gain,
    pred_norm1_bias,
    pred_qkv,
    pred_out,
    pred_norm2_gain,
    pred_norm2_bias,
    pred_fc1,
    pred_fc2,
):
    rows, width = tokens.shape
    narrow = out_grad.shape[1]
    wide_part = norm1_gain.shape[0]
    narrow_part = mask_token.shape[0]
    me = lax.axis_index("fsdp")
    core = me & 1
    wide_small = jnp.pad(
        jnp.stack([norm1_gain, norm1_bias, norm2_gain, norm2_bias]), ((0, SMALL_ROWS - 4), (0, 0))
    )
    narrow_small = jnp.stack(
        [pred_norm1_gain, pred_norm1_bias, pred_norm2_gain, pred_norm2_bias, mask_token]
    )
    here = (jnp.arange(narrow, dtype=jnp.int32) // narrow_part == me)[None, :]
    narrow_small = jnp.where(here, jnp.tile(narrow_small, (1, 8)), jnp.zeros((), BF16))
    narrow_small = jnp.pad(narrow_small, ((0, SMALL_ROWS - 5), (0, 0)))

    clip_ends = jnp.cumsum(clip_lengths[0])
    first_rows = lax.axis_index("seq") * rows + jnp.arange(rows, dtype=jnp.int32)
    past_end = (first_rows[:, None] >= clip_ends[None, :]).astype(jnp.int32)
    rel_rows = first_rows - jnp.sum(clip_lengths[0][None, :] * past_end, axis=1)
    matches = jnp.arange(rows, dtype=jnp.int32)[:, None] == target_pos[0, 0][None, :]
    hit_rows = jnp.sum(matches.astype(F32), axis=1)
    side = jnp.concatenate(
        [position_table(rel_rows, narrow), jnp.broadcast_to(hit_rows[:, None], (rows, LANES))], axis=1
    )
    ends = jnp.pad(jnp.broadcast_to(clip_ends[:, None], (3, LANES)), ((0, 5), (0, 0)))

    whole, kept, narrow_kept, rest, traded = forward_pass(
        tokens,
        out_grad,
        side,
        ends,
        [
            wide_small,
            narrow_small,
            w_qkv,
            w_out,
            w_fc1,
            w_fc2,
            w_embed,
            pred_qkv,
            pred_out,
            pred_fc1,
            pred_fc2,
        ],
        HEADS,
        P_HEADS,
    )
    context_own, entry, side, tokens = rest
    out_grad, ends, context_out, predicted = traded
    smalls = whole[0].reshape(8, SMALL_ROWS, LANES).astype(F32)
    norms = [smalls[:, i].reshape(-1) for i in range(4)]
    narrow_smalls = jnp.sum(whole[1].reshape(8, SMALL_ROWS, narrow).astype(F32), axis=0)
    pred_norms = [narrow_smalls[i] for i in range(4)]
    clip_ends = ends[:3, 0]
    query_clip = clip_index(quarter() * rows + jnp.arange(rows, dtype=jnp.int32), clip_ends)
    key_clip = clip_index(jnp.arange(4 * rows, dtype=jnp.int32), clip_ends)
    target_hit = side[:, narrow]

    grad_pred_in, pred_small, pred_grads = fast_backward(
        out_grad.astype(F32),
        entry,
        narrow_kept,
        pred_norms,
        whole[7],
        whole[8],
        whole[9],
        whole[10],
        P_HEADS,
        (query_clip, key_clip),
        5,
    )
    grad_mask = jnp.sum(target_hit[:, None] * grad_pred_in, axis=0)
    grad_embedded = (grad_pred_in * (1.0 - target_hit[:, None])).astype(BF16)
    grad_embed_w = chip_gradient(context_own, grad_embedded)
    grad_context = jnp.einsum("tp,dp->td", grad_embedded, whole[6], preferred_element_type=F32)
    grad_middle, grad_mixed, ctx_two, ctx_grads = back_to_mixed(
        grad_context, kept, norms, whole[3], whole[4], whole[5]
    )
    wide_grads = jnp.stack(ctx_two).reshape(2, 4, 2, wide_part)
    narrow_grads = jnp.pad(
        jnp.stack(pred_small + [grad_mask]).reshape(5, 4, 2, narrow_part),
        ((0, 0), (0, 0), (0, 0), (0, LANES - narrow_part)),
    )
    small_grads = jnp.concatenate([wide_grads, narrow_grads], axis=0).transpose(2, 1, 0, 3)
    mine = jnp.where(core == 0, small_grads[0], small_grads[1])
    other = jnp.where(core == 0, small_grads[1], small_grads[0])
    small_grads = jnp.pad(mine + swap_cores(other), ((0, 0), (0, SMALL_ROWS - 7), (0, 0)))

    normed, queries, keys_values, mixed, logs, _, _, _, _ = kept
    results = back_and_sum(
        [pred_grads[3], pred_grads[2], pred_grads[1], pred_grads[0], grad_embed_w, small_grads.astype(BF16)]
        + [ctx_grads[2], ctx_grads[1], ctx_grads[0]],
        queries,
        keys_values.reshape(2, width // LANES, 4 * rows, LANES),
        mixed,
        grad_mixed,
        logs,
        query_clip,
        key_clip,
        both_cores(normed).T,
        whole[2].reshape(8, wide_part, 3 * width),
        tokens,
        grad_middle,
        norms[0],
        HEADS,
        6,
    )
    token_grad = results[-1]
    sums = [one.astype(F32) for one in results[:-1]]
    small_a, small_b = sums[5], sums[10]
    narrow_out = [small_a[2 + i, :narrow_part] for i in range(5)]
    return (
        context_out,
        predicted,
        token_grad,
        small_b[0],
        small_b[1],
        sums[9],
        sums[8],
        small_a[0],
        small_a[1],
        sums[7],
        sums[6],
        sums[4],
        narrow_out[4],
        narrow_out[0],
        narrow_out[1],
        sums[3],
        sums[2],
        narrow_out[2],
        narrow_out[3],
        sums[1],
        sums[0],
    )


def solution(mesh):
    body = fast_local if fits_fast(mesh) else local
    return jax.shard_map(
        body,
        mesh=mesh,
        in_specs=(
            P(("fsdp", "seq"), None),
            P("fsdp", None),
            P("fsdp", "seq", None),
            P(("fsdp", "seq"), None),
            P("fsdp"),
            P("fsdp"),
            P("fsdp", None),
            P("fsdp", None),
            P("fsdp"),
            P("fsdp"),
            P("fsdp", None),
            P("fsdp", None),
            P("fsdp", None),
            P("fsdp"),
            P("fsdp"),
            P("fsdp"),
            P("fsdp", None),
            P("fsdp", None),
            P("fsdp"),
            P("fsdp"),
            P("fsdp", None),
            P("fsdp", None),
        ),
        out_specs=(
            P(("fsdp", "seq"), None),
            P(("fsdp", "seq"), None),
            P(("fsdp", "seq"), None),
            P("fsdp"),
            P("fsdp"),
            P("fsdp", None),
            P("fsdp", None),
            P("fsdp"),
            P("fsdp"),
            P("fsdp", None),
            P("fsdp", None),
            P("fsdp", None),
            P("fsdp"),
            P("fsdp"),
            P("fsdp"),
            P("fsdp", None),
            P("fsdp", None),
            P("fsdp"),
            P("fsdp"),
            P("fsdp", None),
            P("fsdp", None),
        ),
        check_vma=False,
    )
```

```python
import math

import jax
import jax.numpy as jnp
from jax import lax
from jax.experimental import pallas as pl
from jax.experimental.pallas import tpu as pltpu
from jax.sharding import PartitionSpec as P

HEADS = 16
PD = 384
P_HEADS = 12


EPSILON = 1e-06
NEG_FILL = -1e30
block_rows = 512


def layer_norm(values, norm_gain, norm_shift):
    center = values - jnp.mean(values, axis=-1, keepdims=True)
    spread = jnp.mean(center * center, axis=-1, keepdims=True)
    return center * lax.rsqrt(spread + EPSILON) * norm_gain + norm_shift


def gelu_exact(values):
    return jax.nn.gelu(values, approximate=False)


def position_table(positions, table_width):
    half_width = table_width // 2
    angle_rates = jnp.exp(
        jnp.arange(half_width, dtype=jnp.float32) * (-2.0 * math.log(10000.0) / table_width)
    )
    angles = positions.astype(jnp.float32)[:, None] * angle_rates[None, :]
    return jnp.concatenate([jnp.sin(angles), jnp.cos(angles)], axis=1)


def clip_index(positions, clip_ends):
    return jnp.sum((positions[:, None] >= clip_ends[None, :]).astype(jnp.int32), axis=1)


def key_step(total_keys):
    return max(min(total_keys, block_rows), total_keys // 8)


def block_scores(queries, key_part, query_clip, key_clip_part, score_scale):
    raw_scores = (
        jnp.einsum("the,khe->htk", queries, key_part, preferred_element_type=jnp.float32)
        * score_scale
    )
    same_clip = query_clip[:, None] == key_clip_part[None, :]
    return jnp.where(same_clip[None], raw_scores, NEG_FILL)


def attend_forward(queries, key_heads, value_heads, query_clip, key_clip):
    row_count, head_count, head_size = queries.shape
    score_scale = head_size ** (-0.5)
    total_keys = key_heads.shape[0]
    step_rows = key_step(total_keys)
    run_max = jnp.full((head_count, row_count), NEG_FILL, jnp.float32)
    run_total = jnp.zeros((head_count, row_count), jnp.float32)
    for key_start in range(0, total_keys, step_rows):
        scores = block_scores(
            queries,
            key_heads[key_start : key_start + step_rows],
            query_clip,
            key_clip[key_start : key_start + step_rows],
            score_scale,
        )
        new_max = jnp.maximum(run_max, jnp.max(scores, axis=2))
        run_total = run_total * jnp.exp(run_max - new_max) + jnp.sum(
            jnp.exp(scores - new_max[:, :, None]), axis=2
        )
        run_max = new_max
    log_total = run_max + jnp.log(run_total)
    output = jnp.zeros((row_count, head_count, head_size), jnp.float32)
    for key_start in range(0, total_keys, step_rows):
        scores = block_scores(
            queries,
            key_heads[key_start : key_start + step_rows],
            query_clip,
            key_clip[key_start : key_start + step_rows],
            score_scale,
        )
        soft_weights = jnp.exp(scores - log_total[:, :, None]).astype(jnp.bfloat16)
        output = output + jnp.einsum(
            "htk,khe->the",
            soft_weights,
            value_heads[key_start : key_start + step_rows],
            preferred_element_type=jnp.float32,
        )
    return (output, log_total)


def attend_backward(
    queries, key_heads, value_heads, query_clip, key_clip, log_total, grad_mixed, output
):
    row_count, head_count, head_size = queries.shape
    score_scale = head_size ** (-0.5)
    total_keys = key_heads.shape[0]
    step_rows = key_step(total_keys)
    row_delta = jnp.sum(grad_mixed.astype(jnp.float32) * output, axis=2).T
    grad_query = jnp.zeros((row_count, head_count, head_size), jnp.float32)
    key_pieces = []
    value_pieces = []
    for key_start in range(0, total_keys, step_rows):
        key_part = key_heads[key_start : key_start + step_rows]
        value_part = value_heads[key_start : key_start + step_rows]
        scores = block_scores(
            queries, key_part, query_clip, key_clip[key_start : key_start + step_rows], score_scale
        )
        soft_weights = jnp.exp(scores - log_total[:, :, None])
        grad_soft = jnp.einsum(
            "the,khe->htk", grad_mixed, value_part, preferred_element_type=jnp.float32
        )
        grad_scores = (soft_weights * (grad_soft - row_delta[:, :, None])).astype(jnp.bfloat16)
        grad_query = grad_query + jnp.einsum(
            "htk,khe->the", grad_scores, key_part, preferred_element_type=jnp.float32
        )
        key_pieces.append(
            jnp.einsum("htk,the->khe", grad_scores, queries, preferred_element_type=jnp.float32)
        )
        value_pieces.append(
            jnp.einsum(
                "htk,the->khe",
                soft_weights.astype(jnp.bfloat16),
                grad_mixed,
                preferred_element_type=jnp.float32,
            )
        )
    key_terms = jnp.concatenate(key_pieces, axis=0) * score_scale
    value_terms = jnp.concatenate(value_pieces, axis=0)
    return (grad_query * score_scale, key_terms, value_terms)


def block_forward(
    residual, norm_params, w_qkv, w_out, w_up, w_down, head_count, query_clip, key_clip
):
    row_count, model_width = residual.shape
    head_size = model_width // head_count
    norm_float = norm_params.astype(jnp.float32)
    normed = layer_norm(residual, norm_float[:, 0], norm_float[:, 1]).astype(jnp.bfloat16)
    qkv = jnp.dot(normed, w_qkv, preferred_element_type=jnp.float32).astype(jnp.bfloat16)
    queries = qkv[:, :model_width].reshape(row_count, head_count, head_size)
    key_local = qkv[:, model_width : 2 * model_width]
    value_local = qkv[:, 2 * model_width :]
    key_full, value_full = (
        lax.all_gather(key_local, "seq", axis=0, tiled=True),
        lax.all_gather(value_local, "seq", axis=0, tiled=True),
    )
    key_heads = key_full.reshape(-1, head_count, head_size)
    value_heads = value_full.reshape(-1, head_count, head_size)
    output, log_total = attend_forward(queries, key_heads, value_heads, query_clip, key_clip)
    mixed = output.reshape(row_count, model_width).astype(jnp.bfloat16)
    middle = residual + jnp.dot(mixed, w_out, preferred_element_type=jnp.float32)
    normed_mid = layer_norm(middle, norm_float[:, 2], norm_float[:, 3]).astype(jnp.bfloat16)
    pre_act = jnp.dot(normed_mid, w_up, preferred_element_type=jnp.float32)
    hidden = gelu_exact(pre_act).astype(jnp.bfloat16)
    result = middle + jnp.dot(hidden, w_down, preferred_element_type=jnp.float32)
    kept = (
        residual,
        normed,
        queries,
        key_local,
        value_local,
        key_heads,
        value_heads,
        output,
        log_total,
        mixed,
        middle,
        normed_mid,
        pre_act,
        hidden,
    )
    return (result, kept)


def block_backward(
    grad_result, kept, norm_params, w_qkv, w_out, w_up, w_down, head_count, query_clip, key_clip
):
    (
        residual,
        normed,
        queries,
        key_local,
        value_local,
        key_heads,
        value_heads,
        output,
        log_total,
        mixed,
        middle,
        normed_mid,
        pre_act,
        hidden,
    ) = kept
    row_count, model_width = residual.shape
    head_size = model_width // head_count
    norm_float = norm_params.astype(jnp.float32)
    grad_low = grad_result.astype(jnp.bfloat16)
    grad_down = jnp.einsum("tf,tw->fw", hidden, grad_low, preferred_element_type=jnp.float32)
    grad_hidden = jnp.einsum("tw,fw->tf", grad_low, w_down, preferred_element_type=jnp.float32)
    gelu_value, gelu_pull = jax.vjp(gelu_exact, pre_act)
    grad_pre = gelu_pull(grad_hidden)[0].astype(jnp.bfloat16)
    grad_up = jnp.einsum("tw,tf->wf", normed_mid, grad_pre, preferred_element_type=jnp.float32)
    grad_normed_mid = jnp.einsum("tf,wf->tw", grad_pre, w_up, preferred_element_type=jnp.float32)
    second_value, second_pull = jax.vjp(layer_norm, middle, norm_float[:, 2], norm_float[:, 3])
    grad_mid_norm, grad_gain_two, grad_shift_two = second_pull(grad_normed_mid)
    grad_middle = grad_result + grad_mid_norm
    grad_branch = grad_middle.astype(jnp.bfloat16)
    grad_out_w = jnp.einsum("tv,tw->vw", mixed, grad_branch, preferred_element_type=jnp.float32)
    grad_mixed = jnp.einsum(
        "tw,vw->tv", grad_branch, w_out, preferred_element_type=jnp.float32
    ).astype(jnp.bfloat16)
    key_full, value_full = (
        lax.all_gather(key_local, "seq", axis=0, tiled=True),
        lax.all_gather(value_local, "seq", axis=0, tiled=True),
    )
    key_heads = key_full.reshape(-1, head_count, head_size)
    value_heads = value_full.reshape(-1, head_count, head_size)
    grad_query, key_terms, value_terms = attend_backward(
        queries,
        key_heads,
        value_heads,
        query_clip,
        key_clip,
        log_total,
        grad_mixed.reshape(row_count, head_count, head_size),
        output,
    )
    grad_key, grad_value = (
        lax.psum_scatter(
            key_terms.reshape(-1, model_width).astype(jnp.bfloat16),
            "seq",
            scatter_dimension=0,
            tiled=True,
        ).astype(jnp.float32),
        lax.psum_scatter(
            value_terms.reshape(-1, model_width).astype(jnp.bfloat16),
            "seq",
            scatter_dimension=0,
            tiled=True,
        ).astype(jnp.float32),
    )
    grad_qkv = jnp.concatenate(
        [grad_query.reshape(row_count, model_width), grad_key, grad_value], axis=1
    ).astype(jnp.bfloat16)
    grad_qkv_w = jnp.einsum("tw,tc->wc", normed, grad_qkv, preferred_element_type=jnp.float32)
    grad_normed = jnp.einsum("tc,wc->tw", grad_qkv, w_qkv, preferred_element_type=jnp.float32)
    first_value, first_pull = jax.vjp(layer_norm, residual, norm_float[:, 0], norm_float[:, 1])
    grad_first_norm, grad_gain_one, grad_shift_one = first_pull(grad_normed)
    grad_norms = jnp.stack([grad_gain_one, grad_shift_one, grad_gain_two, grad_shift_two], axis=1)
    return (grad_middle + grad_first_norm, (grad_norms, grad_qkv_w, grad_out_w, grad_up, grad_down))


def local(
    tokens,
    clip_lengths,
    target_pos,
    out_grad,
    norm1_gain,
    norm1_bias,
    w_qkv,
    w_out,
    norm2_gain,
    norm2_bias,
    w_fc1,
    w_fc2,
    w_embed,
    mask_token,
    pred_norm1_gain,
    pred_norm1_bias,
    pred_qkv,
    pred_out,
    pred_norm2_gain,
    pred_norm2_bias,
    pred_fc1,
    pred_fc2,
):
    row_count = tokens.shape[0]
    group_count = row_count * lax.axis_size("seq")
    lengths = clip_lengths[0]
    clip_ends = jnp.cumsum(lengths)
    local_rows = lax.axis_index("seq") * row_count + jnp.arange(row_count, dtype=jnp.int32)
    query_clip = clip_index(local_rows, clip_ends)
    key_clip = clip_index(jnp.arange(group_count, dtype=jnp.int32), clip_ends)
    past_end = (local_rows[:, None] >= clip_ends[None, :]).astype(jnp.int32)
    rel_rows = local_rows - jnp.sum(lengths[None, :] * past_end, axis=1)
    ctx_small = jnp.stack([norm1_gain, norm1_bias, norm2_gain, norm2_bias], axis=1)
    pred_small = jnp.stack(
        [pred_norm1_gain, pred_norm1_bias, pred_norm2_gain, pred_norm2_bias, mask_token], axis=1
    )
    ctx_params = (
        lax.all_gather(ctx_small, "fsdp", axis=0, tiled=True),
        lax.all_gather(w_qkv, "fsdp", axis=0, tiled=True),
        lax.all_gather(w_out, "fsdp", axis=0, tiled=True),
        lax.all_gather(w_fc1, "fsdp", axis=0, tiled=True),
        lax.all_gather(w_fc2, "fsdp", axis=0, tiled=True),
    )
    pred_params = (
        lax.all_gather(pred_small, "fsdp", axis=0, tiled=True),
        lax.all_gather(w_embed, "fsdp", axis=0, tiled=True),
        lax.all_gather(pred_qkv, "fsdp", axis=0, tiled=True),
        lax.all_gather(pred_out, "fsdp", axis=0, tiled=True),
        lax.all_gather(pred_fc1, "fsdp", axis=0, tiled=True),
        lax.all_gather(pred_fc2, "fsdp", axis=0, tiled=True),
    )
    ctx_result, ctx_kept = block_forward(
        tokens.astype(jnp.float32),
        ctx_params[0],
        ctx_params[1],
        ctx_params[2],
        ctx_params[3],
        ctx_params[4],
        HEADS,
        query_clip,
        key_clip,
    )
    context_out = ctx_result.astype(jnp.bfloat16)
    embedded = jnp.dot(context_out, pred_params[1], preferred_element_type=jnp.float32)
    targets = target_pos[0, 0]
    matches = jnp.arange(row_count, dtype=jnp.int32)[:, None] == targets[None, :]
    placement = matches.astype(jnp.float32)
    target_hit = jnp.sum(placement, axis=1)
    target_rel = jnp.sum(jnp.where(matches, rel_rows[:, None], 0), axis=0)
    mask_rows = pred_params[0][:, 4].astype(jnp.float32)[None, :] + position_table(target_rel, PD)
    placed = jnp.dot(
        placement, mask_rows, precision=lax.Precision.HIGHEST, preferred_element_type=jnp.float32
    )
    pred_in = embedded * (1.0 - target_hit[:, None]) + placed
    pred_result, pred_kept = block_forward(
        pred_in,
        pred_params[0],
        pred_params[2],
        pred_params[3],
        pred_params[4],
        pred_params[5],
        P_HEADS,
        query_clip,
        key_clip,
    )
    predicted = pred_result.astype(jnp.bfloat16)
    pred_back = (
        lax.all_gather(pred_small, "fsdp", axis=0, tiled=True),
        lax.all_gather(w_embed, "fsdp", axis=0, tiled=True),
        lax.all_gather(pred_qkv, "fsdp", axis=0, tiled=True),
        lax.all_gather(pred_out, "fsdp", axis=0, tiled=True),
        lax.all_gather(pred_fc1, "fsdp", axis=0, tiled=True),
        lax.all_gather(pred_fc2, "fsdp", axis=0, tiled=True),
    )
    ctx_back = (
        lax.all_gather(ctx_small, "fsdp", axis=0, tiled=True),
        lax.all_gather(w_qkv, "fsdp", axis=0, tiled=True),
        lax.all_gather(w_out, "fsdp", axis=0, tiled=True),
        lax.all_gather(w_fc1, "fsdp", axis=0, tiled=True),
        lax.all_gather(w_fc2, "fsdp", axis=0, tiled=True),
    )
    grad_pred_in, pred_grads = block_backward(
        out_grad.astype(jnp.float32),
        pred_kept,
        pred_back[0],
        pred_back[2],
        pred_back[3],
        pred_back[4],
        pred_back[5],
        P_HEADS,
        query_clip,
        key_clip,
    )
    grad_mask = jnp.sum(target_hit[:, None] * grad_pred_in, axis=0)
    grad_embedded = (grad_pred_in * (1.0 - target_hit[:, None])).astype(jnp.bfloat16)
    grad_embed_w = jnp.einsum(
        "td,tp->dp", context_out, grad_embedded, preferred_element_type=jnp.float32
    )
    grad_context = jnp.einsum(
        "tp,dp->td", grad_embedded, pred_back[1], preferred_element_type=jnp.float32
    )
    grad_tokens, ctx_grads = block_backward(
        grad_context,
        ctx_kept,
        ctx_back[0],
        ctx_back[1],
        ctx_back[2],
        ctx_back[3],
        ctx_back[4],
        HEADS,
        query_clip,
        key_clip,
    )
    pred_small_grad = jnp.concatenate([pred_grads[0], grad_mask[:, None]], axis=1)
    row_sums = (
        lax.psum_scatter(ctx_grads[0], "fsdp", scatter_dimension=0, tiled=True),
        lax.psum_scatter(ctx_grads[1], "fsdp", scatter_dimension=0, tiled=True),
        lax.psum_scatter(ctx_grads[2], "fsdp", scatter_dimension=0, tiled=True),
        lax.psum_scatter(ctx_grads[3], "fsdp", scatter_dimension=0, tiled=True),
        lax.psum_scatter(ctx_grads[4], "fsdp", scatter_dimension=0, tiled=True),
        lax.psum_scatter(grad_embed_w, "fsdp", scatter_dimension=0, tiled=True),
        lax.psum_scatter(pred_small_grad, "fsdp", scatter_dimension=0, tiled=True),
        lax.psum_scatter(pred_grads[1], "fsdp", scatter_dimension=0, tiled=True),
        lax.psum_scatter(pred_grads[2], "fsdp", scatter_dimension=0, tiled=True),
        lax.psum_scatter(pred_grads[3], "fsdp", scatter_dimension=0, tiled=True),
        lax.psum_scatter(pred_grads[4], "fsdp", scatter_dimension=0, tiled=True),
    )
    summed = (
        lax.psum(row_sums[0].astype(jnp.bfloat16), "seq").astype(jnp.float32),
        lax.psum(row_sums[1].astype(jnp.bfloat16), "seq").astype(jnp.float32),
        lax.psum(row_sums[2].astype(jnp.bfloat16), "seq").astype(jnp.float32),
        lax.psum(row_sums[3].astype(jnp.bfloat16), "seq").astype(jnp.float32),
        lax.psum(row_sums[4].astype(jnp.bfloat16), "seq").astype(jnp.float32),
        lax.psum(row_sums[5].astype(jnp.bfloat16), "seq").astype(jnp.float32),
        lax.psum(row_sums[6].astype(jnp.bfloat16), "seq").astype(jnp.float32),
        lax.psum(row_sums[7].astype(jnp.bfloat16), "seq").astype(jnp.float32),
        lax.psum(row_sums[8].astype(jnp.bfloat16), "seq").astype(jnp.float32),
        lax.psum(row_sums[9].astype(jnp.bfloat16), "seq").astype(jnp.float32),
        lax.psum(row_sums[10].astype(jnp.bfloat16), "seq").astype(jnp.float32),
    )
    return (
        context_out,
        predicted,
        grad_tokens.astype(jnp.bfloat16),
        summed[0][:, 0],
        summed[0][:, 1],
        summed[1],
        summed[2],
        summed[0][:, 2],
        summed[0][:, 3],
        summed[3],
        summed[4],
        summed[5],
        summed[6][:, 4],
        summed[6][:, 0],
        summed[6][:, 1],
        summed[7],
        summed[8],
        summed[6][:, 2],
        summed[6][:, 3],
        summed[9],
        summed[10],
    )


BF16 = jnp.bfloat16
F32 = jnp.float32
MESH = pl.DeviceIdType.MESH
LOG2E = 1.4426950408889634
LN2 = 0.6931471805599453
LANES = 128
SMALL_ROWS = 16
ANYWHERE = pl.BlockSpec(memory_space=pl.ANY)
IN_VMEM = pl.BlockSpec(memory_space=pltpu.VMEM)


def fits_fast(mesh):
    return mesh.shape["fsdp"] == 8 and mesh.shape["seq"] == 4


def fsdp_peer(bit):
    return (lax.axis_index("fsdp") ^ bit, lax.axis_index("seq"))


def seq_peer(index):
    return (lax.axis_index("fsdp"), index)


def enter(peers):
    barrier = pltpu.get_barrier_semaphore()
    for peer in peers:
        pl.semaphore_signal(barrier, inc=1, device_id=peer, device_id_type=MESH)
    pl.semaphore_wait(barrier, len(peers))


def send(src, dst, send_sem, recv_sem, peer):
    return pltpu.make_async_remote_copy(
        src_ref=src,
        dst_ref=dst,
        send_sem=send_sem,
        recv_sem=recv_sem,
        device_id=peer,
        device_id_type=MESH,
    )


def remote_params(collective_id, vmem=None):
    return pltpu.CompilerParams(
        collective_id=collective_id, has_side_effects=True, vmem_limit_bytes=vmem
    )


def mate_z():
    return seq_peer(lax.axis_index("seq") ^ 1)


def quarter():
    return (lax.axis_index("fsdp") & 1) * 2 + (lax.axis_index("seq") & 1)


def across_lanes(left, right):
    return lax.dot_general(left, right, (((1,), (1,)), ((), ())), preferred_element_type=F32)


def forward_pass(tokens, out_grad, side, ends, shards, heads, narrow_heads):
    rows, width = tokens.shape
    narrow = out_grad.shape[1]
    hidden_width = shards[4].shape[1]
    narrow_hidden = shards[9].shape[1]
    shapes = [shard.shape for shard in shards]
    array_count = len(shards)
    units = []
    for index, (shard_rows, columns) in enumerate(shapes):
        if shard_rows * columns >= 100000:
            half = shard_rows // 2
            units.append((index, 0, half, 2, 4))
            units.append((index, half, half, 4, 2))
        else:
            near, far = (2, 4) if len(units) % 2 == 0 else (4, 2)
            units.append((index, 0, shard_rows, near, far))
    count = len(units)
    ahead = 3
    last_unit = {}
    for u, unit in enumerate(units):
        last_unit[unit[0]] = u

    block_widths = ((width, heads, hidden_width, 2), (narrow, narrow_heads, narrow_hidden, 1))
    saved_shapes = []
    for w, _, ff, _ in block_widths:
        saved_shapes += [
            ((w, rows), BF16),
            ((rows, w), BF16),
            ((2, w // LANES, 4, rows, LANES), BF16),
            ((rows, w), BF16),
            ((w // LANES, 8, rows), F32),
            ((rows, w), F32),
            ((w, rows), BF16),
            ((rows, ff), BF16),
            ((w, rows), BF16),
        ]
    per_block = len(saved_shapes) // 2
    saved_shapes += [((width, rows), BF16), ((rows, narrow), F32), (side.shape, F32), ((rows, width), BF16)]
    saved_count = len(saved_shapes)

    def kernel(*refs):
        tokens_ref, out_grad_ref, side_ref, ends_ref = refs[:4]
        sources = refs[4 : 4 + array_count]
        base = 4 + array_count
        weight_outs = refs[base : base + array_count]
        base += array_count
        saved_outs = refs[base : base + saved_count]
        base += saved_count
        out_grad_out, ends_out, context_out, predicted_out, wide_hidden_t, narrow_hidden_t = refs[base : base + 6]
        base += 6
        weights = refs[base : base + array_count]
        base += array_count
        saved = refs[base : base + saved_count]
        base += saved_count
        (
            bias,
            gains,
            narrow_gains,
            ends_buf,
            predicted,
            wide_normed,
            wide_hidden,
            narrow_normed,
            narrow_hid,
            stage,
            stage_sems,
            send_sems,
            recv_sems,
            local_sems,
            weight_sems,
            saved_sems,
            trade_send,
            trade_recv,
            trade_keep,
            key_send,
            key_recv,
        ) = refs[base:]
        context_t, entry, side_buf, token_buf = saved[2 * per_block :]
        context = wide_normed

        me = lax.axis_index("fsdp")
        place = lax.axis_index("seq")
        core = me & 1
        high = place >> 1
        low = place & 1
        mine = quarter()
        trades = core != high
        trade_peer = ((me & 6) | high, core * 2 + low)

        barrier = pltpu.get_barrier_semaphore()
        for peer in (fsdp_peer(1), fsdp_peer(2), fsdp_peer(4), mate_z()):
            pl.semaphore_signal(barrier, inc=1, device_id=peer, device_id_type=MESH)

        @pl.when(trades)
        def _():
            pl.semaphore_signal(barrier, inc=1, device_id=trade_peer, device_id_type=MESH)

        pl.semaphore_wait(barrier, 4 + trades.astype(jnp.int32))


        def trade_copy(i, src, dst):
            return send(src, dst, trade_send.at[i], trade_recv.at[i], trade_peer)

        def keep_copy(i, src, dst):
            return pltpu.make_async_copy(src, dst, trade_keep.at[i])

        traded = [
            (tokens_ref, token_buf),
            (side_ref, side_buf),
            (ends_ref, ends_buf),
            (out_grad_ref, out_grad_out),
            (context, context_out),
            (predicted, predicted_out),
        ]

        def trade_start(i):
            @pl.when(trades)
            def _():
                trade_copy(i, *traded[i]).start()

            @pl.when(jnp.logical_not(trades))
            def _():
                keep_copy(i, *traded[i]).start()

        def trade_arrived(i):
            @pl.when(trades)
            def _():
                trade_copy(i, *traded[i]).wait_recv()

            @pl.when(jnp.logical_not(trades))
            def _():
                keep_copy(i, *traded[i]).wait()

        def trade_sent(i):
            @pl.when(trades)
            def _():
                trade_copy(i, *traded[i]).wait_send()


        def place_of(u, owner):
            index, first, unit_rows, _, _ = units[u]
            start = owner * shapes[index][0] + first
            return weights[index].at[pl.ds(pl.multiple_of(start, 16), unit_rows)]

        def own_shard(u):
            index, first, unit_rows, _, _ = units[u]
            return sources[index].at[pl.ds(first, unit_rows)]

        def weight_copy(u, slot):
            _, _, _, near, far = units[u]
            owner = me ^ (0, 0, near, 0, near, far, near ^ far)[slot]
            bit = (near, far, far, 1, 1, 1, 1)[slot]
            src = own_shard(u) if slot in (0, 1, 3) else place_of(u, owner)
            return send(src, place_of(u, owner), send_sems.at[u, slot], recv_sems.at[u, slot], fsdp_peer(bit))

        def own_weight(u):
            return pltpu.make_async_copy(own_shard(u), place_of(u, me), local_sems.at[u])

        def weight_out(index):
            return pltpu.make_async_copy(weights[index], weight_outs[index], weight_sems.at[index])

        def launch(u):
            for slot in (0, 1, 3):
                weight_copy(u, slot).start()
            own_weight(u).start()

        def arrive(u):
            weight_copy(u, 0).wait_recv()
            weight_copy(u, 2).start()
            weight_copy(u, 4).start()
            weight_copy(u, 1).wait_recv()
            weight_copy(u, 5).start()
            if u + ahead < count:
                launch(u + ahead)

        def relay(u):
            weight_copy(u, 2).wait_recv()
            weight_copy(u, 6).start()

        def complete(u):
            for slot in (3, 4, 5, 6):
                weight_copy(u, slot).wait_recv()
            own_weight(u).wait()
            index = units[u][0]
            if last_unit[index] == u:
                weight_out(index).start()

        ticks = []
        ready = {}
        for u in range(count + 2):
            if u < count:
                ticks.append((arrive, u))
            if 1 <= u <= count:
                ticks.append((relay, u - 1))
            if u >= 2:
                ticks.append((complete, u - 2))
                ready[units[u - 2][0]] = len(ticks)
        position = [0]

        def advance(steps):
            for _ in range(steps):
                if position[0] < len(ticks):
                    step, u = ticks[position[0]]
                    step(u)
                    position[0] += 1

        def need(index):
            while position[0] < ready[index]:
                advance(1)


        def save(i):
            return pltpu.make_async_copy(saved[i], saved_outs[i], saved_sems.at[i])

        def norm_into(dst, get, table, gain_at):
            @pl.loop(0, rows // 64)
            def _(i):
                part = pl.ds(pl.multiple_of(i * 64, 64), 64)
                value = get(part)
                value = value - jnp.mean(value, axis=1, keepdims=True)
                inverse = lax.rsqrt(jnp.mean(value * value, axis=1, keepdims=True) + EPSILON)
                dst[part] = (
                    value * inverse * table[gain_at : gain_at + 1, :] + table[gain_at + 1 : gain_at + 2, :]
                ).astype(BF16)

        def turn(src, dst):
            for c in range(dst.shape[0] // LANES):
                at = slice(c * LANES, (c + 1) * LANES)
                dst[at, :] = src[:, at].T

        def run_block(which, get, table, first_weight, finish, inside):
            w, head_count, ff, in_group = block_widths[which]
            (normed_t, queries, kv, mixed, logs, middle, normed_mid_t, slope, mixed_t) = saved[
                which * per_block : (which + 1) * per_block
            ]
            normed, hidden = ((wide_normed, wide_hidden), (narrow_normed, narrow_hid))[which]
            hidden_out = (wide_hidden_t, narrow_hidden_t)[which]
            w_qkv, w_out, w_up, w_down = [weights[first_weight[i]] for i in range(4)]
            slabs = w // LANES
            groups = slabs // in_group
            head_size = w // head_count
            per_slab = LANES // head_size
            factor = head_size ** (-0.5) * LOG2E
            columns = in_group * LANES

            def kv_copy(kind, g):
                owner = mine ^ 1 if kind == 2 else mine
                part = kv.at[:, pl.ds(g * in_group, in_group), owner]
                return send(
                    part,
                    part,
                    key_send.at[which, kind, g],
                    key_recv.at[which, kind, g],
                    mate_z() if kind == 0 else fsdp_peer(1),
                )

            norm_into(normed, get, table, 0)
            turn(normed, normed_t)
            save(which * per_block).start()
            need(first_weight[0])
            for g in range(groups):
                for kind in range(2):
                    tile = jnp.dot(
                        normed[...],
                        w_qkv[:, pl.ds((1 + kind) * w + g * columns, columns)],
                        preferred_element_type=F32,
                    ).astype(BF16)
                    for k in range(in_group):
                        kv[kind, g * in_group + k, mine] = tile[:, k * LANES : (k + 1) * LANES]
                kv_copy(0, g).start()
                kv_copy(1, g).start()
            for g in range(groups):
                at = pl.ds(g * columns, columns)
                queries[:, at] = jnp.dot(normed[...], w_qkv[:, at], preferred_element_type=F32).astype(BF16)
            save(which * per_block + 1).start()
            advance(inside[0])
            kv_copy(0, 0).wait_recv()
            kv_copy(2, 0).start()

            lane = lax.broadcasted_iota(jnp.int32, (rows, LANES), 1) // head_size
            sub = lax.broadcasted_iota(jnp.int32, (LANES, rows), 0) // head_size

            @pl.loop(0, slabs)
            def _(j):
                g = j // in_group

                @pl.when(j % in_group == 0)
                def _():
                    kv_copy(1, g).wait_recv()
                    kv_copy(2, g).wait_recv()

                at = pl.ds(pl.multiple_of(j * LANES, LANES), LANES)
                own_queries = queries[:, at]
                key_slab = kv[0, j].reshape(4 * rows, LANES)
                values_t = kv[1, j].reshape(4 * rows, LANES).T
                output = jnp.zeros((LANES, rows), F32)
                logs[j] = jnp.zeros((8, rows), F32)
                for head in range(per_slab):
                    own = jnp.where(lane == head, own_queries, jnp.zeros_like(own_queries))
                    scores = across_lanes(key_slab, own) * factor + bias[...]
                    top = jnp.max(scores, axis=0, keepdims=True)
                    soft = jnp.exp2(scores - top)
                    total = jnp.sum(soft, axis=0, keepdims=True)
                    attended = jnp.dot(values_t, soft.astype(BF16), preferred_element_type=F32) / total
                    output = jnp.where(sub == head, attended, output)
                    logs[j, head : head + 1, :] = top + jnp.log2(total)
                mixed[:, at] = output.T.astype(BF16)
                mixed_t[at, :] = output.astype(BF16)

                @pl.when(jnp.logical_and(j % in_group == 0, g + 1 < groups))
                def _():
                    kv_copy(0, g + 1).wait_recv()
                    kv_copy(2, g + 1).start()

                for k in range(slabs):

                    @pl.when(j == k)
                    def _():
                        advance(inside[1])

            for i in (2, 3, 4, 8):
                save(which * per_block + i).start()
            need(first_weight[1])
            step = 2 * LANES if w % (2 * LANES) == 0 else LANES
            for c in range(w // step):
                at = pl.ds(c * step, step)
                middle[:, at] = get(pl.ds(0, rows), at) + jnp.dot(
                    mixed[...], w_out[:, at], preferred_element_type=F32
                )
            save(which * per_block + 5).start()
            norm_into(normed, lambda part: middle[part], table, 2)
            turn(normed, normed_mid_t)
            save(which * per_block + 6).start()
            need(first_weight[2])

            def stage_copy(c):
                return pltpu.make_async_copy(
                    stage.at[c % 2],
                    hidden_out.at[pl.ds(pl.multiple_of(c * 2 * LANES, 2 * LANES), 2 * LANES)],
                    stage_sems.at[c % 2],
                )

            @pl.loop(0, ff // (2 * LANES))
            def _(c):
                at = pl.ds(pl.multiple_of(c * 2 * LANES, 2 * LANES), 2 * LANES)
                pre = jnp.dot(normed[...], w_up[:, at], preferred_element_type=F32)
                below = 0.5 * (1.0 + lax.erf(pre * (0.5**0.5)))
                bell = jnp.exp2(pre * pre * (-0.5 * LOG2E)) * (1.0 / math.sqrt(2.0 * math.pi))
                active = (pre * below).astype(BF16)
                hidden[:, at] = active
                slope[:, at] = (below + pre * bell).astype(BF16)

                @pl.when(c >= 2)
                def _():
                    stage_copy(c - 2).wait()

                stage[c % 2] = active.T
                stage_copy(c).start()

            stage_copy(ff // (2 * LANES) - 2).wait()
            stage_copy(ff // (2 * LANES) - 1).wait()
            save(which * per_block + 7).start()
            need(first_weight[3])
            for c in range(w // step):
                at = pl.ds(c * step, step)
                finish(
                    at, middle[:, at] + jnp.dot(hidden[...], w_down[:, at], preferred_element_type=F32)
                )
            for g in range(groups):
                for kind in range(3):
                    kv_copy(kind, g).wait_send()


        for i in (0, 2, 1):
            trade_start(i)
        for u in range(ahead):
            launch(u)
        trade_start(3)
        need(1)
        for owner in range(8):
            gains[:, owner * LANES : (owner + 1) * LANES] = weights[0][
                owner * SMALL_ROWS : (owner + 1) * SMALL_ROWS, :
            ].astype(F32)
        total = weights[1][0:SMALL_ROWS, :].astype(F32)
        for owner in range(1, 8):
            total = total + weights[1][owner * SMALL_ROWS : (owner + 1) * SMALL_ROWS, :].astype(F32)
        narrow_gains[...] = total
        trade_arrived(2)
        key_row = lax.broadcasted_iota(jnp.int32, (4 * rows, rows), 0)
        query_row = mine * rows + lax.broadcasted_iota(jnp.int32, (4 * rows, rows), 1)
        key_clip = jnp.zeros((4 * rows, rows), jnp.int32)
        query_clip = jnp.zeros((4 * rows, rows), jnp.int32)
        for c in range(3):
            end = ends_buf[c : c + 1, 0:1]
            key_clip = key_clip + (key_row >= end).astype(jnp.int32)
            query_clip = query_clip + (query_row >= end).astype(jnp.int32)
        bias[...] = jnp.where(key_clip == query_clip, 0.0, NEG_FILL)
        trade_arrived(0)
        save(2 * per_block + 3).start()

        def token_rows(part, at=slice(None)):
            return token_buf[part, at].astype(F32)

        def finish_context(at, value):
            context[:, at] = value.astype(BF16)

        run_block(0, token_rows, gains, (2, 3, 4, 5), finish_context, (1, 1))
        trade_start(4)
        turn(context, context_t)
        save(2 * per_block).start()
        need(6)
        trade_arrived(1)
        save(2 * per_block + 2).start()
        embedded = jnp.dot(context[...], weights[6][...], preferred_element_type=F32)
        hit = side_buf[:, narrow : narrow + 1]
        entry[...] = jnp.where(hit > 0.0, narrow_gains[4:5, :] + side_buf[:, 0:narrow], embedded)
        save(2 * per_block + 1).start()

        def entry_rows(part, at=slice(None)):
            return entry[part, at]

        def finish_predicted(at, value):
            predicted[:, at] = value.astype(BF16)

        run_block(1, entry_rows, narrow_gains, (7, 8, 9, 10), finish_predicted, (0, 0))
        trade_start(5)
        advance(len(ticks))
        for u in range(count):
            for slot in range(7):
                weight_copy(u, slot).wait_send()
        for index in range(array_count):
            weight_out(index).wait()
        for i in range(saved_count):
            save(i).wait()
        keep_copy(6, ends_buf, ends_out).start()
        for i in (3, 4, 5):
            trade_arrived(i)
        for i in range(6):
            trade_sent(i)
        keep_copy(6, ends_buf, ends_out).wait()

    gathered = [(8 * shape[0], shape[1]) for shape in shapes]
    out_shape = (
        [jax.ShapeDtypeStruct(shape, BF16) for shape in gathered]
        + [jax.ShapeDtypeStruct(shape, kind) for shape, kind in saved_shapes]
        + [
            jax.ShapeDtypeStruct(out_grad.shape, BF16),
            jax.ShapeDtypeStruct(ends.shape, jnp.int32),
            jax.ShapeDtypeStruct((rows, width), BF16),
            jax.ShapeDtypeStruct((rows, narrow), BF16),
            jax.ShapeDtypeStruct((hidden_width, rows), BF16),
            jax.ShapeDtypeStruct((narrow_hidden, rows), BF16),
        ]
    )
    scratch = (
        [pltpu.VMEM(shape, BF16) for shape in gathered]
        + [pltpu.VMEM(shape, kind) for shape, kind in saved_shapes]
        + [
            pltpu.VMEM((4 * rows, rows), F32),
            pltpu.VMEM((SMALL_ROWS, width), F32),
            pltpu.VMEM((SMALL_ROWS, narrow), F32),
            pltpu.VMEM(ends.shape, jnp.int32),
            pltpu.VMEM((rows, narrow), BF16),
            pltpu.VMEM((rows, width), BF16),
            pltpu.VMEM((rows, hidden_width), BF16),
            pltpu.VMEM((rows, narrow), BF16),
            pltpu.VMEM((rows, narrow_hidden), BF16),
            pltpu.VMEM((2, 2 * LANES, rows), BF16),
            pltpu.SemaphoreType.DMA((2,)),
            pltpu.SemaphoreType.DMA((count, 7)),
            pltpu.SemaphoreType.DMA((count, 7)),
            pltpu.SemaphoreType.DMA((count,)),
            pltpu.SemaphoreType.DMA((array_count,)),
            pltpu.SemaphoreType.DMA((saved_count,)),
            pltpu.SemaphoreType.DMA((6,)),
            pltpu.SemaphoreType.DMA((6,)),
            pltpu.SemaphoreType.DMA((7,)),
            pltpu.SemaphoreType.DMA((2, 3, 4)),
            pltpu.SemaphoreType.DMA((2, 3, 4)),
        ]
    )
    results = pl.pallas_call(
        kernel,
        out_shape=out_shape,
        in_specs=[ANYWHERE] * (4 + array_count),
        out_specs=[ANYWHERE] * len(out_shape),
        scratch_shapes=scratch,
        compiler_params=remote_params(1, 62 << 20),
        name="forward_pass",
    )(tokens, out_grad, side, ends, *shards)
    saved = results[array_count : array_count + saved_count]
    return (
        results[:array_count],
        saved[:per_block],
        saved[per_block : 2 * per_block],
        saved[2 * per_block :],
        results[array_count + saved_count :],
    )


class Unit:
    def __init__(self, index, first, columns, order, place):
        self.index = index
        self.first = first
        self.columns = columns
        self.near, self.far = order
        self.place = place


def cut_columns(shapes, most):
    units = []
    for index, (rows, columns) in enumerate(shapes):
        pieces = 1
        while rows * (columns // pieces) > most and (columns // pieces) % (2 * LANES) == 0:
            pieces *= 2
        for place in range(pieces):
            order = (2, 4) if len(units) % 2 == 0 else (4, 2)
            units.append(Unit(index, place * (columns // pieces), columns // pieces, order, place))
    return units


def back_and_sum(
    partials,
    lefts_t,
    rights,
    queries,
    keys_values,
    mixed,
    grad_mixed,
    logs,
    query_clip,
    key_clip,
    w_qkv,
    tokens,
    grad_middle,
    gain,
    head_count,
    collective_id,
):
    rows, width = queries.shape
    triple = 3 * width
    keys = 4 * rows
    slabs = width // LANES
    head_size = width // head_count
    per_slab = LANES // head_size
    scale = head_size ** (-0.5)
    factor = scale * LOG2E
    part_rows = w_qkv.shape[1]

    given = len(partials)
    formed = [(left.shape[0] // 8, right.shape[1]) for left, right in zip(lefts_t, rights)]
    shapes = [partial.shape[1:] for partial in partials] + formed + [(part_rows, triple), (SMALL_ROWS, LANES)]
    up_index = given + 1
    qkv_index, small_index = given + 3, given + 4
    array_count = given + 5
    ring = 5
    units = cut_columns(shapes, 70000)
    count = len(units)
    pieces = [sum(1 for unit in units if unit.index == index) for index in range(array_count)]

    def piece_shape(index):
        return (shapes[index][0], shapes[index][1] // pieces[index])

    def kernel(*refs):
        sources = refs[:given]
        left_refs = refs[given : given + 4]
        right_refs = refs[given + 4 : given + 7]
        base = given + 7
        (
            q_ref,
            kv_ref,
            mixed_ref,
            grad_ref,
            log_ref,
            query_ref,
            key_ref,
            w_ref,
            tokens_ref,
            middle_ref,
            gain_ref,
        ) = refs[base : base + 11]
        base += 11
        results = refs[base : base + array_count]
        token_out, up_inbox = refs[base + array_count : base + array_count + 2]
        rest = list(refs[base + array_count + 2 :])
        acc, near_in, far_in, outer_in, inner_in = [
            rest[group * array_count : (group + 1) * array_count] for group in range(5)
        ]
        late_out = rest[5 * array_count : 5 * array_count + 4]
        lefts = rest[5 * array_count + 4 : 5 * array_count + 8]
        (
            low_both,
            branch_both,
            up_buf,
            kv_buf,
            give_send,
            give_recv,
            give_own,
            up_sems,
            kv_sems,
            small_out,
            bias,
            dkv,
            core_in,
            z_in,
            dqkv,
            w_buf,
            grad_normed,
            token_buf,
            norm_sums,
            norm_sums_in,
            send_sems,
            recv_sems,
            own_sems,
            out_sems,
            key_send,
            key_recv,
            row_send,
            row_recv,
            w_sems,
        ) = rest[5 * array_count + 8 :]

        me = lax.axis_index("fsdp")
        place = lax.axis_index("seq")
        core = me & 1
        chip = me >> 1
        high = place >> 1
        low = place & 1
        inner = jnp.logical_or(place == 1, place == 2)
        outer = jnp.logical_not(inner)
        trades = core != high
        trade_peer = ((me & 6) | high, core * 2 + low)
        mate = seq_peer(place ^ 1)
        across = seq_peer(3 - place)

        barrier = pltpu.get_barrier_semaphore()
        for peer in (fsdp_peer(1), fsdp_peer(2), fsdp_peer(4), mate):
            pl.semaphore_signal(barrier, inc=1, device_id=peer, device_id_type=MESH)

        @pl.when(inner)
        def _():
            pl.semaphore_signal(barrier, inc=1, device_id=across, device_id_type=MESH)

        @pl.when(trades)
        def _():
            pl.semaphore_signal(barrier, inc=1, device_id=trade_peer, device_id_type=MESH)

        pl.semaphore_wait(barrier, 4 + inner.astype(jnp.int32) + trades.astype(jnp.int32))


        def span(unit):
            return pl.ds(unit.first, unit.columns)

        def chip_of(unit, slot):
            return chip ^ (((slot // 2) * unit.near + (slot % 2) * unit.far) // 2)

        def near_copy(u, slot):
            unit = units[u]
            if given <= unit.index <= qkv_index:
                src = late_out[unit.index - given].at[unit.place % ring, slot]
            elif unit.index == small_index:
                src = small_out.at[slot]
            else:
                src = sources[unit.index].at[chip_of(unit, 2 + slot), :, span(unit)]
            return send(
                src,
                near_in[unit.index].at[unit.place, slot],
                send_sems.at[u, slot],
                recv_sems.at[u, slot],
                fsdp_peer(unit.near),
            )

        def own_copy(u, slot):
            unit = units[u]
            return pltpu.make_async_copy(
                sources[unit.index].at[chip_of(unit, slot), :, span(unit)],
                acc[unit.index].at[unit.place, slot],
                own_sems.at[u, slot],
            )

        def far_copy(u):
            unit = units[u]
            return send(
                acc[unit.index].at[unit.place, 1],
                far_in[unit.index].at[unit.place],
                send_sems.at[u, 2],
                recv_sems.at[u, 2],
                fsdp_peer(unit.far),
            )

        def inward_copy(u):
            unit = units[u]
            return send(
                acc[unit.index].at[unit.place, 0],
                outer_in[unit.index].at[unit.place],
                send_sems.at[u, 3],
                recv_sems.at[u, 3],
                mate,
            )

        def across_copy(u):
            unit = units[u]
            return send(
                outer_in[unit.index].at[unit.place],
                inner_in[unit.index].at[unit.place],
                send_sems.at[u, 4],
                recv_sems.at[u, 4],
                across,
            )

        def outward_copy(u):
            unit = units[u]
            return send(
                acc[unit.index].at[unit.place, 0],
                results[unit.index].at[:, span(unit)],
                send_sems.at[u, 5],
                recv_sems.at[u, 5],
                mate,
            )

        def out_copy(u):
            unit = units[u]
            return pltpu.make_async_copy(
                acc[unit.index].at[unit.place, 0], results[unit.index].at[:, span(unit)], out_sems.at[u]
            )

        def add_into(dst, left, right):
            total_rows, columns = dst.shape
            step = 16
            while total_rows % (2 * step) == 0 and 2 * step * columns <= 32768:
                step *= 2

            @pl.loop(0, total_rows // step)
            def _(i):
                part = pl.ds(pl.multiple_of(i * step, step), step)
                dst[part] = (left[part].astype(F32) + right[part].astype(F32)).astype(BF16)

        def early(u):
            return units[u].index < given

        def near_start(u):
            if given <= units[u].index <= qkv_index:
                form(u)
            elif units[u].index == small_index:
                form_small(u)
            near_copy(u, 1).start()
            near_copy(u, 0).start()

        def stage_far(u):
            unit = units[u]
            for slot in (1, 0):
                near_copy(u, slot).wait_recv()
                if early(u):
                    own_copy(u, slot).wait()
                target = acc[unit.index].at[unit.place, slot]
                add_into(target, target, near_in[unit.index].at[unit.place, slot])
                if slot == 1:
                    far_copy(u).start()

        def stage_inward(u):
            unit = units[u]
            far_copy(u).wait_recv()
            target = acc[unit.index].at[unit.place, 0]
            add_into(target, target, far_in[unit.index].at[unit.place])

            @pl.when(outer)
            def _():
                inward_copy(u).start()

        def stage_across(u):
            unit = units[u]

            @pl.when(inner)
            def _():
                inward_copy(u).wait_recv()
                target = outer_in[unit.index].at[unit.place]
                add_into(target, target, acc[unit.index].at[unit.place, 0])
                across_copy(u).start()

        def stage_outward(u):
            unit = units[u]

            @pl.when(inner)
            def _():
                across_copy(u).wait_recv()
                add_into(
                    acc[unit.index].at[unit.place, 0],
                    outer_in[unit.index].at[unit.place],
                    inner_in[unit.index].at[unit.place],
                )
                outward_copy(u).start()
                out_copy(u).start()

        ahead = 4
        lags = ((stage_far, 0), (stage_inward, 2), (stage_across, 4), (stage_outward, 6))
        total_ticks = count + 6

        def tick(t):
            if t + ahead < count:
                near_start(t + ahead)
            for stage, lag in lags:
                if 0 <= t - lag < count:
                    stage(t - lag)


        half = 2 * rows

        def group(g):
            return pl.ds(2 * g, 2)

        def key_core_copy(g):
            return send(
                dkv.at[:, group(g), pl.ds((core ^ 1) * half, half)],
                core_in.at[:, group(g)],
                key_send.at[0, g],
                key_recv.at[0, g],
                fsdp_peer(1),
            )

        def key_far_copy(g):
            return send(
                core_in.at[:, group(g), pl.ds((low ^ 1) * rows, rows)],
                z_in.at[:, group(g)],
                key_send.at[1, g],
                key_recv.at[1, g],
                mate,
            )

        def key_middle(g):
            key_core_copy(g).wait_recv()
            for kind in range(2):
                for k in range(2):

                    @pl.loop(0, half // LANES)
                    def _(i):
                        part = pl.ds(pl.multiple_of(i * LANES, LANES), LANES)
                        own = pl.ds(pl.multiple_of(core * half + i * LANES, LANES), LANES)
                        core_in[kind, 2 * g + k, part] = (
                            core_in[kind, 2 * g + k, part].astype(F32) + dkv[kind, 2 * g + k, own].astype(F32)
                        ).astype(BF16)

            key_far_copy(g).start()

        def key_end(g):
            key_far_copy(g).wait_recv()
            for kind in range(2):
                for k in range(2):
                    slab = 2 * g + k

                    @pl.loop(0, rows // LANES)
                    def _(i):
                        part = pl.ds(pl.multiple_of(i * LANES, LANES), LANES)
                        own = pl.ds(pl.multiple_of(low * rows + i * LANES, LANES), LANES)
                        total = core_in[kind, slab, own].astype(F32) + z_in[kind, slab, part].astype(F32)
                        dqkv[part, pl.ds((1 + kind) * width + slab * LANES, LANES)] = total.astype(BF16)


        lane = lax.broadcasted_iota(jnp.int32, (rows, LANES), 1) // head_size
        key_lane = lax.broadcasted_iota(jnp.int32, (keys, LANES), 1) // head_size
        sub = lax.broadcasted_iota(jnp.int32, (LANES, rows), 0) // head_size

        def kv_copy(j):
            return pltpu.make_async_copy(kv_ref.at[:, j], kv_buf.at[j % 2], kv_sems.at[j % 2])

        def slab_back(j):
            kv_copy(j).wait()

            @pl.when(j + 1 < slabs)
            def _():
                kv_copy(j + 1).start()

            at = pl.ds(pl.multiple_of(j * LANES, LANES), LANES)
            queries = q_ref[:, at]
            grads = grad_ref[:, at]
            pick = (
                lax.broadcasted_iota(jnp.int32, (8, LANES), 1) // head_size
                == lax.broadcasted_iota(jnp.int32, (8, LANES), 0)
            ).astype(F32)
            deltas = lax.dot_general(
                pick,
                grads.astype(F32) * mixed_ref[:, at].astype(F32),
                (((1,), (1,)), ((), ())),
                precision=lax.Precision.HIGHEST,
                preferred_element_type=F32,
            )
            key_slab = kv_buf[j % 2, 0]
            keys_t = key_slab.T
            dq = jnp.zeros((LANES, rows), F32)
            dk = jnp.zeros((keys, LANES), F32)
            dv = jnp.zeros((keys, LANES), F32)
            slab_logs = log_ref[j]
            for head in range(per_slab):
                own = jnp.where(lane == head, queries, jnp.zeros_like(queries))
                own_grad = jnp.where(lane == head, grads, jnp.zeros_like(grads))
                scores = across_lanes(key_slab, own) * factor + bias[...]
                weights = jnp.exp2(scores - slab_logs[head : head + 1, :])
                grad_soft = across_lanes(kv_buf[j % 2, 1], own_grad)
                grad_scores = (weights * (grad_soft - deltas[head : head + 1, :])).astype(BF16)
                dv = jnp.where(
                    key_lane == head, jnp.dot(weights.astype(BF16), grads, preferred_element_type=F32), dv
                )
                dk = jnp.where(
                    key_lane == head, jnp.dot(grad_scores, queries, preferred_element_type=F32), dk
                )
                dq = jnp.where(sub == head, jnp.dot(keys_t, grad_scores, preferred_element_type=F32), dq)
            dqkv[pl.ds(0, rows), at] = (dq.T * scale).astype(BF16)
            dkv[0, j] = (dk * scale).astype(BF16)
            dkv[1, j] = dv.astype(BF16)


        def row_copy(part):
            columns = pl.ds(0, width) if part == 0 else pl.ds(width, 2 * width)
            return send(
                dqkv.at[pl.ds(0, rows), columns],
                dqkv.at[pl.ds(rows, rows), columns],
                row_send.at[part],
                row_recv.at[part],
                fsdp_peer(1),
            )


        def left_copy(which, p):
            size = lefts_t[which].shape[0] // 8
            owner = 2 * p + (core ^ 1)
            return send(
                left_refs[which].at[pl.ds(pl.multiple_of(owner * size, LANES), size)],
                lefts[which].at[1, p],
                give_send.at[which, p],
                give_recv.at[which, p],
                fsdp_peer(1),
            )

        def left_own(which, p):
            size = lefts_t[which].shape[0] // 8
            owner = 2 * p + core
            return pltpu.make_async_copy(
                left_refs[which].at[pl.ds(pl.multiple_of(owner * size, LANES), size)],
                lefts[which].at[0, p],
                give_own.at[which, p],
            )

        def right_copy(which):
            dst = (low_both.at[pl.ds(rows, rows)], up_inbox, branch_both.at[pl.ds(rows, rows)])[which]
            return send(
                right_refs[which], dst, give_send.at[4, which], give_recv.at[4, which], fsdp_peer(1)
            )

        def right_own(which):
            dst = (low_both, None, branch_both)[which].at[pl.ds(0, rows)]
            return pltpu.make_async_copy(right_refs[which], dst, give_own.at[4, which])

        def give(which):
            for p in range(4):
                left_copy(which, p).start()
                left_own(which, p).start()
            if which < 3:
                right_copy(which).start()
                if which != 1:
                    right_own(which).start()

        def take(which):
            for p in range(4):
                left_copy(which, p).wait_recv()
                left_own(which, p).wait()
            if which < 3:
                right_copy(which).wait_recv()
                if which != 1:
                    right_own(which).wait()

        def up_copies(unit):
            slot = unit.place % 2
            return [
                pltpu.make_async_copy(
                    right_refs[1].at[:, span(unit)], up_buf.at[slot, pl.ds(0, rows)], up_sems.at[slot, 0]
                ),
                pltpu.make_async_copy(
                    up_inbox.at[:, span(unit)], up_buf.at[slot, pl.ds(rows, rows)], up_sems.at[slot, 1]
                ),
            ]

        near_done = set()

        def form(u):
            unit = units[u]
            which = unit.index - given
            if unit.place == 0:
                take(which)
                if unit.index == up_index:
                    for one in up_copies(unit):
                        one.start()
            if unit.place >= ring:
                near_copy(u - ring, 0).wait_send()
                near_copy(u - ring, 1).wait_send()
                near_done.add(u - ring)
            if unit.index == up_index:
                if unit.place + 1 < pieces[up_index]:
                    for one in up_copies(units[u + 1]):
                        one.start()
                for one in up_copies(unit):
                    one.wait()
                right = up_buf.at[unit.place % 2]
            else:
                right = (low_both, None, branch_both, dqkv)[which].at[:, span(unit)]
            for slot in range(4):
                block = jnp.zeros(piece_shape(unit.index), F32)
                for half in range(2):
                    block = block + jnp.dot(
                        lefts[which][half, chip_of(unit, slot)],
                        right[pl.ds(half * rows, rows)],
                        preferred_element_type=F32,
                    )
                if slot < 2:
                    acc[unit.index][unit.place, slot] = block.astype(BF16)
                else:
                    late_out[which][unit.place % ring, slot - 2] = block.astype(BF16)


        blocks = 8

        def w_copy(block):
            return pltpu.make_async_copy(w_ref.at[block], w_buf.at[block % 2], w_sems.at[block % 2])

        def norm_copy():
            return send(norm_sums, norm_sums_in, row_send.at[2], row_recv.at[2], fsdp_peer(1))

        def input_gradient():
            for block in range(blocks):
                w_copy(block).wait()
                grad_normed[:, pl.ds(block * part_rows, part_rows)] = across_lanes(
                    dqkv[pl.ds(0, rows), :], w_buf[block % 2]
                )
                if block + 2 < blocks:
                    w_copy(block + 2).start()
            gain_row = gain_ref[...]
            norm_sums[...] = jnp.zeros_like(norm_sums)
            step = 64
            gain_sum = jnp.zeros((1, width), F32)
            shift_sum = jnp.zeros((1, width), F32)
            for i in range(rows // step):
                part = pl.ds(i * step, step)
                value = tokens_ref[part].astype(F32)
                value = value - jnp.mean(value, axis=1, keepdims=True)
                inverse = lax.rsqrt(jnp.mean(value * value, axis=1, keepdims=True) + EPSILON)
                unit_value = value * inverse
                upper = grad_normed[part]
                gain_sum = gain_sum + jnp.sum(upper * unit_value, axis=0, keepdims=True)
                shift_sum = shift_sum + jnp.sum(upper, axis=0, keepdims=True)
                scaled = upper * gain_row
                inside = (
                    scaled
                    - jnp.mean(scaled, axis=1, keepdims=True)
                    - unit_value * jnp.mean(scaled * unit_value, axis=1, keepdims=True)
                )
                token_buf[part] = (middle_ref[part] + inverse * inside).astype(BF16)
            norm_sums[0:1, :] = gain_sum
            norm_sums[1:2, :] = shift_sum
            norm_copy().start()

            @pl.when(trades)
            def _():
                token_send().start()

            @pl.when(jnp.logical_not(trades))
            def _():
                token_keep().start()

        def token_send():
            return send(token_buf, token_out, row_send.at[3], row_recv.at[3], trade_peer)

        def token_keep():
            return pltpu.make_async_copy(token_buf, token_out, w_sems.at[2])

        def form_small(u):
            unit = units[u]
            norm_copy().wait_recv()
            both = norm_sums[...] + norm_sums_in[...]
            norm_sums_in[...] = both
            for slot in range(4):
                owner = chip_of(unit, slot) * 2 + core
                block = norm_sums_in[:, pl.ds(pl.multiple_of(owner * LANES, LANES), LANES)].astype(BF16)
                if slot < 2:
                    acc[unit.index][unit.place, slot] = block
                else:
                    small_out[slot - 2] = block


        first_late = min(u for u in range(count) if units[u].index == qkv_index)
        for which in range(4):
            give(which)
        for u in range(count):
            if early(u):
                for slot in range(2):
                    own_copy(u, slot).start()
        kv_copy(0).start()
        for u in range(ahead):
            near_start(u)
        w_copy(0).start()
        w_copy(1).start()
        bias[...] = jnp.where(key_ref[...] == query_ref[...], 0.0, NEG_FILL)
        ticks_inside = first_late - ahead

        @pl.loop(0, slabs)
        def _(j):
            slab_back(j)

            @pl.when(j % 2 == 1)
            def _():
                key_core_copy(j // 2).start()

            @pl.when(jnp.logical_and(j % 2 == 0, j >= 2))
            def _():
                key_middle(j // 2 - 1)

            done = 0
            for k in range(slabs):
                until = (k + 1) * ticks_inside // slabs

                @pl.when(j == k)
                def _(done=done, until=until):
                    for t in range(done, until):
                        tick(t)

                done = until

        row_copy(0).start()
        key_middle(slabs // 2 - 1)
        for g in range(slabs // 2):
            key_end(g)
        row_copy(1).start()
        row_copy(0).wait_recv()
        row_copy(1).wait_recv()
        done_input = False
        for t in range(ticks_inside, total_ticks):
            if not done_input and t + ahead >= count - 1:
                input_gradient()
                done_input = True
            tick(t)

        for u in range(count):
            if u not in near_done:
                near_copy(u, 0).wait_send()
                near_copy(u, 1).wait_send()
            far_copy(u).wait_send()
        for which in range(4):
            for p in range(4):
                left_copy(which, p).wait_send()
            if which < 3:
                right_copy(which).wait_send()

        for u in range(count):

            @pl.when(inner)
            def _():
                across_copy(u).wait_send()
                outward_copy(u).wait_send()
                out_copy(u).wait()

            @pl.when(outer)
            def _():
                inward_copy(u).wait_send()
                outward_copy(u).wait_recv()

        for g in range(slabs // 2):
            key_core_copy(g).wait_send()
            key_far_copy(g).wait_send()
        row_copy(0).wait_send()
        row_copy(1).wait_send()
        norm_copy().wait_send()

        @pl.when(trades)
        def _():
            token_send().wait()

        @pl.when(jnp.logical_not(trades))
        def _():
            token_keep().wait()

    scratch = []
    for slots in ((2,), (2,), (), (), ()):
        for index in range(array_count):
            scratch.append(pltpu.VMEM((pieces[index],) + slots + piece_shape(index), BF16))
    for index in range(given, qkv_index + 1):
        scratch.append(pltpu.VMEM((min(ring, pieces[index]), 2) + piece_shape(index), BF16))
    for left in lefts_t:
        scratch.append(pltpu.VMEM((2, 4, left.shape[0] // 8, rows), BF16))
    scratch += [
        pltpu.VMEM((2 * rows, width), BF16),
        pltpu.VMEM((2 * rows, width), BF16),
        pltpu.VMEM((2, 2 * rows, piece_shape(up_index)[1]), BF16),
        pltpu.VMEM((2, 2, keys, LANES), BF16),
        pltpu.SemaphoreType.DMA((5, 4)),
        pltpu.SemaphoreType.DMA((5, 4)),
        pltpu.SemaphoreType.DMA((5, 4)),
        pltpu.SemaphoreType.DMA((2, 2)),
        pltpu.SemaphoreType.DMA((2,)),
        pltpu.VMEM((2, SMALL_ROWS, LANES), BF16),
        pltpu.VMEM((keys, rows), F32),
        pltpu.VMEM((2, slabs, keys, LANES), BF16),
        pltpu.VMEM((2, slabs, 2 * rows, LANES), BF16),
        pltpu.VMEM((2, slabs, rows, LANES), BF16),
        pltpu.VMEM((2 * rows, triple), BF16),
        pltpu.VMEM((2, part_rows, triple), BF16),
        pltpu.VMEM((rows, width), F32),
        pltpu.VMEM((rows, width), BF16),
        pltpu.VMEM((SMALL_ROWS, width), F32),
        pltpu.VMEM((SMALL_ROWS, width), F32),
        pltpu.SemaphoreType.DMA((count, 6)),
        pltpu.SemaphoreType.DMA((count, 6)),
        pltpu.SemaphoreType.DMA((count, 2)),
        pltpu.SemaphoreType.DMA((count,)),
        pltpu.SemaphoreType.DMA((2, slabs // 2)),
        pltpu.SemaphoreType.DMA((2, slabs // 2)),
        pltpu.SemaphoreType.DMA((4,)),
        pltpu.SemaphoreType.DMA((4,)),
        pltpu.SemaphoreType.DMA((3,)),
    ]
    return pl.pallas_call(
        kernel,
        out_shape=[jax.ShapeDtypeStruct(shape, BF16) for shape in shapes]
        + [jax.ShapeDtypeStruct((rows, width), BF16), jax.ShapeDtypeStruct(rights[1].shape, BF16)],
        in_specs=[ANYWHERE] * (given + 7)
        + [IN_VMEM, ANYWHERE]
        + [IN_VMEM] * 5
        + [ANYWHERE]
        + [IN_VMEM] * 3,
        out_specs=[ANYWHERE] * (array_count + 2),
        scratch_shapes=scratch,
        compiler_params=remote_params(collective_id, 61 << 20),
        name="back_and_sum",
    )(
        *partials,
        *lefts_t,
        *rights,
        queries,
        keys_values,
        mixed,
        grad_mixed,
        logs,
        query_clip[None, :],
        key_clip[:, None],
        w_qkv,
        tokens,
        grad_middle,
        gain[None, :],
    )


def sum_keys(terms, collective_id):
    _, rows, width = terms[0].shape
    pieces = 4
    step = rows // pieces
    kinds = len(terms)

    def kernel(*refs):
        sources = refs[:kinds]
        results = refs[kinds : 2 * kinds]
        core_buf, far_buf, send_sems, recv_sems = refs[2 * kinds :]
        mine = quarter()
        enter([fsdp_peer(1), mate_z()])

        def core_copy(kind, piece, other):
            owner = mine ^ 2 ^ other
            return send(
                sources[kind].at[owner, pl.ds(piece * step, step)],
                core_buf.at[kind, other, pl.ds(piece * step, step)],
                send_sems.at[kind, piece, other],
                recv_sems.at[kind, piece, other],
                fsdp_peer(1),
            )

        def far_copy(kind, piece):
            part = pl.ds(piece * step, step)
            return send(
                core_buf.at[kind, 1, part],
                far_buf.at[kind, part],
                send_sems.at[kind, piece, 2],
                recv_sems.at[kind, piece, 2],
                mate_z(),
            )

        order = [(kind, piece) for piece in range(pieces) for kind in range(kinds)]
        for other in (1, 0):
            for kind, piece in order:
                core_copy(kind, piece, other).start()
        for kind, piece in order:
            core_copy(kind, piece, 1).wait_recv()

            @pl.loop(0, step // 16)
            def _(i):
                part = pl.ds(pl.multiple_of(piece * step + i * 16, 16), 16)
                total = core_buf[kind, 1, part].astype(F32) + sources[kind][mine ^ 1, part].astype(F32)
                core_buf[kind, 1, part] = total.astype(BF16)

            far_copy(kind, piece).start()
        for kind, piece in order:
            core_copy(kind, piece, 0).wait_recv()
            far_copy(kind, piece).wait_recv()

            @pl.loop(0, step // 16)
            def _(i):
                part = pl.ds(pl.multiple_of(piece * step + i * 16, 16), 16)
                total = core_buf[kind, 0, part].astype(F32) + sources[kind][mine, part].astype(F32)
                results[kind][part] = (total + far_buf[kind, part].astype(F32)).astype(BF16)

        for kind, piece in order:
            core_copy(kind, piece, 0).wait_send()
            core_copy(kind, piece, 1).wait_send()
            far_copy(kind, piece).wait_send()

    return pl.pallas_call(
        kernel,
        out_shape=[jax.ShapeDtypeStruct((rows, width), BF16)] * kinds,
        in_specs=[IN_VMEM] * kinds,
        out_specs=[IN_VMEM] * kinds,
        scratch_shapes=[
            pltpu.VMEM((kinds, 2, rows, width), BF16),
            pltpu.VMEM((kinds, rows, width), BF16),
            pltpu.SemaphoreType.DMA((kinds, pieces, 3)),
            pltpu.SemaphoreType.DMA((kinds, pieces, 3)),
        ],
        compiler_params=remote_params(collective_id, 40 << 20),
        name="sum_keys",
    )(*terms)


def fill_bias(bias, query_ref, key_ref):
    @pl.when(pl.program_id(0) == 0)
    def _():
        bias[...] = jnp.where(key_ref[...] == query_ref[...], 0.0, NEG_FILL)


def attend_local_back(queries, keys_values, mixed, logs, grad_mixed, query_clip, key_clip, head_count):
    rows, width = queries.shape
    keys = 4 * rows
    slabs = width // LANES
    head_size = width // head_count
    per_slab = LANES // head_size
    scale = head_size ** (-0.5)
    factor = scale * LOG2E

    def kernel(
        q_ref, k_ref, v_ref, mixed_ref, grad_ref, log_ref, query_ref, key_ref, dq_ref, dk_ref, dv_ref, bias
    ):
        fill_bias(bias, query_ref, key_ref)
        lane = lax.broadcasted_iota(jnp.int32, (rows, LANES), 1) // head_size
        key_lane = lax.broadcasted_iota(jnp.int32, (keys, LANES), 1) // head_size
        sub = lax.broadcasted_iota(jnp.int32, (LANES, rows), 0) // head_size
        queries = q_ref[...]
        grads = grad_ref[...]
        pick = (
            lax.broadcasted_iota(jnp.int32, (8, LANES), 1) // head_size
            == lax.broadcasted_iota(jnp.int32, (8, LANES), 0)
        ).astype(F32)
        deltas = lax.dot_general(
            pick,
            grads.astype(F32) * mixed_ref[...].astype(F32),
            (((1,), (1,)), ((), ())),
            precision=lax.Precision.HIGHEST,
            preferred_element_type=F32,
        )
        keys_t = k_ref[...].T
        dq = jnp.zeros((LANES, rows), F32)
        dk = jnp.zeros((keys, LANES), F32)
        dv = jnp.zeros((keys, LANES), F32)
        for head in range(per_slab):
            own = jnp.where(lane == head, queries, jnp.zeros_like(queries))
            own_grad = jnp.where(lane == head, grads, jnp.zeros_like(grads))
            scores = across_lanes(k_ref[...], own) * factor + bias[...]
            weights = jnp.exp2(scores - log_ref[0, head : head + 1, :])
            grad_soft = across_lanes(v_ref[...], own_grad)
            grad_scores = (weights * (grad_soft - deltas[head : head + 1, :])).astype(BF16)
            dv = jnp.where(
                key_lane == head, jnp.dot(weights.astype(BF16), grads, preferred_element_type=F32), dv
            )
            dk = jnp.where(key_lane == head, jnp.dot(grad_scores, queries, preferred_element_type=F32), dk)
            dq = jnp.where(sub == head, jnp.dot(keys_t, grad_scores, preferred_element_type=F32), dq)
        dq_ref[...] = (dq.T * scale).astype(BF16)
        dk_ref[...] = (dk * scale).astype(BF16)
        dv_ref[...] = dv.astype(BF16)

    return pl.pallas_call(
        kernel,
        grid=(slabs,),
        out_shape=[
            jax.ShapeDtypeStruct((rows, width), BF16),
            jax.ShapeDtypeStruct((keys, width), BF16),
            jax.ShapeDtypeStruct((keys, width), BF16),
        ],
        in_specs=[
            pl.BlockSpec((rows, LANES), lambda j: (0, j)),
            pl.BlockSpec((None, None, keys, LANES), lambda j: (0, j, 0, 0)),
            pl.BlockSpec((None, None, keys, LANES), lambda j: (1, j, 0, 0)),
            pl.BlockSpec((rows, LANES), lambda j: (0, j)),
            pl.BlockSpec((rows, LANES), lambda j: (0, j)),
            pl.BlockSpec((1, 8, rows), lambda j: (j, 0, 0)),
            pl.BlockSpec((1, rows), lambda j: (0, 0)),
            pl.BlockSpec((keys, 1), lambda j: (0, 0)),
        ],
        out_specs=[
            pl.BlockSpec((rows, LANES), lambda j: (0, j)),
            pl.BlockSpec((keys, LANES), lambda j: (0, j)),
            pl.BlockSpec((keys, LANES), lambda j: (0, j)),
        ],
        scratch_shapes=[pltpu.VMEM((keys, rows), F32)],
        compiler_params=pltpu.CompilerParams(vmem_limit_bytes=50 << 20),
        name="attend_local_back",
    )(
        queries,
        keys_values,
        keys_values,
        mixed,
        grad_mixed,
        logs,
        query_clip[None, :],
        key_clip[:, None],
    )


def swap_cores(values):
    return lax.ppermute(values, "fsdp", [(f, f ^ 1) for f in range(8)])


def own_rows(values, mine):
    rows, columns = values.shape
    parts = values.reshape(4, 2, rows // 8, columns)
    core = lax.axis_index("fsdp") & 1
    return jnp.where(core == (0 if mine else 1), parts[:, 0], parts[:, 1]).reshape(rows // 2, columns)


def chip_gradient(left_t, right):
    both_left = jnp.concatenate([own_rows(left_t, True), swap_cores(own_rows(left_t, False))], axis=1)
    both_right = jnp.concatenate([right, swap_cores(right)], axis=0)
    grad = jnp.dot(both_left, both_right, preferred_element_type=F32)
    return grad.astype(BF16).reshape(4, grad.shape[0] // 4, grad.shape[1])


def back_to_mixed(grad_result, kept, norms, w_out, w_up, w_down):
    _, _, _, _, _, middle, _, slope, _ = kept
    grad_low = grad_result.astype(BF16)
    grad_hidden = jnp.einsum("tw,fw->tf", grad_low, w_down, preferred_element_type=F32)
    grad_pre = (grad_hidden * slope.astype(F32)).astype(BF16)
    grad_normed_mid = jnp.einsum("tf,wf->tw", grad_pre, w_up, preferred_element_type=F32)
    _, second_pull = jax.vjp(layer_norm, middle, norms[2], norms[3])
    grad_mid_norm, grad_gain_two, grad_shift_two = second_pull(grad_normed_mid)
    grad_middle = grad_result + grad_mid_norm
    grad_branch = grad_middle.astype(BF16)
    grad_mixed = jnp.einsum("tw,vw->tv", grad_branch, w_out, preferred_element_type=F32).astype(BF16)
    return grad_middle, grad_mixed, [grad_gain_two, grad_shift_two], (grad_branch, grad_pre, grad_low)


def fast_backward(
    grad_result, residual, kept, hidden_t, norms, w_qkv, w_out, w_up, w_down, head_count, clips, collective_id
):
    normed_t, queries, keys_values, mixed, logs, middle, normed_mid_t, slope, mixed_t = kept
    rows, width = queries.shape
    grad_middle, grad_mixed, small_two, (grad_branch, grad_pre, grad_low) = back_to_mixed(
        grad_result, kept, norms, w_out, w_up, w_down
    )
    weight_grads = (
        chip_gradient(mixed_t, grad_branch),
        chip_gradient(normed_mid_t, grad_pre),
        chip_gradient(hidden_t, grad_low),
    )
    dq, dk, dv = attend_local_back(
        queries,
        keys_values.reshape(2, width // LANES, 4 * rows, LANES),
        mixed,
        logs,
        grad_mixed,
        clips[0],
        clips[1],
        head_count,
    )
    dk, dv = sum_keys([dk.reshape(4, rows, width), dv.reshape(4, rows, width)], collective_id)
    grad_qkv = jnp.concatenate([dq, dk, dv], axis=1)
    grad_qkv_w = chip_gradient(normed_t, grad_qkv)
    grad_normed = jnp.einsum("tc,wc->tw", grad_qkv, w_qkv, preferred_element_type=F32)
    _, first_pull = jax.vjp(layer_norm, residual, norms[0], norms[1])
    grad_first_norm, grad_gain_one, grad_shift_one = first_pull(grad_normed)
    return (
        grad_middle + grad_first_norm,
        [grad_gain_one, grad_shift_one] + small_two,
        (grad_qkv_w,) + weight_grads,
    )


def fast_local(
    tokens,
    clip_lengths,
    target_pos,
    out_grad,
    norm1_gain,
    norm1_bias,
    w_qkv,
    w_out,
    norm2_gain,
    norm2_bias,
    w_fc1,
    w_fc2,
    w_embed,
    mask_token,
    pred_norm1_gain,
    pred_norm1_bias,
    pred_qkv,
    pred_out,
    pred_norm2_gain,
    pred_norm2_bias,
    pred_fc1,
    pred_fc2,
):
    rows, width = tokens.shape
    narrow = out_grad.shape[1]
    wide_part = norm1_gain.shape[0]
    narrow_part = mask_token.shape[0]
    me = lax.axis_index("fsdp")
    core = me & 1
    wide_small = jnp.pad(
        jnp.stack([norm1_gain, norm1_bias, norm2_gain, norm2_bias]), ((0, SMALL_ROWS - 4), (0, 0))
    )
    narrow_small = jnp.stack(
        [pred_norm1_gain, pred_norm1_bias, pred_norm2_gain, pred_norm2_bias, mask_token]
    )
    here = (jnp.arange(narrow, dtype=jnp.int32) // narrow_part == me)[None, :]
    narrow_small = jnp.where(here, jnp.tile(narrow_small, (1, 8)), jnp.zeros((), BF16))
    narrow_small = jnp.pad(narrow_small, ((0, SMALL_ROWS - 5), (0, 0)))

    clip_ends = jnp.cumsum(clip_lengths[0])
    first_rows = lax.axis_index("seq") * rows + jnp.arange(rows, dtype=jnp.int32)
    past_end = (first_rows[:, None] >= clip_ends[None, :]).astype(jnp.int32)
    rel_rows = first_rows - jnp.sum(clip_lengths[0][None, :] * past_end, axis=1)
    matches = jnp.arange(rows, dtype=jnp.int32)[:, None] == target_pos[0, 0][None, :]
    hit_rows = jnp.sum(matches.astype(F32), axis=1)
    side = jnp.concatenate(
        [position_table(rel_rows, narrow), jnp.broadcast_to(hit_rows[:, None], (rows, LANES))], axis=1
    )
    ends = jnp.pad(jnp.broadcast_to(clip_ends[:, None], (3, LANES)), ((0, 5), (0, 0)))

    whole, kept, narrow_kept, rest, traded = forward_pass(
        tokens,
        out_grad,
        side,
        ends,
        [
            wide_small,
            narrow_small,
            w_qkv,
            w_out,
            w_fc1,
            w_fc2,
            w_embed,
            pred_qkv,
            pred_out,
            pred_fc1,
            pred_fc2,
        ],
        HEADS,
        P_HEADS,
    )
    context_t, entry, side, tokens = rest
    out_grad, ends, context_out, predicted, hidden_t, narrow_hidden_t = traded
    smalls = whole[0].reshape(8, SMALL_ROWS, LANES).astype(F32)
    norms = [smalls[:, i].reshape(-1) for i in range(4)]
    narrow_smalls = jnp.sum(whole[1].reshape(8, SMALL_ROWS, narrow).astype(F32), axis=0)
    pred_norms = [narrow_smalls[i] for i in range(4)]
    clip_ends = ends[:3, 0]
    query_clip = clip_index(quarter() * rows + jnp.arange(rows, dtype=jnp.int32), clip_ends)
    key_clip = clip_index(jnp.arange(4 * rows, dtype=jnp.int32), clip_ends)
    target_hit = side[:, narrow]

    grad_pred_in, pred_small, pred_grads = fast_backward(
        out_grad.astype(F32),
        entry,
        narrow_kept,
        narrow_hidden_t,
        pred_norms,
        whole[7],
        whole[8],
        whole[9],
        whole[10],
        P_HEADS,
        (query_clip, key_clip),
        5,
    )
    grad_mask = jnp.sum(target_hit[:, None] * grad_pred_in, axis=0)
    grad_embedded = (grad_pred_in * (1.0 - target_hit[:, None])).astype(BF16)
    grad_embed_w = chip_gradient(context_t, grad_embedded)
    grad_context = jnp.einsum("tp,dp->td", grad_embedded, whole[6], preferred_element_type=F32)
    grad_middle, grad_mixed, ctx_two, (grad_branch, grad_pre, grad_low) = back_to_mixed(
        grad_context, kept, norms, whole[3], whole[4], whole[5]
    )
    wide_grads = jnp.stack(ctx_two).reshape(2, 4, 2, wide_part)
    narrow_grads = jnp.pad(
        jnp.stack(pred_small + [grad_mask]).reshape(5, 4, 2, narrow_part),
        ((0, 0), (0, 0), (0, 0), (0, LANES - narrow_part)),
    )
    small_grads = jnp.concatenate([wide_grads, narrow_grads], axis=0).transpose(2, 1, 0, 3)
    mine = jnp.where(core == 0, small_grads[0], small_grads[1])
    other = jnp.where(core == 0, small_grads[1], small_grads[0])
    small_grads = jnp.pad(mine + swap_cores(other), ((0, 0), (0, SMALL_ROWS - 7), (0, 0)))

    normed_t, queries, keys_values, mixed, logs, _, normed_mid_t, _, mixed_t = kept
    results = back_and_sum(
        [pred_grads[3], pred_grads[2], pred_grads[1], pred_grads[0], grad_embed_w, small_grads.astype(BF16)],
        [hidden_t, normed_mid_t, mixed_t, normed_t],
        [grad_low, grad_pre, grad_branch],
        queries,
        keys_values.reshape(2, width // LANES, 4 * rows, LANES),
        mixed,
        grad_mixed,
        logs,
        query_clip,
        key_clip,
        whole[2].reshape(8, wide_part, 3 * width),
        tokens,
        grad_middle,
        norms[0],
        HEADS,
        6,
    )
    token_grad = results[-2]
    sums = [one.astype(F32) for one in results[:-2]]
    small_a, small_b = sums[5], sums[10]
    narrow_out = [small_a[2 + i, :narrow_part] for i in range(5)]
    return (
        context_out,
        predicted,
        token_grad,
        small_b[0],
        small_b[1],
        sums[9],
        sums[8],
        small_a[0],
        small_a[1],
        sums[7],
        sums[6],
        sums[4],
        narrow_out[4],
        narrow_out[0],
        narrow_out[1],
        sums[3],
        sums[2],
        narrow_out[2],
        narrow_out[3],
        sums[1],
        sums[0],
    )


def solution(mesh):
    body = fast_local if fits_fast(mesh) else local
    return jax.shard_map(
        body,
        mesh=mesh,
        in_specs=(
            P(("fsdp", "seq"), None),
            P("fsdp", None),
            P("fsdp", "seq", None),
            P(("fsdp", "seq"), None),
            P("fsdp"),
            P("fsdp"),
            P("fsdp", None),
            P("fsdp", None),
            P("fsdp"),
            P("fsdp"),
            P("fsdp", None),
            P("fsdp", None),
            P("fsdp", None),
            P("fsdp"),
            P("fsdp"),
            P("fsdp"),
            P("fsdp", None),
            P("fsdp", None),
            P("fsdp"),
            P("fsdp"),
            P("fsdp", None),
            P("fsdp", None),
        ),
        out_specs=(
            P(("fsdp", "seq"), None),
            P(("fsdp", "seq"), None),
            P(("fsdp", "seq"), None),
            P("fsdp"),
            P("fsdp"),
            P("fsdp", None),
            P("fsdp", None),
            P("fsdp"),
            P("fsdp"),
            P("fsdp", None),
            P("fsdp", None),
            P("fsdp", None),
            P("fsdp"),
            P("fsdp"),
            P("fsdp"),
            P("fsdp", None),
            P("fsdp", None),
            P("fsdp"),
            P("fsdp"),
            P("fsdp", None),
            P("fsdp", None),
        ),
        check_vma=False,
    )
```

```python
import math

import jax
import jax.numpy as jnp
from jax import lax
from jax.experimental import pallas as pl
from jax.experimental.pallas import tpu as pltpu
from jax.sharding import PartitionSpec as P

HEADS = 16
PD = 384
P_HEADS = 12


EPSILON = 1e-06
NEG_FILL = -1e30
block_rows = 512


def layer_norm(values, norm_gain, norm_shift):
    center = values - jnp.mean(values, axis=-1, keepdims=True)
    spread = jnp.mean(center * center, axis=-1, keepdims=True)
    return center * lax.rsqrt(spread + EPSILON) * norm_gain + norm_shift


def gelu_exact(values):
    return jax.nn.gelu(values, approximate=False)


def position_table(positions, table_width):
    half_width = table_width // 2
    angle_rates = jnp.exp(
        jnp.arange(half_width, dtype=jnp.float32) * (-2.0 * math.log(10000.0) / table_width)
    )
    angles = positions.astype(jnp.float32)[:, None] * angle_rates[None, :]
    return jnp.concatenate([jnp.sin(angles), jnp.cos(angles)], axis=1)


def clip_index(positions, clip_ends):
    return jnp.sum((positions[:, None] >= clip_ends[None, :]).astype(jnp.int32), axis=1)


def key_step(total_keys):
    return max(min(total_keys, block_rows), total_keys // 8)


def block_scores(queries, key_part, query_clip, key_clip_part, score_scale):
    raw_scores = (
        jnp.einsum("the,khe->htk", queries, key_part, preferred_element_type=jnp.float32)
        * score_scale
    )
    same_clip = query_clip[:, None] == key_clip_part[None, :]
    return jnp.where(same_clip[None], raw_scores, NEG_FILL)


def attend_forward(queries, key_heads, value_heads, query_clip, key_clip):
    row_count, head_count, head_size = queries.shape
    score_scale = head_size ** (-0.5)
    total_keys = key_heads.shape[0]
    step_rows = key_step(total_keys)
    run_max = jnp.full((head_count, row_count), NEG_FILL, jnp.float32)
    run_total = jnp.zeros((head_count, row_count), jnp.float32)
    for key_start in range(0, total_keys, step_rows):
        scores = block_scores(
            queries,
            key_heads[key_start : key_start + step_rows],
            query_clip,
            key_clip[key_start : key_start + step_rows],
            score_scale,
        )
        new_max = jnp.maximum(run_max, jnp.max(scores, axis=2))
        run_total = run_total * jnp.exp(run_max - new_max) + jnp.sum(
            jnp.exp(scores - new_max[:, :, None]), axis=2
        )
        run_max = new_max
    log_total = run_max + jnp.log(run_total)
    output = jnp.zeros((row_count, head_count, head_size), jnp.float32)
    for key_start in range(0, total_keys, step_rows):
        scores = block_scores(
            queries,
            key_heads[key_start : key_start + step_rows],
            query_clip,
            key_clip[key_start : key_start + step_rows],
            score_scale,
        )
        soft_weights = jnp.exp(scores - log_total[:, :, None]).astype(jnp.bfloat16)
        output = output + jnp.einsum(
            "htk,khe->the",
            soft_weights,
            value_heads[key_start : key_start + step_rows],
            preferred_element_type=jnp.float32,
        )
    return (output, log_total)


def attend_backward(
    queries, key_heads, value_heads, query_clip, key_clip, log_total, grad_mixed, output
):
    row_count, head_count, head_size = queries.shape
    score_scale = head_size ** (-0.5)
    total_keys = key_heads.shape[0]
    step_rows = key_step(total_keys)
    row_delta = jnp.sum(grad_mixed.astype(jnp.float32) * output, axis=2).T
    grad_query = jnp.zeros((row_count, head_count, head_size), jnp.float32)
    key_pieces = []
    value_pieces = []
    for key_start in range(0, total_keys, step_rows):
        key_part = key_heads[key_start : key_start + step_rows]
        value_part = value_heads[key_start : key_start + step_rows]
        scores = block_scores(
            queries, key_part, query_clip, key_clip[key_start : key_start + step_rows], score_scale
        )
        soft_weights = jnp.exp(scores - log_total[:, :, None])
        grad_soft = jnp.einsum(
            "the,khe->htk", grad_mixed, value_part, preferred_element_type=jnp.float32
        )
        grad_scores = (soft_weights * (grad_soft - row_delta[:, :, None])).astype(jnp.bfloat16)
        grad_query = grad_query + jnp.einsum(
            "htk,khe->the", grad_scores, key_part, preferred_element_type=jnp.float32
        )
        key_pieces.append(
            jnp.einsum("htk,the->khe", grad_scores, queries, preferred_element_type=jnp.float32)
        )
        value_pieces.append(
            jnp.einsum(
                "htk,the->khe",
                soft_weights.astype(jnp.bfloat16),
                grad_mixed,
                preferred_element_type=jnp.float32,
            )
        )
    key_terms = jnp.concatenate(key_pieces, axis=0) * score_scale
    value_terms = jnp.concatenate(value_pieces, axis=0)
    return (grad_query * score_scale, key_terms, value_terms)


def block_forward(
    residual, norm_params, w_qkv, w_out, w_up, w_down, head_count, query_clip, key_clip
):
    row_count, model_width = residual.shape
    head_size = model_width // head_count
    norm_float = norm_params.astype(jnp.float32)
    normed = layer_norm(residual, norm_float[:, 0], norm_float[:, 1]).astype(jnp.bfloat16)
    qkv = jnp.dot(normed, w_qkv, preferred_element_type=jnp.float32).astype(jnp.bfloat16)
    queries = qkv[:, :model_width].reshape(row_count, head_count, head_size)
    key_local = qkv[:, model_width : 2 * model_width]
    value_local = qkv[:, 2 * model_width :]
    key_full, value_full = (
        lax.all_gather(key_local, "seq", axis=0, tiled=True),
        lax.all_gather(value_local, "seq", axis=0, tiled=True),
    )
    key_heads = key_full.reshape(-1, head_count, head_size)
    value_heads = value_full.reshape(-1, head_count, head_size)
    output, log_total = attend_forward(queries, key_heads, value_heads, query_clip, key_clip)
    mixed = output.reshape(row_count, model_width).astype(jnp.bfloat16)
    middle = residual + jnp.dot(mixed, w_out, preferred_element_type=jnp.float32)
    normed_mid = layer_norm(middle, norm_float[:, 2], norm_float[:, 3]).astype(jnp.bfloat16)
    pre_act = jnp.dot(normed_mid, w_up, preferred_element_type=jnp.float32)
    hidden = gelu_exact(pre_act).astype(jnp.bfloat16)
    result = middle + jnp.dot(hidden, w_down, preferred_element_type=jnp.float32)
    kept = (
        residual,
        normed,
        queries,
        key_local,
        value_local,
        key_heads,
        value_heads,
        output,
        log_total,
        mixed,
        middle,
        normed_mid,
        pre_act,
        hidden,
    )
    return (result, kept)


def block_backward(
    grad_result, kept, norm_params, w_qkv, w_out, w_up, w_down, head_count, query_clip, key_clip
):
    (
        residual,
        normed,
        queries,
        key_local,
        value_local,
        key_heads,
        value_heads,
        output,
        log_total,
        mixed,
        middle,
        normed_mid,
        pre_act,
        hidden,
    ) = kept
    row_count, model_width = residual.shape
    head_size = model_width // head_count
    norm_float = norm_params.astype(jnp.float32)
    grad_low = grad_result.astype(jnp.bfloat16)
    grad_down = jnp.einsum("tf,tw->fw", hidden, grad_low, preferred_element_type=jnp.float32)
    grad_hidden = jnp.einsum("tw,fw->tf", grad_low, w_down, preferred_element_type=jnp.float32)
    gelu_value, gelu_pull = jax.vjp(gelu_exact, pre_act)
    grad_pre = gelu_pull(grad_hidden)[0].astype(jnp.bfloat16)
    grad_up = jnp.einsum("tw,tf->wf", normed_mid, grad_pre, preferred_element_type=jnp.float32)
    grad_normed_mid = jnp.einsum("tf,wf->tw", grad_pre, w_up, preferred_element_type=jnp.float32)
    second_value, second_pull = jax.vjp(layer_norm, middle, norm_float[:, 2], norm_float[:, 3])
    grad_mid_norm, grad_gain_two, grad_shift_two = second_pull(grad_normed_mid)
    grad_middle = grad_result + grad_mid_norm
    grad_branch = grad_middle.astype(jnp.bfloat16)
    grad_out_w = jnp.einsum("tv,tw->vw", mixed, grad_branch, preferred_element_type=jnp.float32)
    grad_mixed = jnp.einsum(
        "tw,vw->tv", grad_branch, w_out, preferred_element_type=jnp.float32
    ).astype(jnp.bfloat16)
    key_full, value_full = (
        lax.all_gather(key_local, "seq", axis=0, tiled=True),
        lax.all_gather(value_local, "seq", axis=0, tiled=True),
    )
    key_heads = key_full.reshape(-1, head_count, head_size)
    value_heads = value_full.reshape(-1, head_count, head_size)
    grad_query, key_terms, value_terms = attend_backward(
        queries,
        key_heads,
        value_heads,
        query_clip,
        key_clip,
        log_total,
        grad_mixed.reshape(row_count, head_count, head_size),
        output,
    )
    grad_key, grad_value = (
        lax.psum_scatter(
            key_terms.reshape(-1, model_width).astype(jnp.bfloat16),
            "seq",
            scatter_dimension=0,
            tiled=True,
        ).astype(jnp.float32),
        lax.psum_scatter(
            value_terms.reshape(-1, model_width).astype(jnp.bfloat16),
            "seq",
            scatter_dimension=0,
            tiled=True,
        ).astype(jnp.float32),
    )
    grad_qkv = jnp.concatenate(
        [grad_query.reshape(row_count, model_width), grad_key, grad_value], axis=1
    ).astype(jnp.bfloat16)
    grad_qkv_w = jnp.einsum("tw,tc->wc", normed, grad_qkv, preferred_element_type=jnp.float32)
    grad_normed = jnp.einsum("tc,wc->tw", grad_qkv, w_qkv, preferred_element_type=jnp.float32)
    first_value, first_pull = jax.vjp(layer_norm, residual, norm_float[:, 0], norm_float[:, 1])
    grad_first_norm, grad_gain_one, grad_shift_one = first_pull(grad_normed)
    grad_norms = jnp.stack([grad_gain_one, grad_shift_one, grad_gain_two, grad_shift_two], axis=1)
    return (grad_middle + grad_first_norm, (grad_norms, grad_qkv_w, grad_out_w, grad_up, grad_down))


def local(
    tokens,
    clip_lengths,
    target_pos,
    out_grad,
    norm1_gain,
    norm1_bias,
    w_qkv,
    w_out,
    norm2_gain,
    norm2_bias,
    w_fc1,
    w_fc2,
    w_embed,
    mask_token,
    pred_norm1_gain,
    pred_norm1_bias,
    pred_qkv,
    pred_out,
    pred_norm2_gain,
    pred_norm2_bias,
    pred_fc1,
    pred_fc2,
):
    row_count = tokens.shape[0]
    group_count = row_count * lax.axis_size("seq")
    lengths = clip_lengths[0]
    clip_ends = jnp.cumsum(lengths)
    local_rows = lax.axis_index("seq") * row_count + jnp.arange(row_count, dtype=jnp.int32)
    query_clip = clip_index(local_rows, clip_ends)
    key_clip = clip_index(jnp.arange(group_count, dtype=jnp.int32), clip_ends)
    past_end = (local_rows[:, None] >= clip_ends[None, :]).astype(jnp.int32)
    rel_rows = local_rows - jnp.sum(lengths[None, :] * past_end, axis=1)
    ctx_small = jnp.stack([norm1_gain, norm1_bias, norm2_gain, norm2_bias], axis=1)
    pred_small = jnp.stack(
        [pred_norm1_gain, pred_norm1_bias, pred_norm2_gain, pred_norm2_bias, mask_token], axis=1
    )
    ctx_params = (
        lax.all_gather(ctx_small, "fsdp", axis=0, tiled=True),
        lax.all_gather(w_qkv, "fsdp", axis=0, tiled=True),
        lax.all_gather(w_out, "fsdp", axis=0, tiled=True),
        lax.all_gather(w_fc1, "fsdp", axis=0, tiled=True),
        lax.all_gather(w_fc2, "fsdp", axis=0, tiled=True),
    )
    pred_params = (
        lax.all_gather(pred_small, "fsdp", axis=0, tiled=True),
        lax.all_gather(w_embed, "fsdp", axis=0, tiled=True),
        lax.all_gather(pred_qkv, "fsdp", axis=0, tiled=True),
        lax.all_gather(pred_out, "fsdp", axis=0, tiled=True),
        lax.all_gather(pred_fc1, "fsdp", axis=0, tiled=True),
        lax.all_gather(pred_fc2, "fsdp", axis=0, tiled=True),
    )
    ctx_result, ctx_kept = block_forward(
        tokens.astype(jnp.float32),
        ctx_params[0],
        ctx_params[1],
        ctx_params[2],
        ctx_params[3],
        ctx_params[4],
        HEADS,
        query_clip,
        key_clip,
    )
    context_out = ctx_result.astype(jnp.bfloat16)
    embedded = jnp.dot(context_out, pred_params[1], preferred_element_type=jnp.float32)
    targets = target_pos[0, 0]
    matches = jnp.arange(row_count, dtype=jnp.int32)[:, None] == targets[None, :]
    placement = matches.astype(jnp.float32)
    target_hit = jnp.sum(placement, axis=1)
    target_rel = jnp.sum(jnp.where(matches, rel_rows[:, None], 0), axis=0)
    mask_rows = pred_params[0][:, 4].astype(jnp.float32)[None, :] + position_table(target_rel, PD)
    placed = jnp.dot(
        placement, mask_rows, precision=lax.Precision.HIGHEST, preferred_element_type=jnp.float32
    )
    pred_in = embedded * (1.0 - target_hit[:, None]) + placed
    pred_result, pred_kept = block_forward(
        pred_in,
        pred_params[0],
        pred_params[2],
        pred_params[3],
        pred_params[4],
        pred_params[5],
        P_HEADS,
        query_clip,
        key_clip,
    )
    predicted = pred_result.astype(jnp.bfloat16)
    pred_back = (
        lax.all_gather(pred_small, "fsdp", axis=0, tiled=True),
        lax.all_gather(w_embed, "fsdp", axis=0, tiled=True),
        lax.all_gather(pred_qkv, "fsdp", axis=0, tiled=True),
        lax.all_gather(pred_out, "fsdp", axis=0, tiled=True),
        lax.all_gather(pred_fc1, "fsdp", axis=0, tiled=True),
        lax.all_gather(pred_fc2, "fsdp", axis=0, tiled=True),
    )
    ctx_back = (
        lax.all_gather(ctx_small, "fsdp", axis=0, tiled=True),
        lax.all_gather(w_qkv, "fsdp", axis=0, tiled=True),
        lax.all_gather(w_out, "fsdp", axis=0, tiled=True),
        lax.all_gather(w_fc1, "fsdp", axis=0, tiled=True),
        lax.all_gather(w_fc2, "fsdp", axis=0, tiled=True),
    )
    grad_pred_in, pred_grads = block_backward(
        out_grad.astype(jnp.float32),
        pred_kept,
        pred_back[0],
        pred_back[2],
        pred_back[3],
        pred_back[4],
        pred_back[5],
        P_HEADS,
        query_clip,
        key_clip,
    )
    grad_mask = jnp.sum(target_hit[:, None] * grad_pred_in, axis=0)
    grad_embedded = (grad_pred_in * (1.0 - target_hit[:, None])).astype(jnp.bfloat16)
    grad_embed_w = jnp.einsum(
        "td,tp->dp", context_out, grad_embedded, preferred_element_type=jnp.float32
    )
    grad_context = jnp.einsum(
        "tp,dp->td", grad_embedded, pred_back[1], preferred_element_type=jnp.float32
    )
    grad_tokens, ctx_grads = block_backward(
        grad_context,
        ctx_kept,
        ctx_back[0],
        ctx_back[1],
        ctx_back[2],
        ctx_back[3],
        ctx_back[4],
        HEADS,
        query_clip,
        key_clip,
    )
    pred_small_grad = jnp.concatenate([pred_grads[0], grad_mask[:, None]], axis=1)
    row_sums = (
        lax.psum_scatter(ctx_grads[0], "fsdp", scatter_dimension=0, tiled=True),
        lax.psum_scatter(ctx_grads[1], "fsdp", scatter_dimension=0, tiled=True),
        lax.psum_scatter(ctx_grads[2], "fsdp", scatter_dimension=0, tiled=True),
        lax.psum_scatter(ctx_grads[3], "fsdp", scatter_dimension=0, tiled=True),
        lax.psum_scatter(ctx_grads[4], "fsdp", scatter_dimension=0, tiled=True),
        lax.psum_scatter(grad_embed_w, "fsdp", scatter_dimension=0, tiled=True),
        lax.psum_scatter(pred_small_grad, "fsdp", scatter_dimension=0, tiled=True),
        lax.psum_scatter(pred_grads[1], "fsdp", scatter_dimension=0, tiled=True),
        lax.psum_scatter(pred_grads[2], "fsdp", scatter_dimension=0, tiled=True),
        lax.psum_scatter(pred_grads[3], "fsdp", scatter_dimension=0, tiled=True),
        lax.psum_scatter(pred_grads[4], "fsdp", scatter_dimension=0, tiled=True),
    )
    summed = (
        lax.psum(row_sums[0].astype(jnp.bfloat16), "seq").astype(jnp.float32),
        lax.psum(row_sums[1].astype(jnp.bfloat16), "seq").astype(jnp.float32),
        lax.psum(row_sums[2].astype(jnp.bfloat16), "seq").astype(jnp.float32),
        lax.psum(row_sums[3].astype(jnp.bfloat16), "seq").astype(jnp.float32),
        lax.psum(row_sums[4].astype(jnp.bfloat16), "seq").astype(jnp.float32),
        lax.psum(row_sums[5].astype(jnp.bfloat16), "seq").astype(jnp.float32),
        lax.psum(row_sums[6].astype(jnp.bfloat16), "seq").astype(jnp.float32),
        lax.psum(row_sums[7].astype(jnp.bfloat16), "seq").astype(jnp.float32),
        lax.psum(row_sums[8].astype(jnp.bfloat16), "seq").astype(jnp.float32),
        lax.psum(row_sums[9].astype(jnp.bfloat16), "seq").astype(jnp.float32),
        lax.psum(row_sums[10].astype(jnp.bfloat16), "seq").astype(jnp.float32),
    )
    return (
        context_out,
        predicted,
        grad_tokens.astype(jnp.bfloat16),
        summed[0][:, 0],
        summed[0][:, 1],
        summed[1],
        summed[2],
        summed[0][:, 2],
        summed[0][:, 3],
        summed[3],
        summed[4],
        summed[5],
        summed[6][:, 4],
        summed[6][:, 0],
        summed[6][:, 1],
        summed[7],
        summed[8],
        summed[6][:, 2],
        summed[6][:, 3],
        summed[9],
        summed[10],
    )


BF16 = jnp.bfloat16
F32 = jnp.float32
MESH = pl.DeviceIdType.MESH
LOG2E = 1.4426950408889634
LN2 = 0.6931471805599453
LANES = 128
SMALL_ROWS = 16
ANYWHERE = pl.BlockSpec(memory_space=pl.ANY)
IN_VMEM = pl.BlockSpec(memory_space=pltpu.VMEM)


def fits_fast(mesh):
    return mesh.shape["fsdp"] == 8 and mesh.shape["seq"] == 4


def fsdp_peer(bit):
    return (lax.axis_index("fsdp") ^ bit, lax.axis_index("seq"))


def seq_peer(index):
    return (lax.axis_index("fsdp"), index)


def enter(peers):
    barrier = pltpu.get_barrier_semaphore()
    for peer in peers:
        pl.semaphore_signal(barrier, inc=1, device_id=peer, device_id_type=MESH)
    pl.semaphore_wait(barrier, len(peers))


def send(src, dst, send_sem, recv_sem, peer):
    return pltpu.make_async_remote_copy(
        src_ref=src,
        dst_ref=dst,
        send_sem=send_sem,
        recv_sem=recv_sem,
        device_id=peer,
        device_id_type=MESH,
    )


def remote_params(collective_id, vmem=None):
    return pltpu.CompilerParams(
        collective_id=collective_id, has_side_effects=True, vmem_limit_bytes=vmem
    )


def mate_z():
    return seq_peer(lax.axis_index("seq") ^ 1)


def quarter():
    return (lax.axis_index("fsdp") & 1) * 2 + (lax.axis_index("seq") & 1)


def across_lanes(left, right):
    return lax.dot_general(left, right, (((1,), (1,)), ((), ())), preferred_element_type=F32)


def forward_pass(tokens, out_grad, side, ends, shards, heads, narrow_heads):
    rows, width = tokens.shape
    narrow = out_grad.shape[1]
    hidden_width = shards[4].shape[1]
    narrow_hidden = shards[9].shape[1]
    shapes = [shard.shape for shard in shards]
    array_count = len(shards)
    units = []
    for index, (shard_rows, columns) in enumerate(shapes):
        if shard_rows * columns >= 100000:
            half = shard_rows // 2
            units.append((index, 0, half, 2, 4))
            units.append((index, half, half, 4, 2))
        else:
            near, far = (2, 4) if len(units) % 2 == 0 else (4, 2)
            units.append((index, 0, shard_rows, near, far))
    count = len(units)
    ahead = 3
    last_unit = {}
    for u, unit in enumerate(units):
        last_unit[unit[0]] = u

    block_widths = ((width, heads, hidden_width, 2), (narrow, narrow_heads, narrow_hidden, 1))
    saved_shapes = []
    for w, _, ff, _ in block_widths:
        saved_shapes += [
            ((w, rows), BF16),
            ((rows, w), BF16),
            ((2, w // LANES, 4, rows, LANES), BF16),
            ((rows, w), BF16),
            ((w // LANES, 8, rows), F32),
            ((rows, w), F32),
            ((w, rows), BF16),
            ((rows, ff), BF16),
            ((w, rows), BF16),
        ]
    per_block = len(saved_shapes) // 2
    saved_shapes += [((width, rows), BF16), ((rows, narrow), F32), (side.shape, F32), ((rows, width), BF16)]
    saved_shapes += [((SMALL_ROWS, width), F32), ((SMALL_ROWS, narrow), F32)]
    saved_count = len(saved_shapes)

    def kernel(*refs):
        tokens_ref, out_grad_ref, side_ref, ends_ref = refs[:4]
        sources = refs[4 : 4 + array_count]
        base = 4 + array_count
        weight_outs = refs[base : base + array_count]
        base += array_count
        saved_outs = refs[base : base + saved_count]
        base += saved_count
        out_grad_out, ends_out, context_out, predicted_out, wide_hidden_t, narrow_hidden_t = refs[base : base + 6]
        base += 6
        weights = refs[base : base + array_count]
        base += array_count
        saved = refs[base : base + saved_count]
        base += saved_count
        (
            bias,
            ends_buf,
            predicted,
            wide_normed,
            wide_hidden,
            narrow_normed,
            narrow_hid,
            stage,
            stage_sems,
            send_sems,
            recv_sems,
            local_sems,
            weight_sems,
            saved_sems,
            trade_send,
            trade_recv,
            trade_keep,
            key_send,
            key_recv,
        ) = refs[base:]
        context_t, entry, side_buf, token_buf, gains, narrow_gains = saved[2 * per_block :]
        context = wide_normed

        me = lax.axis_index("fsdp")
        place = lax.axis_index("seq")
        core = me & 1
        high = place >> 1
        low = place & 1
        mine = quarter()
        trades = core != high
        trade_peer = ((me & 6) | high, core * 2 + low)

        barrier = pltpu.get_barrier_semaphore()
        for peer in (fsdp_peer(1), fsdp_peer(2), fsdp_peer(4), mate_z()):
            pl.semaphore_signal(barrier, inc=1, device_id=peer, device_id_type=MESH)

        @pl.when(trades)
        def _():
            pl.semaphore_signal(barrier, inc=1, device_id=trade_peer, device_id_type=MESH)

        pl.semaphore_wait(barrier, 4 + trades.astype(jnp.int32))


        def trade_copy(i, src, dst):
            return send(src, dst, trade_send.at[i], trade_recv.at[i], trade_peer)

        def keep_copy(i, src, dst):
            return pltpu.make_async_copy(src, dst, trade_keep.at[i])

        traded = [
            (tokens_ref, token_buf),
            (side_ref, side_buf),
            (ends_ref, ends_buf),
            (out_grad_ref, out_grad_out),
            (context, context_out),
            (predicted, predicted_out),
        ]

        def trade_start(i):
            @pl.when(trades)
            def _():
                trade_copy(i, *traded[i]).start()

            @pl.when(jnp.logical_not(trades))
            def _():
                keep_copy(i, *traded[i]).start()

        def trade_arrived(i):
            @pl.when(trades)
            def _():
                trade_copy(i, *traded[i]).wait_recv()

            @pl.when(jnp.logical_not(trades))
            def _():
                keep_copy(i, *traded[i]).wait()

        def trade_sent(i):
            @pl.when(trades)
            def _():
                trade_copy(i, *traded[i]).wait_send()


        def place_of(u, owner):
            index, first, unit_rows, _, _ = units[u]
            start = owner * shapes[index][0] + first
            return weights[index].at[pl.ds(pl.multiple_of(start, 16), unit_rows)]

        def own_shard(u):
            index, first, unit_rows, _, _ = units[u]
            return sources[index].at[pl.ds(first, unit_rows)]

        def weight_copy(u, slot):
            _, _, _, near, far = units[u]
            owner = me ^ (0, 0, near, 0, near, far, near ^ far)[slot]
            bit = (near, far, far, 1, 1, 1, 1)[slot]
            src = own_shard(u) if slot in (0, 1, 3) else place_of(u, owner)
            return send(src, place_of(u, owner), send_sems.at[u, slot], recv_sems.at[u, slot], fsdp_peer(bit))

        def own_weight(u):
            return pltpu.make_async_copy(own_shard(u), place_of(u, me), local_sems.at[u])

        def weight_out(index):
            return pltpu.make_async_copy(weights[index], weight_outs[index], weight_sems.at[index])

        def launch(u):
            for slot in (0, 1, 3):
                weight_copy(u, slot).start()
            own_weight(u).start()

        def arrive(u):
            weight_copy(u, 0).wait_recv()
            weight_copy(u, 2).start()
            weight_copy(u, 4).start()
            weight_copy(u, 1).wait_recv()
            weight_copy(u, 5).start()
            if u + ahead < count:
                launch(u + ahead)

        def relay(u):
            weight_copy(u, 2).wait_recv()
            weight_copy(u, 6).start()

        def complete(u):
            for slot in (3, 4, 5, 6):
                weight_copy(u, slot).wait_recv()
            own_weight(u).wait()
            index = units[u][0]
            if last_unit[index] == u:
                weight_out(index).start()

        ticks = []
        ready = {}
        for u in range(count + 2):
            if u < count:
                ticks.append((arrive, u))
            if 1 <= u <= count:
                ticks.append((relay, u - 1))
            if u >= 2:
                ticks.append((complete, u - 2))
                ready[units[u - 2][0]] = len(ticks)
        position = [0]

        def advance(steps):
            for _ in range(steps):
                if position[0] < len(ticks):
                    step, u = ticks[position[0]]
                    step(u)
                    position[0] += 1

        def need(index):
            while position[0] < ready[index]:
                advance(1)


        def save(i):
            return pltpu.make_async_copy(saved[i], saved_outs[i], saved_sems.at[i])

        def norm_into(dst, get, table, gain_at):
            @pl.loop(0, rows // 64)
            def _(i):
                part = pl.ds(pl.multiple_of(i * 64, 64), 64)
                value = get(part)
                value = value - jnp.mean(value, axis=1, keepdims=True)
                inverse = lax.rsqrt(jnp.mean(value * value, axis=1, keepdims=True) + EPSILON)
                dst[part] = (
                    value * inverse * table[gain_at : gain_at + 1, :] + table[gain_at + 1 : gain_at + 2, :]
                ).astype(BF16)

        def turn(src, dst):
            for c in range(dst.shape[0] // LANES):
                at = slice(c * LANES, (c + 1) * LANES)
                dst[at, :] = src[:, at].T

        def run_block(which, get, table, first_weight, finish, inside):
            w, head_count, ff, in_group = block_widths[which]
            (normed_t, queries, kv, mixed, logs, middle, normed_mid_t, slope, mixed_t) = saved[
                which * per_block : (which + 1) * per_block
            ]
            normed, hidden = ((wide_normed, wide_hidden), (narrow_normed, narrow_hid))[which]
            hidden_out = (wide_hidden_t, narrow_hidden_t)[which]
            w_qkv, w_out, w_up, w_down = [weights[first_weight[i]] for i in range(4)]
            slabs = w // LANES
            groups = slabs // in_group
            head_size = w // head_count
            per_slab = LANES // head_size
            factor = head_size ** (-0.5) * LOG2E
            columns = in_group * LANES

            def kv_copy(kind, g):
                owner = mine ^ 1 if kind == 2 else mine
                part = kv.at[:, pl.ds(g * in_group, in_group), owner]
                return send(
                    part,
                    part,
                    key_send.at[which, kind, g],
                    key_recv.at[which, kind, g],
                    mate_z() if kind == 0 else fsdp_peer(1),
                )

            norm_into(normed, get, table, 0)
            turn(normed, normed_t)
            save(which * per_block).start()
            need(first_weight[0])
            for g in range(groups):
                for kind in range(2):
                    tile = jnp.dot(
                        normed[...],
                        w_qkv[:, pl.ds((1 + kind) * w + g * columns, columns)],
                        preferred_element_type=F32,
                    ).astype(BF16)
                    for k in range(in_group):
                        kv[kind, g * in_group + k, mine] = tile[:, k * LANES : (k + 1) * LANES]
                kv_copy(0, g).start()
                kv_copy(1, g).start()
            for g in range(groups):
                at = pl.ds(g * columns, columns)
                queries[:, at] = jnp.dot(normed[...], w_qkv[:, at], preferred_element_type=F32).astype(BF16)
            save(which * per_block + 1).start()
            advance(inside[0])
            kv_copy(0, 0).wait_recv()
            kv_copy(2, 0).start()

            lane = lax.broadcasted_iota(jnp.int32, (rows, LANES), 1) // head_size
            sub = lax.broadcasted_iota(jnp.int32, (LANES, rows), 0) // head_size

            @pl.loop(0, slabs)
            def _(j):
                g = j // in_group

                @pl.when(j % in_group == 0)
                def _():
                    kv_copy(1, g).wait_recv()
                    kv_copy(2, g).wait_recv()

                at = pl.ds(pl.multiple_of(j * LANES, LANES), LANES)
                own_queries = queries[:, at]
                key_slab = kv[0, j].reshape(4 * rows, LANES)
                values_t = kv[1, j].reshape(4 * rows, LANES).T
                output = jnp.zeros((LANES, rows), F32)
                logs[j] = jnp.zeros((8, rows), F32)
                for head in range(per_slab):
                    own = jnp.where(lane == head, own_queries, jnp.zeros_like(own_queries))
                    scores = across_lanes(key_slab, own) * factor + bias[...]
                    top = jnp.max(scores, axis=0, keepdims=True)
                    soft = jnp.exp2(scores - top)
                    total = jnp.sum(soft, axis=0, keepdims=True)
                    attended = jnp.dot(values_t, soft.astype(BF16), preferred_element_type=F32) / total
                    output = jnp.where(sub == head, attended, output)
                    logs[j, head : head + 1, :] = top + jnp.log2(total)
                mixed[:, at] = output.T.astype(BF16)
                mixed_t[at, :] = output.astype(BF16)

                @pl.when(jnp.logical_and(j % in_group == 0, g + 1 < groups))
                def _():
                    kv_copy(0, g + 1).wait_recv()
                    kv_copy(2, g + 1).start()

                for k in range(slabs):

                    @pl.when(j == k)
                    def _():
                        advance(inside[1])

            for i in (2, 3, 4, 8):
                save(which * per_block + i).start()
            need(first_weight[1])
            step = 2 * LANES if w % (2 * LANES) == 0 else LANES
            for c in range(w // step):
                at = pl.ds(c * step, step)
                middle[:, at] = get(pl.ds(0, rows), at) + jnp.dot(
                    mixed[...], w_out[:, at], preferred_element_type=F32
                )
            save(which * per_block + 5).start()
            norm_into(normed, lambda part: middle[part], table, 2)
            turn(normed, normed_mid_t)
            save(which * per_block + 6).start()
            need(first_weight[2])

            def stage_copy(c):
                return pltpu.make_async_copy(
                    stage.at[c % 2],
                    hidden_out.at[pl.ds(pl.multiple_of(c * 2 * LANES, 2 * LANES), 2 * LANES)],
                    stage_sems.at[c % 2],
                )

            @pl.loop(0, ff // (2 * LANES))
            def _(c):
                at = pl.ds(pl.multiple_of(c * 2 * LANES, 2 * LANES), 2 * LANES)
                pre = jnp.dot(normed[...], w_up[:, at], preferred_element_type=F32)
                below = 0.5 * (1.0 + lax.erf(pre * (0.5**0.5)))
                bell = jnp.exp2(pre * pre * (-0.5 * LOG2E)) * (1.0 / math.sqrt(2.0 * math.pi))
                active = (pre * below).astype(BF16)
                hidden[:, at] = active
                slope[:, at] = (below + pre * bell).astype(BF16)

                @pl.when(c >= 2)
                def _():
                    stage_copy(c - 2).wait()

                stage[c % 2] = active.T
                stage_copy(c).start()

            stage_copy(ff // (2 * LANES) - 2).wait()
            stage_copy(ff // (2 * LANES) - 1).wait()
            save(which * per_block + 7).start()
            need(first_weight[3])
            for c in range(w // step):
                at = pl.ds(c * step, step)
                finish(
                    at, middle[:, at] + jnp.dot(hidden[...], w_down[:, at], preferred_element_type=F32)
                )
            for g in range(groups):
                for kind in range(3):
                    kv_copy(kind, g).wait_send()


        for i in (0, 2, 1):
            trade_start(i)
        for u in range(ahead):
            launch(u)
        trade_start(3)
        need(1)
        for owner in range(8):
            gains[:, owner * LANES : (owner + 1) * LANES] = weights[0][
                owner * SMALL_ROWS : (owner + 1) * SMALL_ROWS, :
            ].astype(F32)
        total = weights[1][0:SMALL_ROWS, :].astype(F32)
        for owner in range(1, 8):
            total = total + weights[1][owner * SMALL_ROWS : (owner + 1) * SMALL_ROWS, :].astype(F32)
        narrow_gains[...] = total
        save(2 * per_block + 4).start()
        save(2 * per_block + 5).start()
        trade_arrived(2)
        group_bias(bias, ends_buf, rows)
        trade_arrived(0)
        save(2 * per_block + 3).start()

        def token_rows(part, at=slice(None)):
            return token_buf[part, at].astype(F32)

        def finish_context(at, value):
            context[:, at] = value.astype(BF16)

        run_block(0, token_rows, gains, (2, 3, 4, 5), finish_context, (1, 1))
        trade_start(4)
        turn(context, context_t)
        save(2 * per_block).start()
        need(6)
        trade_arrived(1)
        save(2 * per_block + 2).start()
        embedded = jnp.dot(context[...], weights[6][...], preferred_element_type=F32)
        hit = side_buf[:, narrow : narrow + 1]
        entry[...] = jnp.where(hit > 0.0, narrow_gains[4:5, :] + side_buf[:, 0:narrow], embedded)
        save(2 * per_block + 1).start()

        def entry_rows(part, at=slice(None)):
            return entry[part, at]

        def finish_predicted(at, value):
            predicted[:, at] = value.astype(BF16)

        run_block(1, entry_rows, narrow_gains, (7, 8, 9, 10), finish_predicted, (0, 0))
        trade_start(5)
        advance(len(ticks))
        for u in range(count):
            for slot in range(7):
                weight_copy(u, slot).wait_send()
        for index in range(array_count):
            weight_out(index).wait()
        for i in range(saved_count):
            save(i).wait()
        keep_copy(6, ends_buf, ends_out).start()
        for i in (3, 4, 5):
            trade_arrived(i)
        for i in range(6):
            trade_sent(i)
        keep_copy(6, ends_buf, ends_out).wait()

    gathered = [(8 * shape[0], shape[1]) for shape in shapes]
    out_shape = (
        [jax.ShapeDtypeStruct(shape, BF16) for shape in gathered]
        + [jax.ShapeDtypeStruct(shape, kind) for shape, kind in saved_shapes]
        + [
            jax.ShapeDtypeStruct(out_grad.shape, BF16),
            jax.ShapeDtypeStruct(ends.shape, jnp.int32),
            jax.ShapeDtypeStruct((rows, width), BF16),
            jax.ShapeDtypeStruct((rows, narrow), BF16),
            jax.ShapeDtypeStruct((hidden_width, rows), BF16),
            jax.ShapeDtypeStruct((narrow_hidden, rows), BF16),
        ]
    )
    scratch = (
        [pltpu.VMEM(shape, BF16) for shape in gathered]
        + [pltpu.VMEM(shape, kind) for shape, kind in saved_shapes]
        + [
            pltpu.VMEM((4 * rows, rows), F32),
            pltpu.VMEM(ends.shape, jnp.int32),
            pltpu.VMEM((rows, narrow), BF16),
            pltpu.VMEM((rows, width), BF16),
            pltpu.VMEM((rows, hidden_width), BF16),
            pltpu.VMEM((rows, narrow), BF16),
            pltpu.VMEM((rows, narrow_hidden), BF16),
            pltpu.VMEM((2, 2 * LANES, rows), BF16),
            pltpu.SemaphoreType.DMA((2,)),
            pltpu.SemaphoreType.DMA((count, 7)),
            pltpu.SemaphoreType.DMA((count, 7)),
            pltpu.SemaphoreType.DMA((count,)),
            pltpu.SemaphoreType.DMA((array_count,)),
            pltpu.SemaphoreType.DMA((saved_count,)),
            pltpu.SemaphoreType.DMA((6,)),
            pltpu.SemaphoreType.DMA((6,)),
            pltpu.SemaphoreType.DMA((7,)),
            pltpu.SemaphoreType.DMA((2, 3, 4)),
            pltpu.SemaphoreType.DMA((2, 3, 4)),
        ]
    )
    results = pl.pallas_call(
        kernel,
        out_shape=out_shape,
        in_specs=[ANYWHERE] * (4 + array_count),
        out_specs=[ANYWHERE] * len(out_shape),
        scratch_shapes=scratch,
        compiler_params=remote_params(1, 62 << 20),
        name="forward_pass",
    )(tokens, out_grad, side, ends, *shards)
    saved = results[array_count : array_count + saved_count]
    return (
        results[:array_count],
        saved[:per_block],
        saved[per_block : 2 * per_block],
        saved[2 * per_block :],
        results[array_count + saved_count :],
    )


def group_bias(bias, ends, rows):
    mine = quarter()
    key_row = lax.broadcasted_iota(jnp.int32, (4 * rows, rows), 0)
    query_row = mine * rows + lax.broadcasted_iota(jnp.int32, (4 * rows, rows), 1)
    key_clip = jnp.zeros((4 * rows, rows), jnp.int32)
    query_clip = jnp.zeros((4 * rows, rows), jnp.int32)
    for c in range(3):
        end = ends[c : c + 1, 0:1]
        key_clip = key_clip + (key_row >= end).astype(jnp.int32)
        query_clip = query_clip + (query_row >= end).astype(jnp.int32)
    bias[...] = jnp.where(key_clip == query_clip, 0.0, NEG_FILL)


def slab_backward(queries, grads, mixed, logs, key_slab, value_slab, bias, head_size):
    rows = queries.shape[0]
    keys = key_slab.shape[0]
    factor = head_size ** (-0.5) * LOG2E
    lane = lax.broadcasted_iota(jnp.int32, (rows, LANES), 1) // head_size
    key_lane = lax.broadcasted_iota(jnp.int32, (keys, LANES), 1) // head_size
    sub = lax.broadcasted_iota(jnp.int32, (LANES, rows), 0) // head_size
    pick = (
        lax.broadcasted_iota(jnp.int32, (8, LANES), 1) // head_size
        == lax.broadcasted_iota(jnp.int32, (8, LANES), 0)
    ).astype(F32)
    deltas = lax.dot_general(
        pick,
        grads.astype(F32) * mixed.astype(F32),
        (((1,), (1,)), ((), ())),
        precision=lax.Precision.HIGHEST,
        preferred_element_type=F32,
    )
    keys_t = key_slab.T
    dq = jnp.zeros((LANES, rows), F32)
    dk = jnp.zeros((keys, LANES), F32)
    dv = jnp.zeros((keys, LANES), F32)
    for head in range(LANES // head_size):
        own = jnp.where(lane == head, queries, jnp.zeros_like(queries))
        own_grad = jnp.where(lane == head, grads, jnp.zeros_like(grads))
        scores = across_lanes(key_slab, own) * factor + bias[...]
        weights = jnp.exp2(scores - logs[head : head + 1, :])
        grad_soft = across_lanes(value_slab, own_grad)
        grad_scores = (weights * (grad_soft - deltas[head : head + 1, :])).astype(BF16)
        dv = jnp.where(key_lane == head, jnp.dot(weights.astype(BF16), grads, preferred_element_type=F32), dv)
        dk = jnp.where(key_lane == head, jnp.dot(grad_scores, queries, preferred_element_type=F32), dk)
        dq = jnp.where(sub == head, jnp.dot(keys_t, grad_scores, preferred_element_type=F32), dq)
    return dq, dk, dv


def norm_backward(value, upper, gain_row):
    value = value - jnp.mean(value, axis=1, keepdims=True)
    inverse = lax.rsqrt(jnp.mean(value * value, axis=1, keepdims=True) + EPSILON)
    value = value * inverse
    scaled = upper * gain_row
    inside = (
        scaled
        - jnp.mean(scaled, axis=1, keepdims=True)
        - value * jnp.mean(scaled * value, axis=1, keepdims=True)
    )
    return (
        inverse * inside,
        jnp.sum(upper * value, axis=0, keepdims=True),
        jnp.sum(upper, axis=0, keepdims=True),
    )


def middle_back(loads, lefts_t, head_count, collective_id):
    names = list(loads)
    rows, narrow = loads["out_grad"].shape
    width = loads["wide_middle"].shape[1]
    narrow_hidden = loads["narrow_slope"].shape[1]
    wide_hidden = loads["wide_slope"].shape[1]
    slabs = narrow // LANES
    head_size = narrow // head_count
    scale = head_size ** (-0.5)
    keys = 4 * rows
    half = 2 * rows
    sizes = [left.shape[0] // 8 for left in lefts_t]
    right_widths = [narrow, narrow_hidden, narrow, 3 * narrow, narrow]
    grads = len(lefts_t)

    def kernel(*refs):
        load_refs = dict(zip(names, refs[: len(names)]))
        left_refs = refs[len(names) : len(names) + grads]
        base = len(names) + grads
        partials_out = refs[base : base + grads]
        low_out, pre_out, branch_out, middle_out, mixed_out, wide_sums_out, narrow_sums_out = refs[
            base + grads : base + grads + 7
        ]
        base += grads + 7
        bufs = dict(zip(names, refs[base : base + len(names)]))
        base += len(names)
        lefts = refs[base : base + grads]
        rights = refs[base + grads : base + 2 * grads]
        partials = refs[base + 2 * grads : base + 3 * grads]
        base += 3 * grads
        (
            bias,
            dkv,
            core_in,
            z_in,
            upper,
            grad_middle,
            grad_mixed,
            wide_low,
            wide_pre,
            wide_upper,
            wide_branch,
            wide_mixed,
            wide_sums,
            narrow_sums,
            load_sems,
            give_send,
            give_recv,
            give_own,
            right_send,
            right_recv,
            key_send,
            key_recv,
            out_sems,
        ) = refs[base:]
        me = lax.axis_index("fsdp")
        core = me & 1
        low = lax.axis_index("seq") & 1
        enter([fsdp_peer(1), mate_z()])

        def load(name):
            return pltpu.make_async_copy(load_refs[name], bufs[name], load_sems.at[names.index(name)])

        loaded = set()

        def got(name):
            if name not in loaded:
                load(name).wait()
                loaded.add(name)
            return bufs[name]

        def left_copy(which, p):
            owner = 2 * p + (core ^ 1)
            return send(
                left_refs[which].at[pl.ds(pl.multiple_of(owner * sizes[which], 16), sizes[which])],
                lefts[which].at[1, p],
                give_send.at[which, p],
                give_recv.at[which, p],
                fsdp_peer(1),
            )

        def left_own(which, p):
            owner = 2 * p + core
            return pltpu.make_async_copy(
                left_refs[which].at[pl.ds(pl.multiple_of(owner * sizes[which], 16), sizes[which])],
                lefts[which].at[0, p],
                give_own.at[which, p],
            )

        def right_copy(which):
            src = rights[which].at[pl.ds(0, rows)]
            return send(
                src, rights[which].at[pl.ds(rows, rows)], right_send.at[which], right_recv.at[which], fsdp_peer(1)
            )

        outs = [(partials[i], partials_out[i]) for i in range(grads)] + [
            (wide_low, low_out),
            (wide_pre, pre_out),
            (wide_branch, branch_out),
            (grad_middle, middle_out),
            (wide_mixed, mixed_out),
            (wide_sums, wide_sums_out),
            (narrow_sums, narrow_sums_out),
        ]

        def out_copy(i):
            return pltpu.make_async_copy(outs[i][0], outs[i][1], out_sems.at[i])

        def form(which):
            for p in range(4):
                left_copy(which, p).wait_recv()
                left_own(which, p).wait()
            right_copy(which).wait_recv()
            size = 4 * sizes[which]
            step = 512 if size > 512 else size
            total = jnp.dot(
                lefts[which][0].reshape(size, rows), rights[which][pl.ds(0, rows), :], preferred_element_type=F32
            ) + jnp.dot(
                lefts[which][1].reshape(size, rows), rights[which][pl.ds(rows, rows), :], preferred_element_type=F32
            )
            partials[which][...] = total.astype(BF16)
            out_copy(which).start()

        for name in names:
            load(name).start()
        for which in range(grads):
            for p in range(4):
                left_copy(which, p).start()
                left_own(which, p).start()

        own = pl.ds(0, rows)
        narrow_sums[...] = jnp.zeros_like(narrow_sums)
        wide_sums[...] = jnp.zeros_like(wide_sums)
        grads_in = got("out_grad")
        rights[0][own, :] = grads_in[...]
        right_copy(0).start()
        step = 2 * LANES
        got("narrow_down")
        got("narrow_slope")
        for c in range(narrow_hidden // (2 * step)):
            at = pl.ds(c * 2 * step, 2 * step)
            product = across_lanes(grads_in[...], bufs["narrow_down"][at, :])
            rights[1][own, at] = (product * bufs["narrow_slope"][:, at].astype(F32)).astype(BF16)
        right_copy(1).start()
        upper[...] = across_lanes(rights[1][own, :], got("narrow_up")[...])
        table = got("narrow_gains")
        got("narrow_middle")
        chunk = 64
        gain_sum = jnp.zeros((1, narrow), F32)
        shift_sum = jnp.zeros((1, narrow), F32)
        for i in range(rows // chunk):
            part = pl.ds(i * chunk, chunk)
            inner, gain_term, shift_term = norm_backward(
                bufs["narrow_middle"][part], upper[part], table[2:3, :]
            )
            gain_sum, shift_sum = gain_sum + gain_term, shift_sum + shift_term
            total = grads_in[part].astype(F32) + inner
            bufs["narrow_middle"][part] = total
            rights[2][part, :] = total.astype(BF16)
        narrow_sums[6:7, :] = gain_sum
        narrow_sums[7:8, :] = shift_sum
        right_copy(2).start()
        grad_mixed[...] = across_lanes(rights[2][own, :], got("narrow_out")[...]).astype(BF16)
        group_bias(bias, got("ends"), rows)

        got("narrow_queries")
        got("narrow_kv")
        got("narrow_mixed")
        got("narrow_logs")

        def key_core_copy(j):
            return send(
                dkv.at[:, j, pl.ds((core ^ 1) * half, half)],
                core_in.at[:, j],
                key_send.at[0, j],
                key_recv.at[0, j],
                fsdp_peer(1),
            )

        def key_far_copy(j):
            return send(
                core_in.at[:, j, pl.ds((low ^ 1) * rows, rows)],
                z_in.at[:, j],
                key_send.at[1, j],
                key_recv.at[1, j],
                mate_z(),
            )

        def key_middle(j):
            key_core_copy(j).wait_recv()
            for kind in range(2):
                core_in[kind, j] = (
                    core_in[kind, j].astype(F32) + dkv[kind, j, pl.ds(core * half, half)].astype(F32)
                ).astype(BF16)
            key_far_copy(j).start()

        def key_end(j):
            key_far_copy(j).wait_recv()
            for kind in range(2):
                total = core_in[kind, j, pl.ds(low * rows, rows)].astype(F32) + z_in[kind, j].astype(F32)
                at = pl.ds(pl.multiple_of((1 + kind) * narrow + j * LANES, LANES), LANES)
                rights[3][own, at] = total.astype(BF16)

        @pl.loop(0, slabs)
        def _(j):
            at = pl.ds(pl.multiple_of(j * LANES, LANES), LANES)
            dq, dk, dv = slab_backward(
                bufs["narrow_queries"][:, at],
                grad_mixed[:, at],
                bufs["narrow_mixed"][:, at],
                bufs["narrow_logs"][j],
                bufs["narrow_kv"][0, j],
                bufs["narrow_kv"][1, j],
                bias,
                head_size,
            )
            rights[3][own, at] = (dq.T * scale).astype(BF16)
            dkv[0, j] = (dk * scale).astype(BF16)
            dkv[1, j] = dv.astype(BF16)
            key_core_copy(j).start()

            @pl.when(j >= 1)
            def _():
                key_middle(j - 1)

        form(0)
        key_middle(slabs - 1)
        form(1)
        form(2)
        for j in range(slabs):
            key_end(j)
        right_copy(3).start()
        upper[...] = across_lanes(rights[3][own, :], got("narrow_qkv")[...])
        got("entry")
        side = got("side")
        gain_sum = jnp.zeros((1, narrow), F32)
        shift_sum = jnp.zeros((1, narrow), F32)
        mask_sum = jnp.zeros((1, narrow), F32)
        for i in range(rows // chunk):
            part = pl.ds(i * chunk, chunk)
            inner, gain_term, shift_term = norm_backward(bufs["entry"][part], upper[part], table[0:1, :])
            gain_sum, shift_sum = gain_sum + gain_term, shift_sum + shift_term
            total = bufs["narrow_middle"][part] + inner
            hit = side[part, narrow : narrow + 1]
            mask_sum = mask_sum + jnp.sum(hit * total, axis=0, keepdims=True)
            rights[4][part, :] = (total * (1.0 - hit)).astype(BF16)
        narrow_sums[4:5, :] = gain_sum
        narrow_sums[5:6, :] = shift_sum
        narrow_sums[8:9, :] = mask_sum
        out_copy(grads + 6).start()
        right_copy(4).start()

        got("w_embed")
        for c in range(width // step):
            at = pl.ds(c * step, step)
            product = across_lanes(rights[4][own, :], bufs["w_embed"][at, :])
            grad_middle[:, at] = product
            wide_low[:, at] = product.astype(BF16)
        out_copy(grads).start()
        got("wide_down")
        got("wide_slope")

        @pl.loop(0, wide_hidden // (2 * step))
        def _(c):
            at = pl.ds(pl.multiple_of(c * 2 * step, 2 * step), 2 * step)
            product = across_lanes(wide_low[...], bufs["wide_down"][at, :])
            wide_pre[:, at] = (product * bufs["wide_slope"][:, at].astype(F32)).astype(BF16)

        out_copy(grads + 1).start()
        got("wide_up")

        @pl.loop(0, width // step)
        def _(c):
            at = pl.ds(pl.multiple_of(c * step, step), step)
            wide_upper[:, at] = across_lanes(wide_pre[...], bufs["wide_up"][at, :])

        wide_table = got("wide_gains")
        got("wide_middle")
        gain_sum = jnp.zeros((1, width), F32)
        shift_sum = jnp.zeros((1, width), F32)
        for i in range(rows // chunk):
            part = pl.ds(i * chunk, chunk)
            inner, gain_term, shift_term = norm_backward(
                bufs["wide_middle"][part], wide_upper[part], wide_table[2:3, :]
            )
            gain_sum, shift_sum = gain_sum + gain_term, shift_sum + shift_term
            total = grad_middle[part] + inner
            grad_middle[part] = total
            wide_branch[part] = total.astype(BF16)
        wide_sums[2:3, :] = gain_sum
        wide_sums[3:4, :] = shift_sum
        for i in (2, 3, 5):
            out_copy(grads + i).start()
        got("wide_out")
        for c in range(width // step):
            at = pl.ds(c * step, step)
            wide_mixed[:, at] = across_lanes(wide_branch[...], bufs["wide_out"][at, :]).astype(BF16)
        out_copy(grads + 4).start()
        form(3)
        form(4)
        for which in range(grads):
            right_copy(which).wait_send()
            for p in range(4):
                left_copy(which, p).wait_send()
        for j in range(slabs):
            key_core_copy(j).wait_send()
            key_far_copy(j).wait_send()
        for i in range(grads + 7):
            out_copy(i).wait()

    out_shape = [
        jax.ShapeDtypeStruct((4 * size, columns), BF16) for size, columns in zip(sizes, right_widths)
    ] + [
        jax.ShapeDtypeStruct((rows, width), BF16),
        jax.ShapeDtypeStruct((rows, wide_hidden), BF16),
        jax.ShapeDtypeStruct((rows, width), BF16),
        jax.ShapeDtypeStruct((rows, width), F32),
        jax.ShapeDtypeStruct((rows, width), BF16),
        jax.ShapeDtypeStruct((SMALL_ROWS, width), F32),
        jax.ShapeDtypeStruct((SMALL_ROWS, narrow), F32),
    ]
    scratch = (
        [pltpu.VMEM(loads[name].shape, loads[name].dtype) for name in names]
        + [pltpu.VMEM((2, 4, size, rows), BF16) for size in sizes]
        + [pltpu.VMEM((2 * rows, columns), BF16) for columns in right_widths]
        + [pltpu.VMEM((4 * size, columns), BF16) for size, columns in zip(sizes, right_widths)]
        + [
            pltpu.VMEM((keys, rows), F32),
            pltpu.VMEM((2, slabs, keys, LANES), BF16),
            pltpu.VMEM((2, slabs, half, LANES), BF16),
            pltpu.VMEM((2, slabs, rows, LANES), BF16),
            pltpu.VMEM((rows, narrow), F32),
            pltpu.VMEM((rows, width), F32),
            pltpu.VMEM((rows, narrow), BF16),
            pltpu.VMEM((rows, width), BF16),
            pltpu.VMEM((rows, wide_hidden), BF16),
            pltpu.VMEM((rows, width), F32),
            pltpu.VMEM((rows, width), BF16),
            pltpu.VMEM((rows, width), BF16),
            pltpu.VMEM((SMALL_ROWS, width), F32),
            pltpu.VMEM((SMALL_ROWS, narrow), F32),
            pltpu.SemaphoreType.DMA((len(names),)),
            pltpu.SemaphoreType.DMA((grads, 4)),
            pltpu.SemaphoreType.DMA((grads, 4)),
            pltpu.SemaphoreType.DMA((grads, 4)),
            pltpu.SemaphoreType.DMA((grads,)),
            pltpu.SemaphoreType.DMA((grads,)),
            pltpu.SemaphoreType.DMA((2, slabs)),
            pltpu.SemaphoreType.DMA((2, slabs)),
            pltpu.SemaphoreType.DMA((grads + 7,)),
        ]
    )
    return pl.pallas_call(
        kernel,
        out_shape=out_shape,
        in_specs=[ANYWHERE] * (len(names) + grads),
        out_specs=[ANYWHERE] * len(out_shape),
        scratch_shapes=scratch,
        compiler_params=remote_params(collective_id, 60 << 20),
        name="middle_back",
    )(*[loads[name] for name in names], *lefts_t)


class Unit:
    def __init__(self, index, first, columns, order, place):
        self.index = index
        self.first = first
        self.columns = columns
        self.near, self.far = order
        self.place = place


def cut_columns(shapes, most):
    units = []
    for index, (rows, columns) in enumerate(shapes):
        pieces = 1
        while rows * (columns // pieces) > most and (columns // pieces) % (2 * LANES) == 0:
            pieces *= 2
        for place in range(pieces):
            order = (2, 4) if len(units) % 2 == 0 else (4, 2)
            units.append(Unit(index, place * (columns // pieces), columns // pieces, order, place))
    return units


def back_and_sum(
    partials,
    lefts_t,
    rights,
    queries,
    keys_values,
    mixed,
    grad_mixed,
    logs,
    ends,
    w_qkv,
    tokens,
    grad_middle,
    gains,
    wide_sums,
    narrow_sums,
    head_count,
    collective_id,
):
    rows, width = queries.shape
    triple = 3 * width
    keys = 4 * rows
    slabs = width // LANES
    head_size = width // head_count
    per_slab = LANES // head_size
    scale = head_size ** (-0.5)
    factor = scale * LOG2E
    part_rows = w_qkv.shape[1]

    given = len(partials)
    formed = [(left.shape[0] // 8, right.shape[1]) for left, right in zip(lefts_t, rights)]
    shapes = [partial.shape[1:] for partial in partials] + formed + [(part_rows, triple), (SMALL_ROWS, LANES)]
    up_index = given + 1
    qkv_index, small_index = given + 3, given + 4
    array_count = given + 5
    ring = 5
    units = cut_columns(shapes, 70000)
    count = len(units)
    pieces = [sum(1 for unit in units if unit.index == index) for index in range(array_count)]

    def piece_shape(index):
        return (shapes[index][0], shapes[index][1] // pieces[index])

    def kernel(*refs):
        sources = refs[:given]
        left_refs = refs[given : given + 4]
        right_refs = refs[given + 4 : given + 7]
        base = given + 7
        (
            q_ref,
            kv_ref,
            mixed_ref,
            grad_ref,
            log_ref,
            ends_ref,
            w_ref,
            tokens_ref,
            middle_ref,
            gain_ref,
            wide_sums_ref,
            narrow_sums_ref,
        ) = refs[base : base + 12]
        base += 12
        results = refs[base : base + array_count]
        token_out, up_inbox = refs[base + array_count : base + array_count + 2]
        rest = list(refs[base + array_count + 2 :])
        acc, near_in, far_in, outer_in, inner_in = [
            rest[group * array_count : (group + 1) * array_count] for group in range(5)
        ]
        late_out = rest[5 * array_count : 5 * array_count + 4]
        lefts = rest[5 * array_count + 4 : 5 * array_count + 8]
        (
            low_both,
            branch_both,
            up_buf,
            kv_buf,
            give_send,
            give_recv,
            give_own,
            up_sems,
            kv_sems,
            small_out,
            bias,
            dkv,
            core_in,
            z_in,
            dqkv,
            w_buf,
            grad_normed,
            token_buf,
            norm_sums,
            norm_sums_in,
            narrow_in,
            send_sems,
            recv_sems,
            own_sems,
            out_sems,
            key_send,
            key_recv,
            row_send,
            row_recv,
            w_sems,
        ) = rest[5 * array_count + 8 :]

        me = lax.axis_index("fsdp")
        place = lax.axis_index("seq")
        core = me & 1
        chip = me >> 1
        high = place >> 1
        low = place & 1
        inner = jnp.logical_or(place == 1, place == 2)
        outer = jnp.logical_not(inner)
        trades = core != high
        trade_peer = ((me & 6) | high, core * 2 + low)
        mate = seq_peer(place ^ 1)
        across = seq_peer(3 - place)

        barrier = pltpu.get_barrier_semaphore()
        for peer in (fsdp_peer(1), fsdp_peer(2), fsdp_peer(4), mate):
            pl.semaphore_signal(barrier, inc=1, device_id=peer, device_id_type=MESH)

        @pl.when(inner)
        def _():
            pl.semaphore_signal(barrier, inc=1, device_id=across, device_id_type=MESH)

        @pl.when(trades)
        def _():
            pl.semaphore_signal(barrier, inc=1, device_id=trade_peer, device_id_type=MESH)

        pl.semaphore_wait(barrier, 4 + inner.astype(jnp.int32) + trades.astype(jnp.int32))


        def span(unit):
            return pl.ds(unit.first, unit.columns)

        def chip_of(unit, slot):
            return chip ^ (((slot // 2) * unit.near + (slot % 2) * unit.far) // 2)

        def near_copy(u, slot):
            unit = units[u]
            if given <= unit.index <= qkv_index:
                src = late_out[unit.index - given].at[unit.place % ring, slot]
            elif unit.index == small_index:
                src = small_out.at[slot]
            else:
                src = sources[unit.index].at[chip_of(unit, 2 + slot), :, span(unit)]
            return send(
                src,
                near_in[unit.index].at[unit.place, slot],
                send_sems.at[u, slot],
                recv_sems.at[u, slot],
                fsdp_peer(unit.near),
            )

        def own_copy(u, slot):
            unit = units[u]
            return pltpu.make_async_copy(
                sources[unit.index].at[chip_of(unit, slot), :, span(unit)],
                acc[unit.index].at[unit.place, slot],
                own_sems.at[u, slot],
            )

        def far_copy(u):
            unit = units[u]
            return send(
                acc[unit.index].at[unit.place, 1],
                far_in[unit.index].at[unit.place],
                send_sems.at[u, 2],
                recv_sems.at[u, 2],
                fsdp_peer(unit.far),
            )

        def inward_copy(u):
            unit = units[u]
            return send(
                acc[unit.index].at[unit.place, 0],
                outer_in[unit.index].at[unit.place],
                send_sems.at[u, 3],
                recv_sems.at[u, 3],
                mate,
            )

        def across_copy(u):
            unit = units[u]
            return send(
                outer_in[unit.index].at[unit.place],
                inner_in[unit.index].at[unit.place],
                send_sems.at[u, 4],
                recv_sems.at[u, 4],
                across,
            )

        def outward_copy(u):
            unit = units[u]
            return send(
                acc[unit.index].at[unit.place, 0],
                results[unit.index].at[:, span(unit)],
                send_sems.at[u, 5],
                recv_sems.at[u, 5],
                mate,
            )

        def out_copy(u):
            unit = units[u]
            return pltpu.make_async_copy(
                acc[unit.index].at[unit.place, 0], results[unit.index].at[:, span(unit)], out_sems.at[u]
            )

        def add_into(dst, left, right):
            total_rows, columns = dst.shape
            step = 16
            while total_rows % (2 * step) == 0 and 2 * step * columns <= 32768:
                step *= 2

            @pl.loop(0, total_rows // step)
            def _(i):
                part = pl.ds(pl.multiple_of(i * step, step), step)
                dst[part] = (left[part].astype(F32) + right[part].astype(F32)).astype(BF16)

        def early(u):
            return units[u].index < given

        def near_start(u):
            if given <= units[u].index <= qkv_index:
                form(u)
            elif units[u].index == small_index:
                form_small(u)
            near_copy(u, 1).start()
            near_copy(u, 0).start()

        def stage_far(u):
            unit = units[u]
            for slot in (1, 0):
                near_copy(u, slot).wait_recv()
                if early(u):
                    own_copy(u, slot).wait()
                target = acc[unit.index].at[unit.place, slot]
                add_into(target, target, near_in[unit.index].at[unit.place, slot])
                if slot == 1:
                    far_copy(u).start()

        def stage_inward(u):
            unit = units[u]
            far_copy(u).wait_recv()
            target = acc[unit.index].at[unit.place, 0]
            add_into(target, target, far_in[unit.index].at[unit.place])

            @pl.when(outer)
            def _():
                inward_copy(u).start()

        def stage_across(u):
            unit = units[u]

            @pl.when(inner)
            def _():
                inward_copy(u).wait_recv()
                target = outer_in[unit.index].at[unit.place]
                add_into(target, target, acc[unit.index].at[unit.place, 0])
                across_copy(u).start()

        def stage_outward(u):
            unit = units[u]

            @pl.when(inner)
            def _():
                across_copy(u).wait_recv()
                add_into(
                    acc[unit.index].at[unit.place, 0],
                    outer_in[unit.index].at[unit.place],
                    inner_in[unit.index].at[unit.place],
                )
                outward_copy(u).start()
                out_copy(u).start()

        ahead = 4
        lags = ((stage_far, 0), (stage_inward, 2), (stage_across, 4), (stage_outward, 6))
        total_ticks = count + 6

        def tick(t):
            if t + ahead < count:
                near_start(t + ahead)
            for stage, lag in lags:
                if 0 <= t - lag < count:
                    stage(t - lag)


        half = 2 * rows

        def group(g):
            return pl.ds(2 * g, 2)

        def key_core_copy(g):
            return send(
                dkv.at[:, group(g), pl.ds((core ^ 1) * half, half)],
                core_in.at[:, group(g)],
                key_send.at[0, g],
                key_recv.at[0, g],
                fsdp_peer(1),
            )

        def key_far_copy(g):
            return send(
                core_in.at[:, group(g), pl.ds((low ^ 1) * rows, rows)],
                z_in.at[:, group(g)],
                key_send.at[1, g],
                key_recv.at[1, g],
                mate,
            )

        def key_middle(g):
            key_core_copy(g).wait_recv()
            for kind in range(2):
                for k in range(2):

                    @pl.loop(0, half // LANES)
                    def _(i):
                        part = pl.ds(pl.multiple_of(i * LANES, LANES), LANES)
                        own = pl.ds(pl.multiple_of(core * half + i * LANES, LANES), LANES)
                        core_in[kind, 2 * g + k, part] = (
                            core_in[kind, 2 * g + k, part].astype(F32) + dkv[kind, 2 * g + k, own].astype(F32)
                        ).astype(BF16)

            key_far_copy(g).start()

        def key_end(g):
            key_far_copy(g).wait_recv()
            for kind in range(2):
                for k in range(2):
                    slab = 2 * g + k

                    @pl.loop(0, rows // LANES)
                    def _(i):
                        part = pl.ds(pl.multiple_of(i * LANES, LANES), LANES)
                        own = pl.ds(pl.multiple_of(low * rows + i * LANES, LANES), LANES)
                        total = core_in[kind, slab, own].astype(F32) + z_in[kind, slab, part].astype(F32)
                        dqkv[part, pl.ds((1 + kind) * width + slab * LANES, LANES)] = total.astype(BF16)


        def kv_copy(j):
            return pltpu.make_async_copy(kv_ref.at[:, j], kv_buf.at[j % 2], kv_sems.at[j % 2])

        def slab_back(j):
            kv_copy(j).wait()

            @pl.when(j + 1 < slabs)
            def _():
                kv_copy(j + 1).start()

            at = pl.ds(pl.multiple_of(j * LANES, LANES), LANES)
            dq, dk, dv = slab_backward(
                q_ref[:, at],
                grad_ref[:, at],
                mixed_ref[:, at],
                log_ref[j],
                kv_buf[j % 2, 0],
                kv_buf[j % 2, 1],
                bias,
                head_size,
            )
            dqkv[pl.ds(0, rows), at] = (dq.T * scale).astype(BF16)
            dkv[0, j] = (dk * scale).astype(BF16)
            dkv[1, j] = dv.astype(BF16)


        def row_copy(part):
            columns = pl.ds(0, width) if part == 0 else pl.ds(width, 2 * width)
            return send(
                dqkv.at[pl.ds(0, rows), columns],
                dqkv.at[pl.ds(rows, rows), columns],
                row_send.at[part],
                row_recv.at[part],
                fsdp_peer(1),
            )


        def left_copy(which, p):
            size = lefts_t[which].shape[0] // 8
            owner = 2 * p + (core ^ 1)
            return send(
                left_refs[which].at[pl.ds(pl.multiple_of(owner * size, LANES), size)],
                lefts[which].at[1, p],
                give_send.at[which, p],
                give_recv.at[which, p],
                fsdp_peer(1),
            )

        def left_own(which, p):
            size = lefts_t[which].shape[0] // 8
            owner = 2 * p + core
            return pltpu.make_async_copy(
                left_refs[which].at[pl.ds(pl.multiple_of(owner * size, LANES), size)],
                lefts[which].at[0, p],
                give_own.at[which, p],
            )

        def right_copy(which):
            dst = (low_both.at[pl.ds(rows, rows)], up_inbox, branch_both.at[pl.ds(rows, rows)])[which]
            return send(
                right_refs[which], dst, give_send.at[4, which], give_recv.at[4, which], fsdp_peer(1)
            )

        def right_own(which):
            dst = (low_both, None, branch_both)[which].at[pl.ds(0, rows)]
            return pltpu.make_async_copy(right_refs[which], dst, give_own.at[4, which])

        def give(which):
            for p in range(4):
                left_copy(which, p).start()
                left_own(which, p).start()
            if which < 3:
                right_copy(which).start()
                if which != 1:
                    right_own(which).start()

        def take(which):
            for p in range(4):
                left_copy(which, p).wait_recv()
                left_own(which, p).wait()
            if which < 3:
                right_copy(which).wait_recv()
                if which != 1:
                    right_own(which).wait()

        def up_copies(unit):
            slot = unit.place % 2
            return [
                pltpu.make_async_copy(
                    right_refs[1].at[:, span(unit)], up_buf.at[slot, pl.ds(0, rows)], up_sems.at[slot, 0]
                ),
                pltpu.make_async_copy(
                    up_inbox.at[:, span(unit)], up_buf.at[slot, pl.ds(rows, rows)], up_sems.at[slot, 1]
                ),
            ]

        near_done = set()

        def form(u):
            unit = units[u]
            which = unit.index - given
            if unit.place == 0:
                take(which)
                if unit.index == up_index:
                    for one in up_copies(unit):
                        one.start()
            if unit.place >= ring:
                near_copy(u - ring, 0).wait_send()
                near_copy(u - ring, 1).wait_send()
                near_done.add(u - ring)
            if unit.index == up_index:
                if unit.place + 1 < pieces[up_index]:
                    for one in up_copies(units[u + 1]):
                        one.start()
                for one in up_copies(unit):
                    one.wait()
                right = up_buf.at[unit.place % 2]
            else:
                right = (low_both, None, branch_both, dqkv)[which].at[:, span(unit)]
            for slot in range(4):
                block = jnp.zeros(piece_shape(unit.index), F32)
                for half in range(2):
                    block = block + jnp.dot(
                        lefts[which][half, chip_of(unit, slot)],
                        right[pl.ds(half * rows, rows)],
                        preferred_element_type=F32,
                    )
                if slot < 2:
                    acc[unit.index][unit.place, slot] = block.astype(BF16)
                else:
                    late_out[which][unit.place % ring, slot - 2] = block.astype(BF16)


        blocks = 8

        def w_copy(block):
            return pltpu.make_async_copy(w_ref.at[block], w_buf.at[block % 2], w_sems.at[block % 2])

        def norm_copy():
            return send(norm_sums, norm_sums_in, row_send.at[2], row_recv.at[2], fsdp_peer(1))

        def narrow_copy():
            return send(narrow_sums_ref, narrow_in, row_send.at[4], row_recv.at[4], fsdp_peer(1))

        def input_gradient():
            for block in range(blocks):
                w_copy(block).wait()
                grad_normed[:, pl.ds(block * part_rows, part_rows)] = across_lanes(
                    dqkv[pl.ds(0, rows), :], w_buf[block % 2]
                )
                if block + 2 < blocks:
                    w_copy(block + 2).start()
            step = 64
            gain_sum = jnp.zeros((1, width), F32)
            shift_sum = jnp.zeros((1, width), F32)
            for i in range(rows // step):
                part = pl.ds(i * step, step)
                inside, gain_term, shift_term = norm_backward(
                    tokens_ref[part].astype(F32), grad_normed[part], gain_ref[0:1, :]
                )
                gain_sum, shift_sum = gain_sum + gain_term, shift_sum + shift_term
                token_buf[part] = (middle_ref[part] + inside).astype(BF16)
            norm_sums[...] = wide_sums_ref[...]
            norm_sums[0:1, :] = gain_sum
            norm_sums[1:2, :] = shift_sum
            norm_copy().start()

            @pl.when(trades)
            def _():
                token_send().start()

            @pl.when(jnp.logical_not(trades))
            def _():
                token_keep().start()

        def token_send():
            return send(token_buf, token_out, row_send.at[3], row_recv.at[3], trade_peer)

        def token_keep():
            return pltpu.make_async_copy(token_buf, token_out, w_sems.at[2])

        def form_small(u):
            unit = units[u]
            norm_copy().wait_recv()
            narrow_copy().wait_recv()
            norm_sums_in[...] = norm_sums[...] + norm_sums_in[...]
            narrow_both = narrow_sums_ref[...] + narrow_in[...]
            narrow = narrow_both.shape[1]
            narrow_part = narrow // 8
            source_lane = lax.broadcasted_iota(jnp.int32, (narrow, LANES), 0)
            lane = lax.broadcasted_iota(jnp.int32, (narrow, LANES), 1)
            for slot in range(4):
                owner = chip_of(unit, slot) * 2 + core
                picked = jnp.logical_and(source_lane == owner * narrow_part + lane, lane < narrow_part)
                block = norm_sums_in[:, pl.ds(pl.multiple_of(owner * LANES, LANES), LANES)] + jnp.dot(
                    narrow_both,
                    picked.astype(F32),
                    precision=lax.Precision.HIGHEST,
                    preferred_element_type=F32,
                )
                block = block.astype(BF16)
                if slot < 2:
                    acc[unit.index][unit.place, slot] = block
                else:
                    small_out[slot - 2] = block


        first_late = min(u for u in range(count) if units[u].index == qkv_index)
        for which in range(4):
            give(which)
        for u in range(count):
            if early(u):
                for slot in range(2):
                    own_copy(u, slot).start()
        kv_copy(0).start()
        narrow_copy().start()
        for u in range(ahead):
            near_start(u)
        w_copy(0).start()
        w_copy(1).start()
        group_bias(bias, ends_ref, rows)
        ticks_inside = first_late - ahead

        @pl.loop(0, slabs)
        def _(j):
            slab_back(j)

            @pl.when(j % 2 == 1)
            def _():
                key_core_copy(j // 2).start()

            @pl.when(jnp.logical_and(j % 2 == 0, j >= 2))
            def _():
                key_middle(j // 2 - 1)

            done = 0
            for k in range(slabs):
                until = (k + 1) * ticks_inside // slabs

                @pl.when(j == k)
                def _(done=done, until=until):
                    for t in range(done, until):
                        tick(t)

                done = until

        row_copy(0).start()
        key_middle(slabs // 2 - 1)
        for g in range(slabs // 2):
            key_end(g)
        row_copy(1).start()
        row_copy(0).wait_recv()
        row_copy(1).wait_recv()
        done_input = False
        for t in range(ticks_inside, total_ticks):
            if not done_input and t + ahead >= count - 1:
                input_gradient()
                done_input = True
            tick(t)

        for u in range(count):
            if u not in near_done:
                near_copy(u, 0).wait_send()
                near_copy(u, 1).wait_send()
            far_copy(u).wait_send()
        for which in range(4):
            for p in range(4):
                left_copy(which, p).wait_send()
            if which < 3:
                right_copy(which).wait_send()

        for u in range(count):

            @pl.when(inner)
            def _():
                across_copy(u).wait_send()
                outward_copy(u).wait_send()
                out_copy(u).wait()

            @pl.when(outer)
            def _():
                inward_copy(u).wait_send()
                outward_copy(u).wait_recv()

        for g in range(slabs // 2):
            key_core_copy(g).wait_send()
            key_far_copy(g).wait_send()
        row_copy(0).wait_send()
        row_copy(1).wait_send()
        norm_copy().wait_send()
        narrow_copy().wait_send()

        @pl.when(trades)
        def _():
            token_send().wait()

        @pl.when(jnp.logical_not(trades))
        def _():
            token_keep().wait()

    scratch = []
    for slots in ((2,), (2,), (), (), ()):
        for index in range(array_count):
            scratch.append(pltpu.VMEM((pieces[index],) + slots + piece_shape(index), BF16))
    for index in range(given, qkv_index + 1):
        scratch.append(pltpu.VMEM((min(ring, pieces[index]), 2) + piece_shape(index), BF16))
    for left in lefts_t:
        scratch.append(pltpu.VMEM((2, 4, left.shape[0] // 8, rows), BF16))
    scratch += [
        pltpu.VMEM((2 * rows, width), BF16),
        pltpu.VMEM((2 * rows, width), BF16),
        pltpu.VMEM((2, 2 * rows, piece_shape(up_index)[1]), BF16),
        pltpu.VMEM((2, 2, keys, LANES), BF16),
        pltpu.SemaphoreType.DMA((5, 4)),
        pltpu.SemaphoreType.DMA((5, 4)),
        pltpu.SemaphoreType.DMA((5, 4)),
        pltpu.SemaphoreType.DMA((2, 2)),
        pltpu.SemaphoreType.DMA((2,)),
        pltpu.VMEM((2, SMALL_ROWS, LANES), BF16),
        pltpu.VMEM((keys, rows), F32),
        pltpu.VMEM((2, slabs, keys, LANES), BF16),
        pltpu.VMEM((2, slabs, 2 * rows, LANES), BF16),
        pltpu.VMEM((2, slabs, rows, LANES), BF16),
        pltpu.VMEM((2 * rows, triple), BF16),
        pltpu.VMEM((2, part_rows, triple), BF16),
        pltpu.VMEM((rows, width), F32),
        pltpu.VMEM((rows, width), BF16),
        pltpu.VMEM((SMALL_ROWS, width), F32),
        pltpu.VMEM((SMALL_ROWS, width), F32),
        pltpu.VMEM(narrow_sums.shape, F32),
        pltpu.SemaphoreType.DMA((count, 6)),
        pltpu.SemaphoreType.DMA((count, 6)),
        pltpu.SemaphoreType.DMA((count, 2)),
        pltpu.SemaphoreType.DMA((count,)),
        pltpu.SemaphoreType.DMA((2, slabs // 2)),
        pltpu.SemaphoreType.DMA((2, slabs // 2)),
        pltpu.SemaphoreType.DMA((5,)),
        pltpu.SemaphoreType.DMA((5,)),
        pltpu.SemaphoreType.DMA((3,)),
    ]
    return pl.pallas_call(
        kernel,
        out_shape=[jax.ShapeDtypeStruct(shape, BF16) for shape in shapes]
        + [jax.ShapeDtypeStruct((rows, width), BF16), jax.ShapeDtypeStruct(rights[1].shape, BF16)],
        in_specs=[ANYWHERE] * (given + 7)
        + [IN_VMEM, ANYWHERE]
        + [IN_VMEM] * 4
        + [ANYWHERE]
        + [IN_VMEM] * 5,
        out_specs=[ANYWHERE] * (array_count + 2),
        scratch_shapes=scratch,
        compiler_params=remote_params(collective_id, 61 << 20),
        name="back_and_sum",
    )(
        *partials,
        *lefts_t,
        *rights,
        queries,
        keys_values,
        mixed,
        grad_mixed,
        logs,
        ends,
        w_qkv,
        tokens,
        grad_middle,
        gains,
        wide_sums,
        narrow_sums,
    )


def fast_local(
    tokens,
    clip_lengths,
    target_pos,
    out_grad,
    norm1_gain,
    norm1_bias,
    w_qkv,
    w_out,
    norm2_gain,
    norm2_bias,
    w_fc1,
    w_fc2,
    w_embed,
    mask_token,
    pred_norm1_gain,
    pred_norm1_bias,
    pred_qkv,
    pred_out,
    pred_norm2_gain,
    pred_norm2_bias,
    pred_fc1,
    pred_fc2,
):
    rows, width = tokens.shape
    narrow = out_grad.shape[1]
    wide_part = norm1_gain.shape[0]
    narrow_part = mask_token.shape[0]
    me = lax.axis_index("fsdp")
    core = me & 1
    wide_small = jnp.pad(
        jnp.stack([norm1_gain, norm1_bias, norm2_gain, norm2_bias]), ((0, SMALL_ROWS - 4), (0, 0))
    )
    narrow_small = jnp.stack(
        [pred_norm1_gain, pred_norm1_bias, pred_norm2_gain, pred_norm2_bias, mask_token]
    )
    here = (jnp.arange(narrow, dtype=jnp.int32) // narrow_part == me)[None, :]
    narrow_small = jnp.where(here, jnp.tile(narrow_small, (1, 8)), jnp.zeros((), BF16))
    narrow_small = jnp.pad(narrow_small, ((0, SMALL_ROWS - 5), (0, 0)))

    clip_ends = jnp.cumsum(clip_lengths[0])
    first_rows = lax.axis_index("seq") * rows + jnp.arange(rows, dtype=jnp.int32)
    past_end = (first_rows[:, None] >= clip_ends[None, :]).astype(jnp.int32)
    rel_rows = first_rows - jnp.sum(clip_lengths[0][None, :] * past_end, axis=1)
    matches = jnp.arange(rows, dtype=jnp.int32)[:, None] == target_pos[0, 0][None, :]
    hit_rows = jnp.sum(matches.astype(F32), axis=1)
    side = jnp.concatenate(
        [position_table(rel_rows, narrow), jnp.broadcast_to(hit_rows[:, None], (rows, LANES))], axis=1
    )
    ends = jnp.pad(jnp.broadcast_to(clip_ends[:, None], (3, LANES)), ((0, 5), (0, 0)))

    whole, kept, narrow_kept, rest, traded = forward_pass(
        tokens,
        out_grad,
        side,
        ends,
        [
            wide_small,
            narrow_small,
            w_qkv,
            w_out,
            w_fc1,
            w_fc2,
            w_embed,
            pred_qkv,
            pred_out,
            pred_fc1,
            pred_fc2,
        ],
        HEADS,
        P_HEADS,
    )
    context_t, entry, side, tokens, gains, narrow_gains = rest
    out_grad, ends, context_out, predicted, hidden_t, narrow_hidden_t = traded
    normed_t, queries, keys_values, mixed, logs, middle, normed_mid_t, slope, mixed_t = kept
    (
        narrow_normed_t,
        narrow_queries,
        narrow_kv,
        narrow_mixed,
        narrow_logs,
        narrow_middle,
        narrow_mid_t,
        narrow_slope,
        narrow_mixed_t,
    ) = narrow_kept

    results = middle_back(
        dict(
            out_grad=out_grad,
            narrow_down=whole[10],
            narrow_slope=narrow_slope,
            narrow_up=whole[9],
            narrow_gains=narrow_gains,
            narrow_middle=narrow_middle,
            narrow_out=whole[8],
            ends=ends,
            narrow_queries=narrow_queries,
            narrow_kv=narrow_kv.reshape(2, narrow // LANES, 4 * rows, LANES),
            narrow_mixed=narrow_mixed,
            narrow_logs=narrow_logs,
            narrow_qkv=whole[7],
            entry=entry,
            side=side,
            w_embed=whole[6],
            wide_down=whole[5],
            wide_slope=slope,
            wide_up=whole[4],
            wide_gains=gains,
            wide_middle=middle,
            wide_out=whole[3],
        ),
        [narrow_hidden_t, narrow_mid_t, narrow_mixed_t, narrow_normed_t, context_t],
        P_HEADS,
        2,
    )
    partials = [one.reshape(4, one.shape[0] // 4, one.shape[1]) for one in results[:5]]
    grad_low, grad_pre, grad_branch, grad_middle, grad_mixed, wide_sums, narrow_sums = results[5:]
    results = back_and_sum(
        partials,
        [hidden_t, normed_mid_t, mixed_t, normed_t],
        [grad_low, grad_pre, grad_branch],
        queries,
        keys_values.reshape(2, width // LANES, 4 * rows, LANES),
        mixed,
        grad_mixed,
        logs,
        ends,
        whole[2].reshape(8, wide_part, 3 * width),
        tokens,
        grad_middle,
        gains,
        wide_sums,
        narrow_sums,
        HEADS,
        3,
    )
    token_grad = results[-2]
    sums = [one.astype(F32) for one in results[:-2]]
    small = sums[9]
    narrow_out = [small[4 + i, :narrow_part] for i in range(5)]
    return (
        context_out,
        predicted,
        token_grad,
        small[0],
        small[1],
        sums[8],
        sums[7],
        small[2],
        small[3],
        sums[6],
        sums[5],
        sums[4],
        narrow_out[4],
        narrow_out[0],
        narrow_out[1],
        sums[3],
        sums[2],
        narrow_out[2],
        narrow_out[3],
        sums[1],
        sums[0],
    )


def solution(mesh):
    body = fast_local if fits_fast(mesh) else local
    return jax.shard_map(
        body,
        mesh=mesh,
        in_specs=(
            P(("fsdp", "seq"), None),
            P("fsdp", None),
            P("fsdp", "seq", None),
            P(("fsdp", "seq"), None),
            P("fsdp"),
            P("fsdp"),
            P("fsdp", None),
            P("fsdp", None),
            P("fsdp"),
            P("fsdp"),
            P("fsdp", None),
            P("fsdp", None),
            P("fsdp", None),
            P("fsdp"),
            P("fsdp"),
            P("fsdp"),
            P("fsdp", None),
            P("fsdp", None),
            P("fsdp"),
            P("fsdp"),
            P("fsdp", None),
            P("fsdp", None),
        ),
        out_specs=(
            P(("fsdp", "seq"), None),
            P(("fsdp", "seq"), None),
            P(("fsdp", "seq"), None),
            P("fsdp"),
            P("fsdp"),
            P("fsdp", None),
            P("fsdp", None),
            P("fsdp"),
            P("fsdp"),
            P("fsdp", None),
            P("fsdp", None),
            P("fsdp", None),
            P("fsdp"),
            P("fsdp"),
            P("fsdp"),
            P("fsdp", None),
            P("fsdp", None),
            P("fsdp"),
            P("fsdp"),
            P("fsdp", None),
            P("fsdp", None),
        ),
        check_vma=False,
    )
```

```python
import math

import jax
import jax.numpy as jnp
from jax import lax
from jax.experimental import pallas as pl
from jax.experimental.pallas import tpu as pltpu
from jax.sharding import PartitionSpec as P

HEADS = 16
PD = 384
P_HEADS = 12


EPSILON = 1e-06
NEG_FILL = -1e30
block_rows = 512


def layer_norm(values, norm_gain, norm_shift):
    center = values - jnp.mean(values, axis=-1, keepdims=True)
    spread = jnp.mean(center * center, axis=-1, keepdims=True)
    return center * lax.rsqrt(spread + EPSILON) * norm_gain + norm_shift


def gelu_exact(values):
    return jax.nn.gelu(values, approximate=False)


def position_table(positions, table_width):
    half_width = table_width // 2
    angle_rates = jnp.exp(
        jnp.arange(half_width, dtype=jnp.float32) * (-2.0 * math.log(10000.0) / table_width)
    )
    angles = positions.astype(jnp.float32)[:, None] * angle_rates[None, :]
    return jnp.concatenate([jnp.sin(angles), jnp.cos(angles)], axis=1)


def clip_index(positions, clip_ends):
    return jnp.sum((positions[:, None] >= clip_ends[None, :]).astype(jnp.int32), axis=1)


def key_step(total_keys):
    return max(min(total_keys, block_rows), total_keys // 8)


def block_scores(queries, key_part, query_clip, key_clip_part, score_scale):
    raw_scores = (
        jnp.einsum("the,khe->htk", queries, key_part, preferred_element_type=jnp.float32)
        * score_scale
    )
    same_clip = query_clip[:, None] == key_clip_part[None, :]
    return jnp.where(same_clip[None], raw_scores, NEG_FILL)


def attend_forward(queries, key_heads, value_heads, query_clip, key_clip):
    row_count, head_count, head_size = queries.shape
    score_scale = head_size ** (-0.5)
    total_keys = key_heads.shape[0]
    step_rows = key_step(total_keys)
    run_max = jnp.full((head_count, row_count), NEG_FILL, jnp.float32)
    run_total = jnp.zeros((head_count, row_count), jnp.float32)
    for key_start in range(0, total_keys, step_rows):
        scores = block_scores(
            queries,
            key_heads[key_start : key_start + step_rows],
            query_clip,
            key_clip[key_start : key_start + step_rows],
            score_scale,
        )
        new_max = jnp.maximum(run_max, jnp.max(scores, axis=2))
        run_total = run_total * jnp.exp(run_max - new_max) + jnp.sum(
            jnp.exp(scores - new_max[:, :, None]), axis=2
        )
        run_max = new_max
    log_total = run_max + jnp.log(run_total)
    output = jnp.zeros((row_count, head_count, head_size), jnp.float32)
    for key_start in range(0, total_keys, step_rows):
        scores = block_scores(
            queries,
            key_heads[key_start : key_start + step_rows],
            query_clip,
            key_clip[key_start : key_start + step_rows],
            score_scale,
        )
        soft_weights = jnp.exp(scores - log_total[:, :, None]).astype(jnp.bfloat16)
        output = output + jnp.einsum(
            "htk,khe->the",
            soft_weights,
            value_heads[key_start : key_start + step_rows],
            preferred_element_type=jnp.float32,
        )
    return (output, log_total)


def attend_backward(
    queries, key_heads, value_heads, query_clip, key_clip, log_total, grad_mixed, output
):
    row_count, head_count, head_size = queries.shape
    score_scale = head_size ** (-0.5)
    total_keys = key_heads.shape[0]
    step_rows = key_step(total_keys)
    row_delta = jnp.sum(grad_mixed.astype(jnp.float32) * output, axis=2).T
    grad_query = jnp.zeros((row_count, head_count, head_size), jnp.float32)
    key_pieces = []
    value_pieces = []
    for key_start in range(0, total_keys, step_rows):
        key_part = key_heads[key_start : key_start + step_rows]
        value_part = value_heads[key_start : key_start + step_rows]
        scores = block_scores(
            queries, key_part, query_clip, key_clip[key_start : key_start + step_rows], score_scale
        )
        soft_weights = jnp.exp(scores - log_total[:, :, None])
        grad_soft = jnp.einsum(
            "the,khe->htk", grad_mixed, value_part, preferred_element_type=jnp.float32
        )
        grad_scores = (soft_weights * (grad_soft - row_delta[:, :, None])).astype(jnp.bfloat16)
        grad_query = grad_query + jnp.einsum(
            "htk,khe->the", grad_scores, key_part, preferred_element_type=jnp.float32
        )
        key_pieces.append(
            jnp.einsum("htk,the->khe", grad_scores, queries, preferred_element_type=jnp.float32)
        )
        value_pieces.append(
            jnp.einsum(
                "htk,the->khe",
                soft_weights.astype(jnp.bfloat16),
                grad_mixed,
                preferred_element_type=jnp.float32,
            )
        )
    key_terms = jnp.concatenate(key_pieces, axis=0) * score_scale
    value_terms = jnp.concatenate(value_pieces, axis=0)
    return (grad_query * score_scale, key_terms, value_terms)


def block_forward(
    residual, norm_params, w_qkv, w_out, w_up, w_down, head_count, query_clip, key_clip
):
    row_count, model_width = residual.shape
    head_size = model_width // head_count
    norm_float = norm_params.astype(jnp.float32)
    normed = layer_norm(residual, norm_float[:, 0], norm_float[:, 1]).astype(jnp.bfloat16)
    qkv = jnp.dot(normed, w_qkv, preferred_element_type=jnp.float32).astype(jnp.bfloat16)
    queries = qkv[:, :model_width].reshape(row_count, head_count, head_size)
    key_local = qkv[:, model_width : 2 * model_width]
    value_local = qkv[:, 2 * model_width :]
    key_full, value_full = (
        lax.all_gather(key_local, "seq", axis=0, tiled=True),
        lax.all_gather(value_local, "seq", axis=0, tiled=True),
    )
    key_heads = key_full.reshape(-1, head_count, head_size)
    value_heads = value_full.reshape(-1, head_count, head_size)
    output, log_total = attend_forward(queries, key_heads, value_heads, query_clip, key_clip)
    mixed = output.reshape(row_count, model_width).astype(jnp.bfloat16)
    middle = residual + jnp.dot(mixed, w_out, preferred_element_type=jnp.float32)
    normed_mid = layer_norm(middle, norm_float[:, 2], norm_float[:, 3]).astype(jnp.bfloat16)
    pre_act = jnp.dot(normed_mid, w_up, preferred_element_type=jnp.float32)
    hidden = gelu_exact(pre_act).astype(jnp.bfloat16)
    result = middle + jnp.dot(hidden, w_down, preferred_element_type=jnp.float32)
    kept = (
        residual,
        normed,
        queries,
        key_local,
        value_local,
        key_heads,
        value_heads,
        output,
        log_total,
        mixed,
        middle,
        normed_mid,
        pre_act,
        hidden,
    )
    return (result, kept)


def block_backward(
    grad_result, kept, norm_params, w_qkv, w_out, w_up, w_down, head_count, query_clip, key_clip
):
    (
        residual,
        normed,
        queries,
        key_local,
        value_local,
        key_heads,
        value_heads,
        output,
        log_total,
        mixed,
        middle,
        normed_mid,
        pre_act,
        hidden,
    ) = kept
    row_count, model_width = residual.shape
    head_size = model_width // head_count
    norm_float = norm_params.astype(jnp.float32)
    grad_low = grad_result.astype(jnp.bfloat16)
    grad_down = jnp.einsum("tf,tw->fw", hidden, grad_low, preferred_element_type=jnp.float32)
    grad_hidden = jnp.einsum("tw,fw->tf", grad_low, w_down, preferred_element_type=jnp.float32)
    gelu_value, gelu_pull = jax.vjp(gelu_exact, pre_act)
    grad_pre = gelu_pull(grad_hidden)[0].astype(jnp.bfloat16)
    grad_up = jnp.einsum("tw,tf->wf", normed_mid, grad_pre, preferred_element_type=jnp.float32)
    grad_normed_mid = jnp.einsum("tf,wf->tw", grad_pre, w_up, preferred_element_type=jnp.float32)
    second_value, second_pull = jax.vjp(layer_norm, middle, norm_float[:, 2], norm_float[:, 3])
    grad_mid_norm, grad_gain_two, grad_shift_two = second_pull(grad_normed_mid)
    grad_middle = grad_result + grad_mid_norm
    grad_branch = grad_middle.astype(jnp.bfloat16)
    grad_out_w = jnp.einsum("tv,tw->vw", mixed, grad_branch, preferred_element_type=jnp.float32)
    grad_mixed = jnp.einsum(
        "tw,vw->tv", grad_branch, w_out, preferred_element_type=jnp.float32
    ).astype(jnp.bfloat16)
    key_full, value_full = (
        lax.all_gather(key_local, "seq", axis=0, tiled=True),
        lax.all_gather(value_local, "seq", axis=0, tiled=True),
    )
    key_heads = key_full.reshape(-1, head_count, head_size)
    value_heads = value_full.reshape(-1, head_count, head_size)
    grad_query, key_terms, value_terms = attend_backward(
        queries,
        key_heads,
        value_heads,
        query_clip,
        key_clip,
        log_total,
        grad_mixed.reshape(row_count, head_count, head_size),
        output,
    )
    grad_key, grad_value = (
        lax.psum_scatter(
            key_terms.reshape(-1, model_width).astype(jnp.bfloat16),
            "seq",
            scatter_dimension=0,
            tiled=True,
        ).astype(jnp.float32),
        lax.psum_scatter(
            value_terms.reshape(-1, model_width).astype(jnp.bfloat16),
            "seq",
            scatter_dimension=0,
            tiled=True,
        ).astype(jnp.float32),
    )
    grad_qkv = jnp.concatenate(
        [grad_query.reshape(row_count, model_width), grad_key, grad_value], axis=1
    ).astype(jnp.bfloat16)
    grad_qkv_w = jnp.einsum("tw,tc->wc", normed, grad_qkv, preferred_element_type=jnp.float32)
    grad_normed = jnp.einsum("tc,wc->tw", grad_qkv, w_qkv, preferred_element_type=jnp.float32)
    first_value, first_pull = jax.vjp(layer_norm, residual, norm_float[:, 0], norm_float[:, 1])
    grad_first_norm, grad_gain_one, grad_shift_one = first_pull(grad_normed)
    grad_norms = jnp.stack([grad_gain_one, grad_shift_one, grad_gain_two, grad_shift_two], axis=1)
    return (grad_middle + grad_first_norm, (grad_norms, grad_qkv_w, grad_out_w, grad_up, grad_down))


def local(
    tokens,
    clip_lengths,
    target_pos,
    out_grad,
    norm1_gain,
    norm1_bias,
    w_qkv,
    w_out,
    norm2_gain,
    norm2_bias,
    w_fc1,
    w_fc2,
    w_embed,
    mask_token,
    pred_norm1_gain,
    pred_norm1_bias,
    pred_qkv,
    pred_out,
    pred_norm2_gain,
    pred_norm2_bias,
    pred_fc1,
    pred_fc2,
):
    row_count = tokens.shape[0]
    group_count = row_count * lax.axis_size("seq")
    lengths = clip_lengths[0]
    clip_ends = jnp.cumsum(lengths)
    local_rows = lax.axis_index("seq") * row_count + jnp.arange(row_count, dtype=jnp.int32)
    query_clip = clip_index(local_rows, clip_ends)
    key_clip = clip_index(jnp.arange(group_count, dtype=jnp.int32), clip_ends)
    past_end = (local_rows[:, None] >= clip_ends[None, :]).astype(jnp.int32)
    rel_rows = local_rows - jnp.sum(lengths[None, :] * past_end, axis=1)
    ctx_small = jnp.stack([norm1_gain, norm1_bias, norm2_gain, norm2_bias], axis=1)
    pred_small = jnp.stack(
        [pred_norm1_gain, pred_norm1_bias, pred_norm2_gain, pred_norm2_bias, mask_token], axis=1
    )
    ctx_params = (
        lax.all_gather(ctx_small, "fsdp", axis=0, tiled=True),
        lax.all_gather(w_qkv, "fsdp", axis=0, tiled=True),
        lax.all_gather(w_out, "fsdp", axis=0, tiled=True),
        lax.all_gather(w_fc1, "fsdp", axis=0, tiled=True),
        lax.all_gather(w_fc2, "fsdp", axis=0, tiled=True),
    )
    pred_params = (
        lax.all_gather(pred_small, "fsdp", axis=0, tiled=True),
        lax.all_gather(w_embed, "fsdp", axis=0, tiled=True),
        lax.all_gather(pred_qkv, "fsdp", axis=0, tiled=True),
        lax.all_gather(pred_out, "fsdp", axis=0, tiled=True),
        lax.all_gather(pred_fc1, "fsdp", axis=0, tiled=True),
        lax.all_gather(pred_fc2, "fsdp", axis=0, tiled=True),
    )
    ctx_result, ctx_kept = block_forward(
        tokens.astype(jnp.float32),
        ctx_params[0],
        ctx_params[1],
        ctx_params[2],
        ctx_params[3],
        ctx_params[4],
        HEADS,
        query_clip,
        key_clip,
    )
    context_out = ctx_result.astype(jnp.bfloat16)
    embedded = jnp.dot(context_out, pred_params[1], preferred_element_type=jnp.float32)
    targets = target_pos[0, 0]
    matches = jnp.arange(row_count, dtype=jnp.int32)[:, None] == targets[None, :]
    placement = matches.astype(jnp.float32)
    target_hit = jnp.sum(placement, axis=1)
    target_rel = jnp.sum(jnp.where(matches, rel_rows[:, None], 0), axis=0)
    mask_rows = pred_params[0][:, 4].astype(jnp.float32)[None, :] + position_table(target_rel, PD)
    placed = jnp.dot(
        placement, mask_rows, precision=lax.Precision.HIGHEST, preferred_element_type=jnp.float32
    )
    pred_in = embedded * (1.0 - target_hit[:, None]) + placed
    pred_result, pred_kept = block_forward(
        pred_in,
        pred_params[0],
        pred_params[2],
        pred_params[3],
        pred_params[4],
        pred_params[5],
        P_HEADS,
        query_clip,
        key_clip,
    )
    predicted = pred_result.astype(jnp.bfloat16)
    pred_back = (
        lax.all_gather(pred_small, "fsdp", axis=0, tiled=True),
        lax.all_gather(w_embed, "fsdp", axis=0, tiled=True),
        lax.all_gather(pred_qkv, "fsdp", axis=0, tiled=True),
        lax.all_gather(pred_out, "fsdp", axis=0, tiled=True),
        lax.all_gather(pred_fc1, "fsdp", axis=0, tiled=True),
        lax.all_gather(pred_fc2, "fsdp", axis=0, tiled=True),
    )
    ctx_back = (
        lax.all_gather(ctx_small, "fsdp", axis=0, tiled=True),
        lax.all_gather(w_qkv, "fsdp", axis=0, tiled=True),
        lax.all_gather(w_out, "fsdp", axis=0, tiled=True),
        lax.all_gather(w_fc1, "fsdp", axis=0, tiled=True),
        lax.all_gather(w_fc2, "fsdp", axis=0, tiled=True),
    )
    grad_pred_in, pred_grads = block_backward(
        out_grad.astype(jnp.float32),
        pred_kept,
        pred_back[0],
        pred_back[2],
        pred_back[3],
        pred_back[4],
        pred_back[5],
        P_HEADS,
        query_clip,
        key_clip,
    )
    grad_mask = jnp.sum(target_hit[:, None] * grad_pred_in, axis=0)
    grad_embedded = (grad_pred_in * (1.0 - target_hit[:, None])).astype(jnp.bfloat16)
    grad_embed_w = jnp.einsum(
        "td,tp->dp", context_out, grad_embedded, preferred_element_type=jnp.float32
    )
    grad_context = jnp.einsum(
        "tp,dp->td", grad_embedded, pred_back[1], preferred_element_type=jnp.float32
    )
    grad_tokens, ctx_grads = block_backward(
        grad_context,
        ctx_kept,
        ctx_back[0],
        ctx_back[1],
        ctx_back[2],
        ctx_back[3],
        ctx_back[4],
        HEADS,
        query_clip,
        key_clip,
    )
    pred_small_grad = jnp.concatenate([pred_grads[0], grad_mask[:, None]], axis=1)
    row_sums = (
        lax.psum_scatter(ctx_grads[0], "fsdp", scatter_dimension=0, tiled=True),
        lax.psum_scatter(ctx_grads[1], "fsdp", scatter_dimension=0, tiled=True),
        lax.psum_scatter(ctx_grads[2], "fsdp", scatter_dimension=0, tiled=True),
        lax.psum_scatter(ctx_grads[3], "fsdp", scatter_dimension=0, tiled=True),
        lax.psum_scatter(ctx_grads[4], "fsdp", scatter_dimension=0, tiled=True),
        lax.psum_scatter(grad_embed_w, "fsdp", scatter_dimension=0, tiled=True),
        lax.psum_scatter(pred_small_grad, "fsdp", scatter_dimension=0, tiled=True),
        lax.psum_scatter(pred_grads[1], "fsdp", scatter_dimension=0, tiled=True),
        lax.psum_scatter(pred_grads[2], "fsdp", scatter_dimension=0, tiled=True),
        lax.psum_scatter(pred_grads[3], "fsdp", scatter_dimension=0, tiled=True),
        lax.psum_scatter(pred_grads[4], "fsdp", scatter_dimension=0, tiled=True),
    )
    summed = (
        lax.psum(row_sums[0].astype(jnp.bfloat16), "seq").astype(jnp.float32),
        lax.psum(row_sums[1].astype(jnp.bfloat16), "seq").astype(jnp.float32),
        lax.psum(row_sums[2].astype(jnp.bfloat16), "seq").astype(jnp.float32),
        lax.psum(row_sums[3].astype(jnp.bfloat16), "seq").astype(jnp.float32),
        lax.psum(row_sums[4].astype(jnp.bfloat16), "seq").astype(jnp.float32),
        lax.psum(row_sums[5].astype(jnp.bfloat16), "seq").astype(jnp.float32),
        lax.psum(row_sums[6].astype(jnp.bfloat16), "seq").astype(jnp.float32),
        lax.psum(row_sums[7].astype(jnp.bfloat16), "seq").astype(jnp.float32),
        lax.psum(row_sums[8].astype(jnp.bfloat16), "seq").astype(jnp.float32),
        lax.psum(row_sums[9].astype(jnp.bfloat16), "seq").astype(jnp.float32),
        lax.psum(row_sums[10].astype(jnp.bfloat16), "seq").astype(jnp.float32),
    )
    return (
        context_out,
        predicted,
        grad_tokens.astype(jnp.bfloat16),
        summed[0][:, 0],
        summed[0][:, 1],
        summed[1],
        summed[2],
        summed[0][:, 2],
        summed[0][:, 3],
        summed[3],
        summed[4],
        summed[5],
        summed[6][:, 4],
        summed[6][:, 0],
        summed[6][:, 1],
        summed[7],
        summed[8],
        summed[6][:, 2],
        summed[6][:, 3],
        summed[9],
        summed[10],
    )


BF16 = jnp.bfloat16
F32 = jnp.float32
MESH = pl.DeviceIdType.MESH
LOG2E = 1.4426950408889634
LN2 = 0.6931471805599453
LANES = 128
SMALL_ROWS = 16
ANYWHERE = pl.BlockSpec(memory_space=pl.ANY)
IN_VMEM = pl.BlockSpec(memory_space=pltpu.VMEM)


def fits_fast(mesh):
    return mesh.shape["fsdp"] == 8 and mesh.shape["seq"] == 4


def fsdp_peer(bit):
    return (lax.axis_index("fsdp") ^ bit, lax.axis_index("seq"))


def seq_peer(index):
    return (lax.axis_index("fsdp"), index)


def enter(peers):
    barrier = pltpu.get_barrier_semaphore()
    for peer in peers:
        pl.semaphore_signal(barrier, inc=1, device_id=peer, device_id_type=MESH)
    pl.semaphore_wait(barrier, len(peers))


def send(src, dst, send_sem, recv_sem, peer):
    return pltpu.make_async_remote_copy(
        src_ref=src,
        dst_ref=dst,
        send_sem=send_sem,
        recv_sem=recv_sem,
        device_id=peer,
        device_id_type=MESH,
    )


def remote_params(collective_id, vmem=None):
    return pltpu.CompilerParams(
        collective_id=collective_id, has_side_effects=True, vmem_limit_bytes=vmem
    )


def mate_z():
    return seq_peer(lax.axis_index("seq") ^ 1)


def quarter():
    return (lax.axis_index("fsdp") & 1) * 2 + (lax.axis_index("seq") & 1)


def across_lanes(left, right):
    return lax.dot_general(left, right, (((1,), (1,)), ((), ())), preferred_element_type=F32)


def forward_pass(tokens, out_grad, side, ends, shards, heads, narrow_heads):
    rows, width = tokens.shape
    narrow = out_grad.shape[1]
    hidden_width = shards[4].shape[1]
    narrow_hidden = shards[9].shape[1]
    shapes = [shard.shape for shard in shards]
    array_count = len(shards)
    units = []
    for index, (shard_rows, columns) in enumerate(shapes):
        if shard_rows * columns >= 100000:
            half = shard_rows // 2
            units.append((index, 0, half, 2, 4))
            units.append((index, half, half, 4, 2))
        else:
            near, far = (2, 4) if len(units) % 2 == 0 else (4, 2)
            units.append((index, 0, shard_rows, near, far))
    count = len(units)
    ahead = 3
    last_unit = {}
    for u, unit in enumerate(units):
        last_unit[unit[0]] = u

    block_widths = ((width, heads, hidden_width, 2), (narrow, narrow_heads, narrow_hidden, 1))
    saved_shapes = []
    for w, _, ff, _ in block_widths:
        saved_shapes += [
            ((w, rows), BF16),
            ((rows, w), BF16),
            ((2, w // LANES, 4, rows, LANES), BF16),
            ((rows, w), BF16),
            ((w // LANES, 8, rows), F32),
            ((rows, w), F32),
            ((w, rows), BF16),
            ((rows, ff), BF16),
            ((w, rows), BF16),
        ]
    per_block = len(saved_shapes) // 2
    saved_shapes += [((width, rows), BF16), ((rows, narrow), F32), (side.shape, F32), ((rows, width), BF16)]
    saved_shapes += [((SMALL_ROWS, width), F32), ((SMALL_ROWS, narrow), F32)]
    saved_count = len(saved_shapes)

    def kernel(*refs):
        tokens_ref, out_grad_ref, side_ref, ends_ref = refs[:4]
        sources = refs[4 : 4 + array_count]
        base = 4 + array_count
        weight_outs = refs[base : base + array_count]
        base += array_count
        saved_outs = refs[base : base + saved_count]
        base += saved_count
        out_grad_out, ends_out, context_out, predicted_out, wide_hidden_t, narrow_hidden_t = refs[base : base + 6]
        base += 6
        weights = refs[base : base + array_count]
        base += array_count
        saved = refs[base : base + saved_count]
        base += saved_count
        (
            bias,
            ends_buf,
            predicted,
            wide_normed,
            wide_hidden,
            narrow_normed,
            narrow_hid,
            stage,
            stage_sems,
            send_sems,
            recv_sems,
            local_sems,
            weight_sems,
            saved_sems,
            trade_send,
            trade_recv,
            trade_keep,
            key_send,
            key_recv,
        ) = refs[base:]
        context_t, entry, side_buf, token_buf, gains, narrow_gains = saved[2 * per_block :]
        context = wide_normed

        me = lax.axis_index("fsdp")
        place = lax.axis_index("seq")
        core = me & 1
        high = place >> 1
        low = place & 1
        mine = quarter()
        trades = core != high
        trade_peer = ((me & 6) | high, core * 2 + low)

        barrier = pltpu.get_barrier_semaphore()
        for peer in (fsdp_peer(1), fsdp_peer(2), fsdp_peer(4), mate_z()):
            pl.semaphore_signal(barrier, inc=1, device_id=peer, device_id_type=MESH)

        @pl.when(trades)
        def _():
            pl.semaphore_signal(barrier, inc=1, device_id=trade_peer, device_id_type=MESH)

        pl.semaphore_wait(barrier, 4 + trades.astype(jnp.int32))


        def trade_copy(i, src, dst):
            return send(src, dst, trade_send.at[i], trade_recv.at[i], trade_peer)

        def keep_copy(i, src, dst):
            return pltpu.make_async_copy(src, dst, trade_keep.at[i])

        traded = [
            (tokens_ref, token_buf),
            (side_ref, side_buf),
            (ends_ref, ends_buf),
            (out_grad_ref, out_grad_out),
            (context, context_out),
            (predicted, predicted_out),
        ]

        def trade_start(i):
            @pl.when(trades)
            def _():
                trade_copy(i, *traded[i]).start()

            @pl.when(jnp.logical_not(trades))
            def _():
                keep_copy(i, *traded[i]).start()

        def trade_arrived(i):
            @pl.when(trades)
            def _():
                trade_copy(i, *traded[i]).wait_recv()

            @pl.when(jnp.logical_not(trades))
            def _():
                keep_copy(i, *traded[i]).wait()

        def trade_sent(i):
            @pl.when(trades)
            def _():
                trade_copy(i, *traded[i]).wait_send()


        def place_of(u, owner):
            index, first, unit_rows, _, _ = units[u]
            start = owner * shapes[index][0] + first
            return weights[index].at[pl.ds(pl.multiple_of(start, 16), unit_rows)]

        def own_shard(u):
            index, first, unit_rows, _, _ = units[u]
            return sources[index].at[pl.ds(first, unit_rows)]

        def weight_copy(u, slot):
            _, _, _, near, far = units[u]
            owner = me ^ (0, 0, near, 0, near, far, near ^ far)[slot]
            bit = (near, far, far, 1, 1, 1, 1)[slot]
            src = own_shard(u) if slot in (0, 1, 3) else place_of(u, owner)
            return send(src, place_of(u, owner), send_sems.at[u, slot], recv_sems.at[u, slot], fsdp_peer(bit))

        def own_weight(u):
            return pltpu.make_async_copy(own_shard(u), place_of(u, me), local_sems.at[u])

        def weight_out(index):
            return pltpu.make_async_copy(weights[index], weight_outs[index], weight_sems.at[index])

        def launch(u):
            for slot in (0, 1, 3):
                weight_copy(u, slot).start()
            own_weight(u).start()

        def arrive(u):
            weight_copy(u, 0).wait_recv()
            weight_copy(u, 2).start()
            weight_copy(u, 4).start()
            weight_copy(u, 1).wait_recv()
            weight_copy(u, 5).start()
            if u + ahead < count:
                launch(u + ahead)

        def relay(u):
            weight_copy(u, 2).wait_recv()
            weight_copy(u, 6).start()

        def complete(u):
            for slot in (3, 4, 5, 6):
                weight_copy(u, slot).wait_recv()
            own_weight(u).wait()
            index = units[u][0]
            if last_unit[index] == u:
                weight_out(index).start()

        ticks = []
        ready = {}
        for u in range(count + 2):
            if u < count:
                ticks.append((arrive, u))
            if 1 <= u <= count:
                ticks.append((relay, u - 1))
            if u >= 2:
                ticks.append((complete, u - 2))
                ready[units[u - 2][0]] = len(ticks)
        position = [0]

        def advance(steps):
            for _ in range(steps):
                if position[0] < len(ticks):
                    step, u = ticks[position[0]]
                    step(u)
                    position[0] += 1

        def need(index):
            while position[0] < ready[index]:
                advance(1)


        def save(i):
            return pltpu.make_async_copy(saved[i], saved_outs[i], saved_sems.at[i])

        def norm_into(dst, get, table, gain_at):
            @pl.loop(0, rows // 64)
            def _(i):
                part = pl.ds(pl.multiple_of(i * 64, 64), 64)
                value = get(part)
                value = value - jnp.mean(value, axis=1, keepdims=True)
                inverse = lax.rsqrt(jnp.mean(value * value, axis=1, keepdims=True) + EPSILON)
                dst[part] = (
                    value * inverse * table[gain_at : gain_at + 1, :] + table[gain_at + 1 : gain_at + 2, :]
                ).astype(BF16)

        def turn(src, dst):
            for c in range(dst.shape[0] // LANES):
                at = slice(c * LANES, (c + 1) * LANES)
                dst[at, :] = src[:, at].T

        def run_block(which, get, table, first_weight, finish, inside):
            w, head_count, ff, in_group = block_widths[which]
            (normed_t, queries, kv, mixed, logs, middle, normed_mid_t, slope, mixed_t) = saved[
                which * per_block : (which + 1) * per_block
            ]
            normed, hidden = ((wide_normed, wide_hidden), (narrow_normed, narrow_hid))[which]
            hidden_out = (wide_hidden_t, narrow_hidden_t)[which]
            w_qkv, w_out, w_up, w_down = [weights[first_weight[i]] for i in range(4)]
            slabs = w // LANES
            groups = slabs // in_group
            head_size = w // head_count
            per_slab = LANES // head_size
            factor = head_size ** (-0.5) * LOG2E
            columns = in_group * LANES

            def kv_copy(kind, g):
                owner = mine ^ 1 if kind == 2 else mine
                part = kv.at[:, pl.ds(g * in_group, in_group), owner]
                return send(
                    part,
                    part,
                    key_send.at[which, kind, g],
                    key_recv.at[which, kind, g],
                    mate_z() if kind == 0 else fsdp_peer(1),
                )

            norm_into(normed, get, table, 0)
            turn(normed, normed_t)
            save(which * per_block).start()
            need(first_weight[0])
            for g in range(groups):
                for kind in range(2):
                    tile = jnp.dot(
                        normed[...],
                        w_qkv[:, pl.ds((1 + kind) * w + g * columns, columns)],
                        preferred_element_type=F32,
                    ).astype(BF16)
                    for k in range(in_group):
                        kv[kind, g * in_group + k, mine] = tile[:, k * LANES : (k + 1) * LANES]
                kv_copy(0, g).start()
                kv_copy(1, g).start()

            @pl.loop(0, groups)
            def _(g):
                at = pl.ds(pl.multiple_of(g * columns, columns), columns)
                queries[:, at] = jnp.dot(normed[...], w_qkv[:, at], preferred_element_type=F32).astype(BF16)
            save(which * per_block + 1).start()
            advance(inside[0])
            kv_copy(0, 0).wait_recv()
            kv_copy(2, 0).start()

            lane = lax.broadcasted_iota(jnp.int32, (rows, LANES), 1) // head_size
            sub = lax.broadcasted_iota(jnp.int32, (LANES, rows), 0) // head_size

            @pl.loop(0, slabs)
            def _(j):
                g = j // in_group

                @pl.when(j % in_group == 0)
                def _():
                    kv_copy(1, g).wait_recv()
                    kv_copy(2, g).wait_recv()

                at = pl.ds(pl.multiple_of(j * LANES, LANES), LANES)
                own_queries = queries[:, at]
                key_slab = kv[0, j].reshape(4 * rows, LANES)
                values_t = kv[1, j].reshape(4 * rows, LANES).T
                output = jnp.zeros((LANES, rows), F32)
                logs[j] = jnp.zeros((8, rows), F32)
                for head in range(per_slab):
                    own = jnp.where(lane == head, own_queries, jnp.zeros_like(own_queries))
                    scores = across_lanes(key_slab, own) * factor + bias[...]
                    top = jnp.max(scores, axis=0, keepdims=True)
                    soft = jnp.exp2(scores - top)
                    total = jnp.sum(soft, axis=0, keepdims=True)
                    attended = jnp.dot(values_t, soft.astype(BF16), preferred_element_type=F32) / total
                    output = jnp.where(sub == head, attended, output)
                    logs[j, head : head + 1, :] = top + jnp.log2(total)
                mixed[:, at] = output.T.astype(BF16)
                mixed_t[at, :] = output.astype(BF16)

                @pl.when(jnp.logical_and(j % in_group == 0, g + 1 < groups))
                def _():
                    kv_copy(0, g + 1).wait_recv()
                    kv_copy(2, g + 1).start()

                for k in range(slabs):

                    @pl.when(j == k)
                    def _():
                        advance(inside[1])

            for i in (2, 3, 4, 8):
                save(which * per_block + i).start()
            need(first_weight[1])
            step = 2 * LANES if w % (2 * LANES) == 0 else LANES

            @pl.loop(0, w // step)
            def _(c):
                at = pl.ds(pl.multiple_of(c * step, step), step)
                middle[:, at] = get(pl.ds(0, rows), at) + jnp.dot(
                    mixed[...], w_out[:, at], preferred_element_type=F32
                )
            save(which * per_block + 5).start()
            norm_into(normed, lambda part: middle[part], table, 2)
            turn(normed, normed_mid_t)
            save(which * per_block + 6).start()
            need(first_weight[2])

            def stage_copy(c):
                return pltpu.make_async_copy(
                    stage.at[c % 2],
                    hidden_out.at[pl.ds(pl.multiple_of(c * 2 * LANES, 2 * LANES), 2 * LANES)],
                    stage_sems.at[c % 2],
                )

            @pl.loop(0, ff // (2 * LANES))
            def _(c):
                at = pl.ds(pl.multiple_of(c * 2 * LANES, 2 * LANES), 2 * LANES)
                pre = jnp.dot(normed[...], w_up[:, at], preferred_element_type=F32)
                below = 0.5 * (1.0 + lax.erf(pre * (0.5**0.5)))
                bell = jnp.exp2(pre * pre * (-0.5 * LOG2E)) * (1.0 / math.sqrt(2.0 * math.pi))
                active = (pre * below).astype(BF16)
                hidden[:, at] = active
                slope[:, at] = (below + pre * bell).astype(BF16)

                @pl.when(c >= 2)
                def _():
                    stage_copy(c - 2).wait()

                stage[c % 2] = active.T
                stage_copy(c).start()

            stage_copy(ff // (2 * LANES) - 2).wait()
            stage_copy(ff // (2 * LANES) - 1).wait()
            save(which * per_block + 7).start()
            need(first_weight[3])

            @pl.loop(0, w // step)
            def _(c):
                at = pl.ds(pl.multiple_of(c * step, step), step)
                finish(
                    at, middle[:, at] + jnp.dot(hidden[...], w_down[:, at], preferred_element_type=F32)
                )
            for g in range(groups):
                for kind in range(3):
                    kv_copy(kind, g).wait_send()


        for i in (0, 2, 1):
            trade_start(i)
        for u in range(ahead):
            launch(u)
        trade_start(3)
        need(1)
        for owner in range(8):
            gains[:, owner * LANES : (owner + 1) * LANES] = weights[0][
                owner * SMALL_ROWS : (owner + 1) * SMALL_ROWS, :
            ].astype(F32)
        total = weights[1][0:SMALL_ROWS, :].astype(F32)
        for owner in range(1, 8):
            total = total + weights[1][owner * SMALL_ROWS : (owner + 1) * SMALL_ROWS, :].astype(F32)
        narrow_gains[...] = total
        save(2 * per_block + 4).start()
        save(2 * per_block + 5).start()
        trade_arrived(2)
        group_bias(bias, ends_buf, rows)
        trade_arrived(0)
        save(2 * per_block + 3).start()

        def token_rows(part, at=slice(None)):
            return token_buf[part, at].astype(F32)

        def finish_context(at, value):
            context[:, at] = value.astype(BF16)

        run_block(0, token_rows, gains, (2, 3, 4, 5), finish_context, (1, 1))
        trade_start(4)
        turn(context, context_t)
        save(2 * per_block).start()
        need(6)
        trade_arrived(1)
        save(2 * per_block + 2).start()
        embedded = jnp.dot(context[...], weights[6][...], preferred_element_type=F32)
        hit = side_buf[:, narrow : narrow + 1]
        entry[...] = jnp.where(hit > 0.0, narrow_gains[4:5, :] + side_buf[:, 0:narrow], embedded)
        save(2 * per_block + 1).start()

        def entry_rows(part, at=slice(None)):
            return entry[part, at]

        def finish_predicted(at, value):
            predicted[:, at] = value.astype(BF16)

        run_block(1, entry_rows, narrow_gains, (7, 8, 9, 10), finish_predicted, (0, 0))
        trade_start(5)
        advance(len(ticks))
        for u in range(count):
            for slot in range(7):
                weight_copy(u, slot).wait_send()
        for index in range(array_count):
            weight_out(index).wait()
        for i in range(saved_count):
            save(i).wait()
        keep_copy(6, ends_buf, ends_out).start()
        for i in (3, 4, 5):
            trade_arrived(i)
        for i in range(6):
            trade_sent(i)
        keep_copy(6, ends_buf, ends_out).wait()

    gathered = [(8 * shape[0], shape[1]) for shape in shapes]
    out_shape = (
        [jax.ShapeDtypeStruct(shape, BF16) for shape in gathered]
        + [jax.ShapeDtypeStruct(shape, kind) for shape, kind in saved_shapes]
        + [
            jax.ShapeDtypeStruct(out_grad.shape, BF16),
            jax.ShapeDtypeStruct(ends.shape, jnp.int32),
            jax.ShapeDtypeStruct((rows, width), BF16),
            jax.ShapeDtypeStruct((rows, narrow), BF16),
            jax.ShapeDtypeStruct((hidden_width, rows), BF16),
            jax.ShapeDtypeStruct((narrow_hidden, rows), BF16),
        ]
    )
    scratch = (
        [pltpu.VMEM(shape, BF16) for shape in gathered]
        + [pltpu.VMEM(shape, kind) for shape, kind in saved_shapes]
        + [
            pltpu.VMEM((4 * rows, rows), F32),
            pltpu.VMEM(ends.shape, jnp.int32),
            pltpu.VMEM((rows, narrow), BF16),
            pltpu.VMEM((rows, width), BF16),
            pltpu.VMEM((rows, hidden_width), BF16),
            pltpu.VMEM((rows, narrow), BF16),
            pltpu.VMEM((rows, narrow_hidden), BF16),
            pltpu.VMEM((2, 2 * LANES, rows), BF16),
            pltpu.SemaphoreType.DMA((2,)),
            pltpu.SemaphoreType.DMA((count, 7)),
            pltpu.SemaphoreType.DMA((count, 7)),
            pltpu.SemaphoreType.DMA((count,)),
            pltpu.SemaphoreType.DMA((array_count,)),
            pltpu.SemaphoreType.DMA((saved_count,)),
            pltpu.SemaphoreType.DMA((6,)),
            pltpu.SemaphoreType.DMA((6,)),
            pltpu.SemaphoreType.DMA((7,)),
            pltpu.SemaphoreType.DMA((2, 3, 4)),
            pltpu.SemaphoreType.DMA((2, 3, 4)),
        ]
    )
    results = pl.pallas_call(
        kernel,
        out_shape=out_shape,
        in_specs=[ANYWHERE] * (4 + array_count),
        out_specs=[ANYWHERE] * len(out_shape),
        scratch_shapes=scratch,
        compiler_params=remote_params(1, 62 << 20),
        name="forward_pass",
    )(tokens, out_grad, side, ends, *shards)
    saved = results[array_count : array_count + saved_count]
    return (
        results[:array_count],
        saved[:per_block],
        saved[per_block : 2 * per_block],
        saved[2 * per_block :],
        results[array_count + saved_count :],
    )


def group_bias(bias, ends, rows):
    mine = quarter()
    key_row = lax.broadcasted_iota(jnp.int32, (4 * rows, rows), 0)
    query_row = mine * rows + lax.broadcasted_iota(jnp.int32, (4 * rows, rows), 1)
    key_clip = jnp.zeros((4 * rows, rows), jnp.int32)
    query_clip = jnp.zeros((4 * rows, rows), jnp.int32)
    for c in range(3):
        end = ends[c : c + 1, 0:1]
        key_clip = key_clip + (key_row >= end).astype(jnp.int32)
        query_clip = query_clip + (query_row >= end).astype(jnp.int32)
    bias[...] = jnp.where(key_clip == query_clip, 0.0, NEG_FILL)


def slab_backward(queries, grads, mixed, logs, key_slab, value_slab, bias, head_size):
    rows = queries.shape[0]
    keys = key_slab.shape[0]
    factor = head_size ** (-0.5) * LOG2E
    lane = lax.broadcasted_iota(jnp.int32, (rows, LANES), 1) // head_size
    key_lane = lax.broadcasted_iota(jnp.int32, (keys, LANES), 1) // head_size
    sub = lax.broadcasted_iota(jnp.int32, (LANES, rows), 0) // head_size
    pick = (
        lax.broadcasted_iota(jnp.int32, (8, LANES), 1) // head_size
        == lax.broadcasted_iota(jnp.int32, (8, LANES), 0)
    ).astype(F32)
    deltas = lax.dot_general(
        pick,
        grads.astype(F32) * mixed.astype(F32),
        (((1,), (1,)), ((), ())),
        precision=lax.Precision.HIGHEST,
        preferred_element_type=F32,
    )
    keys_t = key_slab.T
    dq = jnp.zeros((LANES, rows), F32)
    dk = jnp.zeros((keys, LANES), F32)
    dv = jnp.zeros((keys, LANES), F32)
    for head in range(LANES // head_size):
        own = jnp.where(lane == head, queries, jnp.zeros_like(queries))
        own_grad = jnp.where(lane == head, grads, jnp.zeros_like(grads))
        scores = across_lanes(key_slab, own) * factor + bias[...]
        weights = jnp.exp2(scores - logs[head : head + 1, :])
        grad_soft = across_lanes(value_slab, own_grad)
        grad_scores = (weights * (grad_soft - deltas[head : head + 1, :])).astype(BF16)
        dv = jnp.where(key_lane == head, jnp.dot(weights.astype(BF16), grads, preferred_element_type=F32), dv)
        dk = jnp.where(key_lane == head, jnp.dot(grad_scores, queries, preferred_element_type=F32), dk)
        dq = jnp.where(sub == head, jnp.dot(keys_t, grad_scores, preferred_element_type=F32), dq)
    return dq, dk, dv


def norm_backward(value, upper, gain_row):
    value = value - jnp.mean(value, axis=1, keepdims=True)
    inverse = lax.rsqrt(jnp.mean(value * value, axis=1, keepdims=True) + EPSILON)
    value = value * inverse
    scaled = upper * gain_row
    inside = (
        scaled
        - jnp.mean(scaled, axis=1, keepdims=True)
        - value * jnp.mean(scaled * value, axis=1, keepdims=True)
    )
    return (
        inverse * inside,
        jnp.sum(upper * value, axis=0, keepdims=True),
        jnp.sum(upper, axis=0, keepdims=True),
    )


def middle_back(loads, lefts_t, head_count, collective_id):
    names = list(loads)
    rows, narrow = loads["out_grad"].shape
    width = loads["wide_middle"].shape[1]
    narrow_hidden = loads["narrow_slope"].shape[1]
    wide_hidden = loads["wide_slope"].shape[1]
    slabs = narrow // LANES
    head_size = narrow // head_count
    scale = head_size ** (-0.5)
    keys = 4 * rows
    half = 2 * rows
    sizes = [left.shape[0] // 8 for left in lefts_t]
    right_widths = [narrow, narrow_hidden, narrow, 3 * narrow, narrow]
    grads = len(lefts_t)

    def kernel(*refs):
        load_refs = dict(zip(names, refs[: len(names)]))
        left_refs = refs[len(names) : len(names) + grads]
        base = len(names) + grads
        partials_out = refs[base : base + grads]
        low_out, pre_out, branch_out, middle_out, mixed_out, wide_sums_out, narrow_sums_out = refs[
            base + grads : base + grads + 7
        ]
        base += grads + 7
        bufs = dict(zip(names, refs[base : base + len(names)]))
        base += len(names)
        lefts = refs[base : base + grads]
        rights = refs[base + grads : base + 2 * grads]
        partials = refs[base + 2 * grads : base + 3 * grads]
        base += 3 * grads
        (
            bias,
            dkv,
            core_in,
            z_in,
            upper,
            grad_middle,
            grad_mixed,
            wide_low,
            wide_pre,
            wide_upper,
            wide_branch,
            wide_mixed,
            wide_sums,
            narrow_sums,
            load_sems,
            give_send,
            give_recv,
            give_own,
            right_send,
            right_recv,
            key_send,
            key_recv,
            out_sems,
        ) = refs[base:]
        me = lax.axis_index("fsdp")
        core = me & 1
        low = lax.axis_index("seq") & 1
        enter([fsdp_peer(1), mate_z()])

        def load(name):
            return pltpu.make_async_copy(load_refs[name], bufs[name], load_sems.at[names.index(name)])

        loaded = set()

        def got(name):
            if name not in loaded:
                load(name).wait()
                loaded.add(name)
            return bufs[name]

        def left_copy(which, p):
            owner = 2 * p + (core ^ 1)
            return send(
                left_refs[which].at[pl.ds(pl.multiple_of(owner * sizes[which], 16), sizes[which])],
                lefts[which].at[1, p],
                give_send.at[which, p],
                give_recv.at[which, p],
                fsdp_peer(1),
            )

        def left_own(which, p):
            owner = 2 * p + core
            return pltpu.make_async_copy(
                left_refs[which].at[pl.ds(pl.multiple_of(owner * sizes[which], 16), sizes[which])],
                lefts[which].at[0, p],
                give_own.at[which, p],
            )

        def right_copy(which):
            src = rights[which].at[pl.ds(0, rows)]
            return send(
                src, rights[which].at[pl.ds(rows, rows)], right_send.at[which], right_recv.at[which], fsdp_peer(1)
            )

        outs = [(partials[i], partials_out[i]) for i in range(grads)] + [
            (wide_low, low_out),
            (wide_pre, pre_out),
            (wide_branch, branch_out),
            (grad_middle, middle_out),
            (wide_mixed, mixed_out),
            (wide_sums, wide_sums_out),
            (narrow_sums, narrow_sums_out),
        ]

        def out_copy(i):
            return pltpu.make_async_copy(outs[i][0], outs[i][1], out_sems.at[i])

        def form(which):
            for p in range(4):
                left_copy(which, p).wait_recv()
                left_own(which, p).wait()
            right_copy(which).wait_recv()
            size = 4 * sizes[which]
            step = 512 if size > 512 else size
            total = jnp.dot(
                lefts[which][0].reshape(size, rows), rights[which][pl.ds(0, rows), :], preferred_element_type=F32
            ) + jnp.dot(
                lefts[which][1].reshape(size, rows), rights[which][pl.ds(rows, rows), :], preferred_element_type=F32
            )
            partials[which][...] = total.astype(BF16)
            out_copy(which).start()

        for name in names:
            load(name).start()
        for which in range(grads):
            for p in range(4):
                left_copy(which, p).start()
                left_own(which, p).start()

        own = pl.ds(0, rows)
        narrow_sums[...] = jnp.zeros_like(narrow_sums)
        wide_sums[...] = jnp.zeros_like(wide_sums)
        grads_in = got("out_grad")
        rights[0][own, :] = grads_in[...]
        right_copy(0).start()
        step = 2 * LANES
        got("narrow_down")
        got("narrow_slope")
        for c in range(narrow_hidden // (2 * step)):
            at = pl.ds(c * 2 * step, 2 * step)
            product = across_lanes(grads_in[...], bufs["narrow_down"][at, :])
            rights[1][own, at] = (product * bufs["narrow_slope"][:, at].astype(F32)).astype(BF16)
        right_copy(1).start()
        upper[...] = across_lanes(rights[1][own, :], got("narrow_up")[...])
        table = got("narrow_gains")
        got("narrow_middle")
        chunk = 64
        gain_sum = jnp.zeros((1, narrow), F32)
        shift_sum = jnp.zeros((1, narrow), F32)
        for i in range(rows // chunk):
            part = pl.ds(i * chunk, chunk)
            inner, gain_term, shift_term = norm_backward(
                bufs["narrow_middle"][part], upper[part], table[2:3, :]
            )
            gain_sum, shift_sum = gain_sum + gain_term, shift_sum + shift_term
            total = grads_in[part].astype(F32) + inner
            bufs["narrow_middle"][part] = total
            rights[2][part, :] = total.astype(BF16)
        narrow_sums[6:7, :] = gain_sum
        narrow_sums[7:8, :] = shift_sum
        right_copy(2).start()
        grad_mixed[...] = across_lanes(rights[2][own, :], got("narrow_out")[...]).astype(BF16)
        group_bias(bias, got("ends"), rows)

        got("narrow_queries")
        got("narrow_kv")
        got("narrow_mixed")
        got("narrow_logs")

        def key_core_copy(j):
            return send(
                dkv.at[:, j, pl.ds((core ^ 1) * half, half)],
                core_in.at[:, j],
                key_send.at[0, j],
                key_recv.at[0, j],
                fsdp_peer(1),
            )

        def key_far_copy(j):
            return send(
                core_in.at[:, j, pl.ds((low ^ 1) * rows, rows)],
                z_in.at[:, j],
                key_send.at[1, j],
                key_recv.at[1, j],
                mate_z(),
            )

        def key_middle(j):
            key_core_copy(j).wait_recv()
            for kind in range(2):
                core_in[kind, j] = (
                    core_in[kind, j].astype(F32) + dkv[kind, j, pl.ds(core * half, half)].astype(F32)
                ).astype(BF16)
            key_far_copy(j).start()

        def key_end(j):
            key_far_copy(j).wait_recv()
            for kind in range(2):
                total = core_in[kind, j, pl.ds(low * rows, rows)].astype(F32) + z_in[kind, j].astype(F32)
                at = pl.ds(pl.multiple_of((1 + kind) * narrow + j * LANES, LANES), LANES)
                rights[3][own, at] = total.astype(BF16)

        @pl.loop(0, slabs)
        def _(j):
            at = pl.ds(pl.multiple_of(j * LANES, LANES), LANES)
            dq, dk, dv = slab_backward(
                bufs["narrow_queries"][:, at],
                grad_mixed[:, at],
                bufs["narrow_mixed"][:, at],
                bufs["narrow_logs"][j],
                bufs["narrow_kv"][0, j],
                bufs["narrow_kv"][1, j],
                bias,
                head_size,
            )
            rights[3][own, at] = (dq.T * scale).astype(BF16)
            dkv[0, j] = (dk * scale).astype(BF16)
            dkv[1, j] = dv.astype(BF16)
            key_core_copy(j).start()

            @pl.when(j >= 1)
            def _():
                key_middle(j - 1)

        form(0)
        key_middle(slabs - 1)
        form(1)
        form(2)
        for j in range(slabs):
            key_end(j)
        right_copy(3).start()
        upper[...] = across_lanes(rights[3][own, :], got("narrow_qkv")[...])
        got("entry")
        side = got("side")
        gain_sum = jnp.zeros((1, narrow), F32)
        shift_sum = jnp.zeros((1, narrow), F32)
        mask_sum = jnp.zeros((1, narrow), F32)
        for i in range(rows // chunk):
            part = pl.ds(i * chunk, chunk)
            inner, gain_term, shift_term = norm_backward(bufs["entry"][part], upper[part], table[0:1, :])
            gain_sum, shift_sum = gain_sum + gain_term, shift_sum + shift_term
            total = bufs["narrow_middle"][part] + inner
            hit = side[part, narrow : narrow + 1]
            mask_sum = mask_sum + jnp.sum(hit * total, axis=0, keepdims=True)
            rights[4][part, :] = (total * (1.0 - hit)).astype(BF16)
        narrow_sums[4:5, :] = gain_sum
        narrow_sums[5:6, :] = shift_sum
        narrow_sums[8:9, :] = mask_sum
        out_copy(grads + 6).start()
        right_copy(4).start()

        got("w_embed")

        @pl.loop(0, width // step)
        def _(c):
            at = pl.ds(pl.multiple_of(c * step, step), step)
            product = across_lanes(rights[4][own, :], bufs["w_embed"][at, :])
            grad_middle[:, at] = product
            wide_low[:, at] = product.astype(BF16)
        out_copy(grads).start()
        got("wide_down")
        got("wide_slope")

        @pl.loop(0, wide_hidden // (2 * step))
        def _(c):
            at = pl.ds(pl.multiple_of(c * 2 * step, 2 * step), 2 * step)
            product = across_lanes(wide_low[...], bufs["wide_down"][at, :])
            wide_pre[:, at] = (product * bufs["wide_slope"][:, at].astype(F32)).astype(BF16)

        out_copy(grads + 1).start()
        got("wide_up")

        @pl.loop(0, width // step)
        def _(c):
            at = pl.ds(pl.multiple_of(c * step, step), step)
            wide_upper[:, at] = across_lanes(wide_pre[...], bufs["wide_up"][at, :])

        wide_table = got("wide_gains")
        got("wide_middle")
        gain_sum = jnp.zeros((1, width), F32)
        shift_sum = jnp.zeros((1, width), F32)
        for i in range(rows // chunk):
            part = pl.ds(i * chunk, chunk)
            inner, gain_term, shift_term = norm_backward(
                bufs["wide_middle"][part], wide_upper[part], wide_table[2:3, :]
            )
            gain_sum, shift_sum = gain_sum + gain_term, shift_sum + shift_term
            total = grad_middle[part] + inner
            grad_middle[part] = total
            wide_branch[part] = total.astype(BF16)
        wide_sums[2:3, :] = gain_sum
        wide_sums[3:4, :] = shift_sum
        for i in (2, 3, 5):
            out_copy(grads + i).start()
        got("wide_out")

        @pl.loop(0, width // step)
        def _(c):
            at = pl.ds(pl.multiple_of(c * step, step), step)
            wide_mixed[:, at] = across_lanes(wide_branch[...], bufs["wide_out"][at, :]).astype(BF16)
        out_copy(grads + 4).start()
        form(3)
        form(4)
        for which in range(grads):
            right_copy(which).wait_send()
            for p in range(4):
                left_copy(which, p).wait_send()
        for j in range(slabs):
            key_core_copy(j).wait_send()
            key_far_copy(j).wait_send()
        for i in range(grads + 7):
            out_copy(i).wait()

    out_shape = [
        jax.ShapeDtypeStruct((4 * size, columns), BF16) for size, columns in zip(sizes, right_widths)
    ] + [
        jax.ShapeDtypeStruct((rows, width), BF16),
        jax.ShapeDtypeStruct((rows, wide_hidden), BF16),
        jax.ShapeDtypeStruct((rows, width), BF16),
        jax.ShapeDtypeStruct((rows, width), F32),
        jax.ShapeDtypeStruct((rows, width), BF16),
        jax.ShapeDtypeStruct((SMALL_ROWS, width), F32),
        jax.ShapeDtypeStruct((SMALL_ROWS, narrow), F32),
    ]
    scratch = (
        [pltpu.VMEM(loads[name].shape, loads[name].dtype) for name in names]
        + [pltpu.VMEM((2, 4, size, rows), BF16) for size in sizes]
        + [pltpu.VMEM((2 * rows, columns), BF16) for columns in right_widths]
        + [pltpu.VMEM((4 * size, columns), BF16) for size, columns in zip(sizes, right_widths)]
        + [
            pltpu.VMEM((keys, rows), F32),
            pltpu.VMEM((2, slabs, keys, LANES), BF16),
            pltpu.VMEM((2, slabs, half, LANES), BF16),
            pltpu.VMEM((2, slabs, rows, LANES), BF16),
            pltpu.VMEM((rows, narrow), F32),
            pltpu.VMEM((rows, width), F32),
            pltpu.VMEM((rows, narrow), BF16),
            pltpu.VMEM((rows, width), BF16),
            pltpu.VMEM((rows, wide_hidden), BF16),
            pltpu.VMEM((rows, width), F32),
            pltpu.VMEM((rows, width), BF16),
            pltpu.VMEM((rows, width), BF16),
            pltpu.VMEM((SMALL_ROWS, width), F32),
            pltpu.VMEM((SMALL_ROWS, narrow), F32),
            pltpu.SemaphoreType.DMA((len(names),)),
            pltpu.SemaphoreType.DMA((grads, 4)),
            pltpu.SemaphoreType.DMA((grads, 4)),
            pltpu.SemaphoreType.DMA((grads, 4)),
            pltpu.SemaphoreType.DMA((grads,)),
            pltpu.SemaphoreType.DMA((grads,)),
            pltpu.SemaphoreType.DMA((2, slabs)),
            pltpu.SemaphoreType.DMA((2, slabs)),
            pltpu.SemaphoreType.DMA((grads + 7,)),
        ]
    )
    return pl.pallas_call(
        kernel,
        out_shape=out_shape,
        in_specs=[ANYWHERE] * (len(names) + grads),
        out_specs=[ANYWHERE] * len(out_shape),
        scratch_shapes=scratch,
        compiler_params=remote_params(collective_id, 60 << 20),
        name="middle_back",
    )(*[loads[name] for name in names], *lefts_t)


class Unit:
    def __init__(self, index, first, columns, order, place):
        self.index = index
        self.first = first
        self.columns = columns
        self.near, self.far = order
        self.place = place


def cut_columns(shapes, most):
    units = []
    for index, (rows, columns) in enumerate(shapes):
        pieces = 1
        while rows * (columns // pieces) > most and (columns // pieces) % (2 * LANES) == 0:
            pieces *= 2
        for place in range(pieces):
            order = (2, 4) if len(units) % 2 == 0 else (4, 2)
            units.append(Unit(index, place * (columns // pieces), columns // pieces, order, place))
    return units


def back_and_sum(
    partials,
    lefts_t,
    rights,
    queries,
    keys_values,
    mixed,
    grad_mixed,
    logs,
    ends,
    w_qkv,
    tokens,
    grad_middle,
    gains,
    wide_sums,
    narrow_sums,
    head_count,
    collective_id,
):
    rows, width = queries.shape
    triple = 3 * width
    keys = 4 * rows
    slabs = width // LANES
    head_size = width // head_count
    per_slab = LANES // head_size
    scale = head_size ** (-0.5)
    factor = scale * LOG2E
    part_rows = w_qkv.shape[1]

    given = len(partials)
    formed = [(left.shape[0] // 8, right.shape[1]) for left, right in zip(lefts_t, rights)]
    shapes = [partial.shape[1:] for partial in partials] + formed + [(part_rows, triple), (SMALL_ROWS, LANES)]
    up_index = given + 1
    qkv_index, small_index = given + 3, given + 4
    array_count = given + 5
    ring = 5
    units = cut_columns(shapes, 70000)
    count = len(units)
    pieces = [sum(1 for unit in units if unit.index == index) for index in range(array_count)]

    def piece_shape(index):
        return (shapes[index][0], shapes[index][1] // pieces[index])

    def kernel(*refs):
        sources = refs[:given]
        left_refs = refs[given : given + 4]
        right_refs = refs[given + 4 : given + 7]
        base = given + 7
        (
            q_ref,
            kv_ref,
            mixed_ref,
            grad_ref,
            log_ref,
            ends_ref,
            w_ref,
            tokens_ref,
            middle_ref,
            gain_ref,
            wide_sums_ref,
            narrow_sums_ref,
        ) = refs[base : base + 12]
        base += 12
        results = refs[base : base + array_count]
        token_out, up_inbox = refs[base + array_count : base + array_count + 2]
        rest = list(refs[base + array_count + 2 :])
        acc, near_in, far_in, outer_in, inner_in = [
            rest[group * array_count : (group + 1) * array_count] for group in range(5)
        ]
        late_out = rest[5 * array_count : 5 * array_count + 4]
        lefts = rest[5 * array_count + 4 : 5 * array_count + 8]
        (
            low_both,
            branch_both,
            up_buf,
            kv_buf,
            give_send,
            give_recv,
            give_own,
            up_sems,
            kv_sems,
            small_out,
            bias,
            dkv,
            core_in,
            z_in,
            dqkv,
            w_buf,
            grad_normed,
            token_buf,
            norm_sums,
            norm_sums_in,
            narrow_in,
            send_sems,
            recv_sems,
            own_sems,
            out_sems,
            key_send,
            key_recv,
            row_send,
            row_recv,
            w_sems,
        ) = rest[5 * array_count + 8 :]

        me = lax.axis_index("fsdp")
        place = lax.axis_index("seq")
        core = me & 1
        chip = me >> 1
        high = place >> 1
        low = place & 1
        inner = jnp.logical_or(place == 1, place == 2)
        outer = jnp.logical_not(inner)
        trades = core != high
        trade_peer = ((me & 6) | high, core * 2 + low)
        mate = seq_peer(place ^ 1)
        across = seq_peer(3 - place)

        barrier = pltpu.get_barrier_semaphore()
        for peer in (fsdp_peer(1), fsdp_peer(2), fsdp_peer(4), mate):
            pl.semaphore_signal(barrier, inc=1, device_id=peer, device_id_type=MESH)

        @pl.when(inner)
        def _():
            pl.semaphore_signal(barrier, inc=1, device_id=across, device_id_type=MESH)

        @pl.when(trades)
        def _():
            pl.semaphore_signal(barrier, inc=1, device_id=trade_peer, device_id_type=MESH)

        pl.semaphore_wait(barrier, 4 + inner.astype(jnp.int32) + trades.astype(jnp.int32))


        def span(unit):
            return pl.ds(unit.first, unit.columns)

        def chip_of(unit, slot):
            return chip ^ (((slot // 2) * unit.near + (slot % 2) * unit.far) // 2)

        def near_copy(u, slot):
            unit = units[u]
            if given <= unit.index <= qkv_index:
                src = late_out[unit.index - given].at[unit.place % ring, slot]
            elif unit.index == small_index:
                src = small_out.at[slot]
            else:
                src = sources[unit.index].at[chip_of(unit, 2 + slot), :, span(unit)]
            return send(
                src,
                near_in[unit.index].at[unit.place, slot],
                send_sems.at[u, slot],
                recv_sems.at[u, slot],
                fsdp_peer(unit.near),
            )

        def own_copy(u, slot):
            unit = units[u]
            return pltpu.make_async_copy(
                sources[unit.index].at[chip_of(unit, slot), :, span(unit)],
                acc[unit.index].at[unit.place, slot],
                own_sems.at[u, slot],
            )

        def far_copy(u):
            unit = units[u]
            return send(
                acc[unit.index].at[unit.place, 1],
                far_in[unit.index].at[unit.place],
                send_sems.at[u, 2],
                recv_sems.at[u, 2],
                fsdp_peer(unit.far),
            )

        def inward_copy(u):
            unit = units[u]
            return send(
                acc[unit.index].at[unit.place, 0],
                outer_in[unit.index].at[unit.place],
                send_sems.at[u, 3],
                recv_sems.at[u, 3],
                mate,
            )

        def across_copy(u):
            unit = units[u]
            return send(
                outer_in[unit.index].at[unit.place],
                inner_in[unit.index].at[unit.place],
                send_sems.at[u, 4],
                recv_sems.at[u, 4],
                across,
            )

        def outward_copy(u):
            unit = units[u]
            return send(
                acc[unit.index].at[unit.place, 0],
                results[unit.index].at[:, span(unit)],
                send_sems.at[u, 5],
                recv_sems.at[u, 5],
                mate,
            )

        def out_copy(u):
            unit = units[u]
            return pltpu.make_async_copy(
                acc[unit.index].at[unit.place, 0], results[unit.index].at[:, span(unit)], out_sems.at[u]
            )

        def add_into(dst, left, right):
            total_rows, columns = dst.shape
            step = 16
            while total_rows % (2 * step) == 0 and 2 * step * columns <= 32768:
                step *= 2

            @pl.loop(0, total_rows // step)
            def _(i):
                part = pl.ds(pl.multiple_of(i * step, step), step)
                dst[part] = (left[part].astype(F32) + right[part].astype(F32)).astype(BF16)

        def early(u):
            return units[u].index < given

        def near_start(u):
            if given <= units[u].index <= qkv_index:
                form(u)
            elif units[u].index == small_index:
                form_small(u)
            near_copy(u, 1).start()
            near_copy(u, 0).start()

        def stage_far(u):
            unit = units[u]
            for slot in (1, 0):
                near_copy(u, slot).wait_recv()
                if early(u):
                    own_copy(u, slot).wait()
                target = acc[unit.index].at[unit.place, slot]
                add_into(target, target, near_in[unit.index].at[unit.place, slot])
                if slot == 1:
                    far_copy(u).start()

        def stage_inward(u):
            unit = units[u]
            far_copy(u).wait_recv()
            target = acc[unit.index].at[unit.place, 0]
            add_into(target, target, far_in[unit.index].at[unit.place])

            @pl.when(outer)
            def _():
                inward_copy(u).start()

        def stage_across(u):
            unit = units[u]

            @pl.when(inner)
            def _():
                inward_copy(u).wait_recv()
                target = outer_in[unit.index].at[unit.place]
                add_into(target, target, acc[unit.index].at[unit.place, 0])
                across_copy(u).start()

        def stage_outward(u):
            unit = units[u]

            @pl.when(inner)
            def _():
                across_copy(u).wait_recv()
                add_into(
                    acc[unit.index].at[unit.place, 0],
                    outer_in[unit.index].at[unit.place],
                    inner_in[unit.index].at[unit.place],
                )
                outward_copy(u).start()
                out_copy(u).start()

        ahead = 4
        lags = ((stage_far, 0), (stage_inward, 2), (stage_across, 4), (stage_outward, 6))
        total_ticks = count + 6

        def tick(t):
            if t + ahead < count:
                near_start(t + ahead)
            for stage, lag in lags:
                if 0 <= t - lag < count:
                    stage(t - lag)


        half = 2 * rows

        def group(g):
            return pl.ds(2 * g, 2)

        def key_core_copy(g):
            return send(
                dkv.at[:, group(g), pl.ds((core ^ 1) * half, half)],
                core_in.at[:, group(g)],
                key_send.at[0, g],
                key_recv.at[0, g],
                fsdp_peer(1),
            )

        def key_far_copy(g):
            return send(
                core_in.at[:, group(g), pl.ds((low ^ 1) * rows, rows)],
                z_in.at[:, group(g)],
                key_send.at[1, g],
                key_recv.at[1, g],
                mate,
            )

        def key_middle(g):
            key_core_copy(g).wait_recv()
            for kind in range(2):
                for k in range(2):

                    @pl.loop(0, half // LANES)
                    def _(i):
                        part = pl.ds(pl.multiple_of(i * LANES, LANES), LANES)
                        own = pl.ds(pl.multiple_of(core * half + i * LANES, LANES), LANES)
                        core_in[kind, 2 * g + k, part] = (
                            core_in[kind, 2 * g + k, part].astype(F32) + dkv[kind, 2 * g + k, own].astype(F32)
                        ).astype(BF16)

            key_far_copy(g).start()

        def key_end(g):
            key_far_copy(g).wait_recv()
            for kind in range(2):
                for k in range(2):
                    slab = 2 * g + k

                    @pl.loop(0, rows // LANES)
                    def _(i):
                        part = pl.ds(pl.multiple_of(i * LANES, LANES), LANES)
                        own = pl.ds(pl.multiple_of(low * rows + i * LANES, LANES), LANES)
                        total = core_in[kind, slab, own].astype(F32) + z_in[kind, slab, part].astype(F32)
                        dqkv[part, pl.ds((1 + kind) * width + slab * LANES, LANES)] = total.astype(BF16)


        def kv_copy(j):
            return pltpu.make_async_copy(kv_ref.at[:, j], kv_buf.at[j % 2], kv_sems.at[j % 2])

        def slab_back(j):
            kv_copy(j).wait()

            @pl.when(j + 1 < slabs)
            def _():
                kv_copy(j + 1).start()

            at = pl.ds(pl.multiple_of(j * LANES, LANES), LANES)
            dq, dk, dv = slab_backward(
                q_ref[:, at],
                grad_ref[:, at],
                mixed_ref[:, at],
                log_ref[j],
                kv_buf[j % 2, 0],
                kv_buf[j % 2, 1],
                bias,
                head_size,
            )
            dqkv[pl.ds(0, rows), at] = (dq.T * scale).astype(BF16)
            dkv[0, j] = (dk * scale).astype(BF16)
            dkv[1, j] = dv.astype(BF16)


        def row_copy(part):
            columns = pl.ds(0, width) if part == 0 else pl.ds(width, 2 * width)
            return send(
                dqkv.at[pl.ds(0, rows), columns],
                dqkv.at[pl.ds(rows, rows), columns],
                row_send.at[part],
                row_recv.at[part],
                fsdp_peer(1),
            )


        def left_copy(which, p):
            size = lefts_t[which].shape[0] // 8
            owner = 2 * p + (core ^ 1)
            return send(
                left_refs[which].at[pl.ds(pl.multiple_of(owner * size, LANES), size)],
                lefts[which].at[1, p],
                give_send.at[which, p],
                give_recv.at[which, p],
                fsdp_peer(1),
            )

        def left_own(which, p):
            size = lefts_t[which].shape[0] // 8
            owner = 2 * p + core
            return pltpu.make_async_copy(
                left_refs[which].at[pl.ds(pl.multiple_of(owner * size, LANES), size)],
                lefts[which].at[0, p],
                give_own.at[which, p],
            )

        def right_copy(which):
            dst = (low_both.at[pl.ds(rows, rows)], up_inbox, branch_both.at[pl.ds(rows, rows)])[which]
            return send(
                right_refs[which], dst, give_send.at[4, which], give_recv.at[4, which], fsdp_peer(1)
            )

        def right_own(which):
            dst = (low_both, None, branch_both)[which].at[pl.ds(0, rows)]
            return pltpu.make_async_copy(right_refs[which], dst, give_own.at[4, which])

        def give(which):
            for p in range(4):
                left_copy(which, p).start()
                left_own(which, p).start()
            if which < 3:
                right_copy(which).start()
                if which != 1:
                    right_own(which).start()

        def take(which):
            for p in range(4):
                left_copy(which, p).wait_recv()
                left_own(which, p).wait()
            if which < 3:
                right_copy(which).wait_recv()
                if which != 1:
                    right_own(which).wait()

        def up_copies(unit):
            slot = unit.place % 2
            return [
                pltpu.make_async_copy(
                    right_refs[1].at[:, span(unit)], up_buf.at[slot, pl.ds(0, rows)], up_sems.at[slot, 0]
                ),
                pltpu.make_async_copy(
                    up_inbox.at[:, span(unit)], up_buf.at[slot, pl.ds(rows, rows)], up_sems.at[slot, 1]
                ),
            ]

        near_done = set()

        def form(u):
            unit = units[u]
            which = unit.index - given
            if unit.place == 0:
                take(which)
                if unit.index == up_index:
                    for one in up_copies(unit):
                        one.start()
            if unit.place >= ring:
                near_copy(u - ring, 0).wait_send()
                near_copy(u - ring, 1).wait_send()
                near_done.add(u - ring)
            if unit.index == up_index:
                if unit.place + 1 < pieces[up_index]:
                    for one in up_copies(units[u + 1]):
                        one.start()
                for one in up_copies(unit):
                    one.wait()
                right = up_buf.at[unit.place % 2]
            else:
                right = (low_both, None, branch_both, dqkv)[which].at[:, span(unit)]
            def block_of(p):
                return (
                    jnp.dot(lefts[which][0, p], right[pl.ds(0, rows)], preferred_element_type=F32)
                    + jnp.dot(lefts[which][1, p], right[pl.ds(rows, rows)], preferred_element_type=F32)
                ).astype(BF16)

            @pl.loop(0, 2)
            def _(slot):
                p = chip ^ (unit.near // 2) ^ (slot * (unit.far // 2))
                late_out[which][unit.place % ring, slot] = block_of(p)

            @pl.loop(0, 2)
            def _(slot):
                acc[unit.index][unit.place, slot] = block_of(chip ^ (slot * (unit.far // 2)))


        blocks = 8

        def w_copy(block):
            return pltpu.make_async_copy(w_ref.at[block], w_buf.at[block % 2], w_sems.at[block % 2])

        def norm_copy():
            return send(norm_sums, norm_sums_in, row_send.at[2], row_recv.at[2], fsdp_peer(1))

        def narrow_copy():
            return send(narrow_sums_ref, narrow_in, row_send.at[4], row_recv.at[4], fsdp_peer(1))

        def input_gradient():
            @pl.loop(0, blocks)
            def _(block):
                w_copy(block).wait()
                at = pl.ds(pl.multiple_of(block * part_rows, part_rows), part_rows)
                grad_normed[:, at] = across_lanes(dqkv[pl.ds(0, rows), :], w_buf[block % 2])

                @pl.when(block + 2 < blocks)
                def _():
                    w_copy(block + 2).start()

            step = 64
            gain_sum = jnp.zeros((1, width), F32)
            shift_sum = jnp.zeros((1, width), F32)
            for i in range(rows // step):
                part = pl.ds(i * step, step)
                inside, gain_term, shift_term = norm_backward(
                    tokens_ref[part].astype(F32), grad_normed[part], gain_ref[0:1, :]
                )
                gain_sum, shift_sum = gain_sum + gain_term, shift_sum + shift_term
                token_buf[part] = (middle_ref[part] + inside).astype(BF16)
            norm_sums[...] = wide_sums_ref[...]
            norm_sums[0:1, :] = gain_sum
            norm_sums[1:2, :] = shift_sum
            norm_copy().start()

            @pl.when(trades)
            def _():
                token_send().start()

            @pl.when(jnp.logical_not(trades))
            def _():
                token_keep().start()

        def token_send():
            return send(token_buf, token_out, row_send.at[3], row_recv.at[3], trade_peer)

        def token_keep():
            return pltpu.make_async_copy(token_buf, token_out, w_sems.at[2])

        def form_small(u):
            unit = units[u]
            norm_copy().wait_recv()
            narrow_copy().wait_recv()
            norm_sums_in[...] = norm_sums[...] + norm_sums_in[...]
            narrow_both = narrow_sums_ref[...] + narrow_in[...]
            narrow = narrow_both.shape[1]
            narrow_part = narrow // 8
            source_lane = lax.broadcasted_iota(jnp.int32, (narrow, LANES), 0)
            lane = lax.broadcasted_iota(jnp.int32, (narrow, LANES), 1)
            for slot in range(4):
                owner = chip_of(unit, slot) * 2 + core
                picked = jnp.logical_and(source_lane == owner * narrow_part + lane, lane < narrow_part)
                block = norm_sums_in[:, pl.ds(pl.multiple_of(owner * LANES, LANES), LANES)] + jnp.dot(
                    narrow_both,
                    picked.astype(F32),
                    precision=lax.Precision.HIGHEST,
                    preferred_element_type=F32,
                )
                block = block.astype(BF16)
                if slot < 2:
                    acc[unit.index][unit.place, slot] = block
                else:
                    small_out[slot - 2] = block


        first_late = min(u for u in range(count) if units[u].index == qkv_index)
        for which in range(4):
            give(which)
        for u in range(count):
            if early(u):
                for slot in range(2):
                    own_copy(u, slot).start()
        kv_copy(0).start()
        narrow_copy().start()
        for u in range(ahead):
            near_start(u)
        w_copy(0).start()
        w_copy(1).start()
        group_bias(bias, ends_ref, rows)
        ticks_inside = first_late - ahead

        @pl.loop(0, slabs)
        def _(j):
            slab_back(j)

            @pl.when(j % 2 == 1)
            def _():
                key_core_copy(j // 2).start()

            @pl.when(jnp.logical_and(j % 2 == 0, j >= 2))
            def _():
                key_middle(j // 2 - 1)

            done = 0
            for k in range(slabs):
                until = (k + 1) * ticks_inside // slabs

                @pl.when(j == k)
                def _(done=done, until=until):
                    for t in range(done, until):
                        tick(t)

                done = until

        row_copy(0).start()
        key_middle(slabs // 2 - 1)
        for g in range(slabs // 2):
            key_end(g)
        row_copy(1).start()
        row_copy(0).wait_recv()
        row_copy(1).wait_recv()
        done_input = False
        for t in range(ticks_inside, total_ticks):
            if not done_input and t + ahead >= count - 1:
                input_gradient()
                done_input = True
            tick(t)

        for u in range(count):
            if u not in near_done:
                near_copy(u, 0).wait_send()
                near_copy(u, 1).wait_send()
            far_copy(u).wait_send()
        for which in range(4):
            for p in range(4):
                left_copy(which, p).wait_send()
            if which < 3:
                right_copy(which).wait_send()

        for u in range(count):

            @pl.when(inner)
            def _():
                across_copy(u).wait_send()
                outward_copy(u).wait_send()
                out_copy(u).wait()

            @pl.when(outer)
            def _():
                inward_copy(u).wait_send()
                outward_copy(u).wait_recv()

        for g in range(slabs // 2):
            key_core_copy(g).wait_send()
            key_far_copy(g).wait_send()
        row_copy(0).wait_send()
        row_copy(1).wait_send()
        norm_copy().wait_send()
        narrow_copy().wait_send()

        @pl.when(trades)
        def _():
            token_send().wait()

        @pl.when(jnp.logical_not(trades))
        def _():
            token_keep().wait()

    scratch = []
    for slots in ((2,), (2,), (), (), ()):
        for index in range(array_count):
            scratch.append(pltpu.VMEM((pieces[index],) + slots + piece_shape(index), BF16))
    for index in range(given, qkv_index + 1):
        scratch.append(pltpu.VMEM((min(ring, pieces[index]), 2) + piece_shape(index), BF16))
    for left in lefts_t:
        scratch.append(pltpu.VMEM((2, 4, left.shape[0] // 8, rows), BF16))
    scratch += [
        pltpu.VMEM((2 * rows, width), BF16),
        pltpu.VMEM((2 * rows, width), BF16),
        pltpu.VMEM((2, 2 * rows, piece_shape(up_index)[1]), BF16),
        pltpu.VMEM((2, 2, keys, LANES), BF16),
        pltpu.SemaphoreType.DMA((5, 4)),
        pltpu.SemaphoreType.DMA((5, 4)),
        pltpu.SemaphoreType.DMA((5, 4)),
        pltpu.SemaphoreType.DMA((2, 2)),
        pltpu.SemaphoreType.DMA((2,)),
        pltpu.VMEM((2, SMALL_ROWS, LANES), BF16),
        pltpu.VMEM((keys, rows), F32),
        pltpu.VMEM((2, slabs, keys, LANES), BF16),
        pltpu.VMEM((2, slabs, 2 * rows, LANES), BF16),
        pltpu.VMEM((2, slabs, rows, LANES), BF16),
        pltpu.VMEM((2 * rows, triple), BF16),
        pltpu.VMEM((2, part_rows, triple), BF16),
        pltpu.VMEM((rows, width), F32),
        pltpu.VMEM((rows, width), BF16),
        pltpu.VMEM((SMALL_ROWS, width), F32),
        pltpu.VMEM((SMALL_ROWS, width), F32),
        pltpu.VMEM(narrow_sums.shape, F32),
        pltpu.SemaphoreType.DMA((count, 6)),
        pltpu.SemaphoreType.DMA((count, 6)),
        pltpu.SemaphoreType.DMA((count, 2)),
        pltpu.SemaphoreType.DMA((count,)),
        pltpu.SemaphoreType.DMA((2, slabs // 2)),
        pltpu.SemaphoreType.DMA((2, slabs // 2)),
        pltpu.SemaphoreType.DMA((5,)),
        pltpu.SemaphoreType.DMA((5,)),
        pltpu.SemaphoreType.DMA((3,)),
    ]
    return pl.pallas_call(
        kernel,
        out_shape=[jax.ShapeDtypeStruct(shape, BF16) for shape in shapes]
        + [jax.ShapeDtypeStruct((rows, width), BF16), jax.ShapeDtypeStruct(rights[1].shape, BF16)],
        in_specs=[ANYWHERE] * (given + 7)
        + [IN_VMEM, ANYWHERE]
        + [IN_VMEM] * 4
        + [ANYWHERE]
        + [IN_VMEM] * 5,
        out_specs=[ANYWHERE] * (array_count + 2),
        scratch_shapes=scratch,
        compiler_params=remote_params(collective_id, 61 << 20),
        name="back_and_sum",
    )(
        *partials,
        *lefts_t,
        *rights,
        queries,
        keys_values,
        mixed,
        grad_mixed,
        logs,
        ends,
        w_qkv,
        tokens,
        grad_middle,
        gains,
        wide_sums,
        narrow_sums,
    )


def widen(arrays):
    count = len(arrays)

    def kernel(*refs):
        sources, results = refs[:count], refs[count : 2 * count]
        narrow, wide = refs[2 * count : 3 * count], refs[3 * count : 4 * count]
        in_sems, out_sems = refs[4 * count :]

        def read(i):
            return pltpu.make_async_copy(sources[i], narrow[i], in_sems.at[i])

        def write(i):
            return pltpu.make_async_copy(wide[i], results[i], out_sems.at[i])

        for i in range(count):
            read(i).start()
        for i in range(count):
            rows, columns = arrays[i].shape
            step = 16
            while rows % (2 * step) == 0 and 2 * step * columns <= 32768:
                step *= 2
            read(i).wait()

            @pl.loop(0, rows // step)
            def _(k):
                part = pl.ds(pl.multiple_of(k * step, step), step)
                wide[i][part] = narrow[i][part].astype(F32)

            write(i).start()
        for i in range(count):
            write(i).wait()

    return pl.pallas_call(
        kernel,
        out_shape=[jax.ShapeDtypeStruct(one.shape, F32) for one in arrays],
        in_specs=[ANYWHERE] * count,
        out_specs=[ANYWHERE] * count,
        scratch_shapes=[pltpu.VMEM(one.shape, BF16) for one in arrays]
        + [pltpu.VMEM(one.shape, F32) for one in arrays]
        + [pltpu.SemaphoreType.DMA((count,)), pltpu.SemaphoreType.DMA((count,))],
        compiler_params=pltpu.CompilerParams(vmem_limit_bytes=61 << 20),
        name="widen",
    )(*arrays)


def fast_local(
    tokens,
    clip_lengths,
    target_pos,
    out_grad,
    norm1_gain,
    norm1_bias,
    w_qkv,
    w_out,
    norm2_gain,
    norm2_bias,
    w_fc1,
    w_fc2,
    w_embed,
    mask_token,
    pred_norm1_gain,
    pred_norm1_bias,
    pred_qkv,
    pred_out,
    pred_norm2_gain,
    pred_norm2_bias,
    pred_fc1,
    pred_fc2,
):
    rows, width = tokens.shape
    narrow = out_grad.shape[1]
    wide_part = norm1_gain.shape[0]
    narrow_part = mask_token.shape[0]
    me = lax.axis_index("fsdp")
    core = me & 1
    wide_small = jnp.pad(
        jnp.stack([norm1_gain, norm1_bias, norm2_gain, norm2_bias]), ((0, SMALL_ROWS - 4), (0, 0))
    )
    narrow_small = jnp.stack(
        [pred_norm1_gain, pred_norm1_bias, pred_norm2_gain, pred_norm2_bias, mask_token]
    )
    here = (jnp.arange(narrow, dtype=jnp.int32) // narrow_part == me)[None, :]
    narrow_small = jnp.where(here, jnp.tile(narrow_small, (1, 8)), jnp.zeros((), BF16))
    narrow_small = jnp.pad(narrow_small, ((0, SMALL_ROWS - 5), (0, 0)))

    clip_ends = jnp.cumsum(clip_lengths[0])
    first_rows = lax.axis_index("seq") * rows + jnp.arange(rows, dtype=jnp.int32)
    past_end = (first_rows[:, None] >= clip_ends[None, :]).astype(jnp.int32)
    rel_rows = first_rows - jnp.sum(clip_lengths[0][None, :] * past_end, axis=1)
    matches = jnp.arange(rows, dtype=jnp.int32)[:, None] == target_pos[0, 0][None, :]
    hit_rows = jnp.sum(matches.astype(F32), axis=1)
    side = jnp.concatenate(
        [position_table(rel_rows, narrow), jnp.broadcast_to(hit_rows[:, None], (rows, LANES))], axis=1
    )
    ends = jnp.pad(jnp.broadcast_to(clip_ends[:, None], (3, LANES)), ((0, 5), (0, 0)))

    whole, kept, narrow_kept, rest, traded = forward_pass(
        tokens,
        out_grad,
        side,
        ends,
        [
            wide_small,
            narrow_small,
            w_qkv,
            w_out,
            w_fc1,
            w_fc2,
            w_embed,
            pred_qkv,
            pred_out,
            pred_fc1,
            pred_fc2,
        ],
        HEADS,
        P_HEADS,
    )
    context_t, entry, side, tokens, gains, narrow_gains = rest
    out_grad, ends, context_out, predicted, hidden_t, narrow_hidden_t = traded
    normed_t, queries, keys_values, mixed, logs, middle, normed_mid_t, slope, mixed_t = kept
    (
        narrow_normed_t,
        narrow_queries,
        narrow_kv,
        narrow_mixed,
        narrow_logs,
        narrow_middle,
        narrow_mid_t,
        narrow_slope,
        narrow_mixed_t,
    ) = narrow_kept

    results = middle_back(
        dict(
            out_grad=out_grad,
            narrow_down=whole[10],
            narrow_slope=narrow_slope,
            narrow_up=whole[9],
            narrow_gains=narrow_gains,
            narrow_middle=narrow_middle,
            narrow_out=whole[8],
            ends=ends,
            narrow_queries=narrow_queries,
            narrow_kv=narrow_kv.reshape(2, narrow // LANES, 4 * rows, LANES),
            narrow_mixed=narrow_mixed,
            narrow_logs=narrow_logs,
            narrow_qkv=whole[7],
            entry=entry,
            side=side,
            w_embed=whole[6],
            wide_down=whole[5],
            wide_slope=slope,
            wide_up=whole[4],
            wide_gains=gains,
            wide_middle=middle,
            wide_out=whole[3],
        ),
        [narrow_hidden_t, narrow_mid_t, narrow_mixed_t, narrow_normed_t, context_t],
        P_HEADS,
        2,
    )
    partials = [one.reshape(4, one.shape[0] // 4, one.shape[1]) for one in results[:5]]
    grad_low, grad_pre, grad_branch, grad_middle, grad_mixed, wide_sums, narrow_sums = results[5:]
    results = back_and_sum(
        partials,
        [hidden_t, normed_mid_t, mixed_t, normed_t],
        [grad_low, grad_pre, grad_branch],
        queries,
        keys_values.reshape(2, width // LANES, 4 * rows, LANES),
        mixed,
        grad_mixed,
        logs,
        ends,
        whole[2].reshape(8, wide_part, 3 * width),
        tokens,
        grad_middle,
        gains,
        wide_sums,
        narrow_sums,
        HEADS,
        3,
    )
    token_grad = results[-2]
    sums = widen(results[:-2])
    small = sums[9]
    narrow_out = [small[4 + i, :narrow_part] for i in range(5)]
    return (
        context_out,
        predicted,
        token_grad,
        small[0],
        small[1],
        sums[8],
        sums[7],
        small[2],
        small[3],
        sums[6],
        sums[5],
        sums[4],
        narrow_out[4],
        narrow_out[0],
        narrow_out[1],
        sums[3],
        sums[2],
        narrow_out[2],
        narrow_out[3],
        sums[1],
        sums[0],
    )


def solution(mesh):
    body = fast_local if fits_fast(mesh) else local
    return jax.shard_map(
        body,
        mesh=mesh,
        in_specs=(
            P(("fsdp", "seq"), None),
            P("fsdp", None),
            P("fsdp", "seq", None),
            P(("fsdp", "seq"), None),
            P("fsdp"),
            P("fsdp"),
            P("fsdp", None),
            P("fsdp", None),
            P("fsdp"),
            P("fsdp"),
            P("fsdp", None),
            P("fsdp", None),
            P("fsdp", None),
            P("fsdp"),
            P("fsdp"),
            P("fsdp"),
            P("fsdp", None),
            P("fsdp", None),
            P("fsdp"),
            P("fsdp"),
            P("fsdp", None),
            P("fsdp", None),
        ),
        out_specs=(
            P(("fsdp", "seq"), None),
            P(("fsdp", "seq"), None),
            P(("fsdp", "seq"), None),
            P("fsdp"),
            P("fsdp"),
            P("fsdp", None),
            P("fsdp", None),
            P("fsdp"),
            P("fsdp"),
            P("fsdp", None),
            P("fsdp", None),
            P("fsdp", None),
            P("fsdp"),
            P("fsdp"),
            P("fsdp"),
            P("fsdp", None),
            P("fsdp", None),
            P("fsdp"),
            P("fsdp"),
            P("fsdp", None),
            P("fsdp", None),
        ),
        check_vma=False,
    )
```

```python
import math

import jax
import jax.numpy as jnp
from jax import lax
from jax.experimental import pallas as pl
from jax.experimental.pallas import tpu as pltpu
from jax.sharding import PartitionSpec as P

HEADS = 16
PD = 384
P_HEADS = 12


EPSILON = 1e-06
NEG_FILL = -1e30
block_rows = 512


def layer_norm(values, norm_gain, norm_shift):
    center = values - jnp.mean(values, axis=-1, keepdims=True)
    spread = jnp.mean(center * center, axis=-1, keepdims=True)
    return center * lax.rsqrt(spread + EPSILON) * norm_gain + norm_shift


def gelu_exact(values):
    return jax.nn.gelu(values, approximate=False)


def position_table(positions, table_width):
    half_width = table_width // 2
    angle_rates = jnp.exp(
        jnp.arange(half_width, dtype=jnp.float32) * (-2.0 * math.log(10000.0) / table_width)
    )
    angles = positions.astype(jnp.float32)[:, None] * angle_rates[None, :]
    return jnp.concatenate([jnp.sin(angles), jnp.cos(angles)], axis=1)


def clip_index(positions, clip_ends):
    return jnp.sum((positions[:, None] >= clip_ends[None, :]).astype(jnp.int32), axis=1)


def key_step(total_keys):
    return max(min(total_keys, block_rows), total_keys // 8)


def block_scores(queries, key_part, query_clip, key_clip_part, score_scale):
    raw_scores = (
        jnp.einsum("the,khe->htk", queries, key_part, preferred_element_type=jnp.float32)
        * score_scale
    )
    same_clip = query_clip[:, None] == key_clip_part[None, :]
    return jnp.where(same_clip[None], raw_scores, NEG_FILL)


def attend_forward(queries, key_heads, value_heads, query_clip, key_clip):
    row_count, head_count, head_size = queries.shape
    score_scale = head_size ** (-0.5)
    total_keys = key_heads.shape[0]
    step_rows = key_step(total_keys)
    run_max = jnp.full((head_count, row_count), NEG_FILL, jnp.float32)
    run_total = jnp.zeros((head_count, row_count), jnp.float32)
    for key_start in range(0, total_keys, step_rows):
        scores = block_scores(
            queries,
            key_heads[key_start : key_start + step_rows],
            query_clip,
            key_clip[key_start : key_start + step_rows],
            score_scale,
        )
        new_max = jnp.maximum(run_max, jnp.max(scores, axis=2))
        run_total = run_total * jnp.exp(run_max - new_max) + jnp.sum(
            jnp.exp(scores - new_max[:, :, None]), axis=2
        )
        run_max = new_max
    log_total = run_max + jnp.log(run_total)
    output = jnp.zeros((row_count, head_count, head_size), jnp.float32)
    for key_start in range(0, total_keys, step_rows):
        scores = block_scores(
            queries,
            key_heads[key_start : key_start + step_rows],
            query_clip,
            key_clip[key_start : key_start + step_rows],
            score_scale,
        )
        soft_weights = jnp.exp(scores - log_total[:, :, None]).astype(jnp.bfloat16)
        output = output + jnp.einsum(
            "htk,khe->the",
            soft_weights,
            value_heads[key_start : key_start + step_rows],
            preferred_element_type=jnp.float32,
        )
    return (output, log_total)


def attend_backward(
    queries, key_heads, value_heads, query_clip, key_clip, log_total, grad_mixed, output
):
    row_count, head_count, head_size = queries.shape
    score_scale = head_size ** (-0.5)
    total_keys = key_heads.shape[0]
    step_rows = key_step(total_keys)
    row_delta = jnp.sum(grad_mixed.astype(jnp.float32) * output, axis=2).T
    grad_query = jnp.zeros((row_count, head_count, head_size), jnp.float32)
    key_pieces = []
    value_pieces = []
    for key_start in range(0, total_keys, step_rows):
        key_part = key_heads[key_start : key_start + step_rows]
        value_part = value_heads[key_start : key_start + step_rows]
        scores = block_scores(
            queries, key_part, query_clip, key_clip[key_start : key_start + step_rows], score_scale
        )
        soft_weights = jnp.exp(scores - log_total[:, :, None])
        grad_soft = jnp.einsum(
            "the,khe->htk", grad_mixed, value_part, preferred_element_type=jnp.float32
        )
        grad_scores = (soft_weights * (grad_soft - row_delta[:, :, None])).astype(jnp.bfloat16)
        grad_query = grad_query + jnp.einsum(
            "htk,khe->the", grad_scores, key_part, preferred_element_type=jnp.float32
        )
        key_pieces.append(
            jnp.einsum("htk,the->khe", grad_scores, queries, preferred_element_type=jnp.float32)
        )
        value_pieces.append(
            jnp.einsum(
                "htk,the->khe",
                soft_weights.astype(jnp.bfloat16),
                grad_mixed,
                preferred_element_type=jnp.float32,
            )
        )
    key_terms = jnp.concatenate(key_pieces, axis=0) * score_scale
    value_terms = jnp.concatenate(value_pieces, axis=0)
    return (grad_query * score_scale, key_terms, value_terms)


def block_forward(
    residual, norm_params, w_qkv, w_out, w_up, w_down, head_count, query_clip, key_clip
):
    row_count, model_width = residual.shape
    head_size = model_width // head_count
    norm_float = norm_params.astype(jnp.float32)
    normed = layer_norm(residual, norm_float[:, 0], norm_float[:, 1]).astype(jnp.bfloat16)
    qkv = jnp.dot(normed, w_qkv, preferred_element_type=jnp.float32).astype(jnp.bfloat16)
    queries = qkv[:, :model_width].reshape(row_count, head_count, head_size)
    key_local = qkv[:, model_width : 2 * model_width]
    value_local = qkv[:, 2 * model_width :]
    key_full, value_full = (
        lax.all_gather(key_local, "seq", axis=0, tiled=True),
        lax.all_gather(value_local, "seq", axis=0, tiled=True),
    )
    key_heads = key_full.reshape(-1, head_count, head_size)
    value_heads = value_full.reshape(-1, head_count, head_size)
    output, log_total = attend_forward(queries, key_heads, value_heads, query_clip, key_clip)
    mixed = output.reshape(row_count, model_width).astype(jnp.bfloat16)
    middle = residual + jnp.dot(mixed, w_out, preferred_element_type=jnp.float32)
    normed_mid = layer_norm(middle, norm_float[:, 2], norm_float[:, 3]).astype(jnp.bfloat16)
    pre_act = jnp.dot(normed_mid, w_up, preferred_element_type=jnp.float32)
    hidden = gelu_exact(pre_act).astype(jnp.bfloat16)
    result = middle + jnp.dot(hidden, w_down, preferred_element_type=jnp.float32)
    kept = (
        residual,
        normed,
        queries,
        key_local,
        value_local,
        key_heads,
        value_heads,
        output,
        log_total,
        mixed,
        middle,
        normed_mid,
        pre_act,
        hidden,
    )
    return (result, kept)


def block_backward(
    grad_result, kept, norm_params, w_qkv, w_out, w_up, w_down, head_count, query_clip, key_clip
):
    (
        residual,
        normed,
        queries,
        key_local,
        value_local,
        key_heads,
        value_heads,
        output,
        log_total,
        mixed,
        middle,
        normed_mid,
        pre_act,
        hidden,
    ) = kept
    row_count, model_width = residual.shape
    head_size = model_width // head_count
    norm_float = norm_params.astype(jnp.float32)
    grad_low = grad_result.astype(jnp.bfloat16)
    grad_down = jnp.einsum("tf,tw->fw", hidden, grad_low, preferred_element_type=jnp.float32)
    grad_hidden = jnp.einsum("tw,fw->tf", grad_low, w_down, preferred_element_type=jnp.float32)
    gelu_value, gelu_pull = jax.vjp(gelu_exact, pre_act)
    grad_pre = gelu_pull(grad_hidden)[0].astype(jnp.bfloat16)
    grad_up = jnp.einsum("tw,tf->wf", normed_mid, grad_pre, preferred_element_type=jnp.float32)
    grad_normed_mid = jnp.einsum("tf,wf->tw", grad_pre, w_up, preferred_element_type=jnp.float32)
    second_value, second_pull = jax.vjp(layer_norm, middle, norm_float[:, 2], norm_float[:, 3])
    grad_mid_norm, grad_gain_two, grad_shift_two = second_pull(grad_normed_mid)
    grad_middle = grad_result + grad_mid_norm
    grad_branch = grad_middle.astype(jnp.bfloat16)
    grad_out_w = jnp.einsum("tv,tw->vw", mixed, grad_branch, preferred_element_type=jnp.float32)
    grad_mixed = jnp.einsum(
        "tw,vw->tv", grad_branch, w_out, preferred_element_type=jnp.float32
    ).astype(jnp.bfloat16)
    key_full, value_full = (
        lax.all_gather(key_local, "seq", axis=0, tiled=True),
        lax.all_gather(value_local, "seq", axis=0, tiled=True),
    )
    key_heads = key_full.reshape(-1, head_count, head_size)
    value_heads = value_full.reshape(-1, head_count, head_size)
    grad_query, key_terms, value_terms = attend_backward(
        queries,
        key_heads,
        value_heads,
        query_clip,
        key_clip,
        log_total,
        grad_mixed.reshape(row_count, head_count, head_size),
        output,
    )
    grad_key, grad_value = (
        lax.psum_scatter(
            key_terms.reshape(-1, model_width).astype(jnp.bfloat16),
            "seq",
            scatter_dimension=0,
            tiled=True,
        ).astype(jnp.float32),
        lax.psum_scatter(
            value_terms.reshape(-1, model_width).astype(jnp.bfloat16),
            "seq",
            scatter_dimension=0,
            tiled=True,
        ).astype(jnp.float32),
    )
    grad_qkv = jnp.concatenate(
        [grad_query.reshape(row_count, model_width), grad_key, grad_value], axis=1
    ).astype(jnp.bfloat16)
    grad_qkv_w = jnp.einsum("tw,tc->wc", normed, grad_qkv, preferred_element_type=jnp.float32)
    grad_normed = jnp.einsum("tc,wc->tw", grad_qkv, w_qkv, preferred_element_type=jnp.float32)
    first_value, first_pull = jax.vjp(layer_norm, residual, norm_float[:, 0], norm_float[:, 1])
    grad_first_norm, grad_gain_one, grad_shift_one = first_pull(grad_normed)
    grad_norms = jnp.stack([grad_gain_one, grad_shift_one, grad_gain_two, grad_shift_two], axis=1)
    return (grad_middle + grad_first_norm, (grad_norms, grad_qkv_w, grad_out_w, grad_up, grad_down))


def local(
    tokens,
    clip_lengths,
    target_pos,
    out_grad,
    norm1_gain,
    norm1_bias,
    w_qkv,
    w_out,
    norm2_gain,
    norm2_bias,
    w_fc1,
    w_fc2,
    w_embed,
    mask_token,
    pred_norm1_gain,
    pred_norm1_bias,
    pred_qkv,
    pred_out,
    pred_norm2_gain,
    pred_norm2_bias,
    pred_fc1,
    pred_fc2,
):
    row_count = tokens.shape[0]
    group_count = row_count * lax.axis_size("seq")
    lengths = clip_lengths[0]
    clip_ends = jnp.cumsum(lengths)
    local_rows = lax.axis_index("seq") * row_count + jnp.arange(row_count, dtype=jnp.int32)
    query_clip = clip_index(local_rows, clip_ends)
    key_clip = clip_index(jnp.arange(group_count, dtype=jnp.int32), clip_ends)
    past_end = (local_rows[:, None] >= clip_ends[None, :]).astype(jnp.int32)
    rel_rows = local_rows - jnp.sum(lengths[None, :] * past_end, axis=1)
    ctx_small = jnp.stack([norm1_gain, norm1_bias, norm2_gain, norm2_bias], axis=1)
    pred_small = jnp.stack(
        [pred_norm1_gain, pred_norm1_bias, pred_norm2_gain, pred_norm2_bias, mask_token], axis=1
    )
    ctx_params = (
        lax.all_gather(ctx_small, "fsdp", axis=0, tiled=True),
        lax.all_gather(w_qkv, "fsdp", axis=0, tiled=True),
        lax.all_gather(w_out, "fsdp", axis=0, tiled=True),
        lax.all_gather(w_fc1, "fsdp", axis=0, tiled=True),
        lax.all_gather(w_fc2, "fsdp", axis=0, tiled=True),
    )
    pred_params = (
        lax.all_gather(pred_small, "fsdp", axis=0, tiled=True),
        lax.all_gather(w_embed, "fsdp", axis=0, tiled=True),
        lax.all_gather(pred_qkv, "fsdp", axis=0, tiled=True),
        lax.all_gather(pred_out, "fsdp", axis=0, tiled=True),
        lax.all_gather(pred_fc1, "fsdp", axis=0, tiled=True),
        lax.all_gather(pred_fc2, "fsdp", axis=0, tiled=True),
    )
    ctx_result, ctx_kept = block_forward(
        tokens.astype(jnp.float32),
        ctx_params[0],
        ctx_params[1],
        ctx_params[2],
        ctx_params[3],
        ctx_params[4],
        HEADS,
        query_clip,
        key_clip,
    )
    context_out = ctx_result.astype(jnp.bfloat16)
    embedded = jnp.dot(context_out, pred_params[1], preferred_element_type=jnp.float32)
    targets = target_pos[0, 0]
    matches = jnp.arange(row_count, dtype=jnp.int32)[:, None] == targets[None, :]
    placement = matches.astype(jnp.float32)
    target_hit = jnp.sum(placement, axis=1)
    target_rel = jnp.sum(jnp.where(matches, rel_rows[:, None], 0), axis=0)
    mask_rows = pred_params[0][:, 4].astype(jnp.float32)[None, :] + position_table(target_rel, PD)
    placed = jnp.dot(
        placement, mask_rows, precision=lax.Precision.HIGHEST, preferred_element_type=jnp.float32
    )
    pred_in = embedded * (1.0 - target_hit[:, None]) + placed
    pred_result, pred_kept = block_forward(
        pred_in,
        pred_params[0],
        pred_params[2],
        pred_params[3],
        pred_params[4],
        pred_params[5],
        P_HEADS,
        query_clip,
        key_clip,
    )
    predicted = pred_result.astype(jnp.bfloat16)
    pred_back = (
        lax.all_gather(pred_small, "fsdp", axis=0, tiled=True),
        lax.all_gather(w_embed, "fsdp", axis=0, tiled=True),
        lax.all_gather(pred_qkv, "fsdp", axis=0, tiled=True),
        lax.all_gather(pred_out, "fsdp", axis=0, tiled=True),
        lax.all_gather(pred_fc1, "fsdp", axis=0, tiled=True),
        lax.all_gather(pred_fc2, "fsdp", axis=0, tiled=True),
    )
    ctx_back = (
        lax.all_gather(ctx_small, "fsdp", axis=0, tiled=True),
        lax.all_gather(w_qkv, "fsdp", axis=0, tiled=True),
        lax.all_gather(w_out, "fsdp", axis=0, tiled=True),
        lax.all_gather(w_fc1, "fsdp", axis=0, tiled=True),
        lax.all_gather(w_fc2, "fsdp", axis=0, tiled=True),
    )
    grad_pred_in, pred_grads = block_backward(
        out_grad.astype(jnp.float32),
        pred_kept,
        pred_back[0],
        pred_back[2],
        pred_back[3],
        pred_back[4],
        pred_back[5],
        P_HEADS,
        query_clip,
        key_clip,
    )
    grad_mask = jnp.sum(target_hit[:, None] * grad_pred_in, axis=0)
    grad_embedded = (grad_pred_in * (1.0 - target_hit[:, None])).astype(jnp.bfloat16)
    grad_embed_w = jnp.einsum(
        "td,tp->dp", context_out, grad_embedded, preferred_element_type=jnp.float32
    )
    grad_context = jnp.einsum(
        "tp,dp->td", grad_embedded, pred_back[1], preferred_element_type=jnp.float32
    )
    grad_tokens, ctx_grads = block_backward(
        grad_context,
        ctx_kept,
        ctx_back[0],
        ctx_back[1],
        ctx_back[2],
        ctx_back[3],
        ctx_back[4],
        HEADS,
        query_clip,
        key_clip,
    )
    pred_small_grad = jnp.concatenate([pred_grads[0], grad_mask[:, None]], axis=1)
    row_sums = (
        lax.psum_scatter(ctx_grads[0], "fsdp", scatter_dimension=0, tiled=True),
        lax.psum_scatter(ctx_grads[1], "fsdp", scatter_dimension=0, tiled=True),
        lax.psum_scatter(ctx_grads[2], "fsdp", scatter_dimension=0, tiled=True),
        lax.psum_scatter(ctx_grads[3], "fsdp", scatter_dimension=0, tiled=True),
        lax.psum_scatter(ctx_grads[4], "fsdp", scatter_dimension=0, tiled=True),
        lax.psum_scatter(grad_embed_w, "fsdp", scatter_dimension=0, tiled=True),
        lax.psum_scatter(pred_small_grad, "fsdp", scatter_dimension=0, tiled=True),
        lax.psum_scatter(pred_grads[1], "fsdp", scatter_dimension=0, tiled=True),
        lax.psum_scatter(pred_grads[2], "fsdp", scatter_dimension=0, tiled=True),
        lax.psum_scatter(pred_grads[3], "fsdp", scatter_dimension=0, tiled=True),
        lax.psum_scatter(pred_grads[4], "fsdp", scatter_dimension=0, tiled=True),
    )
    summed = (
        lax.psum(row_sums[0].astype(jnp.bfloat16), "seq").astype(jnp.float32),
        lax.psum(row_sums[1].astype(jnp.bfloat16), "seq").astype(jnp.float32),
        lax.psum(row_sums[2].astype(jnp.bfloat16), "seq").astype(jnp.float32),
        lax.psum(row_sums[3].astype(jnp.bfloat16), "seq").astype(jnp.float32),
        lax.psum(row_sums[4].astype(jnp.bfloat16), "seq").astype(jnp.float32),
        lax.psum(row_sums[5].astype(jnp.bfloat16), "seq").astype(jnp.float32),
        lax.psum(row_sums[6].astype(jnp.bfloat16), "seq").astype(jnp.float32),
        lax.psum(row_sums[7].astype(jnp.bfloat16), "seq").astype(jnp.float32),
        lax.psum(row_sums[8].astype(jnp.bfloat16), "seq").astype(jnp.float32),
        lax.psum(row_sums[9].astype(jnp.bfloat16), "seq").astype(jnp.float32),
        lax.psum(row_sums[10].astype(jnp.bfloat16), "seq").astype(jnp.float32),
    )
    return (
        context_out,
        predicted,
        grad_tokens.astype(jnp.bfloat16),
        summed[0][:, 0],
        summed[0][:, 1],
        summed[1],
        summed[2],
        summed[0][:, 2],
        summed[0][:, 3],
        summed[3],
        summed[4],
        summed[5],
        summed[6][:, 4],
        summed[6][:, 0],
        summed[6][:, 1],
        summed[7],
        summed[8],
        summed[6][:, 2],
        summed[6][:, 3],
        summed[9],
        summed[10],
    )


BF16 = jnp.bfloat16
F32 = jnp.float32
MESH = pl.DeviceIdType.MESH
LOG2E = 1.4426950408889634
LN2 = 0.6931471805599453
LANES = 128
SMALL_ROWS = 16
ANYWHERE = pl.BlockSpec(memory_space=pl.ANY)
IN_VMEM = pl.BlockSpec(memory_space=pltpu.VMEM)


def fits_fast(mesh):
    return mesh.shape["fsdp"] == 8 and mesh.shape["seq"] == 4


def fsdp_peer(bit):
    return (lax.axis_index("fsdp") ^ bit, lax.axis_index("seq"))


def seq_peer(index):
    return (lax.axis_index("fsdp"), index)


def enter(peers):
    barrier = pltpu.get_barrier_semaphore()
    for peer in peers:
        pl.semaphore_signal(barrier, inc=1, device_id=peer, device_id_type=MESH)
    pl.semaphore_wait(barrier, len(peers))


def send(src, dst, send_sem, recv_sem, peer):
    return pltpu.make_async_remote_copy(
        src_ref=src,
        dst_ref=dst,
        send_sem=send_sem,
        recv_sem=recv_sem,
        device_id=peer,
        device_id_type=MESH,
    )


def remote_params(collective_id, vmem=None):
    return pltpu.CompilerParams(
        collective_id=collective_id, has_side_effects=True, vmem_limit_bytes=vmem
    )


def mate_z():
    return seq_peer(lax.axis_index("seq") ^ 1)


def quarter():
    return (lax.axis_index("fsdp") & 1) * 2 + (lax.axis_index("seq") & 1)


def across_lanes(left, right):
    return lax.dot_general(left, right, (((1,), (1,)), ((), ())), preferred_element_type=F32)


def forward_pass(tokens, out_grad, side, ends, shards, heads, narrow_heads):
    rows, width = tokens.shape
    narrow = out_grad.shape[1]
    hidden_width = shards[4].shape[1]
    narrow_hidden = shards[9].shape[1]
    shapes = [shard.shape for shard in shards]
    array_count = len(shards)
    units = []
    for index, (shard_rows, columns) in enumerate(shapes):
        if shard_rows * columns >= 100000:
            half = shard_rows // 2
            units.append((index, 0, half, 2, 4))
            units.append((index, half, half, 4, 2))
        else:
            near, far = (2, 4) if len(units) % 2 == 0 else (4, 2)
            units.append((index, 0, shard_rows, near, far))
    count = len(units)
    ahead = 3
    last_unit = {}
    for u, unit in enumerate(units):
        last_unit[unit[0]] = u

    block_widths = ((width, heads, hidden_width, 2), (narrow, narrow_heads, narrow_hidden, 1))
    saved_shapes = []
    for w, _, ff, _ in block_widths:
        saved_shapes += [
            ((w, rows), BF16),
            ((rows, w), BF16),
            ((2, w // LANES, 4, rows, LANES), BF16),
            ((rows, w), BF16),
            ((w // LANES, 8, rows), F32),
            ((rows, w), F32),
            ((w, rows), BF16),
            ((rows, ff), BF16),
            ((w, rows), BF16),
        ]
    per_block = len(saved_shapes) // 2
    saved_shapes += [((width, rows), BF16), ((rows, narrow), F32), (side.shape, F32), ((rows, width), BF16)]
    saved_shapes += [((SMALL_ROWS, width), F32), ((SMALL_ROWS, narrow), F32)]
    saved_count = len(saved_shapes)

    def kernel(*refs):
        tokens_ref, out_grad_ref, side_ref, ends_ref = refs[:4]
        sources = refs[4 : 4 + array_count]
        base = 4 + array_count
        weight_outs = refs[base : base + array_count]
        base += array_count
        saved_outs = refs[base : base + saved_count]
        base += saved_count
        out_grad_out, ends_out, context_out, predicted_out, wide_hidden_t, narrow_hidden_t = refs[base : base + 6]
        base += 6
        weights = refs[base : base + array_count]
        base += array_count
        saved = refs[base : base + saved_count]
        base += saved_count
        (
            bias,
            ends_buf,
            predicted,
            wide_normed,
            wide_hidden,
            narrow_normed,
            narrow_hid,
            stage,
            stage_sems,
            send_sems,
            recv_sems,
            local_sems,
            weight_sems,
            saved_sems,
            trade_send,
            trade_recv,
            trade_keep,
            key_send,
            key_recv,
        ) = refs[base:]
        context_t, entry, side_buf, token_buf, gains, narrow_gains = saved[2 * per_block :]
        context = wide_normed

        me = lax.axis_index("fsdp")
        place = lax.axis_index("seq")
        core = me & 1
        high = place >> 1
        low = place & 1
        mine = quarter()
        trades = core != high
        trade_peer = ((me & 6) | high, core * 2 + low)

        barrier = pltpu.get_barrier_semaphore()
        for peer in (fsdp_peer(1), fsdp_peer(2), fsdp_peer(4), mate_z()):
            pl.semaphore_signal(barrier, inc=1, device_id=peer, device_id_type=MESH)

        @pl.when(trades)
        def _():
            pl.semaphore_signal(barrier, inc=1, device_id=trade_peer, device_id_type=MESH)

        pl.semaphore_wait(barrier, 4 + trades.astype(jnp.int32))


        def trade_copy(i, src, dst):
            return send(src, dst, trade_send.at[i], trade_recv.at[i], trade_peer)

        def keep_copy(i, src, dst):
            return pltpu.make_async_copy(src, dst, trade_keep.at[i])

        traded = [
            (tokens_ref, token_buf),
            (side_ref, side_buf),
            (ends_ref, ends_buf),
            (out_grad_ref, out_grad_out),
            (context, context_out),
            (predicted, predicted_out),
        ]

        def trade_start(i):
            @pl.when(trades)
            def _():
                trade_copy(i, *traded[i]).start()

            @pl.when(jnp.logical_not(trades))
            def _():
                keep_copy(i, *traded[i]).start()

        def trade_arrived(i):
            @pl.when(trades)
            def _():
                trade_copy(i, *traded[i]).wait_recv()

            @pl.when(jnp.logical_not(trades))
            def _():
                keep_copy(i, *traded[i]).wait()

        def trade_sent(i):
            @pl.when(trades)
            def _():
                trade_copy(i, *traded[i]).wait_send()


        def place_of(u, owner):
            index, first, unit_rows, _, _ = units[u]
            start = owner * shapes[index][0] + first
            return weights[index].at[pl.ds(pl.multiple_of(start, 16), unit_rows)]

        def own_shard(u):
            index, first, unit_rows, _, _ = units[u]
            return sources[index].at[pl.ds(first, unit_rows)]

        def weight_copy(u, slot):
            _, _, _, near, far = units[u]
            owner = me ^ (0, 0, near, 0, near, far, near ^ far)[slot]
            bit = (near, far, far, 1, 1, 1, 1)[slot]
            src = own_shard(u) if slot in (0, 1, 3) else place_of(u, owner)
            return send(src, place_of(u, owner), send_sems.at[u, slot], recv_sems.at[u, slot], fsdp_peer(bit))

        def own_weight(u):
            return pltpu.make_async_copy(own_shard(u), place_of(u, me), local_sems.at[u])

        def weight_out(index):
            return pltpu.make_async_copy(weights[index], weight_outs[index], weight_sems.at[index])

        def launch(u):
            for slot in (0, 1, 3):
                weight_copy(u, slot).start()
            own_weight(u).start()

        def arrive(u):
            weight_copy(u, 0).wait_recv()
            weight_copy(u, 2).start()
            weight_copy(u, 4).start()
            weight_copy(u, 1).wait_recv()
            weight_copy(u, 5).start()
            if u + ahead < count:
                launch(u + ahead)

        def relay(u):
            weight_copy(u, 2).wait_recv()
            weight_copy(u, 6).start()

        def complete(u):
            for slot in (3, 4, 5, 6):
                weight_copy(u, slot).wait_recv()
            own_weight(u).wait()
            index = units[u][0]
            if last_unit[index] == u:
                weight_out(index).start()

        ticks = []
        ready = {}
        for u in range(count + 2):
            if u < count:
                ticks.append((arrive, u))
            if 1 <= u <= count:
                ticks.append((relay, u - 1))
            if u >= 2:
                ticks.append((complete, u - 2))
                ready[units[u - 2][0]] = len(ticks)
        position = [0]

        def advance(steps):
            for _ in range(steps):
                if position[0] < len(ticks):
                    step, u = ticks[position[0]]
                    step(u)
                    position[0] += 1

        def need(index):
            while position[0] < ready[index]:
                advance(1)


        def save(i):
            return pltpu.make_async_copy(saved[i], saved_outs[i], saved_sems.at[i])

        def norm_into(dst, get, table, gain_at):
            @pl.loop(0, rows // 64)
            def _(i):
                part = pl.ds(pl.multiple_of(i * 64, 64), 64)
                value = get(part)
                value = value - jnp.mean(value, axis=1, keepdims=True)
                inverse = lax.rsqrt(jnp.mean(value * value, axis=1, keepdims=True) + EPSILON)
                dst[part] = (
                    value * inverse * table[gain_at : gain_at + 1, :] + table[gain_at + 1 : gain_at + 2, :]
                ).astype(BF16)

        def turn(src, dst):
            for c in range(dst.shape[0] // LANES):
                at = slice(c * LANES, (c + 1) * LANES)
                dst[at, :] = src[:, at].T

        def run_block(which, get, table, first_weight, finish, inside):
            w, head_count, ff, in_group = block_widths[which]
            (normed_t, queries, kv, mixed, logs, middle, normed_mid_t, slope, mixed_t) = saved[
                which * per_block : (which + 1) * per_block
            ]
            normed, hidden = ((wide_normed, wide_hidden), (narrow_normed, narrow_hid))[which]
            hidden_out = (wide_hidden_t, narrow_hidden_t)[which]
            w_qkv, w_out, w_up, w_down = [weights[first_weight[i]] for i in range(4)]
            slabs = w // LANES
            groups = slabs // in_group
            head_size = w // head_count
            per_slab = LANES // head_size
            factor = head_size ** (-0.5) * LOG2E
            columns = in_group * LANES

            def kv_copy(kind, g):
                owner = mine ^ 1 if kind == 2 else mine
                part = kv.at[:, pl.ds(g * in_group, in_group), owner]
                return send(
                    part,
                    part,
                    key_send.at[which, kind, g],
                    key_recv.at[which, kind, g],
                    mate_z() if kind == 0 else fsdp_peer(1),
                )

            norm_into(normed, get, table, 0)
            turn(normed, normed_t)
            save(which * per_block).start()
            need(first_weight[0])
            for g in range(groups):
                for kind in range(2):
                    tile = jnp.dot(
                        normed[...],
                        w_qkv[:, pl.ds((1 + kind) * w + g * columns, columns)],
                        preferred_element_type=F32,
                    ).astype(BF16)
                    for k in range(in_group):
                        kv[kind, g * in_group + k, mine] = tile[:, k * LANES : (k + 1) * LANES]
                kv_copy(0, g).start()
                kv_copy(1, g).start()

            @pl.loop(0, groups)
            def _(g):
                at = pl.ds(pl.multiple_of(g * columns, columns), columns)
                queries[:, at] = jnp.dot(normed[...], w_qkv[:, at], preferred_element_type=F32).astype(BF16)
            save(which * per_block + 1).start()
            advance(inside[0])
            kv_copy(0, 0).wait_recv()
            kv_copy(2, 0).start()

            lane = lax.broadcasted_iota(jnp.int32, (rows, LANES), 1) // head_size
            sub = lax.broadcasted_iota(jnp.int32, (LANES, rows), 0) // head_size

            @pl.loop(0, slabs)
            def _(j):
                g = j // in_group

                @pl.when(j % in_group == 0)
                def _():
                    kv_copy(1, g).wait_recv()
                    kv_copy(2, g).wait_recv()

                at = pl.ds(pl.multiple_of(j * LANES, LANES), LANES)
                own_queries = queries[:, at]
                key_slab = kv[0, j].reshape(4 * rows, LANES)
                values_t = kv[1, j].reshape(4 * rows, LANES).T
                output = jnp.zeros((LANES, rows), F32)
                logs[j] = jnp.zeros((8, rows), F32)
                for head in range(per_slab):
                    own = jnp.where(lane == head, own_queries, jnp.zeros_like(own_queries))
                    scores = across_lanes(key_slab, own) * factor + bias[...]
                    top = jnp.max(scores, axis=0, keepdims=True)
                    soft = jnp.exp2(scores - top)
                    total = jnp.sum(soft, axis=0, keepdims=True)
                    attended = jnp.dot(values_t, soft.astype(BF16), preferred_element_type=F32) / total
                    output = jnp.where(sub == head, attended, output)
                    logs[j, head : head + 1, :] = top + jnp.log2(total)
                mixed[:, at] = output.T.astype(BF16)
                mixed_t[at, :] = output.astype(BF16)

                @pl.when(jnp.logical_and(j % in_group == 0, g + 1 < groups))
                def _():
                    kv_copy(0, g + 1).wait_recv()
                    kv_copy(2, g + 1).start()

                for k in range(slabs):

                    @pl.when(j == k)
                    def _():
                        advance(inside[1])

            for i in (2, 3, 4, 8):
                save(which * per_block + i).start()
            need(first_weight[1])
            step = 2 * LANES if w % (2 * LANES) == 0 else LANES

            @pl.loop(0, w // step)
            def _(c):
                at = pl.ds(pl.multiple_of(c * step, step), step)
                middle[:, at] = get(pl.ds(0, rows), at) + jnp.dot(
                    mixed[...], w_out[:, at], preferred_element_type=F32
                )
            save(which * per_block + 5).start()
            norm_into(normed, lambda part: middle[part], table, 2)
            turn(normed, normed_mid_t)
            save(which * per_block + 6).start()
            need(first_weight[2])

            def stage_copy(c):
                return pltpu.make_async_copy(
                    stage.at[c % 2],
                    hidden_out.at[pl.ds(pl.multiple_of(c * 2 * LANES, 2 * LANES), 2 * LANES)],
                    stage_sems.at[c % 2],
                )

            @pl.loop(0, ff // (2 * LANES))
            def _(c):
                at = pl.ds(pl.multiple_of(c * 2 * LANES, 2 * LANES), 2 * LANES)
                pre = jnp.dot(normed[...], w_up[:, at], preferred_element_type=F32)
                below = 0.5 * (1.0 + lax.erf(pre * (0.5**0.5)))
                bell = jnp.exp2(pre * pre * (-0.5 * LOG2E)) * (1.0 / math.sqrt(2.0 * math.pi))
                active = (pre * below).astype(BF16)
                hidden[:, at] = active
                slope[:, at] = (below + pre * bell).astype(BF16)

                @pl.when(c >= 2)
                def _():
                    stage_copy(c - 2).wait()

                stage[c % 2] = active.T
                stage_copy(c).start()

            stage_copy(ff // (2 * LANES) - 2).wait()
            stage_copy(ff // (2 * LANES) - 1).wait()
            save(which * per_block + 7).start()
            need(first_weight[3])

            @pl.loop(0, w // step)
            def _(c):
                at = pl.ds(pl.multiple_of(c * step, step), step)
                finish(
                    at, middle[:, at] + jnp.dot(hidden[...], w_down[:, at], preferred_element_type=F32)
                )
            for g in range(groups):
                for kind in range(3):
                    kv_copy(kind, g).wait_send()


        for i in (0, 2, 1):
            trade_start(i)
        for u in range(ahead):
            launch(u)
        trade_start(3)
        need(1)
        for owner in range(8):
            gains[:, owner * LANES : (owner + 1) * LANES] = weights[0][
                owner * SMALL_ROWS : (owner + 1) * SMALL_ROWS, :
            ].astype(F32)
        total = weights[1][0:SMALL_ROWS, :].astype(F32)
        for owner in range(1, 8):
            total = total + weights[1][owner * SMALL_ROWS : (owner + 1) * SMALL_ROWS, :].astype(F32)
        narrow_gains[...] = total
        save(2 * per_block + 4).start()
        save(2 * per_block + 5).start()
        trade_arrived(2)
        group_bias(bias, ends_buf, rows)
        trade_arrived(0)
        save(2 * per_block + 3).start()

        def token_rows(part, at=slice(None)):
            return token_buf[part, at].astype(F32)

        def finish_context(at, value):
            context[:, at] = value.astype(BF16)

        run_block(0, token_rows, gains, (2, 3, 4, 5), finish_context, (1, 1))
        trade_start(4)
        turn(context, context_t)
        save(2 * per_block).start()
        need(6)
        trade_arrived(1)
        save(2 * per_block + 2).start()
        embedded = jnp.dot(context[...], weights[6][...], preferred_element_type=F32)
        hit = side_buf[:, narrow : narrow + 1]
        entry[...] = jnp.where(hit > 0.0, narrow_gains[4:5, :] + side_buf[:, 0:narrow], embedded)
        save(2 * per_block + 1).start()

        def entry_rows(part, at=slice(None)):
            return entry[part, at]

        def finish_predicted(at, value):
            predicted[:, at] = value.astype(BF16)

        run_block(1, entry_rows, narrow_gains, (7, 8, 9, 10), finish_predicted, (0, 0))
        trade_start(5)
        advance(len(ticks))
        for u in range(count):
            for slot in range(7):
                weight_copy(u, slot).wait_send()
        for index in range(array_count):
            weight_out(index).wait()
        for i in range(saved_count):
            save(i).wait()
        keep_copy(6, ends_buf, ends_out).start()
        for i in (3, 4, 5):
            trade_arrived(i)
        for i in range(6):
            trade_sent(i)
        keep_copy(6, ends_buf, ends_out).wait()

    gathered = [(8 * shape[0], shape[1]) for shape in shapes]
    out_shape = (
        [jax.ShapeDtypeStruct(shape, BF16) for shape in gathered]
        + [jax.ShapeDtypeStruct(shape, kind) for shape, kind in saved_shapes]
        + [
            jax.ShapeDtypeStruct(out_grad.shape, BF16),
            jax.ShapeDtypeStruct(ends.shape, jnp.int32),
            jax.ShapeDtypeStruct((rows, width), BF16),
            jax.ShapeDtypeStruct((rows, narrow), BF16),
            jax.ShapeDtypeStruct((hidden_width, rows), BF16),
            jax.ShapeDtypeStruct((narrow_hidden, rows), BF16),
        ]
    )
    scratch = (
        [pltpu.VMEM(shape, BF16) for shape in gathered]
        + [pltpu.VMEM(shape, kind) for shape, kind in saved_shapes]
        + [
            pltpu.VMEM((4 * rows, rows), F32),
            pltpu.VMEM(ends.shape, jnp.int32),
            pltpu.VMEM((rows, narrow), BF16),
            pltpu.VMEM((rows, width), BF16),
            pltpu.VMEM((rows, hidden_width), BF16),
            pltpu.VMEM((rows, narrow), BF16),
            pltpu.VMEM((rows, narrow_hidden), BF16),
            pltpu.VMEM((2, 2 * LANES, rows), BF16),
            pltpu.SemaphoreType.DMA((2,)),
            pltpu.SemaphoreType.DMA((count, 7)),
            pltpu.SemaphoreType.DMA((count, 7)),
            pltpu.SemaphoreType.DMA((count,)),
            pltpu.SemaphoreType.DMA((array_count,)),
            pltpu.SemaphoreType.DMA((saved_count,)),
            pltpu.SemaphoreType.DMA((6,)),
            pltpu.SemaphoreType.DMA((6,)),
            pltpu.SemaphoreType.DMA((7,)),
            pltpu.SemaphoreType.DMA((2, 3, 4)),
            pltpu.SemaphoreType.DMA((2, 3, 4)),
        ]
    )
    results = pl.pallas_call(
        kernel,
        out_shape=out_shape,
        in_specs=[ANYWHERE] * (4 + array_count),
        out_specs=[ANYWHERE] * len(out_shape),
        scratch_shapes=scratch,
        compiler_params=remote_params(1, 62 << 20),
        name="forward_pass",
    )(tokens, out_grad, side, ends, *shards)
    saved = results[array_count : array_count + saved_count]
    return (
        results[:array_count],
        saved[:per_block],
        saved[per_block : 2 * per_block],
        saved[2 * per_block :],
        results[array_count + saved_count :],
    )


def group_bias(bias, ends, rows):
    mine = quarter()
    key_row = lax.broadcasted_iota(jnp.int32, (4 * rows, rows), 0)
    query_row = mine * rows + lax.broadcasted_iota(jnp.int32, (4 * rows, rows), 1)
    key_clip = jnp.zeros((4 * rows, rows), jnp.int32)
    query_clip = jnp.zeros((4 * rows, rows), jnp.int32)
    for c in range(3):
        end = ends[c : c + 1, 0:1]
        key_clip = key_clip + (key_row >= end).astype(jnp.int32)
        query_clip = query_clip + (query_row >= end).astype(jnp.int32)
    bias[...] = jnp.where(key_clip == query_clip, 0.0, NEG_FILL)


def slab_backward(queries, grads, mixed, logs, key_slab, value_slab, bias, head_size):
    rows = queries.shape[0]
    keys = key_slab.shape[0]
    factor = head_size ** (-0.5) * LOG2E
    lane = lax.broadcasted_iota(jnp.int32, (rows, LANES), 1) // head_size
    key_lane = lax.broadcasted_iota(jnp.int32, (keys, LANES), 1) // head_size
    sub = lax.broadcasted_iota(jnp.int32, (LANES, rows), 0) // head_size
    pick = (
        lax.broadcasted_iota(jnp.int32, (8, LANES), 1) // head_size
        == lax.broadcasted_iota(jnp.int32, (8, LANES), 0)
    ).astype(F32)
    deltas = lax.dot_general(
        pick,
        grads.astype(F32) * mixed.astype(F32),
        (((1,), (1,)), ((), ())),
        precision=lax.Precision.HIGHEST,
        preferred_element_type=F32,
    )
    keys_t = key_slab.T
    dq = jnp.zeros((LANES, rows), F32)
    dk = jnp.zeros((keys, LANES), F32)
    dv = jnp.zeros((keys, LANES), F32)
    for head in range(LANES // head_size):
        own = jnp.where(lane == head, queries, jnp.zeros_like(queries))
        own_grad = jnp.where(lane == head, grads, jnp.zeros_like(grads))
        scores = across_lanes(key_slab, own) * factor + bias[...]
        weights = jnp.exp2(scores - logs[head : head + 1, :])
        grad_soft = across_lanes(value_slab, own_grad)
        grad_scores = (weights * (grad_soft - deltas[head : head + 1, :])).astype(BF16)
        dv = jnp.where(key_lane == head, jnp.dot(weights.astype(BF16), grads, preferred_element_type=F32), dv)
        dk = jnp.where(key_lane == head, jnp.dot(grad_scores, queries, preferred_element_type=F32), dk)
        dq = jnp.where(sub == head, jnp.dot(keys_t, grad_scores, preferred_element_type=F32), dq)
    return dq, dk, dv


def norm_backward(value, upper, gain_row):
    value = value - jnp.mean(value, axis=1, keepdims=True)
    inverse = lax.rsqrt(jnp.mean(value * value, axis=1, keepdims=True) + EPSILON)
    value = value * inverse
    scaled = upper * gain_row
    inside = (
        scaled
        - jnp.mean(scaled, axis=1, keepdims=True)
        - value * jnp.mean(scaled * value, axis=1, keepdims=True)
    )
    return (
        inverse * inside,
        jnp.sum(upper * value, axis=0, keepdims=True),
        jnp.sum(upper, axis=0, keepdims=True),
    )


def middle_back(loads, lefts_t, head_count, collective_id):
    names = list(loads)
    rows, narrow = loads["out_grad"].shape
    width = loads["wide_middle"].shape[1]
    narrow_hidden = loads["narrow_slope"].shape[1]
    wide_hidden = loads["wide_slope"].shape[1]
    slabs = narrow // LANES
    head_size = narrow // head_count
    scale = head_size ** (-0.5)
    keys = 4 * rows
    half = 2 * rows
    sizes = [left.shape[0] // 8 for left in lefts_t]
    right_widths = [narrow, narrow_hidden, narrow, 3 * narrow, narrow]
    grads = len(lefts_t)

    def kernel(*refs):
        load_refs = dict(zip(names, refs[: len(names)]))
        left_refs = refs[len(names) : len(names) + grads]
        base = len(names) + grads
        partials_out = refs[base : base + grads]
        low_out, pre_out, branch_out, middle_out, mixed_out, wide_sums_out, narrow_sums_out = refs[
            base + grads : base + grads + 7
        ]
        base += grads + 7
        bufs = dict(zip(names, refs[base : base + len(names)]))
        base += len(names)
        lefts = refs[base : base + grads]
        rights = refs[base + grads : base + 2 * grads]
        partials = refs[base + 2 * grads : base + 3 * grads]
        base += 3 * grads
        (
            bias,
            dkv,
            core_in,
            z_in,
            upper,
            grad_middle,
            grad_mixed,
            wide_low,
            wide_pre,
            wide_upper,
            wide_branch,
            wide_mixed,
            wide_sums,
            narrow_sums,
            load_sems,
            give_send,
            give_recv,
            give_own,
            right_send,
            right_recv,
            key_send,
            key_recv,
            out_sems,
        ) = refs[base:]
        me = lax.axis_index("fsdp")
        core = me & 1
        low = lax.axis_index("seq") & 1
        enter([fsdp_peer(1), mate_z()])

        def load(name):
            return pltpu.make_async_copy(load_refs[name], bufs[name], load_sems.at[names.index(name)])

        loaded = set()

        def got(name):
            if name not in loaded:
                load(name).wait()
                loaded.add(name)
            return bufs[name]

        def left_copy(which, p):
            owner = 2 * p + (core ^ 1)
            return send(
                left_refs[which].at[pl.ds(pl.multiple_of(owner * sizes[which], 16), sizes[which])],
                lefts[which].at[1, p],
                give_send.at[which, p],
                give_recv.at[which, p],
                fsdp_peer(1),
            )

        def left_own(which, p):
            owner = 2 * p + core
            return pltpu.make_async_copy(
                left_refs[which].at[pl.ds(pl.multiple_of(owner * sizes[which], 16), sizes[which])],
                lefts[which].at[0, p],
                give_own.at[which, p],
            )

        def right_copy(which):
            src = rights[which].at[pl.ds(0, rows)]
            return send(
                src, rights[which].at[pl.ds(rows, rows)], right_send.at[which], right_recv.at[which], fsdp_peer(1)
            )

        outs = [(partials[i], partials_out[i]) for i in range(grads)] + [
            (wide_low, low_out),
            (wide_pre, pre_out),
            (wide_branch, branch_out),
            (grad_middle, middle_out),
            (wide_mixed, mixed_out),
            (wide_sums, wide_sums_out),
            (narrow_sums, narrow_sums_out),
        ]

        def out_copy(i):
            return pltpu.make_async_copy(outs[i][0], outs[i][1], out_sems.at[i])

        def form(which):
            for p in range(4):
                left_copy(which, p).wait_recv()
                left_own(which, p).wait()
            right_copy(which).wait_recv()
            size = 4 * sizes[which]
            step = 512 if size > 512 else size
            total = jnp.dot(
                lefts[which][0].reshape(size, rows), rights[which][pl.ds(0, rows), :], preferred_element_type=F32
            ) + jnp.dot(
                lefts[which][1].reshape(size, rows), rights[which][pl.ds(rows, rows), :], preferred_element_type=F32
            )
            partials[which][...] = total.astype(BF16)
            out_copy(which).start()

        late = [name for name in names if name.startswith("w")]
        for name in names:
            if name not in late:
                load(name).start()

        own = pl.ds(0, rows)
        narrow_sums[...] = jnp.zeros_like(narrow_sums)
        wide_sums[...] = jnp.zeros_like(wide_sums)
        grads_in = got("out_grad")
        rights[0][own, :] = grads_in[...]
        right_copy(0).start()
        step = 2 * LANES
        got("narrow_down")
        got("narrow_slope")
        for c in range(narrow_hidden // (2 * step)):
            at = pl.ds(c * 2 * step, 2 * step)
            product = across_lanes(grads_in[...], bufs["narrow_down"][at, :])
            rights[1][own, at] = (product * bufs["narrow_slope"][:, at].astype(F32)).astype(BF16)
        right_copy(1).start()
        upper[...] = across_lanes(rights[1][own, :], got("narrow_up")[...])
        table = got("narrow_gains")
        got("narrow_middle")
        chunk = 64
        gain_sum = jnp.zeros((1, narrow), F32)
        shift_sum = jnp.zeros((1, narrow), F32)
        for i in range(rows // chunk):
            part = pl.ds(i * chunk, chunk)
            inner, gain_term, shift_term = norm_backward(
                bufs["narrow_middle"][part], upper[part], table[2:3, :]
            )
            gain_sum, shift_sum = gain_sum + gain_term, shift_sum + shift_term
            total = grads_in[part].astype(F32) + inner
            bufs["narrow_middle"][part] = total
            rights[2][part, :] = total.astype(BF16)
        narrow_sums[6:7, :] = gain_sum
        narrow_sums[7:8, :] = shift_sum
        right_copy(2).start()
        grad_mixed[...] = across_lanes(rights[2][own, :], got("narrow_out")[...]).astype(BF16)
        for name in late:
            load(name).start()
        for which in range(grads):
            for p in range(4):
                left_copy(which, p).start()
                left_own(which, p).start()
        group_bias(bias, got("ends"), rows)

        got("narrow_queries")
        got("narrow_kv")
        got("narrow_mixed")
        got("narrow_logs")

        def key_core_copy(j):
            return send(
                dkv.at[:, j, pl.ds((core ^ 1) * half, half)],
                core_in.at[:, j],
                key_send.at[0, j],
                key_recv.at[0, j],
                fsdp_peer(1),
            )

        def key_far_copy(j):
            return send(
                core_in.at[:, j, pl.ds((low ^ 1) * rows, rows)],
                z_in.at[:, j],
                key_send.at[1, j],
                key_recv.at[1, j],
                mate_z(),
            )

        def key_middle(j):
            key_core_copy(j).wait_recv()
            for kind in range(2):
                core_in[kind, j] = (
                    core_in[kind, j].astype(F32) + dkv[kind, j, pl.ds(core * half, half)].astype(F32)
                ).astype(BF16)
            key_far_copy(j).start()

        def key_end(j):
            key_far_copy(j).wait_recv()
            for kind in range(2):
                total = core_in[kind, j, pl.ds(low * rows, rows)].astype(F32) + z_in[kind, j].astype(F32)
                at = pl.ds(pl.multiple_of((1 + kind) * narrow + j * LANES, LANES), LANES)
                rights[3][own, at] = total.astype(BF16)

        @pl.loop(0, slabs)
        def _(j):
            at = pl.ds(pl.multiple_of(j * LANES, LANES), LANES)
            dq, dk, dv = slab_backward(
                bufs["narrow_queries"][:, at],
                grad_mixed[:, at],
                bufs["narrow_mixed"][:, at],
                bufs["narrow_logs"][j],
                bufs["narrow_kv"][0, j],
                bufs["narrow_kv"][1, j],
                bias,
                head_size,
            )
            rights[3][own, at] = (dq.T * scale).astype(BF16)
            dkv[0, j] = (dk * scale).astype(BF16)
            dkv[1, j] = dv.astype(BF16)
            key_core_copy(j).start()

            @pl.when(j >= 1)
            def _():
                key_middle(j - 1)

        form(0)
        key_middle(slabs - 1)
        form(1)
        form(2)
        for j in range(slabs):
            key_end(j)
        right_copy(3).start()
        upper[...] = across_lanes(rights[3][own, :], got("narrow_qkv")[...])
        got("entry")
        side = got("side")
        gain_sum = jnp.zeros((1, narrow), F32)
        shift_sum = jnp.zeros((1, narrow), F32)
        mask_sum = jnp.zeros((1, narrow), F32)
        for i in range(rows // chunk):
            part = pl.ds(i * chunk, chunk)
            inner, gain_term, shift_term = norm_backward(bufs["entry"][part], upper[part], table[0:1, :])
            gain_sum, shift_sum = gain_sum + gain_term, shift_sum + shift_term
            total = bufs["narrow_middle"][part] + inner
            hit = side[part, narrow : narrow + 1]
            mask_sum = mask_sum + jnp.sum(hit * total, axis=0, keepdims=True)
            rights[4][part, :] = (total * (1.0 - hit)).astype(BF16)
        narrow_sums[4:5, :] = gain_sum
        narrow_sums[5:6, :] = shift_sum
        narrow_sums[8:9, :] = mask_sum
        out_copy(grads + 6).start()
        right_copy(4).start()

        got("w_embed")

        for c in range(width // step):
            at = pl.ds(c * step, step)
            product = across_lanes(rights[4][own, :], bufs["w_embed"][at, :])
            grad_middle[:, at] = product
            wide_low[:, at] = product.astype(BF16)
        out_copy(grads).start()
        got("wide_down")
        got("wide_slope")

        @pl.loop(0, wide_hidden // (2 * step))
        def _(c):
            at = pl.ds(pl.multiple_of(c * 2 * step, 2 * step), 2 * step)
            product = across_lanes(wide_low[...], bufs["wide_down"][at, :])
            wide_pre[:, at] = (product * bufs["wide_slope"][:, at].astype(F32)).astype(BF16)

        out_copy(grads + 1).start()
        got("wide_up")

        @pl.loop(0, width // step)
        def _(c):
            at = pl.ds(pl.multiple_of(c * step, step), step)
            wide_upper[:, at] = across_lanes(wide_pre[...], bufs["wide_up"][at, :])

        wide_table = got("wide_gains")
        got("wide_middle")
        gain_sum = jnp.zeros((1, width), F32)
        shift_sum = jnp.zeros((1, width), F32)
        for i in range(rows // chunk):
            part = pl.ds(i * chunk, chunk)
            inner, gain_term, shift_term = norm_backward(
                bufs["wide_middle"][part], wide_upper[part], wide_table[2:3, :]
            )
            gain_sum, shift_sum = gain_sum + gain_term, shift_sum + shift_term
            total = grad_middle[part] + inner
            grad_middle[part] = total
            wide_branch[part] = total.astype(BF16)
        wide_sums[2:3, :] = gain_sum
        wide_sums[3:4, :] = shift_sum
        for i in (2, 3, 5):
            out_copy(grads + i).start()
        got("wide_out")

        for c in range(width // step):
            at = pl.ds(c * step, step)
            wide_mixed[:, at] = across_lanes(wide_branch[...], bufs["wide_out"][at, :]).astype(BF16)
        out_copy(grads + 4).start()
        form(3)
        form(4)
        for which in range(grads):
            right_copy(which).wait_send()
            for p in range(4):
                left_copy(which, p).wait_send()
        for j in range(slabs):
            key_core_copy(j).wait_send()
            key_far_copy(j).wait_send()
        for i in range(grads + 7):
            out_copy(i).wait()

    out_shape = [
        jax.ShapeDtypeStruct((4 * size, columns), BF16) for size, columns in zip(sizes, right_widths)
    ] + [
        jax.ShapeDtypeStruct((rows, width), BF16),
        jax.ShapeDtypeStruct((rows, wide_hidden), BF16),
        jax.ShapeDtypeStruct((rows, width), BF16),
        jax.ShapeDtypeStruct((rows, width), F32),
        jax.ShapeDtypeStruct((rows, width), BF16),
        jax.ShapeDtypeStruct((SMALL_ROWS, width), F32),
        jax.ShapeDtypeStruct((SMALL_ROWS, narrow), F32),
    ]
    scratch = (
        [pltpu.VMEM(loads[name].shape, loads[name].dtype) for name in names]
        + [pltpu.VMEM((2, 4, size, rows), BF16) for size in sizes]
        + [pltpu.VMEM((2 * rows, columns), BF16) for columns in right_widths]
        + [pltpu.VMEM((4 * size, columns), BF16) for size, columns in zip(sizes, right_widths)]
        + [
            pltpu.VMEM((keys, rows), F32),
            pltpu.VMEM((2, slabs, keys, LANES), BF16),
            pltpu.VMEM((2, slabs, half, LANES), BF16),
            pltpu.VMEM((2, slabs, rows, LANES), BF16),
            pltpu.VMEM((rows, narrow), F32),
            pltpu.VMEM((rows, width), F32),
            pltpu.VMEM((rows, narrow), BF16),
            pltpu.VMEM((rows, width), BF16),
            pltpu.VMEM((rows, wide_hidden), BF16),
            pltpu.VMEM((rows, width), F32),
            pltpu.VMEM((rows, width), BF16),
            pltpu.VMEM((rows, width), BF16),
            pltpu.VMEM((SMALL_ROWS, width), F32),
            pltpu.VMEM((SMALL_ROWS, narrow), F32),
            pltpu.SemaphoreType.DMA((len(names),)),
            pltpu.SemaphoreType.DMA((grads, 4)),
            pltpu.SemaphoreType.DMA((grads, 4)),
            pltpu.SemaphoreType.DMA((grads, 4)),
            pltpu.SemaphoreType.DMA((grads,)),
            pltpu.SemaphoreType.DMA((grads,)),
            pltpu.SemaphoreType.DMA((2, slabs)),
            pltpu.SemaphoreType.DMA((2, slabs)),
            pltpu.SemaphoreType.DMA((grads + 7,)),
        ]
    )
    return pl.pallas_call(
        kernel,
        out_shape=out_shape,
        in_specs=[ANYWHERE] * (len(names) + grads),
        out_specs=[ANYWHERE] * len(out_shape),
        scratch_shapes=scratch,
        compiler_params=remote_params(collective_id, 60 << 20),
        name="middle_back",
    )(*[loads[name] for name in names], *lefts_t)


class Unit:
    def __init__(self, index, first, columns, order, place):
        self.index = index
        self.first = first
        self.columns = columns
        self.near, self.far = order
        self.place = place


def cut_columns(shapes, most):
    units = []
    for index, (rows, columns) in enumerate(shapes):
        pieces = 1
        while rows * (columns // pieces) > most and (columns // pieces) % (2 * LANES) == 0:
            pieces *= 2
        for place in range(pieces):
            order = (2, 4) if len(units) % 2 == 0 else (4, 2)
            units.append(Unit(index, place * (columns // pieces), columns // pieces, order, place))
    return units


def back_and_sum(
    partials,
    lefts_t,
    rights,
    queries,
    keys_values,
    mixed,
    grad_mixed,
    logs,
    ends,
    w_qkv,
    tokens,
    grad_middle,
    gains,
    wide_sums,
    narrow_sums,
    head_count,
    collective_id,
):
    rows, width = queries.shape
    triple = 3 * width
    keys = 4 * rows
    slabs = width // LANES
    head_size = width // head_count
    per_slab = LANES // head_size
    scale = head_size ** (-0.5)
    factor = scale * LOG2E
    part_rows = w_qkv.shape[1]

    given = len(partials)
    formed = [(left.shape[0] // 8, right.shape[1]) for left, right in zip(lefts_t, rights)]
    shapes = [partial.shape[1:] for partial in partials] + formed + [(part_rows, triple), (SMALL_ROWS, LANES)]
    up_index = given + 1
    qkv_index, small_index = given + 3, given + 4
    array_count = given + 5
    ring = 5
    units = cut_columns(shapes, 70000)
    count = len(units)
    pieces = [sum(1 for unit in units if unit.index == index) for index in range(array_count)]

    def piece_shape(index):
        return (shapes[index][0], shapes[index][1] // pieces[index])

    def kernel(*refs):
        sources = refs[:given]
        left_refs = refs[given : given + 4]
        right_refs = refs[given + 4 : given + 7]
        base = given + 7
        (
            q_ref,
            kv_ref,
            mixed_ref,
            grad_ref,
            log_ref,
            ends_ref,
            w_ref,
            tokens_ref,
            middle_ref,
            gain_ref,
            wide_sums_ref,
            narrow_sums_ref,
        ) = refs[base : base + 12]
        base += 12
        results = refs[base : base + array_count]
        token_out, up_inbox = refs[base + array_count : base + array_count + 2]
        rest = list(refs[base + array_count + 2 :])
        acc, near_in, far_in, outer_in, inner_in = [
            rest[group * array_count : (group + 1) * array_count] for group in range(5)
        ]
        late_out = rest[5 * array_count : 5 * array_count + 4]
        lefts = rest[5 * array_count + 4 : 5 * array_count + 8]
        (
            low_both,
            branch_both,
            up_buf,
            kv_buf,
            give_send,
            give_recv,
            give_own,
            up_sems,
            kv_sems,
            small_out,
            bias,
            dkv,
            core_in,
            z_in,
            dqkv,
            w_buf,
            grad_normed,
            token_buf,
            norm_sums,
            norm_sums_in,
            narrow_in,
            send_sems,
            recv_sems,
            own_sems,
            out_sems,
            key_send,
            key_recv,
            row_send,
            row_recv,
            w_sems,
        ) = rest[5 * array_count + 8 :]

        me = lax.axis_index("fsdp")
        place = lax.axis_index("seq")
        core = me & 1
        chip = me >> 1
        high = place >> 1
        low = place & 1
        inner = jnp.logical_or(place == 1, place == 2)
        outer = jnp.logical_not(inner)
        trades = core != high
        trade_peer = ((me & 6) | high, core * 2 + low)
        mate = seq_peer(place ^ 1)
        across = seq_peer(3 - place)

        barrier = pltpu.get_barrier_semaphore()
        for peer in (fsdp_peer(1), fsdp_peer(2), fsdp_peer(4), mate):
            pl.semaphore_signal(barrier, inc=1, device_id=peer, device_id_type=MESH)

        @pl.when(inner)
        def _():
            pl.semaphore_signal(barrier, inc=1, device_id=across, device_id_type=MESH)

        @pl.when(trades)
        def _():
            pl.semaphore_signal(barrier, inc=1, device_id=trade_peer, device_id_type=MESH)

        pl.semaphore_wait(barrier, 4 + inner.astype(jnp.int32) + trades.astype(jnp.int32))


        def span(unit):
            return pl.ds(unit.first, unit.columns)

        def chip_of(unit, slot):
            return chip ^ (((slot // 2) * unit.near + (slot % 2) * unit.far) // 2)

        def near_copy(u, slot):
            unit = units[u]
            if given <= unit.index <= qkv_index:
                src = late_out[unit.index - given].at[unit.place % ring, slot]
            elif unit.index == small_index:
                src = small_out.at[slot]
            else:
                src = sources[unit.index].at[chip_of(unit, 2 + slot), :, span(unit)]
            return send(
                src,
                near_in[unit.index].at[unit.place, slot],
                send_sems.at[u, slot],
                recv_sems.at[u, slot],
                fsdp_peer(unit.near),
            )

        def own_copy(u, slot):
            unit = units[u]
            return pltpu.make_async_copy(
                sources[unit.index].at[chip_of(unit, slot), :, span(unit)],
                acc[unit.index].at[unit.place, slot],
                own_sems.at[u, slot],
            )

        def far_copy(u):
            unit = units[u]
            return send(
                acc[unit.index].at[unit.place, 1],
                far_in[unit.index].at[unit.place],
                send_sems.at[u, 2],
                recv_sems.at[u, 2],
                fsdp_peer(unit.far),
            )

        def inward_copy(u):
            unit = units[u]
            return send(
                acc[unit.index].at[unit.place, 0],
                outer_in[unit.index].at[unit.place],
                send_sems.at[u, 3],
                recv_sems.at[u, 3],
                mate,
            )

        def across_copy(u):
            unit = units[u]
            return send(
                outer_in[unit.index].at[unit.place],
                inner_in[unit.index].at[unit.place],
                send_sems.at[u, 4],
                recv_sems.at[u, 4],
                across,
            )

        def outward_copy(u):
            unit = units[u]
            return send(
                acc[unit.index].at[unit.place, 0],
                results[unit.index].at[:, span(unit)],
                send_sems.at[u, 5],
                recv_sems.at[u, 5],
                mate,
            )

        def out_copy(u):
            unit = units[u]
            return pltpu.make_async_copy(
                acc[unit.index].at[unit.place, 0], results[unit.index].at[:, span(unit)], out_sems.at[u]
            )

        def add_into(dst, left, right):
            total_rows, columns = dst.shape
            step = 16
            while total_rows % (2 * step) == 0 and 2 * step * columns <= 32768:
                step *= 2

            @pl.loop(0, total_rows // step)
            def _(i):
                part = pl.ds(pl.multiple_of(i * step, step), step)
                dst[part] = (left[part].astype(F32) + right[part].astype(F32)).astype(BF16)

        def early(u):
            return units[u].index < given

        def near_start(u):
            if given <= units[u].index <= qkv_index:
                form(u)
            elif units[u].index == small_index:
                form_small(u)
            near_copy(u, 1).start()
            near_copy(u, 0).start()

        def stage_far(u):
            unit = units[u]
            for slot in (1, 0):
                near_copy(u, slot).wait_recv()
                if early(u):
                    own_copy(u, slot).wait()
                target = acc[unit.index].at[unit.place, slot]
                add_into(target, target, near_in[unit.index].at[unit.place, slot])
                if slot == 1:
                    far_copy(u).start()

        def stage_inward(u):
            unit = units[u]
            far_copy(u).wait_recv()
            target = acc[unit.index].at[unit.place, 0]
            add_into(target, target, far_in[unit.index].at[unit.place])

            @pl.when(outer)
            def _():
                inward_copy(u).start()

        def stage_across(u):
            unit = units[u]

            @pl.when(inner)
            def _():
                inward_copy(u).wait_recv()
                target = outer_in[unit.index].at[unit.place]
                add_into(target, target, acc[unit.index].at[unit.place, 0])
                across_copy(u).start()

        def stage_outward(u):
            unit = units[u]

            @pl.when(inner)
            def _():
                across_copy(u).wait_recv()
                add_into(
                    acc[unit.index].at[unit.place, 0],
                    outer_in[unit.index].at[unit.place],
                    inner_in[unit.index].at[unit.place],
                )
                outward_copy(u).start()
                out_copy(u).start()

        ahead = 4
        lags = ((stage_far, 0), (stage_inward, 2), (stage_across, 4), (stage_outward, 6))
        total_ticks = count + 6

        def tick(t):
            if t + ahead < count:
                near_start(t + ahead)
            for stage, lag in lags:
                if 0 <= t - lag < count:
                    stage(t - lag)


        half = 2 * rows

        def group(g):
            return pl.ds(2 * g, 2)

        def key_core_copy(g):
            return send(
                dkv.at[:, group(g), pl.ds((core ^ 1) * half, half)],
                core_in.at[:, group(g)],
                key_send.at[0, g],
                key_recv.at[0, g],
                fsdp_peer(1),
            )

        def key_far_copy(g):
            return send(
                core_in.at[:, group(g), pl.ds((low ^ 1) * rows, rows)],
                z_in.at[:, group(g)],
                key_send.at[1, g],
                key_recv.at[1, g],
                mate,
            )

        def key_middle(g):
            key_core_copy(g).wait_recv()
            for kind in range(2):
                for k in range(2):

                    @pl.loop(0, half // LANES)
                    def _(i):
                        part = pl.ds(pl.multiple_of(i * LANES, LANES), LANES)
                        own = pl.ds(pl.multiple_of(core * half + i * LANES, LANES), LANES)
                        core_in[kind, 2 * g + k, part] = (
                            core_in[kind, 2 * g + k, part].astype(F32) + dkv[kind, 2 * g + k, own].astype(F32)
                        ).astype(BF16)

            key_far_copy(g).start()

        def key_end(g):
            key_far_copy(g).wait_recv()
            for kind in range(2):
                for k in range(2):
                    slab = 2 * g + k

                    @pl.loop(0, rows // LANES)
                    def _(i):
                        part = pl.ds(pl.multiple_of(i * LANES, LANES), LANES)
                        own = pl.ds(pl.multiple_of(low * rows + i * LANES, LANES), LANES)
                        total = core_in[kind, slab, own].astype(F32) + z_in[kind, slab, part].astype(F32)
                        dqkv[part, pl.ds((1 + kind) * width + slab * LANES, LANES)] = total.astype(BF16)


        def kv_copy(j):
            return pltpu.make_async_copy(kv_ref.at[:, j], kv_buf.at[j % 2], kv_sems.at[j % 2])

        def slab_back(j):
            kv_copy(j).wait()

            @pl.when(j + 1 < slabs)
            def _():
                kv_copy(j + 1).start()

            at = pl.ds(pl.multiple_of(j * LANES, LANES), LANES)
            dq, dk, dv = slab_backward(
                q_ref[:, at],
                grad_ref[:, at],
                mixed_ref[:, at],
                log_ref[j],
                kv_buf[j % 2, 0],
                kv_buf[j % 2, 1],
                bias,
                head_size,
            )
            dqkv[pl.ds(0, rows), at] = (dq.T * scale).astype(BF16)
            dkv[0, j] = (dk * scale).astype(BF16)
            dkv[1, j] = dv.astype(BF16)


        def row_copy(part):
            columns = pl.ds(0, width) if part == 0 else pl.ds(width, 2 * width)
            return send(
                dqkv.at[pl.ds(0, rows), columns],
                dqkv.at[pl.ds(rows, rows), columns],
                row_send.at[part],
                row_recv.at[part],
                fsdp_peer(1),
            )


        def left_copy(which, p):
            size = lefts_t[which].shape[0] // 8
            owner = 2 * p + (core ^ 1)
            return send(
                left_refs[which].at[pl.ds(pl.multiple_of(owner * size, LANES), size)],
                lefts[which].at[1, p],
                give_send.at[which, p],
                give_recv.at[which, p],
                fsdp_peer(1),
            )

        def left_own(which, p):
            size = lefts_t[which].shape[0] // 8
            owner = 2 * p + core
            return pltpu.make_async_copy(
                left_refs[which].at[pl.ds(pl.multiple_of(owner * size, LANES), size)],
                lefts[which].at[0, p],
                give_own.at[which, p],
            )

        def right_copy(which):
            dst = (low_both.at[pl.ds(rows, rows)], up_inbox, branch_both.at[pl.ds(rows, rows)])[which]
            return send(
                right_refs[which], dst, give_send.at[4, which], give_recv.at[4, which], fsdp_peer(1)
            )

        def right_own(which):
            dst = (low_both, None, branch_both)[which].at[pl.ds(0, rows)]
            return pltpu.make_async_copy(right_refs[which], dst, give_own.at[4, which])

        def give(which):
            for p in range(4):
                left_copy(which, p).start()
                left_own(which, p).start()
            if which < 3:
                right_copy(which).start()
                if which != 1:
                    right_own(which).start()

        def take(which):
            for p in range(4):
                left_copy(which, p).wait_recv()
                left_own(which, p).wait()
            if which < 3:
                right_copy(which).wait_recv()
                if which != 1:
                    right_own(which).wait()

        def up_copies(unit):
            slot = unit.place % 2
            return [
                pltpu.make_async_copy(
                    right_refs[1].at[:, span(unit)], up_buf.at[slot, pl.ds(0, rows)], up_sems.at[slot, 0]
                ),
                pltpu.make_async_copy(
                    up_inbox.at[:, span(unit)], up_buf.at[slot, pl.ds(rows, rows)], up_sems.at[slot, 1]
                ),
            ]

        near_done = set()

        def form(u):
            unit = units[u]
            which = unit.index - given
            if unit.place == 0:
                take(which)
                if unit.index == up_index:
                    for one in up_copies(unit):
                        one.start()
            if unit.place >= ring:
                near_copy(u - ring, 0).wait_send()
                near_copy(u - ring, 1).wait_send()
                near_done.add(u - ring)
            if unit.index == up_index:
                if unit.place + 1 < pieces[up_index]:
                    for one in up_copies(units[u + 1]):
                        one.start()
                for one in up_copies(unit):
                    one.wait()
                right = up_buf.at[unit.place % 2]
            else:
                right = (low_both, None, branch_both, dqkv)[which].at[:, span(unit)]
            def block_of(p):
                return (
                    jnp.dot(lefts[which][0, p], right[pl.ds(0, rows)], preferred_element_type=F32)
                    + jnp.dot(lefts[which][1, p], right[pl.ds(rows, rows)], preferred_element_type=F32)
                ).astype(BF16)

            @pl.loop(0, 2)
            def _(slot):
                p = chip ^ (unit.near // 2) ^ (slot * (unit.far // 2))
                late_out[which][unit.place % ring, slot] = block_of(p)

            @pl.loop(0, 2)
            def _(slot):
                acc[unit.index][unit.place, slot] = block_of(chip ^ (slot * (unit.far // 2)))


        blocks = 8

        def w_copy(block):
            return pltpu.make_async_copy(w_ref.at[block], w_buf.at[block % 2], w_sems.at[block % 2])

        def norm_copy():
            return send(norm_sums, norm_sums_in, row_send.at[2], row_recv.at[2], fsdp_peer(1))

        def narrow_copy():
            return send(narrow_sums_ref, narrow_in, row_send.at[4], row_recv.at[4], fsdp_peer(1))

        def input_gradient():
            @pl.loop(0, blocks)
            def _(block):
                w_copy(block).wait()
                at = pl.ds(pl.multiple_of(block * part_rows, part_rows), part_rows)
                grad_normed[:, at] = across_lanes(dqkv[pl.ds(0, rows), :], w_buf[block % 2])

                @pl.when(block + 2 < blocks)
                def _():
                    w_copy(block + 2).start()

            step = 64
            gain_sum = jnp.zeros((1, width), F32)
            shift_sum = jnp.zeros((1, width), F32)
            for i in range(rows // step):
                part = pl.ds(i * step, step)
                inside, gain_term, shift_term = norm_backward(
                    tokens_ref[part].astype(F32), grad_normed[part], gain_ref[0:1, :]
                )
                gain_sum, shift_sum = gain_sum + gain_term, shift_sum + shift_term
                token_buf[part] = (middle_ref[part] + inside).astype(BF16)
            norm_sums[...] = wide_sums_ref[...]
            norm_sums[0:1, :] = gain_sum
            norm_sums[1:2, :] = shift_sum
            norm_copy().start()

            @pl.when(trades)
            def _():
                token_send().start()

            @pl.when(jnp.logical_not(trades))
            def _():
                token_keep().start()

        def token_send():
            return send(token_buf, token_out, row_send.at[3], row_recv.at[3], trade_peer)

        def token_keep():
            return pltpu.make_async_copy(token_buf, token_out, w_sems.at[2])

        def form_small(u):
            unit = units[u]
            norm_copy().wait_recv()
            narrow_copy().wait_recv()
            norm_sums_in[...] = norm_sums[...] + norm_sums_in[...]
            narrow_both = narrow_sums_ref[...] + narrow_in[...]
            narrow = narrow_both.shape[1]
            narrow_part = narrow // 8
            source_lane = lax.broadcasted_iota(jnp.int32, (narrow, LANES), 0)
            lane = lax.broadcasted_iota(jnp.int32, (narrow, LANES), 1)
            for slot in range(4):
                owner = chip_of(unit, slot) * 2 + core
                picked = jnp.logical_and(source_lane == owner * narrow_part + lane, lane < narrow_part)
                block = norm_sums_in[:, pl.ds(pl.multiple_of(owner * LANES, LANES), LANES)] + jnp.dot(
                    narrow_both,
                    picked.astype(F32),
                    precision=lax.Precision.HIGHEST,
                    preferred_element_type=F32,
                )
                block = block.astype(BF16)
                if slot < 2:
                    acc[unit.index][unit.place, slot] = block
                else:
                    small_out[slot - 2] = block


        first_late = min(u for u in range(count) if units[u].index == qkv_index)
        for which in range(4):
            give(which)
        for u in range(count):
            if early(u):
                for slot in range(2):
                    own_copy(u, slot).start()
        kv_copy(0).start()
        narrow_copy().start()
        for u in range(ahead):
            near_start(u)
        w_copy(0).start()
        w_copy(1).start()
        group_bias(bias, ends_ref, rows)
        ticks_inside = first_late - ahead

        @pl.loop(0, slabs)
        def _(j):
            slab_back(j)

            @pl.when(j % 2 == 1)
            def _():
                key_core_copy(j // 2).start()

            @pl.when(jnp.logical_and(j % 2 == 0, j >= 2))
            def _():
                key_middle(j // 2 - 1)

            done = 0
            for k in range(slabs):
                until = (k + 1) * ticks_inside // slabs

                @pl.when(j == k)
                def _(done=done, until=until):
                    for t in range(done, until):
                        tick(t)

                done = until

        row_copy(0).start()
        key_middle(slabs // 2 - 1)
        for g in range(slabs // 2):
            key_end(g)
        row_copy(1).start()
        row_copy(0).wait_recv()
        row_copy(1).wait_recv()
        done_input = False
        for t in range(ticks_inside, total_ticks):
            if not done_input and t + ahead >= count - 1:
                input_gradient()
                done_input = True
            tick(t)

        for u in range(count):
            if u not in near_done:
                near_copy(u, 0).wait_send()
                near_copy(u, 1).wait_send()
            far_copy(u).wait_send()
        for which in range(4):
            for p in range(4):
                left_copy(which, p).wait_send()
            if which < 3:
                right_copy(which).wait_send()

        for u in range(count):

            @pl.when(inner)
            def _():
                across_copy(u).wait_send()
                outward_copy(u).wait_send()
                out_copy(u).wait()

            @pl.when(outer)
            def _():
                inward_copy(u).wait_send()
                outward_copy(u).wait_recv()

        for g in range(slabs // 2):
            key_core_copy(g).wait_send()
            key_far_copy(g).wait_send()
        row_copy(0).wait_send()
        row_copy(1).wait_send()
        norm_copy().wait_send()
        narrow_copy().wait_send()

        @pl.when(trades)
        def _():
            token_send().wait()

        @pl.when(jnp.logical_not(trades))
        def _():
            token_keep().wait()

    scratch = []
    for slots in ((2,), (2,), (), (), ()):
        for index in range(array_count):
            scratch.append(pltpu.VMEM((pieces[index],) + slots + piece_shape(index), BF16))
    for index in range(given, qkv_index + 1):
        scratch.append(pltpu.VMEM((min(ring, pieces[index]), 2) + piece_shape(index), BF16))
    for left in lefts_t:
        scratch.append(pltpu.VMEM((2, 4, left.shape[0] // 8, rows), BF16))
    scratch += [
        pltpu.VMEM((2 * rows, width), BF16),
        pltpu.VMEM((2 * rows, width), BF16),
        pltpu.VMEM((2, 2 * rows, piece_shape(up_index)[1]), BF16),
        pltpu.VMEM((2, 2, keys, LANES), BF16),
        pltpu.SemaphoreType.DMA((5, 4)),
        pltpu.SemaphoreType.DMA((5, 4)),
        pltpu.SemaphoreType.DMA((5, 4)),
        pltpu.SemaphoreType.DMA((2, 2)),
        pltpu.SemaphoreType.DMA((2,)),
        pltpu.VMEM((2, SMALL_ROWS, LANES), BF16),
        pltpu.VMEM((keys, rows), F32),
        pltpu.VMEM((2, slabs, keys, LANES), BF16),
        pltpu.VMEM((2, slabs, 2 * rows, LANES), BF16),
        pltpu.VMEM((2, slabs, rows, LANES), BF16),
        pltpu.VMEM((2 * rows, triple), BF16),
        pltpu.VMEM((2, part_rows, triple), BF16),
        pltpu.VMEM((rows, width), F32),
        pltpu.VMEM((rows, width), BF16),
        pltpu.VMEM((SMALL_ROWS, width), F32),
        pltpu.VMEM((SMALL_ROWS, width), F32),
        pltpu.VMEM(narrow_sums.shape, F32),
        pltpu.SemaphoreType.DMA((count, 6)),
        pltpu.SemaphoreType.DMA((count, 6)),
        pltpu.SemaphoreType.DMA((count, 2)),
        pltpu.SemaphoreType.DMA((count,)),
        pltpu.SemaphoreType.DMA((2, slabs // 2)),
        pltpu.SemaphoreType.DMA((2, slabs // 2)),
        pltpu.SemaphoreType.DMA((5,)),
        pltpu.SemaphoreType.DMA((5,)),
        pltpu.SemaphoreType.DMA((3,)),
    ]
    return pl.pallas_call(
        kernel,
        out_shape=[jax.ShapeDtypeStruct(shape, BF16) for shape in shapes]
        + [jax.ShapeDtypeStruct((rows, width), BF16), jax.ShapeDtypeStruct(rights[1].shape, BF16)],
        in_specs=[ANYWHERE] * (given + 7)
        + [IN_VMEM, ANYWHERE]
        + [IN_VMEM] * 4
        + [ANYWHERE]
        + [IN_VMEM] * 5,
        out_specs=[ANYWHERE] * (array_count + 2),
        scratch_shapes=scratch,
        compiler_params=remote_params(collective_id, 61 << 20),
        name="back_and_sum",
    )(
        *partials,
        *lefts_t,
        *rights,
        queries,
        keys_values,
        mixed,
        grad_mixed,
        logs,
        ends,
        w_qkv,
        tokens,
        grad_middle,
        gains,
        wide_sums,
        narrow_sums,
    )


def widen(arrays, plain):
    count = len(arrays)
    extra = len(plain)
    total = count + extra

    def kernel(*refs):
        sources, results = refs[:total], refs[total : 2 * total]
        narrow, wide = (
            refs[2 * total : 2 * total + count],
            refs[2 * total + count : 2 * total + 2 * count],
        )
        hold = refs[2 * total + 2 * count : 2 * total + 2 * count + extra]
        in_sems, out_sems = refs[2 * total + 2 * count + extra :]

        def read(i):
            dst = narrow[i] if i < count else hold[i - count]
            return pltpu.make_async_copy(sources[i], dst, in_sems.at[i])

        def write(i):
            src = wide[i] if i < count else hold[i - count]
            return pltpu.make_async_copy(src, results[i], out_sems.at[i])

        order = list(range(count, total)) + sorted(range(count), key=lambda i: -arrays[i].size)
        for i in order:
            read(i).start()
        for i in order:
            if i >= count:
                read(i).wait()
                write(i).start()
                continue
            rows, columns = arrays[i].shape
            step = 16
            while rows % (2 * step) == 0 and 2 * step * columns <= 32768:
                step *= 2
            read(i).wait()

            @pl.loop(0, rows // step)
            def _(k):
                part = pl.ds(pl.multiple_of(k * step, step), step)
                wide[i][part] = narrow[i][part].astype(F32)

            write(i).start()
        for i in range(total):
            write(i).wait()

    return pl.pallas_call(
        kernel,
        out_shape=[jax.ShapeDtypeStruct(one.shape, F32) for one in arrays]
        + [jax.ShapeDtypeStruct(one.shape, one.dtype) for one in plain],
        in_specs=[ANYWHERE] * total,
        out_specs=[ANYWHERE] * total,
        scratch_shapes=[pltpu.VMEM(one.shape, BF16) for one in arrays]
        + [pltpu.VMEM(one.shape, F32) for one in arrays]
        + [pltpu.VMEM(one.shape, one.dtype) for one in plain]
        + [pltpu.SemaphoreType.DMA((total,)), pltpu.SemaphoreType.DMA((total,))],
        compiler_params=pltpu.CompilerParams(vmem_limit_bytes=61 << 20),
        name="widen",
    )(*arrays, *plain)


def fast_local(
    tokens,
    clip_lengths,
    target_pos,
    out_grad,
    norm1_gain,
    norm1_bias,
    w_qkv,
    w_out,
    norm2_gain,
    norm2_bias,
    w_fc1,
    w_fc2,
    w_embed,
    mask_token,
    pred_norm1_gain,
    pred_norm1_bias,
    pred_qkv,
    pred_out,
    pred_norm2_gain,
    pred_norm2_bias,
    pred_fc1,
    pred_fc2,
):
    rows, width = tokens.shape
    narrow = out_grad.shape[1]
    wide_part = norm1_gain.shape[0]
    narrow_part = mask_token.shape[0]
    me = lax.axis_index("fsdp")
    core = me & 1
    wide_small = jnp.pad(
        jnp.stack([norm1_gain, norm1_bias, norm2_gain, norm2_bias]), ((0, SMALL_ROWS - 4), (0, 0))
    )
    narrow_small = jnp.stack(
        [pred_norm1_gain, pred_norm1_bias, pred_norm2_gain, pred_norm2_bias, mask_token]
    )
    here = (jnp.arange(narrow, dtype=jnp.int32) // narrow_part == me)[None, :]
    narrow_small = jnp.where(here, jnp.tile(narrow_small, (1, 8)), jnp.zeros((), BF16))
    narrow_small = jnp.pad(narrow_small, ((0, SMALL_ROWS - 5), (0, 0)))

    order = jnp.arange(clip_lengths.shape[1], dtype=jnp.int32)
    clip_ends = jnp.sum(jnp.where(order[None, :] <= order[:, None], clip_lengths, 0), axis=1)
    first_rows = lax.axis_index("seq") * rows + jnp.arange(rows, dtype=jnp.int32)
    past_end = (first_rows[:, None] >= clip_ends[None, :]).astype(jnp.int32)
    rel_rows = first_rows - jnp.sum(clip_lengths[0][None, :] * past_end, axis=1)
    matches = jnp.arange(rows, dtype=jnp.int32)[:, None] == target_pos[0, 0][None, :]
    hit_rows = jnp.sum(matches.astype(F32), axis=1)
    side = jnp.concatenate(
        [position_table(rel_rows, narrow), jnp.broadcast_to(hit_rows[:, None], (rows, LANES))], axis=1
    )
    ends = jnp.pad(jnp.broadcast_to(clip_ends[:, None], (3, LANES)), ((0, 5), (0, 0)))

    whole, kept, narrow_kept, rest, traded = forward_pass(
        tokens,
        out_grad,
        side,
        ends,
        [
            wide_small,
            narrow_small,
            w_qkv,
            w_out,
            w_fc1,
            w_fc2,
            w_embed,
            pred_qkv,
            pred_out,
            pred_fc1,
            pred_fc2,
        ],
        HEADS,
        P_HEADS,
    )
    context_t, entry, side, tokens, gains, narrow_gains = rest
    out_grad, ends, context_out, predicted, hidden_t, narrow_hidden_t = traded
    normed_t, queries, keys_values, mixed, logs, middle, normed_mid_t, slope, mixed_t = kept
    (
        narrow_normed_t,
        narrow_queries,
        narrow_kv,
        narrow_mixed,
        narrow_logs,
        narrow_middle,
        narrow_mid_t,
        narrow_slope,
        narrow_mixed_t,
    ) = narrow_kept

    results = middle_back(
        dict(
            out_grad=out_grad,
            narrow_down=whole[10],
            narrow_slope=narrow_slope,
            narrow_up=whole[9],
            narrow_gains=narrow_gains,
            narrow_middle=narrow_middle,
            narrow_out=whole[8],
            ends=ends,
            narrow_queries=narrow_queries,
            narrow_kv=narrow_kv.reshape(2, narrow // LANES, 4 * rows, LANES),
            narrow_mixed=narrow_mixed,
            narrow_logs=narrow_logs,
            narrow_qkv=whole[7],
            entry=entry,
            side=side,
            w_embed=whole[6],
            wide_down=whole[5],
            wide_slope=slope,
            wide_up=whole[4],
            wide_gains=gains,
            wide_middle=middle,
            wide_out=whole[3],
        ),
        [narrow_hidden_t, narrow_mid_t, narrow_mixed_t, narrow_normed_t, context_t],
        P_HEADS,
        2,
    )
    partials = [one.reshape(4, one.shape[0] // 4, one.shape[1]) for one in results[:5]]
    grad_low, grad_pre, grad_branch, grad_middle, grad_mixed, wide_sums, narrow_sums = results[5:]
    results = back_and_sum(
        partials,
        [hidden_t, normed_mid_t, mixed_t, normed_t],
        [grad_low, grad_pre, grad_branch],
        queries,
        keys_values.reshape(2, width // LANES, 4 * rows, LANES),
        mixed,
        grad_mixed,
        logs,
        ends,
        whole[2].reshape(8, wide_part, 3 * width),
        tokens,
        grad_middle,
        gains,
        wide_sums,
        narrow_sums,
        HEADS,
        3,
    )
    final = widen(results[:-2], [results[-2], context_out, predicted])
    sums, (token_grad, context_out, predicted) = final[:-3], final[-3:]
    small = sums[9]
    narrow_out = [small[4 + i, :narrow_part] for i in range(5)]
    return (
        context_out,
        predicted,
        token_grad,
        small[0],
        small[1],
        sums[8],
        sums[7],
        small[2],
        small[3],
        sums[6],
        sums[5],
        sums[4],
        narrow_out[4],
        narrow_out[0],
        narrow_out[1],
        sums[3],
        sums[2],
        narrow_out[2],
        narrow_out[3],
        sums[1],
        sums[0],
    )


def solution(mesh):
    body = fast_local if fits_fast(mesh) else local
    return jax.shard_map(
        body,
        mesh=mesh,
        in_specs=(
            P(("fsdp", "seq"), None),
            P("fsdp", None),
            P("fsdp", "seq", None),
            P(("fsdp", "seq"), None),
            P("fsdp"),
            P("fsdp"),
            P("fsdp", None),
            P("fsdp", None),
            P("fsdp"),
            P("fsdp"),
            P("fsdp", None),
            P("fsdp", None),
            P("fsdp", None),
            P("fsdp"),
            P("fsdp"),
            P("fsdp"),
            P("fsdp", None),
            P("fsdp", None),
            P("fsdp"),
            P("fsdp"),
            P("fsdp", None),
            P("fsdp", None),
        ),
        out_specs=(
            P(("fsdp", "seq"), None),
            P(("fsdp", "seq"), None),
            P(("fsdp", "seq"), None),
            P("fsdp"),
            P("fsdp"),
            P("fsdp", None),
            P("fsdp", None),
            P("fsdp"),
            P("fsdp"),
            P("fsdp", None),
            P("fsdp", None),
            P("fsdp", None),
            P("fsdp"),
            P("fsdp"),
            P("fsdp"),
            P("fsdp", None),
            P("fsdp", None),
            P("fsdp"),
            P("fsdp"),
            P("fsdp", None),
            P("fsdp", None),
        ),
        check_vma=False,
    )
```

```python
import math

import jax
import jax.numpy as jnp
from jax import lax
from jax.experimental import pallas as pl
from jax.experimental.pallas import tpu as pltpu
from jax.sharding import PartitionSpec as P

HEADS = 16
PD = 384
P_HEADS = 12


EPSILON = 1e-06
NEG_FILL = -1e30
block_rows = 512


def layer_norm(values, norm_gain, norm_shift):
    center = values - jnp.mean(values, axis=-1, keepdims=True)
    spread = jnp.mean(center * center, axis=-1, keepdims=True)
    return center * lax.rsqrt(spread + EPSILON) * norm_gain + norm_shift


def gelu_exact(values):
    return jax.nn.gelu(values, approximate=False)


def position_table(positions, table_width):
    half_width = table_width // 2
    angle_rates = jnp.exp(
        jnp.arange(half_width, dtype=jnp.float32) * (-2.0 * math.log(10000.0) / table_width)
    )
    angles = positions.astype(jnp.float32)[:, None] * angle_rates[None, :]
    return jnp.concatenate([jnp.sin(angles), jnp.cos(angles)], axis=1)


def clip_index(positions, clip_ends):
    return jnp.sum((positions[:, None] >= clip_ends[None, :]).astype(jnp.int32), axis=1)


def key_step(total_keys):
    return max(min(total_keys, block_rows), total_keys // 8)


def block_scores(queries, key_part, query_clip, key_clip_part, score_scale):
    raw_scores = (
        jnp.einsum("the,khe->htk", queries, key_part, preferred_element_type=jnp.float32)
        * score_scale
    )
    same_clip = query_clip[:, None] == key_clip_part[None, :]
    return jnp.where(same_clip[None], raw_scores, NEG_FILL)


def attend_forward(queries, key_heads, value_heads, query_clip, key_clip):
    row_count, head_count, head_size = queries.shape
    score_scale = head_size ** (-0.5)
    total_keys = key_heads.shape[0]
    step_rows = key_step(total_keys)
    run_max = jnp.full((head_count, row_count), NEG_FILL, jnp.float32)
    run_total = jnp.zeros((head_count, row_count), jnp.float32)
    for key_start in range(0, total_keys, step_rows):
        scores = block_scores(
            queries,
            key_heads[key_start : key_start + step_rows],
            query_clip,
            key_clip[key_start : key_start + step_rows],
            score_scale,
        )
        new_max = jnp.maximum(run_max, jnp.max(scores, axis=2))
        run_total = run_total * jnp.exp(run_max - new_max) + jnp.sum(
            jnp.exp(scores - new_max[:, :, None]), axis=2
        )
        run_max = new_max
    log_total = run_max + jnp.log(run_total)
    output = jnp.zeros((row_count, head_count, head_size), jnp.float32)
    for key_start in range(0, total_keys, step_rows):
        scores = block_scores(
            queries,
            key_heads[key_start : key_start + step_rows],
            query_clip,
            key_clip[key_start : key_start + step_rows],
            score_scale,
        )
        soft_weights = jnp.exp(scores - log_total[:, :, None]).astype(jnp.bfloat16)
        output = output + jnp.einsum(
            "htk,khe->the",
            soft_weights,
            value_heads[key_start : key_start + step_rows],
            preferred_element_type=jnp.float32,
        )
    return (output, log_total)


def attend_backward(
    queries, key_heads, value_heads, query_clip, key_clip, log_total, grad_mixed, output
):
    row_count, head_count, head_size = queries.shape
    score_scale = head_size ** (-0.5)
    total_keys = key_heads.shape[0]
    step_rows = key_step(total_keys)
    row_delta = jnp.sum(grad_mixed.astype(jnp.float32) * output, axis=2).T
    grad_query = jnp.zeros((row_count, head_count, head_size), jnp.float32)
    key_pieces = []
    value_pieces = []
    for key_start in range(0, total_keys, step_rows):
        key_part = key_heads[key_start : key_start + step_rows]
        value_part = value_heads[key_start : key_start + step_rows]
        scores = block_scores(
            queries, key_part, query_clip, key_clip[key_start : key_start + step_rows], score_scale
        )
        soft_weights = jnp.exp(scores - log_total[:, :, None])
        grad_soft = jnp.einsum(
            "the,khe->htk", grad_mixed, value_part, preferred_element_type=jnp.float32
        )
        grad_scores = (soft_weights * (grad_soft - row_delta[:, :, None])).astype(jnp.bfloat16)
        grad_query = grad_query + jnp.einsum(
            "htk,khe->the", grad_scores, key_part, preferred_element_type=jnp.float32
        )
        key_pieces.append(
            jnp.einsum("htk,the->khe", grad_scores, queries, preferred_element_type=jnp.float32)
        )
        value_pieces.append(
            jnp.einsum(
                "htk,the->khe",
                soft_weights.astype(jnp.bfloat16),
                grad_mixed,
                preferred_element_type=jnp.float32,
            )
        )
    key_terms = jnp.concatenate(key_pieces, axis=0) * score_scale
    value_terms = jnp.concatenate(value_pieces, axis=0)
    return (grad_query * score_scale, key_terms, value_terms)


def block_forward(
    residual, norm_params, w_qkv, w_out, w_up, w_down, head_count, query_clip, key_clip
):
    row_count, model_width = residual.shape
    head_size = model_width // head_count
    norm_float = norm_params.astype(jnp.float32)
    normed = layer_norm(residual, norm_float[:, 0], norm_float[:, 1]).astype(jnp.bfloat16)
    qkv = jnp.dot(normed, w_qkv, preferred_element_type=jnp.float32).astype(jnp.bfloat16)
    queries = qkv[:, :model_width].reshape(row_count, head_count, head_size)
    key_local = qkv[:, model_width : 2 * model_width]
    value_local = qkv[:, 2 * model_width :]
    key_full, value_full = (
        lax.all_gather(key_local, "seq", axis=0, tiled=True),
        lax.all_gather(value_local, "seq", axis=0, tiled=True),
    )
    key_heads = key_full.reshape(-1, head_count, head_size)
    value_heads = value_full.reshape(-1, head_count, head_size)
    output, log_total = attend_forward(queries, key_heads, value_heads, query_clip, key_clip)
    mixed = output.reshape(row_count, model_width).astype(jnp.bfloat16)
    middle = residual + jnp.dot(mixed, w_out, preferred_element_type=jnp.float32)
    normed_mid = layer_norm(middle, norm_float[:, 2], norm_float[:, 3]).astype(jnp.bfloat16)
    pre_act = jnp.dot(normed_mid, w_up, preferred_element_type=jnp.float32)
    hidden = gelu_exact(pre_act).astype(jnp.bfloat16)
    result = middle + jnp.dot(hidden, w_down, preferred_element_type=jnp.float32)
    kept = (
        residual,
        normed,
        queries,
        key_local,
        value_local,
        key_heads,
        value_heads,
        output,
        log_total,
        mixed,
        middle,
        normed_mid,
        pre_act,
        hidden,
    )
    return (result, kept)


def block_backward(
    grad_result, kept, norm_params, w_qkv, w_out, w_up, w_down, head_count, query_clip, key_clip
):
    (
        residual,
        normed,
        queries,
        key_local,
        value_local,
        key_heads,
        value_heads,
        output,
        log_total,
        mixed,
        middle,
        normed_mid,
        pre_act,
        hidden,
    ) = kept
    row_count, model_width = residual.shape
    head_size = model_width // head_count
    norm_float = norm_params.astype(jnp.float32)
    grad_low = grad_result.astype(jnp.bfloat16)
    grad_down = jnp.einsum("tf,tw->fw", hidden, grad_low, preferred_element_type=jnp.float32)
    grad_hidden = jnp.einsum("tw,fw->tf", grad_low, w_down, preferred_element_type=jnp.float32)
    gelu_value, gelu_pull = jax.vjp(gelu_exact, pre_act)
    grad_pre = gelu_pull(grad_hidden)[0].astype(jnp.bfloat16)
    grad_up = jnp.einsum("tw,tf->wf", normed_mid, grad_pre, preferred_element_type=jnp.float32)
    grad_normed_mid = jnp.einsum("tf,wf->tw", grad_pre, w_up, preferred_element_type=jnp.float32)
    second_value, second_pull = jax.vjp(layer_norm, middle, norm_float[:, 2], norm_float[:, 3])
    grad_mid_norm, grad_gain_two, grad_shift_two = second_pull(grad_normed_mid)
    grad_middle = grad_result + grad_mid_norm
    grad_branch = grad_middle.astype(jnp.bfloat16)
    grad_out_w = jnp.einsum("tv,tw->vw", mixed, grad_branch, preferred_element_type=jnp.float32)
    grad_mixed = jnp.einsum(
        "tw,vw->tv", grad_branch, w_out, preferred_element_type=jnp.float32
    ).astype(jnp.bfloat16)
    key_full, value_full = (
        lax.all_gather(key_local, "seq", axis=0, tiled=True),
        lax.all_gather(value_local, "seq", axis=0, tiled=True),
    )
    key_heads = key_full.reshape(-1, head_count, head_size)
    value_heads = value_full.reshape(-1, head_count, head_size)
    grad_query, key_terms, value_terms = attend_backward(
        queries,
        key_heads,
        value_heads,
        query_clip,
        key_clip,
        log_total,
        grad_mixed.reshape(row_count, head_count, head_size),
        output,
    )
    grad_key, grad_value = (
        lax.psum_scatter(
            key_terms.reshape(-1, model_width).astype(jnp.bfloat16),
            "seq",
            scatter_dimension=0,
            tiled=True,
        ).astype(jnp.float32),
        lax.psum_scatter(
            value_terms.reshape(-1, model_width).astype(jnp.bfloat16),
            "seq",
            scatter_dimension=0,
            tiled=True,
        ).astype(jnp.float32),
    )
    grad_qkv = jnp.concatenate(
        [grad_query.reshape(row_count, model_width), grad_key, grad_value], axis=1
    ).astype(jnp.bfloat16)
    grad_qkv_w = jnp.einsum("tw,tc->wc", normed, grad_qkv, preferred_element_type=jnp.float32)
    grad_normed = jnp.einsum("tc,wc->tw", grad_qkv, w_qkv, preferred_element_type=jnp.float32)
    first_value, first_pull = jax.vjp(layer_norm, residual, norm_float[:, 0], norm_float[:, 1])
    grad_first_norm, grad_gain_one, grad_shift_one = first_pull(grad_normed)
    grad_norms = jnp.stack([grad_gain_one, grad_shift_one, grad_gain_two, grad_shift_two], axis=1)
    return (grad_middle + grad_first_norm, (grad_norms, grad_qkv_w, grad_out_w, grad_up, grad_down))


def local(
    tokens,
    clip_lengths,
    target_pos,
    out_grad,
    norm1_gain,
    norm1_bias,
    w_qkv,
    w_out,
    norm2_gain,
    norm2_bias,
    w_fc1,
    w_fc2,
    w_embed,
    mask_token,
    pred_norm1_gain,
    pred_norm1_bias,
    pred_qkv,
    pred_out,
    pred_norm2_gain,
    pred_norm2_bias,
    pred_fc1,
    pred_fc2,
):
    row_count = tokens.shape[0]
    group_count = row_count * lax.axis_size("seq")
    lengths = clip_lengths[0]
    clip_ends = jnp.cumsum(lengths)
    local_rows = lax.axis_index("seq") * row_count + jnp.arange(row_count, dtype=jnp.int32)
    query_clip = clip_index(local_rows, clip_ends)
    key_clip = clip_index(jnp.arange(group_count, dtype=jnp.int32), clip_ends)
    past_end = (local_rows[:, None] >= clip_ends[None, :]).astype(jnp.int32)
    rel_rows = local_rows - jnp.sum(lengths[None, :] * past_end, axis=1)
    ctx_small = jnp.stack([norm1_gain, norm1_bias, norm2_gain, norm2_bias], axis=1)
    pred_small = jnp.stack(
        [pred_norm1_gain, pred_norm1_bias, pred_norm2_gain, pred_norm2_bias, mask_token], axis=1
    )
    ctx_params = (
        lax.all_gather(ctx_small, "fsdp", axis=0, tiled=True),
        lax.all_gather(w_qkv, "fsdp", axis=0, tiled=True),
        lax.all_gather(w_out, "fsdp", axis=0, tiled=True),
        lax.all_gather(w_fc1, "fsdp", axis=0, tiled=True),
        lax.all_gather(w_fc2, "fsdp", axis=0, tiled=True),
    )
    pred_params = (
        lax.all_gather(pred_small, "fsdp", axis=0, tiled=True),
        lax.all_gather(w_embed, "fsdp", axis=0, tiled=True),
        lax.all_gather(pred_qkv, "fsdp", axis=0, tiled=True),
        lax.all_gather(pred_out, "fsdp", axis=0, tiled=True),
        lax.all_gather(pred_fc1, "fsdp", axis=0, tiled=True),
        lax.all_gather(pred_fc2, "fsdp", axis=0, tiled=True),
    )
    ctx_result, ctx_kept = block_forward(
        tokens.astype(jnp.float32),
        ctx_params[0],
        ctx_params[1],
        ctx_params[2],
        ctx_params[3],
        ctx_params[4],
        HEADS,
        query_clip,
        key_clip,
    )
    context_out = ctx_result.astype(jnp.bfloat16)
    embedded = jnp.dot(context_out, pred_params[1], preferred_element_type=jnp.float32)
    targets = target_pos[0, 0]
    matches = jnp.arange(row_count, dtype=jnp.int32)[:, None] == targets[None, :]
    placement = matches.astype(jnp.float32)
    target_hit = jnp.sum(placement, axis=1)
    target_rel = jnp.sum(jnp.where(matches, rel_rows[:, None], 0), axis=0)
    mask_rows = pred_params[0][:, 4].astype(jnp.float32)[None, :] + position_table(target_rel, PD)
    placed = jnp.dot(
        placement, mask_rows, precision=lax.Precision.HIGHEST, preferred_element_type=jnp.float32
    )
    pred_in = embedded * (1.0 - target_hit[:, None]) + placed
    pred_result, pred_kept = block_forward(
        pred_in,
        pred_params[0],
        pred_params[2],
        pred_params[3],
        pred_params[4],
        pred_params[5],
        P_HEADS,
        query_clip,
        key_clip,
    )
    predicted = pred_result.astype(jnp.bfloat16)
    pred_back = (
        lax.all_gather(pred_small, "fsdp", axis=0, tiled=True),
        lax.all_gather(w_embed, "fsdp", axis=0, tiled=True),
        lax.all_gather(pred_qkv, "fsdp", axis=0, tiled=True),
        lax.all_gather(pred_out, "fsdp", axis=0, tiled=True),
        lax.all_gather(pred_fc1, "fsdp", axis=0, tiled=True),
        lax.all_gather(pred_fc2, "fsdp", axis=0, tiled=True),
    )
    ctx_back = (
        lax.all_gather(ctx_small, "fsdp", axis=0, tiled=True),
        lax.all_gather(w_qkv, "fsdp", axis=0, tiled=True),
        lax.all_gather(w_out, "fsdp", axis=0, tiled=True),
        lax.all_gather(w_fc1, "fsdp", axis=0, tiled=True),
        lax.all_gather(w_fc2, "fsdp", axis=0, tiled=True),
    )
    grad_pred_in, pred_grads = block_backward(
        out_grad.astype(jnp.float32),
        pred_kept,
        pred_back[0],
        pred_back[2],
        pred_back[3],
        pred_back[4],
        pred_back[5],
        P_HEADS,
        query_clip,
        key_clip,
    )
    grad_mask = jnp.sum(target_hit[:, None] * grad_pred_in, axis=0)
    grad_embedded = (grad_pred_in * (1.0 - target_hit[:, None])).astype(jnp.bfloat16)
    grad_embed_w = jnp.einsum(
        "td,tp->dp", context_out, grad_embedded, preferred_element_type=jnp.float32
    )
    grad_context = jnp.einsum(
        "tp,dp->td", grad_embedded, pred_back[1], preferred_element_type=jnp.float32
    )
    grad_tokens, ctx_grads = block_backward(
        grad_context,
        ctx_kept,
        ctx_back[0],
        ctx_back[1],
        ctx_back[2],
        ctx_back[3],
        ctx_back[4],
        HEADS,
        query_clip,
        key_clip,
    )
    pred_small_grad = jnp.concatenate([pred_grads[0], grad_mask[:, None]], axis=1)
    row_sums = (
        lax.psum_scatter(ctx_grads[0], "fsdp", scatter_dimension=0, tiled=True),
        lax.psum_scatter(ctx_grads[1], "fsdp", scatter_dimension=0, tiled=True),
        lax.psum_scatter(ctx_grads[2], "fsdp", scatter_dimension=0, tiled=True),
        lax.psum_scatter(ctx_grads[3], "fsdp", scatter_dimension=0, tiled=True),
        lax.psum_scatter(ctx_grads[4], "fsdp", scatter_dimension=0, tiled=True),
        lax.psum_scatter(grad_embed_w, "fsdp", scatter_dimension=0, tiled=True),
        lax.psum_scatter(pred_small_grad, "fsdp", scatter_dimension=0, tiled=True),
        lax.psum_scatter(pred_grads[1], "fsdp", scatter_dimension=0, tiled=True),
        lax.psum_scatter(pred_grads[2], "fsdp", scatter_dimension=0, tiled=True),
        lax.psum_scatter(pred_grads[3], "fsdp", scatter_dimension=0, tiled=True),
        lax.psum_scatter(pred_grads[4], "fsdp", scatter_dimension=0, tiled=True),
    )
    summed = (
        lax.psum(row_sums[0].astype(jnp.bfloat16), "seq").astype(jnp.float32),
        lax.psum(row_sums[1].astype(jnp.bfloat16), "seq").astype(jnp.float32),
        lax.psum(row_sums[2].astype(jnp.bfloat16), "seq").astype(jnp.float32),
        lax.psum(row_sums[3].astype(jnp.bfloat16), "seq").astype(jnp.float32),
        lax.psum(row_sums[4].astype(jnp.bfloat16), "seq").astype(jnp.float32),
        lax.psum(row_sums[5].astype(jnp.bfloat16), "seq").astype(jnp.float32),
        lax.psum(row_sums[6].astype(jnp.bfloat16), "seq").astype(jnp.float32),
        lax.psum(row_sums[7].astype(jnp.bfloat16), "seq").astype(jnp.float32),
        lax.psum(row_sums[8].astype(jnp.bfloat16), "seq").astype(jnp.float32),
        lax.psum(row_sums[9].astype(jnp.bfloat16), "seq").astype(jnp.float32),
        lax.psum(row_sums[10].astype(jnp.bfloat16), "seq").astype(jnp.float32),
    )
    return (
        context_out,
        predicted,
        grad_tokens.astype(jnp.bfloat16),
        summed[0][:, 0],
        summed[0][:, 1],
        summed[1],
        summed[2],
        summed[0][:, 2],
        summed[0][:, 3],
        summed[3],
        summed[4],
        summed[5],
        summed[6][:, 4],
        summed[6][:, 0],
        summed[6][:, 1],
        summed[7],
        summed[8],
        summed[6][:, 2],
        summed[6][:, 3],
        summed[9],
        summed[10],
    )


BF16 = jnp.bfloat16
F32 = jnp.float32
MESH = pl.DeviceIdType.MESH
LOG2E = 1.4426950408889634
LN2 = 0.6931471805599453
LANES = 128
SMALL_ROWS = 16
ANYWHERE = pl.BlockSpec(memory_space=pl.ANY)
IN_VMEM = pl.BlockSpec(memory_space=pltpu.VMEM)


def fits_fast(mesh):
    return mesh.shape["fsdp"] == 8 and mesh.shape["seq"] == 4


def fsdp_peer(bit):
    return (lax.axis_index("fsdp") ^ bit, lax.axis_index("seq"))


def seq_peer(index):
    return (lax.axis_index("fsdp"), index)


def enter(peers):
    barrier = pltpu.get_barrier_semaphore()
    for peer in peers:
        pl.semaphore_signal(barrier, inc=1, device_id=peer, device_id_type=MESH)
    pl.semaphore_wait(barrier, len(peers))


def send(src, dst, send_sem, recv_sem, peer):
    return pltpu.make_async_remote_copy(
        src_ref=src,
        dst_ref=dst,
        send_sem=send_sem,
        recv_sem=recv_sem,
        device_id=peer,
        device_id_type=MESH,
    )


def remote_params(collective_id, vmem=None):
    return pltpu.CompilerParams(
        collective_id=collective_id, has_side_effects=True, vmem_limit_bytes=vmem
    )


def mate_z():
    return seq_peer(lax.axis_index("seq") ^ 1)


def quarter():
    return (lax.axis_index("fsdp") & 1) * 2 + (lax.axis_index("seq") & 1)


def across_lanes(left, right):
    return lax.dot_general(left, right, (((1,), (1,)), ((), ())), preferred_element_type=F32)


def forward_pass(tokens, out_grad, side, ends, shards, heads, narrow_heads):
    rows, width = tokens.shape
    narrow = out_grad.shape[1]
    hidden_width = shards[4].shape[1]
    narrow_hidden = shards[9].shape[1]
    shapes = [shard.shape for shard in shards]
    array_count = len(shards)
    units = []
    for index, (shard_rows, columns) in enumerate(shapes):
        if shard_rows * columns >= 100000:
            half = shard_rows // 2
            units.append((index, 0, half, 2, 4))
            units.append((index, half, half, 4, 2))
        else:
            near, far = (2, 4) if len(units) % 2 == 0 else (4, 2)
            units.append((index, 0, shard_rows, near, far))
    count = len(units)
    ahead = 3
    last_unit = {}
    for u, unit in enumerate(units):
        last_unit[unit[0]] = u

    block_widths = ((width, heads, hidden_width, 2), (narrow, narrow_heads, narrow_hidden, 1))
    saved_shapes = []
    for w, _, ff, _ in block_widths:
        saved_shapes += [
            ((w, rows), BF16),
            ((rows, w), BF16),
            ((2, w // LANES, 4, rows, LANES), BF16),
            ((rows, w), BF16),
            ((w // LANES, 8, rows), F32),
            ((rows, w), F32),
            ((w, rows), BF16),
            ((rows, ff), BF16),
            ((w, rows), BF16),
        ]
    per_block = len(saved_shapes) // 2
    saved_shapes += [((width, rows), BF16), ((rows, narrow), F32), (side.shape, F32), ((rows, width), BF16)]
    saved_shapes += [((SMALL_ROWS, width), F32), ((SMALL_ROWS, narrow), F32)]
    saved_count = len(saved_shapes)

    def kernel(*refs):
        tokens_ref, out_grad_ref, side_ref, ends_ref = refs[:4]
        sources = refs[4 : 4 + array_count]
        base = 4 + array_count
        weight_outs = refs[base : base + array_count]
        base += array_count
        saved_outs = refs[base : base + saved_count]
        base += saved_count
        out_grad_out, ends_out, context_out, predicted_out, wide_hidden_t, narrow_hidden_t = refs[base : base + 6]
        base += 6
        weights = refs[base : base + array_count]
        base += array_count
        saved = refs[base : base + saved_count]
        base += saved_count
        (
            bias,
            ends_buf,
            predicted,
            wide_normed,
            wide_hidden,
            narrow_normed,
            narrow_hid,
            stage,
            stage_sems,
            send_sems,
            recv_sems,
            local_sems,
            weight_sems,
            saved_sems,
            trade_send,
            trade_recv,
            trade_keep,
            key_send,
            key_recv,
        ) = refs[base:]
        context_t, entry, side_buf, token_buf, gains, narrow_gains = saved[2 * per_block :]
        context = wide_normed

        me = lax.axis_index("fsdp")
        place = lax.axis_index("seq")
        core = me & 1
        high = place >> 1
        low = place & 1
        mine = quarter()
        trades = core != high
        trade_peer = ((me & 6) | high, core * 2 + low)

        barrier = pltpu.get_barrier_semaphore()
        for peer in (fsdp_peer(1), fsdp_peer(2), fsdp_peer(4), mate_z()):
            pl.semaphore_signal(barrier, inc=1, device_id=peer, device_id_type=MESH)

        @pl.when(trades)
        def _():
            pl.semaphore_signal(barrier, inc=1, device_id=trade_peer, device_id_type=MESH)

        pl.semaphore_wait(barrier, 4 + trades.astype(jnp.int32))


        def trade_copy(i, src, dst):
            return send(src, dst, trade_send.at[i], trade_recv.at[i], trade_peer)

        def keep_copy(i, src, dst):
            return pltpu.make_async_copy(src, dst, trade_keep.at[i])

        traded = [
            (tokens_ref, token_buf),
            (side_ref, side_buf),
            (ends_ref, ends_buf),
            (out_grad_ref, out_grad_out),
            (context, context_out),
            (predicted, predicted_out),
        ]

        def trade_start(i):
            @pl.when(trades)
            def _():
                trade_copy(i, *traded[i]).start()

            @pl.when(jnp.logical_not(trades))
            def _():
                keep_copy(i, *traded[i]).start()

        def trade_arrived(i):
            @pl.when(trades)
            def _():
                trade_copy(i, *traded[i]).wait_recv()

            @pl.when(jnp.logical_not(trades))
            def _():
                keep_copy(i, *traded[i]).wait()

        def trade_sent(i):
            @pl.when(trades)
            def _():
                trade_copy(i, *traded[i]).wait_send()


        def place_of(u, owner):
            index, first, unit_rows, _, _ = units[u]
            start = owner * shapes[index][0] + first
            return weights[index].at[pl.ds(pl.multiple_of(start, 16), unit_rows)]

        def own_shard(u):
            index, first, unit_rows, _, _ = units[u]
            return sources[index].at[pl.ds(first, unit_rows)]

        def weight_copy(u, slot):
            _, _, _, near, far = units[u]
            owner = me ^ (0, 0, near, 0, near, far, near ^ far)[slot]
            bit = (near, far, far, 1, 1, 1, 1)[slot]
            src = own_shard(u) if slot in (0, 1, 3) else place_of(u, owner)
            return send(src, place_of(u, owner), send_sems.at[u, slot], recv_sems.at[u, slot], fsdp_peer(bit))

        def own_weight(u):
            return pltpu.make_async_copy(own_shard(u), place_of(u, me), local_sems.at[u])

        def weight_out(index):
            return pltpu.make_async_copy(weights[index], weight_outs[index], weight_sems.at[index])

        def launch(u):
            for slot in (0, 1, 3):
                weight_copy(u, slot).start()
            own_weight(u).start()

        def arrive(u):
            weight_copy(u, 0).wait_recv()
            weight_copy(u, 2).start()
            weight_copy(u, 4).start()
            weight_copy(u, 1).wait_recv()
            weight_copy(u, 5).start()
            if u + ahead < count:
                launch(u + ahead)

        def relay(u):
            weight_copy(u, 2).wait_recv()
            weight_copy(u, 6).start()

        def complete(u):
            for slot in (3, 4, 5, 6):
                weight_copy(u, slot).wait_recv()
            own_weight(u).wait()
            index = units[u][0]
            if last_unit[index] == u:
                weight_out(index).start()

        ticks = []
        ready = {}
        for u in range(count + 2):
            if u < count:
                ticks.append((arrive, u))
            if 1 <= u <= count:
                ticks.append((relay, u - 1))
            if u >= 2:
                ticks.append((complete, u - 2))
                ready[units[u - 2][0]] = len(ticks)
        position = [0]

        def advance(steps):
            for _ in range(steps):
                if position[0] < len(ticks):
                    step, u = ticks[position[0]]
                    step(u)
                    position[0] += 1

        def need(index):
            while position[0] < ready[index]:
                advance(1)


        def save(i):
            return pltpu.make_async_copy(saved[i], saved_outs[i], saved_sems.at[i])

        def norm_into(dst, get, table, gain_at):
            @pl.loop(0, rows // 64)
            def _(i):
                part = pl.ds(pl.multiple_of(i * 64, 64), 64)
                value = get(part)
                value = value - jnp.mean(value, axis=1, keepdims=True)
                inverse = lax.rsqrt(jnp.mean(value * value, axis=1, keepdims=True) + EPSILON)
                dst[part] = (
                    value * inverse * table[gain_at : gain_at + 1, :] + table[gain_at + 1 : gain_at + 2, :]
                ).astype(BF16)

        def turn(src, dst):
            for c in range(dst.shape[0] // LANES):
                at = slice(c * LANES, (c + 1) * LANES)
                dst[at, :] = src[:, at].T

        def run_block(which, get, table, first_weight, finish, inside):
            w, head_count, ff, in_group = block_widths[which]
            (normed_t, queries, kv, mixed, logs, middle, normed_mid_t, slope, mixed_t) = saved[
                which * per_block : (which + 1) * per_block
            ]
            normed, hidden = ((wide_normed, wide_hidden), (narrow_normed, narrow_hid))[which]
            hidden_out = (wide_hidden_t, narrow_hidden_t)[which]
            w_qkv, w_out, w_up, w_down = [weights[first_weight[i]] for i in range(4)]
            slabs = w // LANES
            groups = slabs // in_group
            head_size = w // head_count
            per_slab = LANES // head_size
            factor = head_size ** (-0.5) * LOG2E
            columns = in_group * LANES

            def kv_copy(kind, g):
                owner = mine ^ 1 if kind == 2 else mine
                part = kv.at[:, pl.ds(g * in_group, in_group), owner]
                return send(
                    part,
                    part,
                    key_send.at[which, kind, g],
                    key_recv.at[which, kind, g],
                    mate_z() if kind == 0 else fsdp_peer(1),
                )

            norm_into(normed, get, table, 0)
            turn(normed, normed_t)
            save(which * per_block).start()
            need(first_weight[0])
            for g in range(groups):
                for kind in range(2):
                    tile = jnp.dot(
                        normed[...],
                        w_qkv[:, pl.ds((1 + kind) * w + g * columns, columns)],
                        preferred_element_type=F32,
                    ).astype(BF16)
                    for k in range(in_group):
                        kv[kind, g * in_group + k, mine] = tile[:, k * LANES : (k + 1) * LANES]
                kv_copy(0, g).start()
                kv_copy(1, g).start()

            @pl.loop(0, groups)
            def _(g):
                at = pl.ds(pl.multiple_of(g * columns, columns), columns)
                queries[:, at] = jnp.dot(normed[...], w_qkv[:, at], preferred_element_type=F32).astype(BF16)
            save(which * per_block + 1).start()
            advance(inside[0])
            kv_copy(0, 0).wait_recv()
            kv_copy(2, 0).start()

            lane = lax.broadcasted_iota(jnp.int32, (rows, LANES), 1) // head_size
            sub = lax.broadcasted_iota(jnp.int32, (LANES, rows), 0) // head_size

            @pl.loop(0, slabs)
            def _(j):
                g = j // in_group

                @pl.when(j % in_group == 0)
                def _():
                    kv_copy(1, g).wait_recv()
                    kv_copy(2, g).wait_recv()

                at = pl.ds(pl.multiple_of(j * LANES, LANES), LANES)
                own_queries = queries[:, at]
                key_slab = kv[0, j].reshape(4 * rows, LANES)
                values_t = kv[1, j].reshape(4 * rows, LANES).T
                output = jnp.zeros((LANES, rows), F32)
                logs[j] = jnp.zeros((8, rows), F32)
                for head in range(per_slab):
                    own = jnp.where(lane == head, own_queries, jnp.zeros_like(own_queries))
                    scores = across_lanes(key_slab, own) * factor + bias[...]
                    top = jnp.max(scores, axis=0, keepdims=True)
                    soft = jnp.exp2(scores - top)
                    total = jnp.sum(soft, axis=0, keepdims=True)
                    attended = jnp.dot(values_t, soft.astype(BF16), preferred_element_type=F32) / total
                    output = jnp.where(sub == head, attended, output)
                    logs[j, head : head + 1, :] = top + jnp.log2(total)
                mixed[:, at] = output.T.astype(BF16)
                mixed_t[at, :] = output.astype(BF16)

                @pl.when(jnp.logical_and(j % in_group == 0, g + 1 < groups))
                def _():
                    kv_copy(0, g + 1).wait_recv()
                    kv_copy(2, g + 1).start()

                for k in range(slabs):

                    @pl.when(j == k)
                    def _():
                        advance(inside[1])

            for i in (2, 3, 4, 8):
                save(which * per_block + i).start()
            need(first_weight[1])
            step = 2 * LANES if w % (2 * LANES) == 0 else LANES

            @pl.loop(0, w // step)
            def _(c):
                at = pl.ds(pl.multiple_of(c * step, step), step)
                middle[:, at] = get(pl.ds(0, rows), at) + jnp.dot(
                    mixed[...], w_out[:, at], preferred_element_type=F32
                )
            save(which * per_block + 5).start()
            norm_into(normed, lambda part: middle[part], table, 2)
            turn(normed, normed_mid_t)
            save(which * per_block + 6).start()
            need(first_weight[2])

            def stage_copy(c):
                return pltpu.make_async_copy(
                    stage.at[c % 2],
                    hidden_out.at[pl.ds(pl.multiple_of(c * 2 * LANES, 2 * LANES), 2 * LANES)],
                    stage_sems.at[c % 2],
                )

            @pl.loop(0, ff // (2 * LANES))
            def _(c):
                at = pl.ds(pl.multiple_of(c * 2 * LANES, 2 * LANES), 2 * LANES)
                pre = jnp.dot(normed[...], w_up[:, at], preferred_element_type=F32)
                below = 0.5 * (1.0 + lax.erf(pre * (0.5**0.5)))
                bell = jnp.exp2(pre * pre * (-0.5 * LOG2E)) * (1.0 / math.sqrt(2.0 * math.pi))
                active = (pre * below).astype(BF16)
                hidden[:, at] = active
                slope[:, at] = (below + pre * bell).astype(BF16)

                @pl.when(c >= 2)
                def _():
                    stage_copy(c - 2).wait()

                stage[c % 2] = active.T
                stage_copy(c).start()

            stage_copy(ff // (2 * LANES) - 2).wait()
            stage_copy(ff // (2 * LANES) - 1).wait()
            save(which * per_block + 7).start()
            need(first_weight[3])

            @pl.loop(0, w // step)
            def _(c):
                at = pl.ds(pl.multiple_of(c * step, step), step)
                finish(
                    at, middle[:, at] + jnp.dot(hidden[...], w_down[:, at], preferred_element_type=F32)
                )
            for g in range(groups):
                for kind in range(3):
                    kv_copy(kind, g).wait_send()


        for i in (0, 2, 1):
            trade_start(i)
        for u in range(ahead):
            launch(u)
        trade_start(3)
        need(1)
        for owner in range(8):
            gains[:, owner * LANES : (owner + 1) * LANES] = weights[0][
                owner * SMALL_ROWS : (owner + 1) * SMALL_ROWS, :
            ].astype(F32)
        total = weights[1][0:SMALL_ROWS, :].astype(F32)
        for owner in range(1, 8):
            total = total + weights[1][owner * SMALL_ROWS : (owner + 1) * SMALL_ROWS, :].astype(F32)
        narrow_gains[...] = total
        save(2 * per_block + 4).start()
        save(2 * per_block + 5).start()
        trade_arrived(2)
        group_bias(bias, ends_buf, rows)
        trade_arrived(0)
        save(2 * per_block + 3).start()

        def token_rows(part, at=slice(None)):
            return token_buf[part, at].astype(F32)

        def finish_context(at, value):
            context[:, at] = value.astype(BF16)

        run_block(0, token_rows, gains, (2, 3, 4, 5), finish_context, (1, 1))
        trade_start(4)
        turn(context, context_t)
        save(2 * per_block).start()
        need(6)
        trade_arrived(1)
        save(2 * per_block + 2).start()
        embedded = jnp.dot(context[...], weights[6][...], preferred_element_type=F32)
        hit = side_buf[:, narrow : narrow + 1]
        entry[...] = jnp.where(hit > 0.0, narrow_gains[4:5, :] + side_buf[:, 0:narrow], embedded)
        save(2 * per_block + 1).start()

        def entry_rows(part, at=slice(None)):
            return entry[part, at]

        def finish_predicted(at, value):
            predicted[:, at] = value.astype(BF16)

        run_block(1, entry_rows, narrow_gains, (7, 8, 9, 10), finish_predicted, (0, 0))
        trade_start(5)
        advance(len(ticks))
        for u in range(count):
            for slot in range(7):
                weight_copy(u, slot).wait_send()
        for index in range(array_count):
            weight_out(index).wait()
        for i in range(saved_count):
            save(i).wait()
        keep_copy(6, ends_buf, ends_out).start()
        for i in (3, 4, 5):
            trade_arrived(i)
        for i in range(6):
            trade_sent(i)
        keep_copy(6, ends_buf, ends_out).wait()

    gathered = [(8 * shape[0], shape[1]) for shape in shapes]
    out_shape = (
        [jax.ShapeDtypeStruct(shape, BF16) for shape in gathered]
        + [jax.ShapeDtypeStruct(shape, kind) for shape, kind in saved_shapes]
        + [
            jax.ShapeDtypeStruct(out_grad.shape, BF16),
            jax.ShapeDtypeStruct(ends.shape, jnp.int32),
            jax.ShapeDtypeStruct((rows, width), BF16),
            jax.ShapeDtypeStruct((rows, narrow), BF16),
            jax.ShapeDtypeStruct((hidden_width, rows), BF16),
            jax.ShapeDtypeStruct((narrow_hidden, rows), BF16),
        ]
    )
    scratch = (
        [pltpu.VMEM(shape, BF16) for shape in gathered]
        + [pltpu.VMEM(shape, kind) for shape, kind in saved_shapes]
        + [
            pltpu.VMEM((4 * rows, rows), F32),
            pltpu.VMEM(ends.shape, jnp.int32),
            pltpu.VMEM((rows, narrow), BF16),
            pltpu.VMEM((rows, width), BF16),
            pltpu.VMEM((rows, hidden_width), BF16),
            pltpu.VMEM((rows, narrow), BF16),
            pltpu.VMEM((rows, narrow_hidden), BF16),
            pltpu.VMEM((2, 2 * LANES, rows), BF16),
            pltpu.SemaphoreType.DMA((2,)),
            pltpu.SemaphoreType.DMA((count, 7)),
            pltpu.SemaphoreType.DMA((count, 7)),
            pltpu.SemaphoreType.DMA((count,)),
            pltpu.SemaphoreType.DMA((array_count,)),
            pltpu.SemaphoreType.DMA((saved_count,)),
            pltpu.SemaphoreType.DMA((6,)),
            pltpu.SemaphoreType.DMA((6,)),
            pltpu.SemaphoreType.DMA((7,)),
            pltpu.SemaphoreType.DMA((2, 3, 4)),
            pltpu.SemaphoreType.DMA((2, 3, 4)),
        ]
    )
    results = pl.pallas_call(
        kernel,
        out_shape=out_shape,
        in_specs=[ANYWHERE] * (4 + array_count),
        out_specs=[ANYWHERE] * len(out_shape),
        scratch_shapes=scratch,
        compiler_params=remote_params(1, 62 << 20),
        name="forward_pass",
    )(tokens, out_grad, side, ends, *shards)
    saved = results[array_count : array_count + saved_count]
    return (
        results[:array_count],
        saved[:per_block],
        saved[per_block : 2 * per_block],
        saved[2 * per_block :],
        results[array_count + saved_count :],
    )


def group_bias(bias, ends, rows):
    mine = quarter()
    key_row = lax.broadcasted_iota(jnp.int32, (4 * rows, rows), 0)
    query_row = mine * rows + lax.broadcasted_iota(jnp.int32, (4 * rows, rows), 1)
    key_clip = jnp.zeros((4 * rows, rows), jnp.int32)
    query_clip = jnp.zeros((4 * rows, rows), jnp.int32)
    for c in range(3):
        end = ends[c : c + 1, 0:1]
        key_clip = key_clip + (key_row >= end).astype(jnp.int32)
        query_clip = query_clip + (query_row >= end).astype(jnp.int32)
    bias[...] = jnp.where(key_clip == query_clip, 0.0, NEG_FILL)


def slab_backward(queries, grads, mixed, logs, key_slab, value_slab, bias, head_size):
    rows = queries.shape[0]
    keys = key_slab.shape[0]
    factor = head_size ** (-0.5) * LOG2E
    lane = lax.broadcasted_iota(jnp.int32, (rows, LANES), 1) // head_size
    key_lane = lax.broadcasted_iota(jnp.int32, (keys, LANES), 1) // head_size
    sub = lax.broadcasted_iota(jnp.int32, (LANES, rows), 0) // head_size
    pick = (
        lax.broadcasted_iota(jnp.int32, (8, LANES), 1) // head_size
        == lax.broadcasted_iota(jnp.int32, (8, LANES), 0)
    ).astype(F32)
    deltas = lax.dot_general(
        pick,
        grads.astype(F32) * mixed.astype(F32),
        (((1,), (1,)), ((), ())),
        precision=lax.Precision.HIGHEST,
        preferred_element_type=F32,
    )
    keys_t = key_slab.T
    dq = jnp.zeros((LANES, rows), F32)
    dk = jnp.zeros((keys, LANES), F32)
    dv = jnp.zeros((keys, LANES), F32)
    for head in range(LANES // head_size):
        own = jnp.where(lane == head, queries, jnp.zeros_like(queries))
        own_grad = jnp.where(lane == head, grads, jnp.zeros_like(grads))
        scores = across_lanes(key_slab, own) * factor + bias[...]
        weights = jnp.exp2(scores - logs[head : head + 1, :])
        grad_soft = across_lanes(value_slab, own_grad)
        grad_scores = (weights * (grad_soft - deltas[head : head + 1, :])).astype(BF16)
        dv = jnp.where(key_lane == head, jnp.dot(weights.astype(BF16), grads, preferred_element_type=F32), dv)
        dk = jnp.where(key_lane == head, jnp.dot(grad_scores, queries, preferred_element_type=F32), dk)
        dq = jnp.where(sub == head, jnp.dot(keys_t, grad_scores, preferred_element_type=F32), dq)
    return dq, dk, dv


def norm_backward(value, upper, gain_row):
    value = value - jnp.mean(value, axis=1, keepdims=True)
    inverse = lax.rsqrt(jnp.mean(value * value, axis=1, keepdims=True) + EPSILON)
    value = value * inverse
    scaled = upper * gain_row
    inside = (
        scaled
        - jnp.mean(scaled, axis=1, keepdims=True)
        - value * jnp.mean(scaled * value, axis=1, keepdims=True)
    )
    return (
        inverse * inside,
        jnp.sum(upper * value, axis=0, keepdims=True),
        jnp.sum(upper, axis=0, keepdims=True),
    )


def middle_back(loads, lefts_t, head_count, collective_id):
    names = list(loads)
    rows, narrow = loads["out_grad"].shape
    width = loads["wide_middle"].shape[1]
    narrow_hidden = loads["narrow_slope"].shape[1]
    wide_hidden = loads["wide_slope"].shape[1]
    slabs = narrow // LANES
    head_size = narrow // head_count
    scale = head_size ** (-0.5)
    keys = 4 * rows
    half = 2 * rows
    sizes = [left.shape[0] // 8 for left in lefts_t]
    right_widths = [narrow, narrow_hidden, narrow, 3 * narrow, narrow]
    grads = len(lefts_t)

    def kernel(*refs):
        load_refs = dict(zip(names, refs[: len(names)]))
        left_refs = refs[len(names) : len(names) + grads]
        base = len(names) + grads
        partials_out = refs[base : base + grads]
        low_out, pre_out, branch_out, middle_out, mixed_out, wide_sums_out, narrow_sums_out = refs[
            base + grads : base + grads + 7
        ]
        base += grads + 7
        bufs = dict(zip(names, refs[base : base + len(names)]))
        base += len(names)
        lefts = refs[base : base + grads]
        rights = refs[base + grads : base + 2 * grads]
        partials = refs[base + 2 * grads : base + 3 * grads]
        base += 3 * grads
        (
            bias,
            dkv,
            core_in,
            z_in,
            upper,
            grad_middle,
            grad_mixed,
            wide_low,
            wide_pre,
            wide_upper,
            wide_branch,
            wide_mixed,
            wide_sums,
            narrow_sums,
            load_sems,
            give_send,
            give_recv,
            give_own,
            right_send,
            right_recv,
            key_send,
            key_recv,
            out_sems,
        ) = refs[base:]
        me = lax.axis_index("fsdp")
        core = me & 1
        low = lax.axis_index("seq") & 1
        enter([fsdp_peer(1), mate_z()])

        def load(name):
            return pltpu.make_async_copy(load_refs[name], bufs[name], load_sems.at[names.index(name)])

        loaded = set()

        def got(name):
            if name not in loaded:
                load(name).wait()
                loaded.add(name)
            return bufs[name]

        def left_copy(which, p):
            owner = 2 * p + (core ^ 1)
            return send(
                left_refs[which].at[pl.ds(pl.multiple_of(owner * sizes[which], 16), sizes[which])],
                lefts[which].at[1, p],
                give_send.at[which, p],
                give_recv.at[which, p],
                fsdp_peer(1),
            )

        def left_own(which, p):
            owner = 2 * p + core
            return pltpu.make_async_copy(
                left_refs[which].at[pl.ds(pl.multiple_of(owner * sizes[which], 16), sizes[which])],
                lefts[which].at[0, p],
                give_own.at[which, p],
            )

        def right_copy(which):
            src = rights[which].at[pl.ds(0, rows)]
            return send(
                src, rights[which].at[pl.ds(rows, rows)], right_send.at[which], right_recv.at[which], fsdp_peer(1)
            )

        outs = [(partials[i], partials_out[i]) for i in range(grads)] + [
            (wide_low, low_out),
            (wide_pre, pre_out),
            (wide_branch, branch_out),
            (grad_middle, middle_out),
            (wide_mixed, mixed_out),
            (wide_sums, wide_sums_out),
            (narrow_sums, narrow_sums_out),
        ]

        def out_copy(i):
            return pltpu.make_async_copy(outs[i][0], outs[i][1], out_sems.at[i])

        def form(which):
            for p in range(4):
                left_copy(which, p).wait_recv()
                left_own(which, p).wait()
            right_copy(which).wait_recv()
            size = 4 * sizes[which]
            step = 512 if size > 512 else size
            total = jnp.dot(
                lefts[which][0].reshape(size, rows), rights[which][pl.ds(0, rows), :], preferred_element_type=F32
            ) + jnp.dot(
                lefts[which][1].reshape(size, rows), rights[which][pl.ds(rows, rows), :], preferred_element_type=F32
            )
            partials[which][...] = total.astype(BF16)
            out_copy(which).start()

        late = [name for name in names if name.startswith("w")]
        for name in names:
            if name not in late:
                load(name).start()

        own = pl.ds(0, rows)
        narrow_sums[...] = jnp.zeros_like(narrow_sums)
        wide_sums[...] = jnp.zeros_like(wide_sums)
        grads_in = got("out_grad")
        rights[0][own, :] = grads_in[...]
        right_copy(0).start()
        step = 2 * LANES
        got("narrow_down")
        got("narrow_slope")
        for c in range(narrow_hidden // (2 * step)):
            at = pl.ds(c * 2 * step, 2 * step)
            product = across_lanes(grads_in[...], bufs["narrow_down"][at, :])
            rights[1][own, at] = (product * bufs["narrow_slope"][:, at].astype(F32)).astype(BF16)
        right_copy(1).start()
        upper[...] = across_lanes(rights[1][own, :], got("narrow_up")[...])
        table = got("narrow_gains")
        got("narrow_middle")
        chunk = 64
        gain_sum = jnp.zeros((1, narrow), F32)
        shift_sum = jnp.zeros((1, narrow), F32)
        for i in range(rows // chunk):
            part = pl.ds(i * chunk, chunk)
            inner, gain_term, shift_term = norm_backward(
                bufs["narrow_middle"][part], upper[part], table[2:3, :]
            )
            gain_sum, shift_sum = gain_sum + gain_term, shift_sum + shift_term
            total = grads_in[part].astype(F32) + inner
            bufs["narrow_middle"][part] = total
            rights[2][part, :] = total.astype(BF16)
        narrow_sums[6:7, :] = gain_sum
        narrow_sums[7:8, :] = shift_sum
        right_copy(2).start()
        grad_mixed[...] = across_lanes(rights[2][own, :], got("narrow_out")[...]).astype(BF16)
        for name in late:
            load(name).start()
        for which in range(grads):
            for p in range(4):
                left_copy(which, p).start()
                left_own(which, p).start()
        group_bias(bias, got("ends"), rows)

        got("narrow_queries")
        got("narrow_kv")
        got("narrow_mixed")
        got("narrow_logs")

        def key_core_copy(j):
            return send(
                dkv.at[:, j, pl.ds((core ^ 1) * half, half)],
                core_in.at[:, j],
                key_send.at[0, j],
                key_recv.at[0, j],
                fsdp_peer(1),
            )

        def key_far_copy(j):
            return send(
                core_in.at[:, j, pl.ds((low ^ 1) * rows, rows)],
                z_in.at[:, j],
                key_send.at[1, j],
                key_recv.at[1, j],
                mate_z(),
            )

        def key_middle(j):
            key_core_copy(j).wait_recv()
            for kind in range(2):
                core_in[kind, j] = (
                    core_in[kind, j].astype(F32) + dkv[kind, j, pl.ds(core * half, half)].astype(F32)
                ).astype(BF16)
            key_far_copy(j).start()

        def key_end(j):
            key_far_copy(j).wait_recv()
            for kind in range(2):
                total = core_in[kind, j, pl.ds(low * rows, rows)].astype(F32) + z_in[kind, j].astype(F32)
                at = pl.ds(pl.multiple_of((1 + kind) * narrow + j * LANES, LANES), LANES)
                rights[3][own, at] = total.astype(BF16)

        @pl.loop(0, slabs)
        def _(j):
            at = pl.ds(pl.multiple_of(j * LANES, LANES), LANES)
            dq, dk, dv = slab_backward(
                bufs["narrow_queries"][:, at],
                grad_mixed[:, at],
                bufs["narrow_mixed"][:, at],
                bufs["narrow_logs"][j],
                bufs["narrow_kv"][0, j],
                bufs["narrow_kv"][1, j],
                bias,
                head_size,
            )
            rights[3][own, at] = (dq.T * scale).astype(BF16)
            dkv[0, j] = (dk * scale).astype(BF16)
            dkv[1, j] = dv.astype(BF16)
            key_core_copy(j).start()

            @pl.when(j >= 1)
            def _():
                key_middle(j - 1)

        form(0)
        key_middle(slabs - 1)
        form(1)
        form(2)
        for j in range(slabs):
            key_end(j)
        right_copy(3).start()
        upper[...] = across_lanes(rights[3][own, :], got("narrow_qkv")[...])
        got("entry")
        side = got("side")
        gain_sum = jnp.zeros((1, narrow), F32)
        shift_sum = jnp.zeros((1, narrow), F32)
        mask_sum = jnp.zeros((1, narrow), F32)
        for i in range(rows // chunk):
            part = pl.ds(i * chunk, chunk)
            inner, gain_term, shift_term = norm_backward(bufs["entry"][part], upper[part], table[0:1, :])
            gain_sum, shift_sum = gain_sum + gain_term, shift_sum + shift_term
            total = bufs["narrow_middle"][part] + inner
            hit = side[part, narrow : narrow + 1]
            mask_sum = mask_sum + jnp.sum(hit * total, axis=0, keepdims=True)
            rights[4][part, :] = (total * (1.0 - hit)).astype(BF16)
        narrow_sums[4:5, :] = gain_sum
        narrow_sums[5:6, :] = shift_sum
        narrow_sums[8:9, :] = mask_sum
        out_copy(grads + 6).start()
        right_copy(4).start()

        got("w_embed")

        for c in range(width // step):
            at = pl.ds(c * step, step)
            product = across_lanes(rights[4][own, :], bufs["w_embed"][at, :])
            grad_middle[:, at] = product
            wide_low[:, at] = product.astype(BF16)
        out_copy(grads).start()
        got("wide_down")
        got("wide_slope")

        @pl.loop(0, wide_hidden // (2 * step))
        def _(c):
            at = pl.ds(pl.multiple_of(c * 2 * step, 2 * step), 2 * step)
            product = across_lanes(wide_low[...], bufs["wide_down"][at, :])
            wide_pre[:, at] = (product * bufs["wide_slope"][:, at].astype(F32)).astype(BF16)

        out_copy(grads + 1).start()
        got("wide_up")

        @pl.loop(0, width // step)
        def _(c):
            at = pl.ds(pl.multiple_of(c * step, step), step)
            wide_upper[:, at] = across_lanes(wide_pre[...], bufs["wide_up"][at, :])

        wide_table = got("wide_gains")
        got("wide_middle")
        gain_sum = jnp.zeros((1, width), F32)
        shift_sum = jnp.zeros((1, width), F32)
        for i in range(rows // chunk):
            part = pl.ds(i * chunk, chunk)
            inner, gain_term, shift_term = norm_backward(
                bufs["wide_middle"][part], wide_upper[part], wide_table[2:3, :]
            )
            gain_sum, shift_sum = gain_sum + gain_term, shift_sum + shift_term
            total = grad_middle[part] + inner
            grad_middle[part] = total
            wide_branch[part] = total.astype(BF16)
        wide_sums[2:3, :] = gain_sum
        wide_sums[3:4, :] = shift_sum
        for i in (2, 3, 5):
            out_copy(grads + i).start()
        got("wide_out")

        for c in range(width // step):
            at = pl.ds(c * step, step)
            wide_mixed[:, at] = across_lanes(wide_branch[...], bufs["wide_out"][at, :]).astype(BF16)
        out_copy(grads + 4).start()
        form(3)
        form(4)
        for which in range(grads):
            right_copy(which).wait_send()
            for p in range(4):
                left_copy(which, p).wait_send()
        for j in range(slabs):
            key_core_copy(j).wait_send()
            key_far_copy(j).wait_send()
        for i in range(grads + 7):
            out_copy(i).wait()

    out_shape = [
        jax.ShapeDtypeStruct((4 * size, columns), BF16) for size, columns in zip(sizes, right_widths)
    ] + [
        jax.ShapeDtypeStruct((rows, width), BF16),
        jax.ShapeDtypeStruct((rows, wide_hidden), BF16),
        jax.ShapeDtypeStruct((rows, width), BF16),
        jax.ShapeDtypeStruct((rows, width), F32),
        jax.ShapeDtypeStruct((rows, width), BF16),
        jax.ShapeDtypeStruct((SMALL_ROWS, width), F32),
        jax.ShapeDtypeStruct((SMALL_ROWS, narrow), F32),
    ]
    scratch = (
        [pltpu.VMEM(loads[name].shape, loads[name].dtype) for name in names]
        + [pltpu.VMEM((2, 4, size, rows), BF16) for size in sizes]
        + [pltpu.VMEM((2 * rows, columns), BF16) for columns in right_widths]
        + [pltpu.VMEM((4 * size, columns), BF16) for size, columns in zip(sizes, right_widths)]
        + [
            pltpu.VMEM((keys, rows), F32),
            pltpu.VMEM((2, slabs, keys, LANES), BF16),
            pltpu.VMEM((2, slabs, half, LANES), BF16),
            pltpu.VMEM((2, slabs, rows, LANES), BF16),
            pltpu.VMEM((rows, narrow), F32),
            pltpu.VMEM((rows, width), F32),
            pltpu.VMEM((rows, narrow), BF16),
            pltpu.VMEM((rows, width), BF16),
            pltpu.VMEM((rows, wide_hidden), BF16),
            pltpu.VMEM((rows, width), F32),
            pltpu.VMEM((rows, width), BF16),
            pltpu.VMEM((rows, width), BF16),
            pltpu.VMEM((SMALL_ROWS, width), F32),
            pltpu.VMEM((SMALL_ROWS, narrow), F32),
            pltpu.SemaphoreType.DMA((len(names),)),
            pltpu.SemaphoreType.DMA((grads, 4)),
            pltpu.SemaphoreType.DMA((grads, 4)),
            pltpu.SemaphoreType.DMA((grads, 4)),
            pltpu.SemaphoreType.DMA((grads,)),
            pltpu.SemaphoreType.DMA((grads,)),
            pltpu.SemaphoreType.DMA((2, slabs)),
            pltpu.SemaphoreType.DMA((2, slabs)),
            pltpu.SemaphoreType.DMA((grads + 7,)),
        ]
    )
    return pl.pallas_call(
        kernel,
        out_shape=out_shape,
        in_specs=[ANYWHERE] * (len(names) + grads),
        out_specs=[ANYWHERE] * len(out_shape),
        scratch_shapes=scratch,
        compiler_params=remote_params(collective_id, 60 << 20),
        name="middle_back",
    )(*[loads[name] for name in names], *lefts_t)


class Unit:
    def __init__(self, index, first, columns, order, place):
        self.index = index
        self.first = first
        self.columns = columns
        self.near, self.far = order
        self.place = place


def cut_columns(shapes, most):
    units = []
    for index, (rows, columns) in enumerate(shapes):
        pieces = 1
        while rows * (columns // pieces) > most and (columns // pieces) % (2 * LANES) == 0:
            pieces *= 2
        for place in range(pieces):
            order = (2, 4) if len(units) % 2 == 0 else (4, 2)
            units.append(Unit(index, place * (columns // pieces), columns // pieces, order, place))
    return units


def back_and_sum(
    partials,
    lefts_t,
    rights,
    queries,
    keys_values,
    mixed,
    grad_mixed,
    logs,
    ends,
    w_qkv,
    tokens,
    grad_middle,
    gains,
    wide_sums,
    narrow_sums,
    head_count,
    collective_id,
):
    rows, width = queries.shape
    triple = 3 * width
    keys = 4 * rows
    slabs = width // LANES
    head_size = width // head_count
    per_slab = LANES // head_size
    scale = head_size ** (-0.5)
    factor = scale * LOG2E
    part_rows = w_qkv.shape[1]

    given = len(partials)
    formed = [(left.shape[0] // 8, right.shape[1]) for left, right in zip(lefts_t, rights)]
    shapes = [partial.shape[1:] for partial in partials] + formed + [(part_rows, triple), (SMALL_ROWS, LANES)]
    up_index = given + 1
    qkv_index, small_index = given + 3, given + 4
    array_count = given + 5
    ring = 5
    units = cut_columns(shapes, 70000)
    count = len(units)
    pieces = [sum(1 for unit in units if unit.index == index) for index in range(array_count)]

    def piece_shape(index):
        return (shapes[index][0], shapes[index][1] // pieces[index])

    def kernel(*refs):
        sources = refs[:given]
        left_refs = refs[given : given + 4]
        right_refs = refs[given + 4 : given + 7]
        base = given + 7
        (
            q_ref,
            kv_ref,
            mixed_ref,
            grad_ref,
            log_ref,
            ends_ref,
            w_ref,
            tokens_ref,
            middle_ref,
            gain_ref,
            wide_sums_ref,
            narrow_sums_ref,
        ) = refs[base : base + 12]
        base += 12
        results = refs[base : base + array_count]
        token_out, up_inbox = refs[base + array_count : base + array_count + 2]
        rest = list(refs[base + array_count + 2 :])
        acc, near_in, far_in, outer_in, inner_in = [
            rest[group * array_count : (group + 1) * array_count] for group in range(5)
        ]
        late_out = rest[5 * array_count : 5 * array_count + 4]
        lefts = rest[5 * array_count + 4 : 5 * array_count + 8]
        (
            low_both,
            branch_both,
            up_buf,
            kv_buf,
            give_send,
            give_recv,
            give_own,
            up_sems,
            kv_sems,
            small_out,
            bias,
            dkv,
            core_in,
            z_in,
            dqkv,
            w_buf,
            grad_normed,
            token_buf,
            norm_sums,
            norm_sums_in,
            narrow_in,
            send_sems,
            recv_sems,
            own_sems,
            out_sems,
            key_send,
            key_recv,
            row_send,
            row_recv,
            w_sems,
        ) = rest[5 * array_count + 8 :]

        me = lax.axis_index("fsdp")
        place = lax.axis_index("seq")
        core = me & 1
        chip = me >> 1
        high = place >> 1
        low = place & 1
        inner = jnp.logical_or(place == 1, place == 2)
        outer = jnp.logical_not(inner)
        trades = core != high
        trade_peer = ((me & 6) | high, core * 2 + low)
        mate = seq_peer(place ^ 1)
        across = seq_peer(3 - place)

        barrier = pltpu.get_barrier_semaphore()
        for peer in (fsdp_peer(1), fsdp_peer(2), fsdp_peer(4), mate):
            pl.semaphore_signal(barrier, inc=1, device_id=peer, device_id_type=MESH)

        @pl.when(inner)
        def _():
            pl.semaphore_signal(barrier, inc=1, device_id=across, device_id_type=MESH)

        @pl.when(trades)
        def _():
            pl.semaphore_signal(barrier, inc=1, device_id=trade_peer, device_id_type=MESH)

        pl.semaphore_wait(barrier, 4 + inner.astype(jnp.int32) + trades.astype(jnp.int32))


        def span(unit):
            return pl.ds(unit.first, unit.columns)

        def chip_of(unit, slot):
            return chip ^ (((slot // 2) * unit.near + (slot % 2) * unit.far) // 2)

        def near_copy(u, slot):
            unit = units[u]
            if given <= unit.index <= qkv_index:
                src = late_out[unit.index - given].at[unit.place % ring, slot]
            elif unit.index == small_index:
                src = small_out.at[slot]
            else:
                src = sources[unit.index].at[chip_of(unit, 2 + slot), :, span(unit)]
            return send(
                src,
                near_in[unit.index].at[unit.place, slot],
                send_sems.at[u, slot],
                recv_sems.at[u, slot],
                fsdp_peer(unit.near),
            )

        def own_copy(u, slot):
            unit = units[u]
            return pltpu.make_async_copy(
                sources[unit.index].at[chip_of(unit, slot), :, span(unit)],
                acc[unit.index].at[unit.place, slot],
                own_sems.at[u, slot],
            )

        def far_copy(u):
            unit = units[u]
            return send(
                acc[unit.index].at[unit.place, 1],
                far_in[unit.index].at[unit.place],
                send_sems.at[u, 2],
                recv_sems.at[u, 2],
                fsdp_peer(unit.far),
            )

        def inward_copy(u):
            unit = units[u]
            return send(
                acc[unit.index].at[unit.place, 0],
                outer_in[unit.index].at[unit.place],
                send_sems.at[u, 3],
                recv_sems.at[u, 3],
                mate,
            )

        def across_copy(u):
            unit = units[u]
            return send(
                outer_in[unit.index].at[unit.place],
                inner_in[unit.index].at[unit.place],
                send_sems.at[u, 4],
                recv_sems.at[u, 4],
                across,
            )

        def outward_copy(u):
            unit = units[u]
            return send(
                acc[unit.index].at[unit.place, 0],
                results[unit.index].at[:, span(unit)],
                send_sems.at[u, 5],
                recv_sems.at[u, 5],
                mate,
            )

        def out_copy(u):
            unit = units[u]
            return pltpu.make_async_copy(
                acc[unit.index].at[unit.place, 0], results[unit.index].at[:, span(unit)], out_sems.at[u]
            )

        def add_into(dst, left, right):
            total_rows, columns = dst.shape
            step = 16
            while total_rows % (2 * step) == 0 and 2 * step * columns <= 32768:
                step *= 2

            @pl.loop(0, total_rows // step)
            def _(i):
                part = pl.ds(pl.multiple_of(i * step, step), step)
                dst[part] = (left[part].astype(F32) + right[part].astype(F32)).astype(BF16)

        def early(u):
            return units[u].index < given

        def near_start(u):
            if given <= units[u].index <= qkv_index:
                form(u)
            elif units[u].index == small_index:
                form_small(u)
            near_copy(u, 1).start()
            near_copy(u, 0).start()

        def stage_far(u):
            unit = units[u]
            for slot in (1, 0):
                near_copy(u, slot).wait_recv()
                if early(u):
                    own_copy(u, slot).wait()
                target = acc[unit.index].at[unit.place, slot]
                add_into(target, target, near_in[unit.index].at[unit.place, slot])
                if slot == 1:
                    far_copy(u).start()

        def stage_inward(u):
            unit = units[u]
            far_copy(u).wait_recv()
            target = acc[unit.index].at[unit.place, 0]
            add_into(target, target, far_in[unit.index].at[unit.place])

            @pl.when(outer)
            def _():
                inward_copy(u).start()

        def stage_across(u):
            unit = units[u]

            @pl.when(inner)
            def _():
                inward_copy(u).wait_recv()
                target = outer_in[unit.index].at[unit.place]
                add_into(target, target, acc[unit.index].at[unit.place, 0])
                across_copy(u).start()

        def stage_outward(u):
            unit = units[u]

            @pl.when(inner)
            def _():
                across_copy(u).wait_recv()
                add_into(
                    acc[unit.index].at[unit.place, 0],
                    outer_in[unit.index].at[unit.place],
                    inner_in[unit.index].at[unit.place],
                )
                outward_copy(u).start()
                out_copy(u).start()

        ahead = 4
        lags = ((stage_far, 0), (stage_inward, 2), (stage_across, 4), (stage_outward, 6))
        total_ticks = count + 6

        def tick(t):
            if t + ahead < count:
                near_start(t + ahead)
            for stage, lag in lags:
                if 0 <= t - lag < count:
                    stage(t - lag)


        half = 2 * rows

        def group(g):
            return pl.ds(2 * g, 2)

        def key_core_copy(g):
            return send(
                dkv.at[:, group(g), pl.ds((core ^ 1) * half, half)],
                core_in.at[:, group(g)],
                key_send.at[0, g],
                key_recv.at[0, g],
                fsdp_peer(1),
            )

        def key_far_copy(g):
            return send(
                core_in.at[:, group(g), pl.ds((low ^ 1) * rows, rows)],
                z_in.at[:, group(g)],
                key_send.at[1, g],
                key_recv.at[1, g],
                mate,
            )

        def key_middle(g):
            key_core_copy(g).wait_recv()
            for kind in range(2):
                for k in range(2):

                    @pl.loop(0, half // LANES)
                    def _(i):
                        part = pl.ds(pl.multiple_of(i * LANES, LANES), LANES)
                        own = pl.ds(pl.multiple_of(core * half + i * LANES, LANES), LANES)
                        core_in[kind, 2 * g + k, part] = (
                            core_in[kind, 2 * g + k, part].astype(F32) + dkv[kind, 2 * g + k, own].astype(F32)
                        ).astype(BF16)

            key_far_copy(g).start()

        def key_end(g):
            key_far_copy(g).wait_recv()
            for kind in range(2):
                for k in range(2):
                    slab = 2 * g + k

                    @pl.loop(0, rows // LANES)
                    def _(i):
                        part = pl.ds(pl.multiple_of(i * LANES, LANES), LANES)
                        own = pl.ds(pl.multiple_of(low * rows + i * LANES, LANES), LANES)
                        total = core_in[kind, slab, own].astype(F32) + z_in[kind, slab, part].astype(F32)
                        dqkv[part, pl.ds((1 + kind) * width + slab * LANES, LANES)] = total.astype(BF16)


        def kv_copy(j):
            return pltpu.make_async_copy(kv_ref.at[:, j], kv_buf.at[j % 2], kv_sems.at[j % 2])

        def slab_back(j):
            kv_copy(j).wait()

            @pl.when(j + 1 < slabs)
            def _():
                kv_copy(j + 1).start()

            at = pl.ds(pl.multiple_of(j * LANES, LANES), LANES)
            dq, dk, dv = slab_backward(
                q_ref[:, at],
                grad_ref[:, at],
                mixed_ref[:, at],
                log_ref[j],
                kv_buf[j % 2, 0],
                kv_buf[j % 2, 1],
                bias,
                head_size,
            )
            dqkv[pl.ds(0, rows), at] = (dq.T * scale).astype(BF16)
            dkv[0, j] = (dk * scale).astype(BF16)
            dkv[1, j] = dv.astype(BF16)


        def row_copy(part):
            columns = pl.ds(0, width) if part == 0 else pl.ds(width, 2 * width)
            return send(
                dqkv.at[pl.ds(0, rows), columns],
                dqkv.at[pl.ds(rows, rows), columns],
                row_send.at[part],
                row_recv.at[part],
                fsdp_peer(1),
            )


        def left_copy(which, p):
            size = lefts_t[which].shape[0] // 8
            owner = 2 * p + (core ^ 1)
            return send(
                left_refs[which].at[pl.ds(pl.multiple_of(owner * size, LANES), size)],
                lefts[which].at[1, p],
                give_send.at[which, p],
                give_recv.at[which, p],
                fsdp_peer(1),
            )

        def left_own(which, p):
            size = lefts_t[which].shape[0] // 8
            owner = 2 * p + core
            return pltpu.make_async_copy(
                left_refs[which].at[pl.ds(pl.multiple_of(owner * size, LANES), size)],
                lefts[which].at[0, p],
                give_own.at[which, p],
            )

        def right_copy(which):
            dst = (low_both.at[pl.ds(rows, rows)], up_inbox, branch_both.at[pl.ds(rows, rows)])[which]
            return send(
                right_refs[which], dst, give_send.at[4, which], give_recv.at[4, which], fsdp_peer(1)
            )

        def right_own(which):
            dst = (low_both, None, branch_both)[which].at[pl.ds(0, rows)]
            return pltpu.make_async_copy(right_refs[which], dst, give_own.at[4, which])

        def give(which):
            for p in range(4):
                left_copy(which, p).start()
                left_own(which, p).start()
            if which < 3:
                right_copy(which).start()
                if which != 1:
                    right_own(which).start()

        def take(which):
            for p in range(4):
                left_copy(which, p).wait_recv()
                left_own(which, p).wait()
            if which < 3:
                right_copy(which).wait_recv()
                if which != 1:
                    right_own(which).wait()

        def up_copies(unit):
            slot = unit.place % 2
            return [
                pltpu.make_async_copy(
                    right_refs[1].at[:, span(unit)], up_buf.at[slot, pl.ds(0, rows)], up_sems.at[slot, 0]
                ),
                pltpu.make_async_copy(
                    up_inbox.at[:, span(unit)], up_buf.at[slot, pl.ds(rows, rows)], up_sems.at[slot, 1]
                ),
            ]

        near_done = set()

        def form(u):
            unit = units[u]
            which = unit.index - given
            if unit.place == 0:
                take(which)
                if unit.index == up_index:
                    for one in up_copies(unit):
                        one.start()
            if unit.place >= ring:
                near_copy(u - ring, 0).wait_send()
                near_copy(u - ring, 1).wait_send()
                near_done.add(u - ring)
            if unit.index == up_index:
                if unit.place + 1 < pieces[up_index]:
                    for one in up_copies(units[u + 1]):
                        one.start()
                for one in up_copies(unit):
                    one.wait()
                right = up_buf.at[unit.place % 2]
            else:
                right = (low_both, None, branch_both, dqkv)[which].at[:, span(unit)]
            def block_of(p):
                return (
                    jnp.dot(lefts[which][0, p], right[pl.ds(0, rows)], preferred_element_type=F32)
                    + jnp.dot(lefts[which][1, p], right[pl.ds(rows, rows)], preferred_element_type=F32)
                ).astype(BF16)

            @pl.loop(0, 2)
            def _(slot):
                p = chip ^ (unit.near // 2) ^ (slot * (unit.far // 2))
                late_out[which][unit.place % ring, slot] = block_of(p)

            @pl.loop(0, 2)
            def _(slot):
                acc[unit.index][unit.place, slot] = block_of(chip ^ (slot * (unit.far // 2)))


        blocks = 8

        def w_copy(block):
            return pltpu.make_async_copy(w_ref.at[block], w_buf.at[block % 2], w_sems.at[block % 2])

        def norm_copy():
            return send(norm_sums, norm_sums_in, row_send.at[2], row_recv.at[2], fsdp_peer(1))

        def narrow_copy():
            return send(narrow_sums_ref, narrow_in, row_send.at[4], row_recv.at[4], fsdp_peer(1))

        def input_gradient():
            @pl.loop(0, blocks)
            def _(block):
                w_copy(block).wait()
                at = pl.ds(pl.multiple_of(block * part_rows, part_rows), part_rows)
                grad_normed[:, at] = across_lanes(dqkv[pl.ds(0, rows), :], w_buf[block % 2])

                @pl.when(block + 2 < blocks)
                def _():
                    w_copy(block + 2).start()

            step = 64
            gain_sum = jnp.zeros((1, width), F32)
            shift_sum = jnp.zeros((1, width), F32)
            for i in range(rows // step):
                part = pl.ds(i * step, step)
                inside, gain_term, shift_term = norm_backward(
                    tokens_ref[part].astype(F32), grad_normed[part], gain_ref[0:1, :]
                )
                gain_sum, shift_sum = gain_sum + gain_term, shift_sum + shift_term
                token_buf[part] = (middle_ref[part] + inside).astype(BF16)
            norm_sums[...] = wide_sums_ref[...]
            norm_sums[0:1, :] = gain_sum
            norm_sums[1:2, :] = shift_sum
            norm_copy().start()

            @pl.when(trades)
            def _():
                token_send().start()

            @pl.when(jnp.logical_not(trades))
            def _():
                token_keep().start()

        def token_send():
            return send(token_buf, token_out, row_send.at[3], row_recv.at[3], trade_peer)

        def token_keep():
            return pltpu.make_async_copy(token_buf, token_out, w_sems.at[2])

        def form_small(u):
            unit = units[u]
            norm_copy().wait_recv()
            narrow_copy().wait_recv()
            norm_sums_in[...] = norm_sums[...] + norm_sums_in[...]
            narrow_both = narrow_sums_ref[...] + narrow_in[...]
            narrow = narrow_both.shape[1]
            narrow_part = narrow // 8
            source_lane = lax.broadcasted_iota(jnp.int32, (narrow, LANES), 0)
            lane = lax.broadcasted_iota(jnp.int32, (narrow, LANES), 1)
            for slot in range(4):
                owner = chip_of(unit, slot) * 2 + core
                picked = jnp.logical_and(source_lane == owner * narrow_part + lane, lane < narrow_part)
                block = norm_sums_in[:, pl.ds(pl.multiple_of(owner * LANES, LANES), LANES)] + jnp.dot(
                    narrow_both,
                    picked.astype(F32),
                    precision=lax.Precision.HIGHEST,
                    preferred_element_type=F32,
                )
                block = block.astype(BF16)
                if slot < 2:
                    acc[unit.index][unit.place, slot] = block
                else:
                    small_out[slot - 2] = block


        first_late = min(u for u in range(count) if units[u].index == qkv_index)
        for u in range(ahead):
            near_start(u)
        for which in range(4):
            give(which)
        for u in range(count):
            if early(u):
                for slot in range(2):
                    own_copy(u, slot).start()
        kv_copy(0).start()
        narrow_copy().start()
        w_copy(0).start()
        w_copy(1).start()
        group_bias(bias, ends_ref, rows)
        ticks_inside = first_late - ahead

        @pl.loop(0, slabs)
        def _(j):
            slab_back(j)

            @pl.when(j % 2 == 1)
            def _():
                key_core_copy(j // 2).start()

            @pl.when(jnp.logical_and(j % 2 == 0, j >= 2))
            def _():
                key_middle(j // 2 - 1)

            done = 0
            for k in range(slabs):
                until = (k + 1) * ticks_inside // slabs

                @pl.when(j == k)
                def _(done=done, until=until):
                    for t in range(done, until):
                        tick(t)

                done = until

        row_copy(0).start()
        key_middle(slabs // 2 - 1)
        for g in range(slabs // 2):
            key_end(g)
        row_copy(1).start()
        row_copy(0).wait_recv()
        row_copy(1).wait_recv()
        done_input = False
        for t in range(ticks_inside, total_ticks):
            if not done_input and t + ahead >= count - 1:
                input_gradient()
                done_input = True
            tick(t)

        for u in range(count):
            if u not in near_done:
                near_copy(u, 0).wait_send()
                near_copy(u, 1).wait_send()
            far_copy(u).wait_send()
        for which in range(4):
            for p in range(4):
                left_copy(which, p).wait_send()
            if which < 3:
                right_copy(which).wait_send()

        for u in range(count):

            @pl.when(inner)
            def _():
                across_copy(u).wait_send()
                outward_copy(u).wait_send()
                out_copy(u).wait()

            @pl.when(outer)
            def _():
                inward_copy(u).wait_send()
                outward_copy(u).wait_recv()

        for g in range(slabs // 2):
            key_core_copy(g).wait_send()
            key_far_copy(g).wait_send()
        row_copy(0).wait_send()
        row_copy(1).wait_send()
        norm_copy().wait_send()
        narrow_copy().wait_send()

        @pl.when(trades)
        def _():
            token_send().wait()

        @pl.when(jnp.logical_not(trades))
        def _():
            token_keep().wait()

    scratch = []
    for slots in ((2,), (2,), (), (), ()):
        for index in range(array_count):
            scratch.append(pltpu.VMEM((pieces[index],) + slots + piece_shape(index), BF16))
    for index in range(given, qkv_index + 1):
        scratch.append(pltpu.VMEM((min(ring, pieces[index]), 2) + piece_shape(index), BF16))
    for left in lefts_t:
        scratch.append(pltpu.VMEM((2, 4, left.shape[0] // 8, rows), BF16))
    scratch += [
        pltpu.VMEM((2 * rows, width), BF16),
        pltpu.VMEM((2 * rows, width), BF16),
        pltpu.VMEM((2, 2 * rows, piece_shape(up_index)[1]), BF16),
        pltpu.VMEM((2, 2, keys, LANES), BF16),
        pltpu.SemaphoreType.DMA((5, 4)),
        pltpu.SemaphoreType.DMA((5, 4)),
        pltpu.SemaphoreType.DMA((5, 4)),
        pltpu.SemaphoreType.DMA((2, 2)),
        pltpu.SemaphoreType.DMA((2,)),
        pltpu.VMEM((2, SMALL_ROWS, LANES), BF16),
        pltpu.VMEM((keys, rows), F32),
        pltpu.VMEM((2, slabs, keys, LANES), BF16),
        pltpu.VMEM((2, slabs, 2 * rows, LANES), BF16),
        pltpu.VMEM((2, slabs, rows, LANES), BF16),
        pltpu.VMEM((2 * rows, triple), BF16),
        pltpu.VMEM((2, part_rows, triple), BF16),
        pltpu.VMEM((rows, width), F32),
        pltpu.VMEM((rows, width), BF16),
        pltpu.VMEM((SMALL_ROWS, width), F32),
        pltpu.VMEM((SMALL_ROWS, width), F32),
        pltpu.VMEM(narrow_sums.shape, F32),
        pltpu.SemaphoreType.DMA((count, 6)),
        pltpu.SemaphoreType.DMA((count, 6)),
        pltpu.SemaphoreType.DMA((count, 2)),
        pltpu.SemaphoreType.DMA((count,)),
        pltpu.SemaphoreType.DMA((2, slabs // 2)),
        pltpu.SemaphoreType.DMA((2, slabs // 2)),
        pltpu.SemaphoreType.DMA((5,)),
        pltpu.SemaphoreType.DMA((5,)),
        pltpu.SemaphoreType.DMA((3,)),
    ]
    return pl.pallas_call(
        kernel,
        out_shape=[jax.ShapeDtypeStruct(shape, BF16) for shape in shapes]
        + [jax.ShapeDtypeStruct((rows, width), BF16), jax.ShapeDtypeStruct(rights[1].shape, BF16)],
        in_specs=[ANYWHERE] * (given + 7)
        + [IN_VMEM, ANYWHERE]
        + [IN_VMEM] * 4
        + [ANYWHERE]
        + [IN_VMEM] * 5,
        out_specs=[ANYWHERE] * (array_count + 2),
        scratch_shapes=scratch,
        compiler_params=remote_params(collective_id, 61 << 20),
        name="back_and_sum",
    )(
        *partials,
        *lefts_t,
        *rights,
        queries,
        keys_values,
        mixed,
        grad_mixed,
        logs,
        ends,
        w_qkv,
        tokens,
        grad_middle,
        gains,
        wide_sums,
        narrow_sums,
    )


def widen(arrays, plain):
    count = len(arrays)
    extra = len(plain)
    total = count + extra

    def kernel(*refs):
        sources, results = refs[:total], refs[total : 2 * total]
        narrow, wide = (
            refs[2 * total : 2 * total + count],
            refs[2 * total + count : 2 * total + 2 * count],
        )
        hold = refs[2 * total + 2 * count : 2 * total + 2 * count + extra]
        in_sems, out_sems = refs[2 * total + 2 * count + extra :]

        def read(i):
            dst = narrow[i] if i < count else hold[i - count]
            return pltpu.make_async_copy(sources[i], dst, in_sems.at[i])

        def write(i):
            src = wide[i] if i < count else hold[i - count]
            return pltpu.make_async_copy(src, results[i], out_sems.at[i])

        order = list(range(count, total)) + sorted(range(count), key=lambda i: -arrays[i].size)
        for i in order:
            read(i).start()
        for i in order:
            if i >= count:
                read(i).wait()
                write(i).start()
                continue
            rows, columns = arrays[i].shape
            step = 16
            while rows % (2 * step) == 0 and 2 * step * columns <= 32768:
                step *= 2
            read(i).wait()

            @pl.loop(0, rows // step)
            def _(k):
                part = pl.ds(pl.multiple_of(k * step, step), step)
                wide[i][part] = narrow[i][part].astype(F32)

            write(i).start()
        for i in range(total):
            write(i).wait()

    return pl.pallas_call(
        kernel,
        out_shape=[jax.ShapeDtypeStruct(one.shape, F32) for one in arrays]
        + [jax.ShapeDtypeStruct(one.shape, one.dtype) for one in plain],
        in_specs=[ANYWHERE] * total,
        out_specs=[ANYWHERE] * total,
        scratch_shapes=[pltpu.VMEM(one.shape, BF16) for one in arrays]
        + [pltpu.VMEM(one.shape, F32) for one in arrays]
        + [pltpu.VMEM(one.shape, one.dtype) for one in plain]
        + [pltpu.SemaphoreType.DMA((total,)), pltpu.SemaphoreType.DMA((total,))],
        compiler_params=pltpu.CompilerParams(vmem_limit_bytes=61 << 20),
        name="widen",
    )(*arrays, *plain)


def fast_local(
    tokens,
    clip_lengths,
    target_pos,
    out_grad,
    norm1_gain,
    norm1_bias,
    w_qkv,
    w_out,
    norm2_gain,
    norm2_bias,
    w_fc1,
    w_fc2,
    w_embed,
    mask_token,
    pred_norm1_gain,
    pred_norm1_bias,
    pred_qkv,
    pred_out,
    pred_norm2_gain,
    pred_norm2_bias,
    pred_fc1,
    pred_fc2,
):
    rows, width = tokens.shape
    narrow = out_grad.shape[1]
    wide_part = norm1_gain.shape[0]
    narrow_part = mask_token.shape[0]
    me = lax.axis_index("fsdp")
    core = me & 1
    wide_small = jnp.pad(
        jnp.stack([norm1_gain, norm1_bias, norm2_gain, norm2_bias]), ((0, SMALL_ROWS - 4), (0, 0))
    )
    narrow_small = jnp.stack(
        [pred_norm1_gain, pred_norm1_bias, pred_norm2_gain, pred_norm2_bias, mask_token]
    )
    here = (jnp.arange(narrow, dtype=jnp.int32) // narrow_part == me)[None, :]
    narrow_small = jnp.where(here, jnp.tile(narrow_small, (1, 8)), jnp.zeros((), BF16))
    narrow_small = jnp.pad(narrow_small, ((0, SMALL_ROWS - 5), (0, 0)))

    order = jnp.arange(clip_lengths.shape[1], dtype=jnp.int32)
    clip_ends = jnp.sum(jnp.where(order[None, :] <= order[:, None], clip_lengths, 0), axis=1)
    first_rows = lax.axis_index("seq") * rows + jnp.arange(rows, dtype=jnp.int32)
    past_end = (first_rows[:, None] >= clip_ends[None, :]).astype(jnp.int32)
    rel_rows = first_rows - jnp.sum(clip_lengths[0][None, :] * past_end, axis=1)
    matches = jnp.arange(rows, dtype=jnp.int32)[:, None] == target_pos[0, 0][None, :]
    hit_rows = jnp.sum(matches.astype(F32), axis=1)
    side = jnp.concatenate(
        [position_table(rel_rows, narrow), jnp.broadcast_to(hit_rows[:, None], (rows, LANES))], axis=1
    )
    ends = jnp.pad(jnp.broadcast_to(clip_ends[:, None], (3, LANES)), ((0, 5), (0, 0)))

    whole, kept, narrow_kept, rest, traded = forward_pass(
        tokens,
        out_grad,
        side,
        ends,
        [
            wide_small,
            narrow_small,
            w_qkv,
            w_out,
            w_fc1,
            w_fc2,
            w_embed,
            pred_qkv,
            pred_out,
            pred_fc1,
            pred_fc2,
        ],
        HEADS,
        P_HEADS,
    )
    context_t, entry, side, tokens, gains, narrow_gains = rest
    out_grad, ends, context_out, predicted, hidden_t, narrow_hidden_t = traded
    normed_t, queries, keys_values, mixed, logs, middle, normed_mid_t, slope, mixed_t = kept
    (
        narrow_normed_t,
        narrow_queries,
        narrow_kv,
        narrow_mixed,
        narrow_logs,
        narrow_middle,
        narrow_mid_t,
        narrow_slope,
        narrow_mixed_t,
    ) = narrow_kept

    results = middle_back(
        dict(
            out_grad=out_grad,
            narrow_down=whole[10],
            narrow_slope=narrow_slope,
            narrow_up=whole[9],
            narrow_gains=narrow_gains,
            narrow_middle=narrow_middle,
            narrow_out=whole[8],
            ends=ends,
            narrow_queries=narrow_queries,
            narrow_kv=narrow_kv.reshape(2, narrow // LANES, 4 * rows, LANES),
            narrow_mixed=narrow_mixed,
            narrow_logs=narrow_logs,
            narrow_qkv=whole[7],
            entry=entry,
            side=side,
            w_embed=whole[6],
            wide_down=whole[5],
            wide_slope=slope,
            wide_up=whole[4],
            wide_gains=gains,
            wide_middle=middle,
            wide_out=whole[3],
        ),
        [narrow_hidden_t, narrow_mid_t, narrow_mixed_t, narrow_normed_t, context_t],
        P_HEADS,
        2,
    )
    partials = [one.reshape(4, one.shape[0] // 4, one.shape[1]) for one in results[:5]]
    grad_low, grad_pre, grad_branch, grad_middle, grad_mixed, wide_sums, narrow_sums = results[5:]
    results = back_and_sum(
        partials,
        [hidden_t, normed_mid_t, mixed_t, normed_t],
        [grad_low, grad_pre, grad_branch],
        queries,
        keys_values.reshape(2, width // LANES, 4 * rows, LANES),
        mixed,
        grad_mixed,
        logs,
        ends,
        whole[2].reshape(8, wide_part, 3 * width),
        tokens,
        grad_middle,
        gains,
        wide_sums,
        narrow_sums,
        HEADS,
        3,
    )
    final = widen(results[:-3], [results[-2], context_out, predicted])
    sums, (token_grad, context_out, predicted) = final[:-3], final[-3:]
    small = results[-3].astype(F32)
    narrow_out = [small[4 + i, :narrow_part] for i in range(5)]
    return (
        context_out,
        predicted,
        token_grad,
        small[0],
        small[1],
        sums[8],
        sums[7],
        small[2],
        small[3],
        sums[6],
        sums[5],
        sums[4],
        narrow_out[4],
        narrow_out[0],
        narrow_out[1],
        sums[3],
        sums[2],
        narrow_out[2],
        narrow_out[3],
        sums[1],
        sums[0],
    )


def solution(mesh):
    body = fast_local if fits_fast(mesh) else local
    return jax.shard_map(
        body,
        mesh=mesh,
        in_specs=(
            P(("fsdp", "seq"), None),
            P("fsdp", None),
            P("fsdp", "seq", None),
            P(("fsdp", "seq"), None),
            P("fsdp"),
            P("fsdp"),
            P("fsdp", None),
            P("fsdp", None),
            P("fsdp"),
            P("fsdp"),
            P("fsdp", None),
            P("fsdp", None),
            P("fsdp", None),
            P("fsdp"),
            P("fsdp"),
            P("fsdp"),
            P("fsdp", None),
            P("fsdp", None),
            P("fsdp"),
            P("fsdp"),
            P("fsdp", None),
            P("fsdp", None),
        ),
        out_specs=(
            P(("fsdp", "seq"), None),
            P(("fsdp", "seq"), None),
            P(("fsdp", "seq"), None),
            P("fsdp"),
            P("fsdp"),
            P("fsdp", None),
            P("fsdp", None),
            P("fsdp"),
            P("fsdp"),
            P("fsdp", None),
            P("fsdp", None),
            P("fsdp", None),
            P("fsdp"),
            P("fsdp"),
            P("fsdp"),
            P("fsdp", None),
            P("fsdp", None),
            P("fsdp"),
            P("fsdp"),
            P("fsdp", None),
            P("fsdp", None),
        ),
        check_vma=False,
    )
```
